32 devices in a mesh: dp: 8 (over z, x), fsdp: 4 (over y, core).
Axes of the slice: x: 2, y: 2, z: 4, core: 2. Of those that a mesh axis runs over, the one named last changes fastest.
Arguments:
- block_in: float32 [32, 334, 1152], P(('dp', 'fsdp')), may hold values from -6 to 6
- skip_in: float32 [32, 334, 1152], P(('dp', 'fsdp')), may hold values from -6 to 6
- out_grad: float32 [32, 334, 1152], P(('dp', 'fsdp')), may hold values from -6 to 6
- caption_len: int32 [32], P(('dp', 'fsdp')), may hold values from 1 to 77
- skip_w: float32 [2654208], P(('dp', 'fsdp')), may hold values from -0.125 to 0.125
- qkv_w: float32 [3981312], P(('dp', 'fsdp')), may hold values from -0.1875 to 0.1875
- proj_w: float32 [1327104], P(('dp', 'fsdp')), may hold values from -1.5 to 1.5
- fc1_w: float32 [5308416], P(('dp', 'fsdp')), may hold values from -0.1875 to 0.1875
- fc2_w: float32 [5308416], P(('dp', 'fsdp')), may hold values from -0.09375 to 0.09375
- vectors: float32 [12672], P('dp'), may hold values from -0.9 to 1.5
Outputs:
- block_out: float32 [32, 334, 1152], P(('dp', 'fsdp'))
- in_grad: float32 [32, 334, 1152], P(('dp', 'fsdp'))
- skip_grad: float32 [32, 334, 1152], P(('dp', 'fsdp'))
- skip_w_grad: float32 [2654208], P(('dp', 'fsdp'))
- qkv_w_grad: float32 [3981312], P(('dp', 'fsdp'))
- proj_w_grad: float32 [1327104], P(('dp', 'fsdp'))
- fc1_w_grad: float32 [5308416], P(('dp', 'fsdp'))
- fc2_w_grad: float32 [5308416], P(('dp', 'fsdp'))
- vectors_grad: float32 [12672], P('dp')
The draws below stay inside these ranges and needn't reach their ends.
All inputs are finite; a program needn't handle non-finite values.
Results may differ from the reference program's by a relative error of at most 0.012.
Values may be sent and summed in bfloat16 or wider, within the bound.
A program may use at most 320 MiB of HBM per device.

```python
import jax
import jax.numpy as jnp
from jax import lax

D = 1152
HEADS = 16
FF = 4608
CAPTION = 77
ITEMS_DEV = 1
SEQ = 334
ITEMS = 32
N_FSDP = 4


def draw_vectors(key, part):
    keys = jax.random.split(key, 2)
    gains = jax.random.uniform(keys[0], (2, D), jnp.float32, 0.5, 1.5)
    shifts = 0.3 * jax.random.truncated_normal(keys[1], -3.0, 3.0, (5 * D + FF,), jnp.float32)
    return jnp.concatenate([gains[0], shifts[0:D], gains[1], shifts[D:2 * D], shifts[2 * D:]])


def touch_ends(entries, stream_key, low, high):
    spot = [jax.random.randint(jax.random.fold_in(stream_key, axis), (), 0, length) for axis, length in enumerate(entries.shape)]
    widest = entries.shape.index(max(entries.shape))
    next_to = spot[:widest] + [(spot[widest] + 1) % entries.shape[widest]] + spot[widest + 1:]
    return entries.at[tuple(spot)].set(low).at[tuple(next_to)].set(high)


def levels(own_key, shape, shards, least, high):
    level = 1.0
    for dim, shards_of in shards:
        heights = jax.random.uniform(jax.random.fold_in(jax.random.fold_in(own_key, 6), dim), (shards_of,), jnp.float32, least / len(shards), high / len(shards))
        level = level * jnp.repeat(jnp.exp(heights), shape[dim] // shards_of).reshape((-1,) + (1,) * (len(shape) - 1 - dim))
    return level


def gaussian(own_key, extent, scale, bound, cuts=(), held_as=jnp.bfloat16):
    values = jax.random.normal(own_key, extent, jnp.float32) * scale
    if len(cuts) > 0:
        values = levels(own_key, extent, cuts, -0.22, 0.18) * values
    return jnp.clip(values, min=-bound, max=bound).astype(held_as)


def setup_inputs(seed: int = 0) -> dict:
    splits = jax.random.split(jax.random.key(seed), 11)
    return {
        "block_in": gaussian(splits[0], (ITEMS, SEQ, D), 1.0, 6.0, ((0, 32),), jnp.float32),
        "skip_in": gaussian(splits[1], (ITEMS, SEQ, D), 1.0, 6.0, ((0, 32),), jnp.float32),
        "out_grad": gaussian(splits[2], (ITEMS, SEQ, D), 1.0, 6.0, ((0, 32),), jnp.float32),
        "caption_len": touch_ends(jax.random.randint(splits[3], (ITEMS,), 1, CAPTION + 1), jax.random.fold_in(splits[3], 1), 1, CAPTION).astype(jnp.int32),
        "skip_w": gaussian(splits[4], (2 * D * D,), (2 * D) ** -0.5, 0.125, ((0, 32),), jnp.float32),
        "qkv_w": gaussian(splits[5], (3 * D * D,), D ** -0.5, 0.1875, ((0, 32),), jnp.float32),
        "proj_w": gaussian(splits[6], (D * D,), (max(D // 64, 1)) ** -0.5, 1.5, ((0, 32),), jnp.float32),
        "fc1_w": gaussian(splits[7], (D * FF,), D ** -0.5, 0.1875, ((0, 32),), jnp.float32),
        "fc2_w": gaussian(splits[8], (FF * D,), FF ** -0.5, 0.09375, ((0, 32),), jnp.float32),
        "vectors": draw_vectors(jax.random.fold_in(splits[10], 71), 0),
    }


@jax.custom_vjp
def low(v):
    return lax.optimization_barrier(v.astype(jnp.bfloat16)).astype(jnp.float32)

@jax.custom_vjp
def low_back(v):
    return v

def low_keep(v):
    return (low(v), None)

def low_pass(kept, grad):
    return (grad,)

def back_keep(v):
    return (v, None)

def back_low(kept, grad):
    return (low(grad),)
low.defvjp(low_keep, low_pass)
low_back.defvjp(back_keep, back_low)
epsilon = 1e-05
masked_value = -1e+30

def norm_rows(value, gain, shift):
    center = value - lax.optimization_barrier(jnp.mean(value, -1, keepdims=True))
    spread = lax.optimization_barrier(jnp.mean(center * center, -1, keepdims=True))
    return center * lax.rsqrt(spread + epsilon) * gain + shift

def key_valid(caption_len, length, caption):
    place = lax.broadcasted_iota(jnp.int32, (caption_len.shape[0], length), 1)
    return (place < 1 + caption_len[:, None]) | (place >= 1 + caption)

def forward(block_in, skip_in, valid, skip_m, qkv_m, proj_m, fc1_m, fc2_m, vec):
    best = lax.Precision.HIGHEST
    items, length, width = block_in.shape
    heads = HEADS
    head_dim = width // heads
    rows = items * length
    gain_one = vec[0:width]
    shift_one = vec[width:2 * width]
    gain_two = vec[2 * width:3 * width]
    shift_two = vec[3 * width:4 * width]
    skip_bias = vec[4 * width:5 * width]
    proj_bias = vec[5 * width:6 * width]
    fc2_bias = vec[6 * width:7 * width]
    fc1_bias = vec[7 * width:]
    joined = low(jnp.concatenate([block_in, skip_in], -1).reshape(rows, 2 * width))
    first = low_back(jnp.dot(joined, low(skip_m), precision=best) + skip_bias)
    normed_one = low(norm_rows(first, gain_one, shift_one))
    triple = low(low_back(jnp.dot(normed_one, low(qkv_m), precision=best)))
    triple = triple.reshape(items, length, 3, heads, head_dim)
    query = triple[:, :, 0]
    keys = triple[:, :, 1]
    values = triple[:, :, 2]
    raw = jnp.einsum('ishd,ithd->ihst', query, keys, precision=best) * head_dim ** (-0.5)
    scores = low_back(jnp.where(valid[:, None, None, :], raw, masked_value))
    top = lax.optimization_barrier(jnp.max(scores, -1, keepdims=True))
    expd = jnp.exp(scores - top)
    total = lax.optimization_barrier(jnp.sum(expd, -1, keepdims=True))
    probs = expd / total
    mixed = low(low_back(jnp.einsum('ihst,ithd->ishd', low(probs), values, precision=best)))
    mixed = mixed.reshape(rows, width)
    second = first + low_back(jnp.dot(mixed, low(proj_m), precision=best) + proj_bias)
    normed_two = low(norm_rows(second, gain_two, shift_two))
    inner = low_back(jnp.dot(normed_two, low(fc1_m), precision=best) + fc1_bias)
    active = low(jax.nn.gelu(inner, approximate=False))
    result = second + low_back(jnp.dot(active, low(fc2_m), precision=best) + fc2_bias)
    return result.reshape(items, length, width)

def reference(block_in, skip_in, out_grad, caption_len, skip_w, qkv_w, proj_w, fc1_w, fc2_w, vectors):
    width = D
    hidden = FF
    mats = (skip_w.reshape(2 * width, width), qkv_w.reshape(width, 3 * width), proj_w.reshape(width, width), fc1_w.reshape(width, hidden), fc2_w.reshape(hidden, width))
    group = ITEMS_DEV * N_FSDP
    count = ITEMS // group

    def split(value):
        return value.reshape((count, group) + value.shape[1:])

    def step(sums, packed):
        part_in, part_skip, part_grad, part_len = packed
        valid = key_valid(part_len, SEQ, CAPTION)

        def run(first_in, second_in, m_skip, m_qkv, m_proj, m_one, m_two, vec):
            return forward(first_in, second_in, valid, m_skip, m_qkv, m_proj, m_one, m_two, vec)
        result, pull = jax.vjp(run, part_in, part_skip, mats[0], mats[1], mats[2], mats[3], mats[4], vectors)
        grads = pull(part_grad)
        sums = tuple((total + piece for total, piece in zip(sums, grads[2:])))
        return (sums, (result, grads[0], grads[1]))
    start = tuple((jnp.zeros_like(mat) for mat in mats)) + (jnp.zeros_like(vectors),)
    sums, (outs, in_grads, skip_grads) = lax.scan(step, start, (split(block_in), split(skip_in), split(out_grad), split(caption_len)))
    full = (ITEMS, SEQ, D)
    return (outs.reshape(full), in_grads.reshape(full), skip_grads.reshape(full), sums[0].reshape(-1), sums[1].reshape(-1), sums[2].reshape(-1), sums[3].reshape(-1), sums[4].reshape(-1), sums[5])
```

```python
import functools

import jax
import jax.numpy as jnp
from jax import lax
from jax.experimental import pallas as pl
from jax.experimental.pallas import tpu as pltpu
from jax.sharding import PartitionSpec as P

HEADS = 16
FF = 4608
CAPTION = 77


epsilon = 1e-05
masked_value = -1e30


def norm_rows(value, gain, shift):
    center = value - jnp.mean(value, -1, keepdims=True)
    spread = jnp.mean(center * center, -1, keepdims=True)
    return center * lax.rsqrt(spread + epsilon) * gain + shift


def gelu_exact(value):
    return jax.nn.gelu(value, approximate=False)


def key_valid(caption_len, length, caption):
    place = lax.broadcasted_iota(jnp.int32, (caption_len.shape[0], length), 1)
    return (place < 1 + caption_len[:, None]) | (place >= 1 + caption)


def product(left, right):
    return jnp.dot(left, right, preferred_element_type=jnp.float32)


def left_product(left, right):
    return lax.dot_general(
        left, right, (((0,), (0,)), ((), ())), preferred_element_type=jnp.float32
    )


def right_product(left, right):
    return lax.dot_general(
        left, right, (((1,), (1,)), ((), ())), preferred_element_type=jnp.float32
    )


def whole_rows(width, dp, fsdp):
    return fsdp == 4 and dp % 2 == 0 and width % (dp * 16) == 0


def unpack(flat, width, hidden):
    return (
        flat[0].reshape(2 * width, width),
        flat[1].reshape(width, 3 * width),
        flat[2].reshape(width, width),
        flat[3].reshape(width, hidden),
        flat[4].reshape(hidden, width),
    )


def attention_scores(query, keys, valid, scale):
    raw = jnp.einsum("ishd,ithd->ihst", query, keys, preferred_element_type=jnp.float32) * scale
    return jnp.where(valid[:, None, None, :], raw, masked_value)


def column_sum(value):
    return jnp.sum(value.astype(jnp.float32), 0)


def flat_piece(left, right):
    grad_rows = left_product(left, right).reshape(-1)
    return grad_rows


MESH = pl.DeviceIdType.MESH
BF=jnp.bfloat16; F32=jnp.float32

def gather_kernel(Z, wide, rows, lanes_a,
                  skip_ref, qkv_ref, proj_ref, fc1_ref, fc2_ref, vec_ref,
                  skip_o, qp_o, fc1_o, fc2_o, vec_o,
                  own, mine, give, take, send, recv, lsem, psend, precv, vsend, vrecv):
    dp = lax.axis_index("dp"); f = lax.axis_index("fsdp")
    z = dp // 2; x = dp % 2; y = f // 2; c = f % 2
    nt = wide // 128
    half = rows // 2
    A = pl.ds(0, lanes_a); C = pl.ds(lanes_a, wide - lanes_a)
    zs = [(lax.rem(z + k, Z) * 2 + x, f) for k in range(1, Z)]
    xp = (z * 2 + 1 - x, f)
    yp = (dp, (1 - y) * 2 + c)
    pp = (dp, y * 2 + 1 - c)
    ndp = 2 * Z
    others = [(lax.rem(dp + k, ndp), f) for k in range(1, ndp)]
    bar = pltpu.get_barrier_semaphore()
    for d in others + [yp, pp]:
        pl.semaphore_signal(bar, inc=1, device_id=d, device_id_type=MESH)
    for j in range(nt):
        cols = slice(128 * j, 128 * j + 128)
        own[0, :, cols] = skip_ref[pl.ds(j, rows, stride=nt), :].astype(BF)
        own[5, :, cols] = fc2_ref[pl.ds(j, rows, stride=nt), :].astype(BF)
        own[6, :, cols] = fc2_ref[pl.ds(j + nt * rows, rows, stride=nt), :].astype(BF)
        q = [qkv_ref[pl.ds(nt * v + j, half, stride=3 * nt), :] for v in range(3)]
        q.append(proj_ref[pl.ds(j, half, stride=nt), :])
        g = [fc1_ref[pl.ds(nt * v + j, half, stride=4 * nt), :] for v in range(4)]
        four = q + g
        for i in range(4):
            a, b = four[2 * i], four[2 * i + 1]
            mine[i, 0:half, cols] = jnp.where(c == 0, a, b)
            give[i, 0:half, cols] = jnp.where(c == 0, b, a).astype(BF)
    pl.semaphore_wait(bar, len(others) + 2)
    vcopies = []
    for k, d in enumerate(others):
        cp = pltpu.make_async_remote_copy(vec_ref, vec_o.at[dp], vsend.at[k], vrecv.at[k], device_id=d, device_id_type=MESH)
        cp.start(); vcopies.append(cp)
    lv = pltpu.make_async_copy(vec_ref, vec_o.at[dp], lsem.at[7])
    lv.start()
    pc = [pltpu.make_async_remote_copy(give.at[i], take.at[i], psend.at[i], precv.at[i], device_id=pp, device_id_type=MESH) for i in range(4)]
    for cp in pc: cp.start()

    def unit(i, cc):
        if i == 0: return skip_o.at[:, :, :, cc]
        if i in (1, 2): return qp_o.at[2 * (i - 1) + cc]
        if i in (3, 4): return fc1_o.at[2 * (i - 3) + cc]
        return fc2_o.at[:, :, :, 2 * cc + (i - 5)]
    nz = Z - 1
    waits = []
    def rc(i, slot, src, dst, dev):
        cp = pltpu.make_async_remote_copy(src, dst, send.at[i, slot], recv.at[i, slot], device_id=dev, device_id_type=MESH)
        cp.start(); waits.append(cp)
    def got(i, slot, dst):
        pltpu.make_async_remote_copy(dst, dst, send.at[i, slot], recv.at[i, slot], device_id=pp, device_id_type=MESH).wait_recv()
    def stage1(i):
        U = unit(i, c)
        if i in (1, 2, 3, 4):
            pc[i - 1].wait_recv()
            a = mine[i - 1, 0:half, :]
            b = take[i - 1, :, :].astype(F32)[0:half]
            lo = jnp.where(c == 0, a, b); hi = jnp.where(c == 0, b, a)
            own[i, :, :] = jnp.concatenate([lo, hi], 0).astype(BF)
        lc = pltpu.make_async_copy(own.at[i], U.at[z, x, y], lsem.at[i]); lc.start()
        rc(i, 2 * nz, own.at[i, :, C], U.at[z, x, y, :, C], yp)
        for k in range(1, Z):
            rc(i, k - 1, own.at[i, :, A], U.at[z, x, y, :, A], zs[k - 1])
        return lc
    def stage2(i, lc):
        U = unit(i, c)
        lc.wait()
        got(i, 2 * nz, U.at[z, x, 1 - y, :, C])
        for k in range(1, Z):
            rc(i, nz + k - 1, U.at[z, x, :, :, C], U.at[z, x, :, :, C], zs[k - 1])
        for k in range(1, Z):
            got(i, k - 1, U.at[lax.rem(z - k + Z, Z), x, y, :, A])
        L = U.at[:, x, y, :, A]
        rc(i, 2 * nz + 1, L, L, xp)
        rc(i, 2 * nz + 2, L, L, yp)
        rc(i, 2 * nz + 5, L, L, pp)
    def stage3(i):
        U = unit(i, c)
        for k in range(1, Z):
            got(i, nz + k - 1, U.at[lax.rem(z - k + Z, Z), x, :, :, C])
        L = U.at[:, x, :, :, C]
        rc(i, 2 * nz + 4, L, L, xp)
        rc(i, 2 * nz + 6, L, L, pp)
        L = U.at[:, 1 - x, y, :, A]
        got(i, 2 * nz + 1, L)
        rc(i, 2 * nz + 3, L, L, yp)
        rc(i, 2 * nz + 7, L, L, pp)
    def stage4(i):
        U = unit(i, c)
        L = U.at[:, x, 1 - y, :, A]
        got(i, 2 * nz + 2, L); rc(i, 2 * nz + 8, L, L, pp)
        L = U.at[:, 1 - x, 1 - y, :, A]
        got(i, 2 * nz + 3, L); rc(i, 2 * nz + 9, L, L, pp)
        L = U.at[:, 1 - x, :, :, C]
        got(i, 2 * nz + 4, L); rc(i, 2 * nz + 10, L, L, pp)
    def arrived(i):
        U = unit(i, 1 - c)
        got(i, 2 * nz + 5, U.at[:, x, y, :, A])
        got(i, 2 * nz + 7, U.at[:, 1 - x, y, :, A])
        got(i, 2 * nz + 8, U.at[:, x, 1 - y, :, A])
        got(i, 2 * nz + 9, U.at[:, 1 - x, 1 - y, :, A])
        got(i, 2 * nz + 6, U.at[:, x, :, :, C])
        got(i, 2 * nz + 10, U.at[:, 1 - x, :, :, C])
    lc = {}
    lc[0] = stage1(0)
    for i in range(7):
        stage2(i, lc[i])
        if i < 6: lc[i + 1] = stage1(i + 1)
        stage3(i)
        if i > 0: stage4(i - 1)
    stage4(6)
    for i in range(7): arrived(i)
    for cp in waits: cp.wait_send()
    for cp in pc: cp.wait_send()
    lv.wait()
    for k, cp in enumerate(vcopies):
        cp.wait_send()
        pltpu.make_async_remote_copy(vec_ref, vec_o.at[lax.rem(dp - (k + 1) + ndp, ndp)], vsend.at[k], vrecv.at[k], device_id=pp, device_id_type=MESH).wait_recv()

def gather(skip, qkv, proj, fc1, fc2, vectors, dpn, wide):
    Z = dpn // 2; rows = skip.shape[0] // wide
    lanes_a = (wide // 128 * 2 + 1) // 3 * 128
    U = (Z, 2, 2, rows, wide)
    hbm = pl.BlockSpec(memory_space=pl.ANY); vm = pl.BlockSpec(memory_space=pltpu.VMEM)
    ns = 2 * (Z - 1) + 11
    nv = vectors.shape[0]
    D = pltpu.SemaphoreType.DMA
    half = -(-rows // 2 // 16) * 16
    return pl.pallas_call(
        functools.partial(gather_kernel, Z, wide, rows, lanes_a),
        out_shape=(jax.ShapeDtypeStruct((Z, 2, 2, 2, rows, wide), BF), jax.ShapeDtypeStruct((4,) + U, BF),
                   jax.ShapeDtypeStruct((4,) + U, BF), jax.ShapeDtypeStruct((Z, 2, 2, 4, rows, wide), BF),
                   jax.ShapeDtypeStruct((dpn, 1, nv), F32)),
        in_specs=[vm] * 6, out_specs=(hbm,) * 5,
        scratch_shapes=[pltpu.VMEM((7, rows, wide), BF), pltpu.VMEM((4, half, wide), F32), pltpu.VMEM((4, half, wide), BF), pltpu.VMEM((4, half, wide), BF),
                        D((7, ns)), D((7, ns)), D((8,)), D((4,)), D((4,)), D((dpn - 1,)), D((dpn - 1,))],
        compiler_params=pltpu.CompilerParams(collective_id=0, has_side_effects=True, vmem_limit_bytes=32 << 20),
        name="gather",
    )(*(w.reshape(-1, 128) for w in (skip, qkv, proj, fc1, fc2)), vectors.reshape(1, nv))


def body(block_in, skip_in, out_grad, caption_len, skip_w, qkv_w, proj_w, fc1_w, fc2_w, vectors):
    items, length, width = block_in.shape
    heads = HEADS
    head_dim = width // heads
    hidden = FF
    rows = items * length
    scale = head_dim ** (-0.5)
    owners = lax.axis_size(("dp", "fsdp"))
    if whole_rows(width, lax.axis_size("dp"), lax.axis_size("fsdp")):
        skip_u, qp_u, fc1_u, fc2_u, vec = gather(
            skip_w, qkv_w, proj_w, fc1_w, fc2_w, vectors, lax.axis_size("dp"), width
        )
        skip_m = skip_u.reshape(2 * width, width)
        qp_u = qp_u.reshape(4, width, width)
        qkv_m = jnp.concatenate([qp_u[0], qp_u[1], qp_u[2]], 1)
        proj_m = qp_u[3]
        fc1_m = jnp.concatenate([t.reshape(width, width) for t in fc1_u], 1)
        fc2_m = fc2_u.reshape(hidden, width)
        vec = vec.reshape(-1)
    else:
        gathered = tuple(
            lax.all_gather(w.astype(jnp.bfloat16), ("dp", "fsdp"), axis=0, tiled=True)
            for w in (skip_w, qkv_w, proj_w, fc1_w, fc2_w)
        )
        skip_m, qkv_m, proj_m, fc1_m, fc2_m = unpack(gathered, width, hidden)
        vec = lax.all_gather(vectors, "dp", axis=0, tiled=True)
    gain_one = vec[0:width]
    shift_one = vec[width : 2 * width]
    gain_two = vec[2 * width : 3 * width]
    shift_two = vec[3 * width : 4 * width]
    skip_bias = vec[4 * width : 5 * width]
    proj_bias = vec[5 * width : 6 * width]
    fc2_bias = vec[6 * width : 7 * width]
    fc1_bias = vec[7 * width :]
    valid = key_valid(caption_len, length, CAPTION)
    joined = jnp.concatenate([block_in, skip_in], -1).reshape(rows, 2 * width).astype(jnp.bfloat16)
    first = product(joined, skip_m) + skip_bias
    normed_one = norm_rows(first, gain_one, shift_one).astype(jnp.bfloat16)
    triple = (
        product(normed_one, qkv_m).astype(jnp.bfloat16).reshape(items, length, 3, heads, head_dim)
    )
    query = triple[:, :, 0]
    keys = triple[:, :, 1]
    values = triple[:, :, 2]
    scores = attention_scores(query, keys, valid, scale)
    top = jnp.max(scores, -1, keepdims=True)
    expd = jnp.exp(scores - top)
    total = jnp.sum(expd, -1, keepdims=True)
    probs = expd / total
    log_total = top + jnp.log(total)
    mixed = (
        jnp.einsum(
            "ihst,ithd->ishd",
            probs.astype(jnp.bfloat16),
            values,
            preferred_element_type=jnp.float32,
        )
        .astype(jnp.bfloat16)
        .reshape(rows, width)
    )
    second = first + (product(mixed, proj_m) + proj_bias)
    normed_two = norm_rows(second, gain_two, shift_two).astype(jnp.bfloat16)
    inner = product(normed_two, fc1_m) + fc1_bias
    active = gelu_exact(inner).astype(jnp.bfloat16)
    block_out = second + (product(active, fc2_m) + fc2_bias)
    grad_out = out_grad.reshape(rows, width)
    grad_mlp = grad_out.astype(jnp.bfloat16)
    d_fc2_bias = column_sum(grad_mlp)
    d_active = right_product(grad_mlp, fc2_m)
    gelu_value, gelu_pull = jax.vjp(gelu_exact, inner)
    grad_inner = gelu_pull(d_active)[0].astype(jnp.bfloat16)
    d_fc1_bias = column_sum(grad_inner)
    d_normed_two = right_product(grad_inner, fc1_m)
    norm_value_two, norm_pull_two = jax.vjp(norm_rows, second, gain_two, shift_two)
    d_second_norm, d_gain_two, d_shift_two = norm_pull_two(d_normed_two)
    grad_second = grad_out + d_second_norm
    grad_attn = grad_second.astype(jnp.bfloat16)
    d_proj_bias = column_sum(grad_attn)
    grad_mixed = (
        right_product(grad_attn, proj_m)
        .astype(jnp.bfloat16)
        .reshape(items, length, heads, head_dim)
    )
    again_scores = attention_scores(query, keys, valid, scale)
    again_probs = jnp.exp(again_scores - log_total)
    d_probs = jnp.einsum("ishd,ithd->ihst", grad_mixed, values, preferred_element_type=jnp.float32)
    inner_sum = jnp.sum(again_probs * d_probs, -1, keepdims=True)
    grad_scores = (again_probs * (d_probs - inner_sum)).astype(jnp.bfloat16)
    d_query = (
        jnp.einsum("ihst,ithd->ishd", grad_scores, keys, preferred_element_type=jnp.float32) * scale
    )
    d_keys = (
        jnp.einsum("ihst,ishd->ithd", grad_scores, query, preferred_element_type=jnp.float32)
        * scale
    )
    d_values = jnp.einsum(
        "ihst,ishd->ithd",
        again_probs.astype(jnp.bfloat16),
        grad_mixed,
        preferred_element_type=jnp.float32,
    )
    grad_triple = (
        jnp.stack([d_query, d_keys, d_values], 2).astype(jnp.bfloat16).reshape(rows, 3 * width)
    )
    d_normed_one = right_product(grad_triple, qkv_m)
    norm_value_one, norm_pull_one = jax.vjp(norm_rows, first, gain_one, shift_one)
    d_first_norm, d_gain_one, d_shift_one = norm_pull_one(d_normed_one)
    grad_first = (grad_second + d_first_norm).astype(jnp.bfloat16)
    d_skip_bias = column_sum(grad_first)
    grad_joined = right_product(grad_first, skip_m).reshape(items, length, 2 * width)
    in_grad = grad_joined[:, :, 0:width]
    skip_grad = grad_joined[:, :, width:]
    pairs = (
        (joined, grad_first),
        (normed_one, grad_triple),
        (mixed, grad_attn),
        (normed_two, grad_inner),
        (active, grad_mlp),
    )
    shard_sizes = [pair[0].shape[1] * pair[1].shape[1] // owners for pair in pairs]
    blocks = []
    for pair, owner_share in zip(pairs, shard_sizes):
        blocks.append(
            flat_piece(pair[0], pair[1]).reshape(1 * lax.axis_size(("dp", "fsdp")), owner_share)
        )
    owned = lax.psum_scatter(
        jnp.concatenate(blocks, 1), ("dp", "fsdp"), scatter_dimension=0, tiled=True
    ).reshape(-1)
    pieces = []
    offset = 0
    for share in shard_sizes:
        pieces.append(owned[offset : offset + share])
        offset = offset + share
    vec_grad = jnp.concatenate(
        [
            d_gain_one,
            d_shift_one,
            d_gain_two,
            d_shift_two,
            d_skip_bias,
            d_proj_bias,
            d_fc2_bias,
            d_fc1_bias,
        ]
    )
    vec_rows = lax.psum_scatter(vec_grad, "dp", scatter_dimension=0, tiled=True)
    vec_total = lax.psum(vec_rows, "fsdp")
    return (
        block_out.reshape(items, length, width),
        in_grad,
        skip_grad,
        pieces[0],
        pieces[1],
        pieces[2],
        pieces[3],
        pieces[4],
        vec_total,
    )


def solution(mesh):
    placed = (
        P(("dp", "fsdp"), None, None),
        P(("dp", "fsdp"), None, None),
        P(("dp", "fsdp"), None, None),
        P(("dp", "fsdp")),
        P(("dp", "fsdp")),
        P(("dp", "fsdp")),
        P(("dp", "fsdp")),
        P(("dp", "fsdp")),
        P(("dp", "fsdp")),
        P("dp"),
    )
    return jax.shard_map(
        body,
        mesh=mesh,
        in_specs=placed,
        out_specs=(
            P(("dp", "fsdp"), None, None),
            P(("dp", "fsdp"), None, None),
            P(("dp", "fsdp"), None, None),
            P(("dp", "fsdp")),
            P(("dp", "fsdp")),
            P(("dp", "fsdp")),
            P(("dp", "fsdp")),
            P(("dp", "fsdp")),
            P("dp"),
        ),
        check_vma=False,
    )
```

```python
import functools

import jax
import jax.numpy as jnp
from jax import lax
from jax.experimental import pallas as pl
from jax.experimental.pallas import tpu as pltpu
from jax.sharding import PartitionSpec as P

HEADS = 16
FF = 4608
CAPTION = 77


epsilon = 1e-05
masked_value = -1e30


def norm_rows(value, gain, shift):
    center = value - jnp.mean(value, -1, keepdims=True)
    spread = jnp.mean(center * center, -1, keepdims=True)
    return center * lax.rsqrt(spread + epsilon) * gain + shift


def gelu_exact(value):
    return jax.nn.gelu(value, approximate=False)


def key_valid(caption_len, length, caption):
    place = lax.broadcasted_iota(jnp.int32, (caption_len.shape[0], length), 1)
    return (place < 1 + caption_len[:, None]) | (place >= 1 + caption)


def product(left, right):
    return jnp.dot(left, right, preferred_element_type=jnp.float32)


def left_product(left, right):
    return lax.dot_general(
        left, right, (((0,), (0,)), ((), ())), preferred_element_type=jnp.float32
    )


def right_product(left, right):
    return lax.dot_general(
        left, right, (((1,), (1,)), ((), ())), preferred_element_type=jnp.float32
    )


def unpack(flat, width, hidden):
    return (
        flat[0].reshape(2 * width, width),
        flat[1].reshape(width, 3 * width),
        flat[2].reshape(width, width),
        flat[3].reshape(width, hidden),
        flat[4].reshape(hidden, width),
    )


def attention_scores(query, keys, valid, scale):
    raw = jnp.einsum("ishd,ithd->ihst", query, keys, preferred_element_type=jnp.float32) * scale
    return jnp.where(valid[:, None, None, :], raw, masked_value)


def column_sum(value):
    return jnp.sum(value.astype(jnp.float32), 0)


def flat_piece(left, right):
    grad_rows = left_product(left, right).reshape(-1)
    return grad_rows


MESH = pl.DeviceIdType.MESH
BF=jnp.bfloat16; F32=jnp.float32

def gather_kernel(Z, wide, rows, lanes_a,
                  skip_ref, qkv_ref, proj_ref, fc1_ref, fc2_ref, vec_ref,
                  skip_o, qp_o, fc1_o, fc2_o, vec_o,
                  own, mine, give, take, send, recv, lsem, psend, precv, vsend, vrecv):
    dp = lax.axis_index("dp"); f = lax.axis_index("fsdp")
    z = dp // 2; x = dp % 2; y = f // 2; c = f % 2
    nt = wide // 128
    half = rows // 2
    A = pl.ds(0, lanes_a); C = pl.ds(lanes_a, wide - lanes_a)
    zs = [(lax.rem(z + k, Z) * 2 + x, f) for k in range(1, Z)]
    xp = (z * 2 + 1 - x, f)
    yp = (dp, (1 - y) * 2 + c)
    pp = (dp, y * 2 + 1 - c)
    ndp = 2 * Z
    others = [(lax.rem(dp + k, ndp), f) for k in range(1, ndp)]
    bar = pltpu.get_barrier_semaphore()
    for d in others + [yp, pp]:
        pl.semaphore_signal(bar, inc=1, device_id=d, device_id_type=MESH)
    for j in range(nt):
        cols = slice(128 * j, 128 * j + 128)
        own[0, :, cols] = skip_ref[pl.ds(j, rows, stride=nt), :].astype(BF)
        own[5, :, cols] = fc2_ref[pl.ds(j, rows, stride=nt), :].astype(BF)
        own[6, :, cols] = fc2_ref[pl.ds(j + nt * rows, rows, stride=nt), :].astype(BF)
        q = [qkv_ref[pl.ds(nt * v + j, half, stride=3 * nt), :] for v in range(3)]
        q.append(proj_ref[pl.ds(j, half, stride=nt), :])
        g = [fc1_ref[pl.ds(nt * v + j, half, stride=4 * nt), :] for v in range(4)]
        four = q + g
        for i in range(4):
            a, b = four[2 * i], four[2 * i + 1]
            mine[i, 0:half, cols] = jnp.where(c == 0, a, b)
            give[i, 0:half, cols] = jnp.where(c == 0, b, a).astype(BF)
    pl.semaphore_wait(bar, len(others) + 2)
    vcopies = []
    for k, d in enumerate(others):
        cp = pltpu.make_async_remote_copy(vec_ref, vec_o.at[dp], vsend.at[k], vrecv.at[k], device_id=d, device_id_type=MESH)
        cp.start(); vcopies.append(cp)
    lv = pltpu.make_async_copy(vec_ref, vec_o.at[dp], lsem.at[7])
    lv.start()
    pc = [pltpu.make_async_remote_copy(give.at[i], take.at[i], psend.at[i], precv.at[i], device_id=pp, device_id_type=MESH) for i in range(4)]
    for cp in pc: cp.start()

    def unit(i, cc):
        if i == 0: return skip_o.at[:, :, :, cc]
        if i in (1, 2): return qp_o.at[2 * (i - 1) + cc]
        if i in (3, 4): return fc1_o.at[2 * (i - 3) + cc]
        return fc2_o.at[:, :, :, 2 * cc + (i - 5)]
    nz = Z - 1
    waits = []
    def rc(i, slot, src, dst, dev):
        cp = pltpu.make_async_remote_copy(src, dst, send.at[i, slot], recv.at[i, slot], device_id=dev, device_id_type=MESH)
        cp.start(); waits.append(cp)
    def got(i, slot, dst):
        pltpu.make_async_remote_copy(dst, dst, send.at[i, slot], recv.at[i, slot], device_id=pp, device_id_type=MESH).wait_recv()
    def stage1(i):
        U = unit(i, c)
        if i in (1, 2, 3, 4):
            pc[i - 1].wait_recv()
            a = mine[i - 1, 0:half, :]
            b = take[i - 1, :, :].astype(F32)[0:half]
            lo = jnp.where(c == 0, a, b); hi = jnp.where(c == 0, b, a)
            own[i, :, :] = jnp.concatenate([lo, hi], 0).astype(BF)
        lc = pltpu.make_async_copy(own.at[i], U.at[z, x, y], lsem.at[i]); lc.start()
        rc(i, 2 * nz, own.at[i, :, C], U.at[z, x, y, :, C], yp)
        for k in range(1, Z):
            rc(i, k - 1, own.at[i, :, A], U.at[z, x, y, :, A], zs[k - 1])
        return lc
    def stage2(i, lc):
        U = unit(i, c)
        lc.wait()
        got(i, 2 * nz, U.at[z, x, 1 - y, :, C])
        for k in range(1, Z):
            rc(i, nz + k - 1, U.at[z, x, :, :, C], U.at[z, x, :, :, C], zs[k - 1])
        for k in range(1, Z):
            got(i, k - 1, U.at[lax.rem(z - k + Z, Z), x, y, :, A])
        L = U.at[:, x, y, :, A]
        rc(i, 2 * nz + 1, L, L, xp)
        rc(i, 2 * nz + 2, L, L, yp)
        rc(i, 2 * nz + 5, L, L, pp)
    def stage3(i):
        U = unit(i, c)
        for k in range(1, Z):
            got(i, nz + k - 1, U.at[lax.rem(z - k + Z, Z), x, :, :, C])
        L = U.at[:, x, :, :, C]
        rc(i, 2 * nz + 4, L, L, xp)
        rc(i, 2 * nz + 6, L, L, pp)
        L = U.at[:, 1 - x, y, :, A]
        got(i, 2 * nz + 1, L)
        rc(i, 2 * nz + 3, L, L, yp)
        rc(i, 2 * nz + 7, L, L, pp)
    def stage4(i):
        U = unit(i, c)
        L = U.at[:, x, 1 - y, :, A]
        got(i, 2 * nz + 2, L); rc(i, 2 * nz + 8, L, L, pp)
        L = U.at[:, 1 - x, 1 - y, :, A]
        got(i, 2 * nz + 3, L); rc(i, 2 * nz + 9, L, L, pp)
        L = U.at[:, 1 - x, :, :, C]
        got(i, 2 * nz + 4, L); rc(i, 2 * nz + 10, L, L, pp)
    def arrived(i):
        U = unit(i, 1 - c)
        got(i, 2 * nz + 5, U.at[:, x, y, :, A])
        got(i, 2 * nz + 7, U.at[:, 1 - x, y, :, A])
        got(i, 2 * nz + 8, U.at[:, x, 1 - y, :, A])
        got(i, 2 * nz + 9, U.at[:, 1 - x, 1 - y, :, A])
        got(i, 2 * nz + 6, U.at[:, x, :, :, C])
        got(i, 2 * nz + 10, U.at[:, 1 - x, :, :, C])
    lc = {}
    lc[0] = stage1(0)
    for i in range(7):
        stage2(i, lc[i])
        if i < 6: lc[i + 1] = stage1(i + 1)
        stage3(i)
        if i > 0: stage4(i - 1)
    stage4(6)
    for i in range(7): arrived(i)
    for cp in waits: cp.wait_send()
    for cp in pc: cp.wait_send()
    lv.wait()
    for k, cp in enumerate(vcopies):
        cp.wait_send()
        pltpu.make_async_remote_copy(vec_ref, vec_o.at[lax.rem(dp - (k + 1) + ndp, ndp)], vsend.at[k], vrecv.at[k], device_id=pp, device_id_type=MESH).wait_recv()

def gather(skip, qkv, proj, fc1, fc2, vectors, dpn, wide):
    Z = dpn // 2; rows = skip.shape[0] // wide
    lanes_a = (wide // 128 * 2 + 1) // 3 * 128
    U = (Z, 2, 2, rows, wide)
    hbm = pl.BlockSpec(memory_space=pl.ANY); vm = pl.BlockSpec(memory_space=pltpu.VMEM)
    ns = 2 * (Z - 1) + 11
    nv = vectors.shape[0]
    D = pltpu.SemaphoreType.DMA
    half = -(-rows // 2 // 16) * 16
    return pl.pallas_call(
        functools.partial(gather_kernel, Z, wide, rows, lanes_a),
        out_shape=(jax.ShapeDtypeStruct((Z, 2, 2, 2, rows, wide), BF), jax.ShapeDtypeStruct((4,) + U, BF),
                   jax.ShapeDtypeStruct((4,) + U, BF), jax.ShapeDtypeStruct((Z, 2, 2, 4, rows, wide), BF),
                   jax.ShapeDtypeStruct((dpn, 1, nv), F32)),
        in_specs=[vm] * 6, out_specs=(hbm,) * 5,
        scratch_shapes=[pltpu.VMEM((7, rows, wide), BF), pltpu.VMEM((4, half, wide), F32), pltpu.VMEM((4, half, wide), BF), pltpu.VMEM((4, half, wide), BF),
                        D((7, ns)), D((7, ns)), D((8,)), D((4,)), D((4,)), D((dpn - 1,)), D((dpn - 1,))],
        compiler_params=pltpu.CompilerParams(collective_id=0, has_side_effects=True, vmem_limit_bytes=32 << 20),
        name="gather",
    )(*(w.reshape(-1, 128) for w in (skip, qkv, proj, fc1, fc2)), vectors.reshape(1, nv))


def scatter_kernel(Z, wide, rows, lanes_a, length,
                   z_ref, gm_ref, m_ref, gu_ref, o_ref, ga_ref, n_ref, t_ref, j_ref, g_ref, vec_ref,
                   skip_o, qkv_o, proj_o, fc1_o, fc2_o, vec_o,
                   left, right, part, ra1, ra2, ra3, rc1, rc2, rc3, keep, give, take, vgot, vall,
                   lsem, xsend, xrecv, send, recv, psend, precv, vsend, vrecv, wsend, wrecv):
    dp = lax.axis_index("dp"); f = lax.axis_index("fsdp")
    z = dp // 2; x = dp % 2; y = f // 2; c = f % 2
    nt = wide // 128
    half = rows // 2
    A = pl.ds(0, lanes_a); C = pl.ds(lanes_a, wide - lanes_a)
    zi = [lax.rem(z + k, Z) for k in range(1, Z)]
    zs = [(t * 2 + x, f) for t in zi]
    xp = (z * 2 + 1 - x, f)
    yp = (dp, (1 - y) * 2 + c)
    pp = (dp, y * 2 + 1 - c)
    ndp = 2 * Z
    dps = [(lax.rem(dp + k, ndp), f) for k in range(1, ndp)]
    fs = [(dp, lax.rem(f + k, 4)) for k in range(1, 4)]
    bar = pltpu.get_barrier_semaphore()
    for d in dps + fs:
        pl.semaphore_signal(bar, inc=1, device_id=d, device_id_type=MESH)
    pl.semaphore_wait(bar, len(dps) + len(fs))

    def cols(ref, unit):
        return ref.at[:, pl.ds(pl.multiple_of(unit * wide, 128), wide)]
    own_rows = pl.ds(0, length); other_rows = pl.ds(length, length)
    copies = {}
    def pair(n, src_own, src_other, dst):
        a = pltpu.make_async_copy(src_own, dst.at[own_rows], lsem.at[n])
        b = pltpu.make_async_remote_copy(src_other, dst.at[other_rows], xsend.at[n], xrecv.at[n], device_id=pp, device_id_type=MESH)
        a.start(); b.start()
        return a, b
    o = 1 - c
    copies[0] = pair(0, cols(z_ref, 2 * c), cols(z_ref, 2 * o), left.at[0])
    copies[1] = pair(1, gm_ref, gm_ref, right.at[0])
    copies[2] = pair(2, cols(z_ref, 2 * c + 1), cols(z_ref, 2 * o + 1), left.at[1])
    copies[3] = pair(3, m_ref, m_ref, left.at[2])
    copies[4] = pair(4, cols(gu_ref, c), cols(gu_ref, o), right.at[1])
    copies[5] = pair(5, cols(gu_ref, 2 + c), cols(gu_ref, 2 + o), right.at[2])
    @pl.when(c == 0)
    def _():
        pair(6, n_ref, o_ref, left.at[3])
        pair(7, cols(t_ref, 2), ga_ref, right.at[3])
    @pl.when(c == 1)
    def _():
        pair(6, o_ref, n_ref, left.at[3])
        pair(7, ga_ref, cols(t_ref, 2), right.at[3])
    for n, dst in ((6, left.at[3]), (7, right.at[3])):
        copies[n] = (
            pltpu.make_async_copy(g_ref, dst.at[own_rows], lsem.at[n]),
            pltpu.make_async_remote_copy(g_ref, dst.at[other_rows], xsend.at[n], xrecv.at[n], device_id=pp, device_id_type=MESH),
        )
    copies[8] = pair(8, n_ref, n_ref, left.at[4])
    copies[9] = pair(9, cols(t_ref, c), cols(t_ref, o), right.at[4])
    copies[10] = pair(10, cols(j_ref, c), cols(j_ref, o), left.at[5])
    copies[11] = pair(11, g_ref, g_ref, right.at[5])
    need = [(0, 1), (2,), (3, 4), (5,), (6, 7), (8, 9), (10, 11)]
    which = [(0, 0), (1, 0), (2, 1), (2, 2), (3, 3), (4, 4), (5, 5)]

    vcopies = []
    for k, d in enumerate(dps):
        cp = pltpu.make_async_remote_copy(vec_ref.at[d[0]], vgot.at[k], vsend.at[k], vrecv.at[k], device_id=d, device_id_type=MESH)
        cp.start(); vcopies.append(cp)

    started = {j: [] for j in range(7)}
    def rc(j, slot, src, dst, dev):
        cp = pltpu.make_async_remote_copy(src, dst, send.at[j, slot], recv.at[j, slot], device_id=dev, device_id_type=MESH)
        cp.start(); started[j].append(cp)
    def got(j, slot, dst):
        pltpu.make_async_remote_copy(dst, dst, send.at[j, slot], recv.at[j, slot], device_id=pp, device_id_type=MESH).wait_recv()
    nz = Z - 1
    nb = part.shape[0]

    def stage1(j):
        for n in need[j]:
            copies[n][0].wait(); copies[n][1].wait_recv()
        if j >= nb:
            for cp in started[j - nb]: cp.wait_send()
        D = part.at[j % nb]
        li, ri = which[j]
        step = wide - lanes_a
        def chunk(n, _):
            lanes = pl.ds(pl.multiple_of(n * step, 128), step)
            r = lax.dot_general(left[li], right[ri, :, lanes], (((0,), (0,)), ((), ())), preferred_element_type=F32)
            D[:, :, :, :, lanes] = r.reshape(Z, 2, 2, rows, step).astype(BF)
            return _
        lax.fori_loop(0, wide // step, chunk, 0)
        rc(j, 0, D.at[:, 1 - x, 1 - y, :, A], ra1.at[j, 0], yp)
        rc(j, 2, D.at[:, 1 - x, :, :, C], rc1.at[j], xp)
        rc(j, 1, D.at[:, x, 1 - y, :, A], ra1.at[j, 1], yp)
    def add(D, at, got_ref):
        D[at] = (D[at].astype(F32) + got_ref[...].astype(F32)).astype(BF)
    def stage2(j):
        D = part.at[j % nb]
        got(j, 0, ra1.at[j, 0])
        for zz in range(Z):
            va = D.at[zz, 1 - x, y, :, A]
            va[...] = (va[...].astype(F32) + ra1[j, 0, zz].astype(F32)).astype(BF)
        rc(j, 3, D.at[:, 1 - x, y, :, A], ra2.at[j], xp)
        got(j, 2, rc1.at[j])
        for zz in range(Z):
            for yy in range(2):
                va = D.at[zz, x, yy, :, C]
                va[...] = (va[...].astype(F32) + rc1[j, zz, yy].astype(F32)).astype(BF)
        for k in range(nz):
            rc(j, 4 + k, D.at[zi[k], x, :, :, C], rc2.at[j, k], zs[k])
    def stage3(j):
        D = part.at[j % nb]
        got(j, 1, ra1.at[j, 1])
        got(j, 3, ra2.at[j])
        for zz in range(Z):
            va = D.at[zz, x, y, :, A]
            va[...] = (va[...].astype(F32) + ra1[j, 1, zz].astype(F32) + ra2[j, zz].astype(F32)).astype(BF)
        for k in range(nz):
            rc(j, 4 + nz + k, D.at[zi[k], x, y, :, A], ra3.at[j, k], zs[k])
        for k in range(nz):
            got(j, 4 + k, rc2.at[j, k])
        for yy in range(2):
            va = D.at[z, x, yy, :, C]
            t = va[...].astype(F32)
            for k in range(nz):
                t = t + rc2[j, k, yy].astype(F32)
            va[...] = t.astype(BF)
        rc(j, 4 + 2 * nz, D.at[z, x, 1 - y, :, C], rc3.at[j], yp)
    pcopies = {}
    def lay(ref, val, first, stride, n):
        for t in range(nt):
            ref[pl.ds(first + t, n, stride=stride), :] = val[:, 128 * t:128 * t + 128]
    def stage4(j):
        D = part.at[j % nb]
        for k in range(nz):
            got(j, 4 + nz + k, ra3.at[j, k])
        got(j, 4 + 2 * nz, rc3.at[j])
        a = D[z, x, y, :, 0:lanes_a].astype(F32)
        for k in range(nz):
            a = a + ra3[j, k].astype(F32)
        b = D[z, x, y, :, lanes_a:wide].astype(F32) + rc3[j].astype(F32)
        v = jnp.concatenate([a, b], 1)
        if j in (0, 1):
            lay(fc2_o, v, j * rows * nt, nt, rows)
        elif j == 6:
            lay(skip_o, v, 0, nt, rows)
        else:
            lo = v[0:half]; hi = v[half:rows]
            keep[j - 2, 0:half, :] = jnp.where(c == 0, lo, hi)
            give[j - 2, 0:half, :] = jnp.where(c == 0, hi, lo)
            cp = pltpu.make_async_remote_copy(give.at[j - 2], take.at[j - 2], psend.at[j - 2], precv.at[j - 2], device_id=pp, device_id_type=MESH)
            cp.start(); pcopies[j] = cp
    def stage5(j):
        pcopies[j].wait_recv()
        mine = keep[j - 2, 0:half, :]; theirs = take[j - 2, 0:half, :]
        first = jnp.where(c == 0, mine, theirs); second = jnp.where(c == 0, theirs, mine)
        if j in (2, 3):
            lay(fc1_o, first, nt * 2 * (j - 2), 4 * nt, half)
            lay(fc1_o, second, nt * (2 * (j - 2) + 1), 4 * nt, half)
        elif j == 5:
            lay(qkv_o, first, 0, 3 * nt, half)
            lay(qkv_o, second, nt, 3 * nt, half)
        else:
            lay(qkv_o, first, 2 * nt, 3 * nt, half)
            lay(proj_o, second, 0, nt, half)
    def vec_first():
        s = vec_ref[dp]
        for k in range(len(dps)):
            pltpu.make_async_remote_copy(vgot.at[k], vgot.at[k], vsend.at[k], vrecv.at[k], device_id=pp, device_id_type=MESH).wait_recv()
            s = s + vgot[k]
        vall[f] = s
        for k, d in enumerate(fs):
            cp = pltpu.make_async_remote_copy(vall.at[f], vall.at[f], wsend.at[k], wrecv.at[k], device_id=d, device_id_type=MESH)
            cp.start(); vcopies.append(cp)
    def vec_last():
        for k in range(3):
            src = lax.rem(f - (k + 1) + 4, 4)
            pltpu.make_async_remote_copy(vall.at[src], vall.at[src], wsend.at[k], wrecv.at[k], device_id=pp, device_id_type=MESH).wait_recv()
        vec_o[...] = vall[0] + vall[1] + vall[2] + vall[3]
    for j in range(7 + 4):
        if j < 7: stage1(j)
        if j == 1: vec_first()
        if j == 2: vec_last()
        if 0 <= j - 1 < 7: stage2(j - 1)
        if 0 <= j - 2 < 7: stage3(j - 2)
        if 0 <= j - 3 < 7: stage4(j - 3)
        if 2 <= j - 4 < 6: stage5(j - 4)
    for j in range(max(0, 7 - nb), 7):
        for cp in started[j]: cp.wait_send()
    for cp in pcopies.values(): cp.wait_send()
    for cp in vcopies: cp.wait_send()
    for a, b in copies.values(): b.wait_send()

def scatter(acts, vec_grad, dpn, wide):
    Z = dpn // 2; length = acts[0].shape[0]
    rows = 2 * wide // (4 * dpn)
    lanes_a = (wide // 128 * 2 + 1) // 3 * 128
    lc = wide - lanes_a
    hbm = pl.BlockSpec(memory_space=pl.ANY); vm = pl.BlockSpec(memory_space=pltpu.VMEM)
    D = pltpu.SemaphoreType.DMA
    half = rows // 2; hp = -(-half // 8) * 8
    nv = vec_grad.shape[0] // dpn
    nz = Z - 1; ns = 5 + 2 * nz
    nb = 4
    V = pltpu.VMEM
    outs = [rows * wide // 128, 3 * half * wide // 128, half * wide // 128, 4 * half * wide // 128, 2 * rows * wide // 128]
    res = pl.pallas_call(
        functools.partial(scatter_kernel, Z, wide, rows, lanes_a, length),
        out_shape=tuple(jax.ShapeDtypeStruct((n, 128), F32) for n in outs) + (jax.ShapeDtypeStruct((1, nv), F32),),
        in_specs=[hbm] * 10 + [vm], out_specs=(vm,) * 6,
        scratch_shapes=[V((6, 2 * length, wide), BF), V((6, 2 * length, wide), BF), V((nb, Z, 2, 2, rows, wide), BF),
                        V((7, 2, Z, rows, lanes_a), BF), V((7, Z, rows, lanes_a), BF), V((7, nz, rows, lanes_a), BF),
                        V((7, Z, 2, rows, lc), BF), V((7, nz, 2, rows, lc), BF), V((7, rows, lc), BF),
                        V((4, hp, wide), F32), V((4, hp, wide), F32), V((4, hp, wide), F32),
                        V((dpn - 1, 1, nv), F32), V((4, 1, nv), F32),
                        D((12,)), D((12,)), D((12,)), D((7, ns)), D((7, ns)), D((4,)), D((4,)), D((dpn - 1,)), D((dpn - 1,)), D((3,)), D((3,))],
        compiler_params=pltpu.CompilerParams(collective_id=1, has_side_effects=True, vmem_limit_bytes=62 << 20),
        name="scatter",
    )(*acts, vec_grad.reshape(dpn, 1, nv))
    return tuple(r.reshape(-1) for r in res)


def whole_rows(width, dp, fsdp, items):
    return fsdp == 4 and dp % 2 == 0 and width % (dp * 16) == 0 and items == 1


def pad_rows(value, rows):
    return jnp.pad(value, ((0, rows - value.shape[0]), (0, 0)))


def by_unit(value, units, chips):
    rows, wide = value.shape
    return value.reshape(rows, chips, units, -1).transpose(0, 2, 1, 3).reshape(rows, wide)


def fast_body(block_in, skip_in, out_grad, caption_len, skip_w, qkv_w, proj_w, fc1_w, fc2_w, vectors):
    items, length, width = block_in.shape
    heads = HEADS
    head_dim = width // heads
    hidden = FF
    scale = head_dim ** (-0.5)
    dpn = lax.axis_size("dp")
    chips = 2 * dpn
    rows = -(-length // 16) * 16
    skip_u, qp_u, fc1_u, fc2_u, vec = gather(skip_w, qkv_w, proj_w, fc1_w, fc2_w, vectors, dpn, width)
    skip_m = skip_u.reshape(2 * width, width)
    qp_m = qp_u.reshape(4, width, width)
    fc1_m = fc1_u.reshape(hidden // width, width, width)
    fc2_m = fc2_u.reshape(hidden, width)
    vec = vec.reshape(-1)
    gain_one = vec[0:width]
    shift_one = vec[width : 2 * width]
    gain_two = vec[2 * width : 3 * width]
    shift_two = vec[3 * width : 4 * width]
    skip_bias = vec[4 * width : 5 * width]
    proj_bias = vec[5 * width : 6 * width]
    fc2_bias = vec[6 * width : 7 * width]
    fc1_bias = vec[7 * width :]
    place = lax.broadcasted_iota(jnp.int32, (1, rows), 1)
    valid = ((place < 1 + caption_len[:, None]) | (place >= 1 + CAPTION)) & (place < length)
    joined = pad_rows(jnp.concatenate([block_in[0], skip_in[0]], -1).astype(jnp.bfloat16), rows)
    first = product(joined, skip_m) + skip_bias
    normed_one = norm_rows(first, gain_one, shift_one).astype(jnp.bfloat16)
    query, keys, values = (
        product(normed_one, qp_m[i]).astype(jnp.bfloat16).reshape(items, rows, heads, head_dim)
        for i in range(3)
    )
    scores = attention_scores(query, keys, valid, scale)
    top = jnp.max(scores, -1, keepdims=True)
    expd = jnp.exp(scores - top)
    total = jnp.sum(expd, -1, keepdims=True)
    probs = expd / total
    log_total = top + jnp.log(total)
    mixed = (
        jnp.einsum("ihst,ithd->ishd", probs.astype(jnp.bfloat16), values, preferred_element_type=jnp.float32)
        .astype(jnp.bfloat16)
        .reshape(rows, width)
    )
    second = first + (product(mixed, qp_m[3]) + proj_bias)
    normed_two = norm_rows(second, gain_two, shift_two).astype(jnp.bfloat16)
    inner = (
        jnp.concatenate([product(normed_two, fc1_m[i]) for i in range(hidden // width)], 1) + fc1_bias
    )
    active = gelu_exact(inner).astype(jnp.bfloat16)
    block_out = second + (product(active, fc2_m) + fc2_bias)
    grad_out = pad_rows(out_grad[0], rows)
    grad_mlp = grad_out.astype(jnp.bfloat16)
    d_fc2_bias = column_sum(grad_mlp)
    d_active = right_product(grad_mlp, fc2_m)
    gelu_value, gelu_pull = jax.vjp(gelu_exact, inner)
    grad_inner = gelu_pull(d_active)[0].astype(jnp.bfloat16)
    d_fc1_bias = column_sum(grad_inner)
    d_normed_two = sum(
        right_product(grad_inner[:, width * i : width * (i + 1)], fc1_m[i])
        for i in range(hidden // width)
    )
    norm_value_two, norm_pull_two = jax.vjp(norm_rows, second, gain_two, shift_two)
    d_second_norm, d_gain_two, d_shift_two = norm_pull_two(d_normed_two)
    grad_second = grad_out + d_second_norm
    grad_attn = grad_second.astype(jnp.bfloat16)
    d_proj_bias = column_sum(grad_attn)
    grad_mixed = (
        right_product(grad_attn, qp_m[3]).astype(jnp.bfloat16).reshape(items, rows, heads, head_dim)
    )
    again_scores = attention_scores(query, keys, valid, scale)
    again_probs = jnp.exp(again_scores - log_total)
    d_probs = jnp.einsum("ishd,ithd->ihst", grad_mixed, values, preferred_element_type=jnp.float32)
    inner_sum = jnp.sum(again_probs * d_probs, -1, keepdims=True)
    grad_scores = (again_probs * (d_probs - inner_sum)).astype(jnp.bfloat16)
    d_query = jnp.einsum("ihst,ithd->ishd", grad_scores, keys, preferred_element_type=jnp.float32) * scale
    d_keys = jnp.einsum("ihst,ishd->ithd", grad_scores, query, preferred_element_type=jnp.float32) * scale
    d_values = jnp.einsum(
        "ihst,ishd->ithd", again_probs.astype(jnp.bfloat16), grad_mixed, preferred_element_type=jnp.float32
    )
    grad_triple = jnp.concatenate(
        [t.reshape(rows, width).astype(jnp.bfloat16) for t in (d_query, d_keys, d_values)], 1
    )
    d_normed_one = sum(
        right_product(grad_triple[:, width * i : width * (i + 1)], qp_m[i]) for i in range(3)
    )
    norm_value_one, norm_pull_one = jax.vjp(norm_rows, first, gain_one, shift_one)
    d_first_norm, d_gain_one, d_shift_one = norm_pull_one(d_normed_one)
    grad_first = (grad_second + d_first_norm).astype(jnp.bfloat16)
    d_skip_bias = column_sum(grad_first)
    in_grad = right_product(grad_first[:length], skip_m[:width])
    skip_grad = right_product(grad_first[:length], skip_m[width:])
    vec_grad = jnp.concatenate(
        [d_gain_one, d_shift_one, d_gain_two, d_shift_two, d_skip_bias, d_proj_bias, d_fc2_bias, d_fc1_bias]
    )
    pieces = scatter(
        (
            by_unit(active, hidden // width, chips),
            grad_mlp,
            normed_two,
            grad_inner,
            mixed,
            grad_attn,
            normed_one,
            grad_triple,
            by_unit(joined, 2, chips),
            grad_first,
        ),
        vec_grad,
        dpn,
        width,
    )
    shape = block_in.shape
    return (block_out[:length].reshape(shape), in_grad.reshape(shape), skip_grad.reshape(shape)) + pieces


def body(block_in, skip_in, out_grad, caption_len, skip_w, qkv_w, proj_w, fc1_w, fc2_w, vectors):
    items, length, width = block_in.shape
    if whole_rows(width, lax.axis_size("dp"), lax.axis_size("fsdp"), items):
        return fast_body(
            block_in, skip_in, out_grad, caption_len, skip_w, qkv_w, proj_w, fc1_w, fc2_w, vectors
        )
    heads = HEADS
    head_dim = width // heads
    hidden = FF
    rows = items * length
    scale = head_dim ** (-0.5)
    gathered = (
        lax.all_gather(skip_w.astype(jnp.bfloat16), ("dp", "fsdp"), axis=0, tiled=True),
        lax.all_gather(qkv_w.astype(jnp.bfloat16), ("dp", "fsdp"), axis=0, tiled=True),
        lax.all_gather(proj_w.astype(jnp.bfloat16), ("dp", "fsdp"), axis=0, tiled=True),
        lax.all_gather(fc1_w.astype(jnp.bfloat16), ("dp", "fsdp"), axis=0, tiled=True),
        lax.all_gather(fc2_w.astype(jnp.bfloat16), ("dp", "fsdp"), axis=0, tiled=True),
    )
    skip_m, qkv_m, proj_m, fc1_m, fc2_m = unpack(gathered, width, hidden)
    vec = lax.all_gather(vectors, "dp", axis=0, tiled=True)
    gain_one = vec[0:width]
    shift_one = vec[width : 2 * width]
    gain_two = vec[2 * width : 3 * width]
    shift_two = vec[3 * width : 4 * width]
    skip_bias = vec[4 * width : 5 * width]
    proj_bias = vec[5 * width : 6 * width]
    fc2_bias = vec[6 * width : 7 * width]
    fc1_bias = vec[7 * width :]
    valid = key_valid(caption_len, length, CAPTION)
    joined = jnp.concatenate([block_in, skip_in], -1).reshape(rows, 2 * width).astype(jnp.bfloat16)
    first = product(joined, skip_m) + skip_bias
    normed_one = norm_rows(first, gain_one, shift_one).astype(jnp.bfloat16)
    triple = (
        product(normed_one, qkv_m).astype(jnp.bfloat16).reshape(items, length, 3, heads, head_dim)
    )
    query = triple[:, :, 0]
    keys = triple[:, :, 1]
    values = triple[:, :, 2]
    scores = attention_scores(query, keys, valid, scale)
    top = jnp.max(scores, -1, keepdims=True)
    expd = jnp.exp(scores - top)
    total = jnp.sum(expd, -1, keepdims=True)
    probs = expd / total
    log_total = top + jnp.log(total)
    mixed = (
        jnp.einsum(
            "ihst,ithd->ishd",
            probs.astype(jnp.bfloat16),
            values,
            preferred_element_type=jnp.float32,
        )
        .astype(jnp.bfloat16)
        .reshape(rows, width)
    )
    second = first + (product(mixed, proj_m) + proj_bias)
    normed_two = norm_rows(second, gain_two, shift_two).astype(jnp.bfloat16)
    inner = product(normed_two, fc1_m) + fc1_bias
    active = gelu_exact(inner).astype(jnp.bfloat16)
    block_out = second + (product(active, fc2_m) + fc2_bias)
    again = (
        lax.all_gather(skip_w.astype(jnp.bfloat16), ("dp", "fsdp"), axis=0, tiled=True),
        lax.all_gather(qkv_w.astype(jnp.bfloat16), ("dp", "fsdp"), axis=0, tiled=True),
        lax.all_gather(proj_w.astype(jnp.bfloat16), ("dp", "fsdp"), axis=0, tiled=True),
        lax.all_gather(fc1_w.astype(jnp.bfloat16), ("dp", "fsdp"), axis=0, tiled=True),
        lax.all_gather(fc2_w.astype(jnp.bfloat16), ("dp", "fsdp"), axis=0, tiled=True),
    )
    skip_m, qkv_m, proj_m, fc1_m, fc2_m = unpack(again, width, hidden)
    grad_out = out_grad.reshape(rows, width)
    grad_mlp = grad_out.astype(jnp.bfloat16)
    d_fc2_bias = column_sum(grad_mlp)
    d_active = right_product(grad_mlp, fc2_m)
    gelu_value, gelu_pull = jax.vjp(gelu_exact, inner)
    grad_inner = gelu_pull(d_active)[0].astype(jnp.bfloat16)
    d_fc1_bias = column_sum(grad_inner)
    d_normed_two = right_product(grad_inner, fc1_m)
    norm_value_two, norm_pull_two = jax.vjp(norm_rows, second, gain_two, shift_two)
    d_second_norm, d_gain_two, d_shift_two = norm_pull_two(d_normed_two)
    grad_second = grad_out + d_second_norm
    grad_attn = grad_second.astype(jnp.bfloat16)
    d_proj_bias = column_sum(grad_attn)
    grad_mixed = (
        right_product(grad_attn, proj_m)
        .astype(jnp.bfloat16)
        .reshape(items, length, heads, head_dim)
    )
    again_scores = attention_scores(query, keys, valid, scale)
    again_probs = jnp.exp(again_scores - log_total)
    d_probs = jnp.einsum("ishd,ithd->ihst", grad_mixed, values, preferred_element_type=jnp.float32)
    inner_sum = jnp.sum(again_probs * d_probs, -1, keepdims=True)
    grad_scores = (again_probs * (d_probs - inner_sum)).astype(jnp.bfloat16)
    d_query = (
        jnp.einsum("ihst,ithd->ishd", grad_scores, keys, preferred_element_type=jnp.float32) * scale
    )
    d_keys = (
        jnp.einsum("ihst,ishd->ithd", grad_scores, query, preferred_element_type=jnp.float32)
        * scale
    )
    d_values = jnp.einsum(
        "ihst,ishd->ithd",
        again_probs.astype(jnp.bfloat16),
        grad_mixed,
        preferred_element_type=jnp.float32,
    )
    grad_triple = (
        jnp.stack([d_query, d_keys, d_values], 2).astype(jnp.bfloat16).reshape(rows, 3 * width)
    )
    d_normed_one = right_product(grad_triple, qkv_m)
    norm_value_one, norm_pull_one = jax.vjp(norm_rows, first, gain_one, shift_one)
    d_first_norm, d_gain_one, d_shift_one = norm_pull_one(d_normed_one)
    grad_first = (grad_second + d_first_norm).astype(jnp.bfloat16)
    d_skip_bias = column_sum(grad_first)
    grad_joined = right_product(grad_first, skip_m).reshape(items, length, 2 * width)
    in_grad = grad_joined[:, :, 0:width]
    skip_grad = grad_joined[:, :, width:]
    owners = lax.axis_size(("dp", "fsdp"))
    pairs = (
        (joined, grad_first),
        (normed_one, grad_triple),
        (mixed, grad_attn),
        (normed_two, grad_inner),
        (active, grad_mlp),
    )
    shard_sizes = [pair[0].shape[1] * pair[1].shape[1] // owners for pair in pairs]
    blocks = []
    for pair, owner_share in zip(pairs, shard_sizes):
        blocks.append(
            flat_piece(pair[0], pair[1]).reshape(1 * lax.axis_size(("dp", "fsdp")), owner_share)
        )
    owned = lax.psum_scatter(
        jnp.concatenate(blocks, 1), ("dp", "fsdp"), scatter_dimension=0, tiled=True
    ).reshape(-1)
    pieces = []
    offset = 0
    for share in shard_sizes:
        pieces.append(owned[offset : offset + share])
        offset = offset + share
    vec_grad = jnp.concatenate(
        [
            d_gain_one,
            d_shift_one,
            d_gain_two,
            d_shift_two,
            d_skip_bias,
            d_proj_bias,
            d_fc2_bias,
            d_fc1_bias,
        ]
    )
    vec_rows = lax.psum_scatter(vec_grad, "dp", scatter_dimension=0, tiled=True)
    vec_total = lax.psum(vec_rows, "fsdp")
    return (
        block_out.reshape(items, length, width),
        in_grad,
        skip_grad,
        pieces[0],
        pieces[1],
        pieces[2],
        pieces[3],
        pieces[4],
        vec_total,
    )


def solution(mesh):
    placed = (
        P(("dp", "fsdp"), None, None),
        P(("dp", "fsdp"), None, None),
        P(("dp", "fsdp"), None, None),
        P(("dp", "fsdp")),
        P(("dp", "fsdp")),
        P(("dp", "fsdp")),
        P(("dp", "fsdp")),
        P(("dp", "fsdp")),
        P(("dp", "fsdp")),
        P("dp"),
    )
    return jax.shard_map(
        body,
        mesh=mesh,
        in_specs=placed,
        out_specs=(
            P(("dp", "fsdp"), None, None),
            P(("dp", "fsdp"), None, None),
            P(("dp", "fsdp"), None, None),
            P(("dp", "fsdp")),
            P(("dp", "fsdp")),
            P(("dp", "fsdp")),
            P(("dp", "fsdp")),
            P(("dp", "fsdp")),
            P("dp"),
        ),
        check_vma=False,
    )
```

```python
import functools

import jax
import jax.numpy as jnp
from jax import lax
from jax.experimental import pallas as pl
from jax.experimental.pallas import tpu as pltpu
from jax.sharding import PartitionSpec as P

HEADS = 16
FF = 4608
CAPTION = 77


epsilon = 1e-05
masked_value = -1e30


def norm_rows(value, gain, shift):
    center = value - jnp.mean(value, -1, keepdims=True)
    spread = jnp.mean(center * center, -1, keepdims=True)
    return center * lax.rsqrt(spread + epsilon) * gain + shift


def gelu_exact(value):
    return jax.nn.gelu(value, approximate=False)


def key_valid(caption_len, length, caption):
    place = lax.broadcasted_iota(jnp.int32, (caption_len.shape[0], length), 1)
    return (place < 1 + caption_len[:, None]) | (place >= 1 + caption)


def product(left, right):
    return jnp.dot(left, right, preferred_element_type=jnp.float32)


def left_product(left, right):
    return lax.dot_general(
        left, right, (((0,), (0,)), ((), ())), preferred_element_type=jnp.float32
    )


def right_product(left, right):
    return lax.dot_general(
        left, right, (((1,), (1,)), ((), ())), preferred_element_type=jnp.float32
    )


def unpack(flat, width, hidden):
    return (
        flat[0].reshape(2 * width, width),
        flat[1].reshape(width, 3 * width),
        flat[2].reshape(width, width),
        flat[3].reshape(width, hidden),
        flat[4].reshape(hidden, width),
    )


def attention_scores(query, keys, valid, scale):
    raw = jnp.einsum("ishd,ithd->ihst", query, keys, preferred_element_type=jnp.float32) * scale
    return jnp.where(valid[:, None, None, :], raw, masked_value)


def column_sum(value):
    return jnp.sum(value.astype(jnp.float32), 0)


def flat_piece(left, right):
    grad_rows = left_product(left, right).reshape(-1)
    return grad_rows


MESH = pl.DeviceIdType.MESH
BF=jnp.bfloat16; F32=jnp.float32
SPLIT = 384


def unit_lanes(value, units, chips):
    seg = value.shape[1] // (units * chips)
    return [
        jnp.concatenate([value[:, (s * units + u) * seg : (s * units + u + 1) * seg] for s in range(chips)], 1)
        for u in range(units)
    ]


def row_loop(total, step, fn):
    def one(n, carry):
        fn(pl.ds(pl.multiple_of(n * step, step), step))
        return carry
    lax.fori_loop(0, total // step, one, 0)


def forward_kernel(Z, wide, rows, lanes_a, length, padded,
                   cap_ref, skip_ref, qkv_ref, proj_ref, fc1_ref, fc2_ref, vec_ref, in_ref, sk_ref, og_ref,
                   skip_o, qp_o, fc1_o, fc2_o, vec_o, out_o, j_o, h0_o, a_o, t_o, mix_o, h1_o, m_o, z_o, gm_o, gu_o,
                   own, mine, give, take, vbuf, vecs, b1s, xin, gin, jn, jp, h0, a, t, oacc, mix, h1, m, zz, der, gm, gu, tmp, acc, wbuf,
                   send, recv, lsem, psend, precv, vsend, vrecv, isem, osem, wsem):
    dp = lax.axis_index("dp"); f = lax.axis_index("fsdp")
    z = dp // 2; x = dp % 2; y = f // 2; c = f % 2
    nt = wide // 128
    half = rows // 2
    chips = 4 * Z
    A = pl.ds(0, lanes_a); C = pl.ds(lanes_a, wide - lanes_a)
    zs = [(lax.rem(z + k, Z) * 2 + x, f) for k in range(1, Z)]
    xp = (z * 2 + 1 - x, f)
    yp = (dp, (1 - y) * 2 + c)
    pp = (dp, y * 2 + 1 - c)
    ndp = 2 * Z
    others = [(lax.rem(dp + k, ndp), f) for k in range(1, ndp)]
    bar = pltpu.get_barrier_semaphore()
    for d in others + [yp, pp]:
        pl.semaphore_signal(bar, inc=1, device_id=d, device_id_type=MESH)
    loads = [
        pltpu.make_async_copy(in_ref, xin.at[0], isem.at[0]),
        pltpu.make_async_copy(sk_ref, xin.at[1], isem.at[1]),
        pltpu.make_async_copy(og_ref, gin, isem.at[2]),
    ]
    for cp in loads: cp.start()
    for j in range(nt):
        own[0, :, 128 * j:128 * j + 128] = skip_ref[pl.ds(j, rows, stride=nt), :].astype(BF)
    pl.semaphore_wait(bar, len(others) + 2)

    nz = Z - 1
    waits = []
    def rc(i, slot, src, dst, dev):
        cp = pltpu.make_async_remote_copy(src, dst, send.at[i, slot], recv.at[i, slot], device_id=dev, device_id_type=MESH)
        cp.start(); waits.append(cp)
    def got(i, slot, dst):
        pltpu.make_async_remote_copy(dst, dst, send.at[i, slot], recv.at[i, slot], device_id=pp, device_id_type=MESH).wait_recv()
    def unit(i, cc):
        if i == 0: return skip_o.at[:, :, :, cc]
        if i in (1, 2): return qp_o.at[2 * (i - 1) + cc]
        if i in (3, 4): return fc1_o.at[2 * (i - 3) + cc]
        return fc2_o.at[2 * cc + (i - 5)]
    pc = {}
    lc = {}
    def stage1(i):
        U = unit(i, c)
        if i in (1, 2, 3, 4):
            pc[i].wait_recv()
            p = mine[i - 1, 0:half, :]
            q = take[i - 1, :, :].astype(F32)[0:half]
            lo = jnp.where(c == 0, p, q); hi = jnp.where(c == 0, q, p)
            own[i, :, :] = jnp.concatenate([lo, hi], 0).astype(BF)
        lc[i] = pltpu.make_async_copy(own.at[i], U.at[z, x, y], lsem.at[i]); lc[i].start()
        rc(i, 2 * nz, own.at[i, :, C], U.at[z, x, y, :, C], yp)
        for k in range(1, Z):
            rc(i, k - 1, own.at[i, :, A], U.at[z, x, y, :, A], zs[k - 1])
    def stage2(i):
        U = unit(i, c)
        lc[i].wait()
        got(i, 2 * nz, U.at[z, x, 1 - y, :, C])
        for k in range(1, Z):
            rc(i, nz + k - 1, U.at[z, x, :, :, C], U.at[z, x, :, :, C], zs[k - 1])
        for k in range(1, Z):
            got(i, k - 1, U.at[lax.rem(z - k + Z, Z), x, y, :, A])
        L = U.at[:, x, y, :, A]
        rc(i, 2 * nz + 1, L, L, xp)
        rc(i, 2 * nz + 2, L, L, yp)
        rc(i, 2 * nz + 5, L, L, pp)
    def stage3(i):
        U = unit(i, c)
        for k in range(1, Z):
            got(i, nz + k - 1, U.at[lax.rem(z - k + Z, Z), x, :, :, C])
        L = U.at[:, x, :, :, C]
        rc(i, 2 * nz + 4, L, L, xp)
        rc(i, 2 * nz + 6, L, L, pp)
        L = U.at[:, 1 - x, y, :, A]
        got(i, 2 * nz + 1, L)
        rc(i, 2 * nz + 3, L, L, yp)
        rc(i, 2 * nz + 7, L, L, pp)
    def stage4(i):
        U = unit(i, c)
        L = U.at[:, x, 1 - y, :, A]
        got(i, 2 * nz + 2, L); rc(i, 2 * nz + 8, L, L, pp)
        L = U.at[:, 1 - x, 1 - y, :, A]
        got(i, 2 * nz + 3, L); rc(i, 2 * nz + 9, L, L, pp)
        L = U.at[:, 1 - x, :, :, C]
        got(i, 2 * nz + 4, L); rc(i, 2 * nz + 10, L, L, pp)
    def arrived(i):
        U = unit(i, 1 - c)
        got(i, 2 * nz + 5, U.at[:, x, y, :, A])
        got(i, 2 * nz + 7, U.at[:, 1 - x, y, :, A])
        got(i, 2 * nz + 8, U.at[:, x, 1 - y, :, A])
        got(i, 2 * nz + 9, U.at[:, 1 - x, 1 - y, :, A])
        got(i, 2 * nz + 6, U.at[:, x, :, :, C])
        got(i, 2 * nz + 10, U.at[:, 1 - x, :, :, C])
    def exchange(i, first, second):
        mine[i - 1, 0:half, :] = jnp.where(c == 0, first, second)
        give[i - 1, 0:half, :] = jnp.where(c == 0, second, first).astype(BF)
        pc[i] = pltpu.make_async_remote_copy(give.at[i - 1], take.at[i - 1], psend.at[i - 1], precv.at[i - 1], device_id=pp, device_id_type=MESH)
        pc[i].start()

    stage1(0)
    vcopies = []
    for k, d in enumerate(others):
        cp = pltpu.make_async_remote_copy(vec_ref, vbuf.at[dp], vsend.at[k], vrecv.at[k], device_id=d, device_id_type=MESH)
        cp.start(); vcopies.append(cp)
    vbuf[dp] = vec_ref[...]
    def read(ref, first, stride):
        return jnp.concatenate([ref[pl.ds(first + j, half, stride=stride), :] for j in range(nt)], 1)
    exchange(1, read(qkv_ref, 0, 3 * nt), read(qkv_ref, nt, 3 * nt))
    exchange(2, read(qkv_ref, 2 * nt, 3 * nt), read(proj_ref, 0, nt))
    def prepare_late():
        for j in range(nt):
            own[5, :, 128 * j:128 * j + 128] = fc2_ref[pl.ds(j, rows, stride=nt), :].astype(BF)
            own[6, :, 128 * j:128 * j + 128] = fc2_ref[pl.ds(j + nt * rows, rows, stride=nt), :].astype(BF)
        nat = jnp.concatenate([read(fc1_ref, nt * v, 4 * nt) for v in range(4)], 1)
        u = unit_lanes(nat, 4, chips)
        exchange(3, u[0], u[1])
        exchange(4, u[2], u[3])

    emitted = []
    def emit(src, dst):
        cp = pltpu.make_async_copy(src, dst, osem.at[len(emitted)])
        cp.start(); emitted.append(cp)
    def weight(n, ref):
        cp = pltpu.make_async_copy(ref, wbuf.at[n % 2], wsem.at[n % 2])
        cp.start()
        return cp
    def both_skip(ref, k):
        for i in range(Z // 2):
            pltpu.make_async_copy(ref.at[k * (Z // 2) + i], wbuf.at[k, pl.ds(2 * i, 2)], wsem.at[k]).start()
    def weight_wait(k):
        pltpu.make_async_copy(wbuf.at[k], wbuf.at[k], wsem.at[k]).wait()
    def cols(k, l):
        return wbuf[k, :, :, :, :, l].reshape(wide, SPLIT)
    def lanes_loop(fn):
        def one(n, carry):
            fn(pl.ds(pl.multiple_of(n * SPLIT, 128), SPLIT))
            return carry
        lax.fori_loop(0, wide // SPLIT, one, 0)
    def vector(n):
        return vecs[0:1, n * wide:(n + 1) * wide]
    def norm(src, gain, shift, dst):
        def one(r):
            v = src[r, :]
            cen = v - jnp.mean(v, -1, keepdims=True)
            s = jnp.mean(cen * cen, -1, keepdims=True)
            dst[r, :] = (cen * lax.rsqrt(s + epsilon) * gain + shift).astype(BF)
        row_loop(padded, 16, one)
    def inputs():
        for cp in loads: cp.wait()
        tail = padded - 16
        jn[tail:padded, :] = jnp.zeros((16, 2 * wide), BF)
        gm[tail:padded, :] = jnp.zeros((16, wide), BF)
        full = length // 16 * 16
        def one(r):
            jn[r, 0:wide] = xin[0, r, :].astype(BF)
            jn[r, wide:2 * wide] = xin[1, r, :].astype(BF)
            gm[r, :] = gin[r, :].astype(BF)
        row_loop(full, 16, one)
        if length > full:
            r = slice(full, length)
            jn[r, 0:wide] = xin[0, r, :].astype(BF)
            jn[r, wide:2 * wide] = xin[1, r, :].astype(BF)
            gm[r, :] = gin[r, :].astype(BF)
        def two(r):
            u = unit_lanes(jn[r, :], 2, chips)
            jp[0, r, :] = u[0]
            jp[1, r, :] = u[1]
        row_loop(padded, 16, two)
        emit(jp, j_o)
        emit(gm, gm_o)
    def vectors():
        for k in range(len(others)):
            pltpu.make_async_remote_copy(vec_ref, vbuf.at[lax.rem(dp - (k + 1) + ndp, ndp)], vsend.at[k], vrecv.at[k], device_id=pp, device_id_type=MESH).wait_recv()
        vecs[...] = jnp.concatenate([vbuf[k] for k in range(ndp)], 1)
        b = unit_lanes(vecs[0:1, 7 * wide:11 * wide], 4, chips)
        for u in range(4): b1s[u] = b[u]
    def first_part():
        arrived(0)
        for k in range(2): both_skip(skip_o, k)
        for k in range(2): weight_wait(k)
        def one(l):
            v = jnp.dot(jn[:, 0:wide], cols(0, l), preferred_element_type=F32)
            v = v + jnp.dot(jn[:, wide:2 * wide], cols(1, l), preferred_element_type=F32)
            h0[:, l] = v + vecs[0:1, pl.ds(4 * wide + l.start, SPLIT)]
        lanes_loop(one)
        norm(h0, vector(0), vector(1), a)
        emit(h0, h0_o)
        emit(a, a_o)
    def project(n, u):
        def one(l):
            t[u, :, l] = jnp.dot(a[...], cols(n % 2, l), preferred_element_type=F32).astype(BF)
        lanes_loop(one)
    def query_keys():
        arrived(1)
        w = [weight(u, qp_o.at[u]) for u in range(2)]
        for u in range(2):
            w[u].wait()
            project(u, u)
    def values():
        arrived(2)
        w = [weight(0, qp_o.at[2]), weight(1, qp_o.at[3])]
        for cp in w: cp.wait()
        project(0, 2)
        emit(t, t_o)
    hd = wide // HEADS
    def attend(first, last):
        cap = cap_ref[0]
        key = lax.broadcasted_iota(jnp.int32, (1, padded), 1)
        live = ((key < 1 + cap) | (key >= 1 + CAPTION)) & (key < length)
        def head(h, carry):
            base = pl.multiple_of(jnp.minimum((h * hd) // 128, nt - 2) * 128, 128)
            win = pl.ds(base, 256)
            lane = lax.broadcasted_iota(jnp.int32, (1, 256), 1) + (base - h * hd)
            inside = (lane >= 0) & (lane < hd)
            q = jnp.where(inside, t[0, :, win].astype(F32), 0.0).astype(BF)
            s = lax.dot_general(q, t[1, :, win], (((1,), (1,)), ((), ())), preferred_element_type=F32) * hd ** (-0.5)
            s = jnp.where(live, s, masked_value)
            e = jnp.exp(s - jnp.max(s, -1, keepdims=True))
            p = (e / jnp.sum(e, -1, keepdims=True)).astype(BF)
            v = jnp.dot(p, t[2, :, win], preferred_element_type=F32)
            oacc[:, win] = jnp.where(inside, v, oacc[:, win])
            return carry
        lax.fori_loop(first, last, head, 0)
    def second_part():
        def cast(r): mix[r, :] = oacc[r, :].astype(BF)
        row_loop(padded, 16, cast)
        emit(mix, mix_o)
        def one(l):
            v = jnp.dot(mix[...], cols(1, l), preferred_element_type=F32)
            h1[:, l] = h0[:, l] + (v + vecs[0:1, pl.ds(5 * wide + l.start, SPLIT)])
        lanes_loop(one)
        norm(h1, vector(2), vector(3), m)
        emit(h1, h1_o)
        emit(m, m_o)
        def start(r): acc[r, :] = h1[r, :] + vector(6)
        row_loop(padded, 16, start)
    def widen_load(i):
        arrived(i)
        return [weight(k, fc1_o.at[2 * (i - 3) + k]) for k in range(2)]
    def widen(u, w):
        w[u % 2].wait()
        def one(l):
            tmp[:, l] = jnp.dot(m[...], cols(u % 2, l), preferred_element_type=F32)
        lanes_loop(one)
        def two(r):
            v = tmp[r, :] + b1s[u]
            cdf = 0.5 * (1.0 + lax.erf(v * 0.7071067811865476))
            pdf = jnp.exp(-0.5 * v * v) * 0.3989422804014327
            zz[u, r, :] = (v * cdf).astype(BF)
            der[u, r, :] = cdf + v * pdf
        row_loop(padded, 16, two)
    def narrow(i):
        arrived(i)
        us = [i - 5, 2 + i - 5]
        w = [weight(k, fc2_o.at[us[k]]) for k in range(2)]
        for k in range(2):
            w[k].wait()
            u = us[k]
            def one(l):
                w = cols(k, l)
                acc[:, l] += jnp.dot(zz[u], w, preferred_element_type=F32)
                tmp[...] += lax.dot_general(gm[:, l], w, (((1,), (1,)), ((), ())), preferred_element_type=F32)
            tmp[...] = jnp.zeros_like(tmp)
            lanes_loop(one)
            def two(r):
                gu[u, r, :] = (tmp[r, :] * der[u, r, :]).astype(BF)
            row_loop(padded, 16, two)

    stage2(0)
    prepare_late()
    stage1(1)
    stage3(0)
    inputs()
    vectors()
    stage2(1); stage1(2)
    stage3(1); stage4(0)
    first_part()
    stage2(2); stage1(3)
    stage3(2); stage4(1)
    query_keys()
    stage2(3); stage1(4)
    stage3(3); stage4(2)
    oacc[...] = jnp.zeros_like(oacc)
    values()
    attend(0, 4)
    stage2(4); stage1(5)
    attend(4, 11)
    stage3(4); stage4(3)
    attend(11, 16)
    second_part()
    stage2(5); stage1(6)
    w = widen_load(3)
    widen(0, w)
    stage3(5); stage4(4)
    widen(1, w)
    stage2(6)
    w = widen_load(4)
    widen(2, w)
    stage3(6); stage4(5)
    widen(3, w)
    emit(zz, z_o)
    narrow(5)
    stage4(6)
    narrow(6)
    emit(gu, gu_o)
    full = length // 16 * 16
    def last(r): gin[r, :] = acc[r, :]
    row_loop(full, 16, last)
    if length > full: gin[full:length, :] = acc[full:length, :]
    emit(gin, out_o)
    emit(vecs, vec_o)
    for cp in emitted: cp.wait()
    for cp in waits: cp.wait_send()
    for cp in pc.values(): cp.wait_send()
    for cp in vcopies: cp.wait_send()


def forward(cap, skip, qkv, proj, fc1, fc2, vectors, block_in, skip_in, out_grad, dpn):
    length, wide = block_in.shape
    Z = dpn // 2; rows = skip.shape[0] // wide
    padded = -(-length // 16) * 16
    lanes_a = (wide // 128 * 2 + 1) // 3 * 128
    U = (Z, 2, 2, rows, wide)
    hbm = pl.BlockSpec(memory_space=pl.ANY); vm = pl.BlockSpec(memory_space=pltpu.VMEM)
    ns = 2 * (Z - 1) + 11
    nv = vectors.shape[0]
    D = pltpu.SemaphoreType.DMA
    V = pltpu.VMEM
    half = -(-rows // 2 // 16) * 16
    S = jax.ShapeDtypeStruct
    act = (padded, wide)
    return pl.pallas_call(
        functools.partial(forward_kernel, Z, wide, rows, lanes_a, length, padded),
        out_shape=(S((Z, 2, 2, 2, rows, wide), BF), S((4,) + U, BF), S((4,) + U, BF), S((4,) + U, BF), S((1, nv * dpn), F32),
                   S((length, wide), F32), S((2,) + act, BF), S(act, F32), S(act, BF), S((3,) + act, BF), S(act, BF), S(act, F32), S(act, BF),
                   S((4,) + act, BF), S(act, BF), S((4,) + act, BF)),
        in_specs=[pl.BlockSpec(memory_space=pltpu.SMEM)] + [vm] * 6 + [hbm] * 3, out_specs=(hbm,) * 16,
        scratch_shapes=[V((7, rows, wide), BF), V((4, half, wide), F32), V((4, half, wide), BF), V((4, half, wide), BF),
                        V((dpn, 1, nv), F32), V((1, nv * dpn), F32), V((4, 1, wide), F32), V((2, length, wide), F32), V((length, wide), F32),
                        V((padded, 2 * wide), BF), V((2,) + act, BF), V(act, F32), V(act, BF), V((3,) + act, BF), V(act, F32), V(act, BF), V(act, F32), V(act, BF),
                        V((4,) + act, BF), V((4,) + act, F32), V(act, BF), V((4,) + act, BF), V(act, F32), V(act, F32), V((2,) + U, BF),
                        D((7, ns)), D((7, ns)), D((7,)), D((4,)), D((4,)), D((dpn - 1,)), D((dpn - 1,)), D((3,)), D((12,)), D((2,))],
        compiler_params=pltpu.CompilerParams(collective_id=0, has_side_effects=True, vmem_limit_bytes=60 << 20),
        name="forward",
    )(cap, *(w.reshape(-1, 128) for w in (skip, qkv, proj, fc1, fc2)), vectors.reshape(1, nv), block_in, skip_in, out_grad)


def natural_lanes(units, chips):
    seg = units[0].shape[1] // chips
    return jnp.concatenate([u[:, s * seg : (s + 1) * seg] for s in range(chips) for u in units], 1)


def backward_kernel(Z, wide, rows, lanes_a, length, padded,
                    cap_ref, vec_ref, skip_ref, qp_ref, fc1_ref, og_ref, j_ref, h0_ref, a_ref, t_ref, mix_ref, h1_ref, m_ref, z_ref, gm_ref, gu_ref,
                    in_o, sk_o, skip_o, qkv_o, proj_o, fc1_o, fc2_o, vec_o,
                    left, right, part, ra1, ra2, ra3, rc1, rc2, rc3, keep, give, take, vpart, vgot, vall,
                    gin, hid, gsum, dacc, out2, gus, t, do, ga, dt, g0, sums, gacc, wbuf,
                    xlsem, xsend, xrecv, send, recv, psend, precv, vsend, vrecv, wsend, wrecv, isem, usem, wsem, osem, free):
    dp = lax.axis_index("dp"); f = lax.axis_index("fsdp")
    z = dp // 2; x = dp % 2; y = f // 2; c = f % 2
    nt = wide // 128
    half = rows // 2
    chips = 4 * Z
    A = pl.ds(0, lanes_a); C = pl.ds(lanes_a, wide - lanes_a)
    zi = [lax.rem(z + k, Z) for k in range(1, Z)]
    zs = [(i * 2 + x, f) for i in zi]
    xp = (z * 2 + 1 - x, f)
    yp = (dp, (1 - y) * 2 + c)
    pp = (dp, y * 2 + 1 - c)
    ndp = 2 * Z
    dps = [(lax.rem(dp + k, ndp), f) for k in range(1, ndp)]
    fs = [(dp, lax.rem(f + k, 4)) for k in range(1, 4)]
    bar = pltpu.get_barrier_semaphore()
    for d in dps + fs:
        pl.semaphore_signal(bar, inc=1, device_id=d, device_id_type=MESH)

    own_rows = pl.ds(0, padded); other_rows = pl.ds(padded, padded)
    o = 1 - c
    locals_ = {}
    def mine(n, src, dst):
        cp = pltpu.make_async_copy(src, dst.at[own_rows], xlsem.at[n]); cp.start()
        locals_[n] = cp
    def theirs(n, src, dst):
        cp = pltpu.make_async_remote_copy(src, dst.at[other_rows], xsend.at[n], xrecv.at[n], device_id=pp, device_id_type=MESH)
        cp.start(); locals_[n + 100] = cp
    early = [
        (0, z_ref.at[2 * c], z_ref.at[2 * o], left.at[0]),
        (1, gm_ref, gm_ref, right.at[0]),
        (2, z_ref.at[2 * c + 1], z_ref.at[2 * o + 1], left.at[1]),
        (3, m_ref, m_ref, left.at[2]),
        (4, gu_ref.at[c], gu_ref.at[o], right.at[1]),
        (5, gu_ref.at[2 + c], gu_ref.at[2 + o], right.at[2]),
    ]
    for n, s, _, d in early: mine(n, s, d)
    loads = [
        pltpu.make_async_copy(og_ref, gin, isem.at[0]),
        pltpu.make_async_copy(h1_ref, hid, isem.at[1]),
        pltpu.make_async_copy(t_ref, t, isem.at[2]),
    ]
    for cp in loads: cp.start()
    pl.semaphore_wait(bar, len(dps) + len(fs))
    for n, _, s, d in early: theirs(n, s, d)
    need = [(0, 1), (2,), (3, 4), (5,), (6, 7), (8, 9), (10, 11)]
    which = [(0, 0), (1, 0), (2, 1), (2, 2), (0, 0), (1, 1), (2, 2)]

    started = {j: [] for j in range(7)}
    def rc(j, slot, src, dst, dev):
        cp = pltpu.make_async_remote_copy(src, dst, send.at[j, slot], recv.at[j, slot], device_id=dev, device_id_type=MESH)
        cp.start(); started[j].append(cp)
    def got(j, slot, dst):
        pltpu.make_async_remote_copy(dst, dst, send.at[j, slot], recv.at[j, slot], device_id=pp, device_id_type=MESH).wait_recv()
    nz = Z - 1
    nb = 4

    def stage1(j):
        for n in need[j]:
            if n in (6, 7):
                pltpu.make_async_copy(gm_ref, left.at[0, own_rows], xlsem.at[n]).wait()
                pltpu.make_async_remote_copy(gm_ref, left.at[0, other_rows], xsend.at[n], xrecv.at[n], device_id=pp, device_id_type=MESH).wait_recv()
            else:
                locals_[n].wait(); locals_[n + 100].wait_recv()
        if j >= nb:
            for cp in started[j - nb]: cp.wait_send()
        D = part.at[j % nb]
        li, ri = which[j]
        step = wide - lanes_a
        def chunk(n, carry):
            lanes = pl.ds(pl.multiple_of(n * step, 128), step)
            r = lax.dot_general(left[li], right[ri, :, lanes], (((0,), (0,)), ((), ())), preferred_element_type=F32)
            D[:, :, :, :, lanes] = r.reshape(Z, 2, 2, rows, step).astype(BF)
            return carry
        lax.fori_loop(0, wide // step, chunk, 0)
        b = j % nb
        rc(j, 0, D.at[:, 1 - x, 1 - y, :, A], ra1.at[b, 0], yp)
        rc(j, 2, D.at[:, 1 - x, :, :, C], rc1.at[b], xp)
        rc(j, 1, D.at[:, x, 1 - y, :, A], ra1.at[b, 1], yp)
    def stage2(j):
        b = j % nb
        D = part.at[b]
        got(j, 0, ra1.at[b, 0])
        for zz in range(Z):
            va = D.at[zz, 1 - x, y, :, A]
            va[...] = (va[...].astype(F32) + ra1[b, 0, zz].astype(F32)).astype(BF)
        rc(j, 3, D.at[:, 1 - x, y, :, A], ra2.at[b], xp)
        got(j, 2, rc1.at[b])
        for zz in range(Z):
            for yy in range(2):
                va = D.at[zz, x, yy, :, C]
                va[...] = (va[...].astype(F32) + rc1[b, zz, yy].astype(F32)).astype(BF)
        for k in range(nz):
            rc(j, 4 + k, D.at[zi[k], x, :, :, C], rc2.at[b, k], zs[k])
    def stage3(j):
        b = j % nb
        D = part.at[b]
        got(j, 1, ra1.at[b, 1])
        got(j, 3, ra2.at[b])
        for zz in range(Z):
            va = D.at[zz, x, y, :, A]
            va[...] = (va[...].astype(F32) + ra1[b, 1, zz].astype(F32) + ra2[b, zz].astype(F32)).astype(BF)
        for k in range(nz):
            rc(j, 4 + nz + k, D.at[zi[k], x, y, :, A], ra3.at[b, k], zs[k])
        for k in range(nz):
            got(j, 4 + k, rc2.at[b, k])
        for yy in range(2):
            va = D.at[z, x, yy, :, C]
            s = va[...].astype(F32)
            for k in range(nz):
                s = s + rc2[b, k, yy].astype(F32)
            va[...] = s.astype(BF)
        rc(j, 4 + 2 * nz, D.at[z, x, 1 - y, :, C], rc3.at[b], yp)
    pcopies = {}
    def lay(ref, val, first, stride, n):
        for i in range(val.shape[1] // 128):
            ref[pl.ds(first + i, n, stride=stride), :] = val[:, 128 * i:128 * i + 128]
    def stage4(j):
        b = j % nb
        D = part.at[b]
        for k in range(nz):
            got(j, 4 + nz + k, ra3.at[b, k])
        got(j, 4 + 2 * nz, rc3.at[b])
        p = D[z, x, y, :, 0:lanes_a].astype(F32)
        for k in range(nz):
            p = p + ra3[b, k].astype(F32)
        q = D[z, x, y, :, lanes_a:wide].astype(F32) + rc3[b].astype(F32)
        v = jnp.concatenate([p, q], 1)
        if j in (0, 1):
            lay(fc2_o, v, j * rows * nt, nt, rows)
        elif j == 6:
            lay(skip_o, v, 0, nt, rows)
        else:
            lo = v[0:half]; hi = v[half:rows]
            keep[j - 2, 0:half, :] = jnp.where(c == 0, lo, hi)
            give[j - 2, 0:half, :] = jnp.where(c == 0, hi, lo)
            cp = pltpu.make_async_remote_copy(give.at[j - 2], take.at[j - 2], psend.at[j - 2], precv.at[j - 2], device_id=pp, device_id_type=MESH)
            cp.start(); pcopies[j] = cp
    def both(j):
        pcopies[j].wait_recv()
        p = keep[j - 2, 0:half, :]; q = take[j - 2, 0:half, :]
        return jnp.where(c == 0, p, q), jnp.where(c == 0, q, p)
    def stage5(j):
        if j == 3:
            lay(fc1_o, natural_lanes(both(2) + both(3), chips), 0, 4 * nt, half)
        elif j == 5:
            first, second = both(5)
            lay(qkv_o, first, 0, 3 * nt, half)
            lay(qkv_o, second, nt, 3 * nt, half)
        elif j == 4:
            first, second = both(4)
            lay(qkv_o, first, 2 * nt, 3 * nt, half)
            lay(proj_o, second, 0, nt, half)

    def weight(n, ref):
        cp = pltpu.make_async_copy(ref, wbuf.at[n % 2], wsem.at[n % 2])
        cp.start()
        return cp
    def both_skip(ref, k):
        for i in range(Z // 2):
            pltpu.make_async_copy(ref.at[k * (Z // 2) + i], wbuf.at[k, pl.ds(2 * i, 2)], wsem.at[k]).start()
    def weight_wait(k):
        pltpu.make_async_copy(wbuf.at[k], wbuf.at[k], wsem.at[k]).wait()
    def cols(k, l):
        return wbuf[k, :, :, :, :, l].reshape(wide, SPLIT)
    def lanes_loop(fn):
        def one(n, carry):
            fn(pl.ds(pl.multiple_of(n * SPLIT, 128), SPLIT))
            return carry
        lax.fori_loop(0, wide // SPLIT, one, 0)
    def vector(n):
        return vec_ref[0:1, n * wide:(n + 1) * wide]
    def zero(n): gacc[n] = jnp.zeros((8, wide), F32)
    def add_rows(n, v):
        gacc[n] += v[0:8] + v[8:16]
    def close(n):
        return jnp.sum(gacc[n], 0, keepdims=True)
    def norm_back(dy, src, gain, fn):
        zero(0); zero(1); zero(2)
        def one(r):
            d = dy[r, :]
            v = src[r, :]
            cen = v - jnp.mean(v, -1, keepdims=True)
            rs = lax.rsqrt(jnp.mean(cen * cen, -1, keepdims=True) + epsilon)
            xh = cen * rs
            dx = d * gain
            g = rs * (dx - jnp.mean(dx, -1, keepdims=True) - xh * jnp.mean(dx * xh, -1, keepdims=True))
            add_rows(0, d * xh)
            add_rows(1, d)
            fn(r, g)
        row_loop(padded, 16, one)
    def turned(dst, lhs, n, fresh):
        if fresh: dst[...] = jnp.zeros_like(dst)
        def one(l):
            dst[...] += lax.dot_general(lhs[:, l], cols(n, l), (((1,), (1,)), ((), ())), preferred_element_type=F32)
        lanes_loop(one)
    def widen_back():
        def load(u):
            cp = pltpu.make_async_copy(gu_ref.at[u], gus.at[u % 2], usem.at[u % 2]); cp.start()
            return (cp, weight(u, fc1_ref.at[u]))
        w = [load(0), load(1)]
        for u in range(4):
            for cp in w[u]: cp.wait()
            turned(dacc, gus.at[u % 2], u % 2, u == 0)
            zero(0)
            def one(r): add_rows(0, gus[u % 2, r, :].astype(F32))
            row_loop(padded, 16, one)
            sums[7 + u] = close(0)
            if u < 2: w.append(load(u + 2))
    def norm_two():
        weight(0, qp_ref.at[3])
        for cp in loads: cp.wait()
        full = length // 16 * 16
        if padded > full:
            gsum[padded - 16:padded, :] = jnp.zeros((16, wide), F32)
        def copy(r): gsum[r, :] = gin[r, :]
        row_loop(full, 16, copy)
        if length > full: gsum[full:length, :] = gin[full:length, :]
        def fn(r, g):
            s = gsum[r, :] + g
            gsum[r, :] = s
            b = s.astype(BF)
            ga[r, :] = b
            add_rows(2, b.astype(F32))
        norm_back(dacc, hid, vector(2), fn)
        sums[2] = close(0); sums[3] = close(1); sums[5] = close(2)
        pltpu.make_async_copy(h0_ref, hid, isem.at[1]).start()
        zero(0)
        def one(r): add_rows(0, right[0, r, :].astype(F32))
        row_loop(padded, 16, one)
        sums[6] = close(0)
        pltpu.make_async_copy(qp_ref.at[3], wbuf.at[0], wsem.at[0]).wait()
        turned(dacc, ga, 0, True)
        def two(r): do[r, :] = dacc[r, :].astype(BF)
        row_loop(padded, 16, two)
    hd = wide // HEADS
    def attend(first, last):
        cap = cap_ref[0]
        key = lax.broadcasted_iota(jnp.int32, (padded, 1), 0)
        live = ((key < 1 + cap) | (key >= 1 + CAPTION)) & (key < length)
        def head(h, carry):
            base = pl.multiple_of(jnp.minimum((h * hd) // 128, nt - 2) * 128, 128)
            win = pl.ds(base, 256)
            lane = lax.broadcasted_iota(jnp.int32, (1, 256), 1) + (base - h * hd)
            inside = (lane >= 0) & (lane < hd)
            q = jnp.where(inside, t[0, :, win].astype(F32), 0.0).astype(BF)
            k = t[1, :, win]
            g = jnp.where(inside, do[:, win].astype(F32), 0.0).astype(BF)
            s = lax.dot_general(k, q, (((1,), (1,)), ((), ())), preferred_element_type=F32) * hd ** (-0.5)
            s = jnp.where(live, s, masked_value)
            e = jnp.exp(s - jnp.max(s, 0, keepdims=True))
            p = e * (1.0 / jnp.sum(e, 0, keepdims=True))
            d = lax.dot_general(t[2, :, win], g, (((1,), (1,)), ((), ())), preferred_element_type=F32)
            ds = (p * (d - jnp.sum(p * d, 0, keepdims=True))).astype(BF)
            dq = lax.dot_general(ds, k, (((0,), (0,)), ((), ())), preferred_element_type=F32) * hd ** (-0.5)
            dk = jnp.dot(ds, q, preferred_element_type=F32) * hd ** (-0.5)
            dv = jnp.dot(p.astype(BF), g, preferred_element_type=F32)
            for i, v in enumerate((dq, dk, dv)):
                dt[i, :, win] = jnp.where(inside, v, dt[i, :, win].astype(F32)).astype(BF)
            return carry
        lax.fori_loop(first, last, head, 0)
    def late_left():
        pl.semaphore_signal(free, inc=1, device_id=pp, device_id_type=MESH)
        pl.semaphore_wait(free, 1)
        @pl.when(c == 0)
        def _():
            pltpu.make_async_copy(a_ref, left.at[0, own_rows], xlsem.at[6]).start()
            pltpu.make_async_remote_copy(mix_ref, left.at[0, other_rows], xsend.at[6], xrecv.at[6], device_id=pp, device_id_type=MESH).start()
        @pl.when(c == 1)
        def _():
            pltpu.make_async_copy(mix_ref, left.at[0, own_rows], xlsem.at[6]).start()
            pltpu.make_async_remote_copy(a_ref, left.at[0, other_rows], xsend.at[6], xrecv.at[6], device_id=pp, device_id_type=MESH).start()
        mine(8, a_ref, left.at[1]); theirs(8, a_ref, left.at[1])
        mine(10, j_ref.at[c], left.at[2]); theirs(10, j_ref.at[o], left.at[2])
    def late_right():
        @pl.when(c == 0)
        def _():
            pltpu.make_async_copy(dt.at[2], right.at[0, own_rows], xlsem.at[7]).start()
            pltpu.make_async_remote_copy(ga, right.at[0, other_rows], xsend.at[7], xrecv.at[7], device_id=pp, device_id_type=MESH).start()
        @pl.when(c == 1)
        def _():
            pltpu.make_async_copy(ga, right.at[0, own_rows], xlsem.at[7]).start()
            pltpu.make_async_remote_copy(dt.at[2], right.at[0, other_rows], xsend.at[7], xrecv.at[7], device_id=pp, device_id_type=MESH).start()
        mine(9, dt.at[c], right.at[1]); theirs(9, dt.at[o], right.at[1])
    def project_back():
        w = [weight(0, qp_ref.at[0]), weight(1, qp_ref.at[1])]
        for i in range(3):
            w[i].wait()
            turned(dacc, dt.at[i], i % 2, i == 0)
            if i == 0: w.append(weight(2, qp_ref.at[2]))
    def norm_one():
        pltpu.make_async_copy(h0_ref, hid, isem.at[1]).wait()
        def fn(r, g):
            b = (gsum[r, :] + g).astype(BF)
            g0[r, :] = b
            add_rows(2, b.astype(F32))
        norm_back(dacc, hid, vector(0), fn)
        sums[0] = close(0); sums[1] = close(1); sums[4] = close(2)
        mine(11, g0, right.at[2]); theirs(11, g0, right.at[2])
    def join_back():
        for k in range(2): both_skip(skip_ref, k)
        full = length // 16 * 16
        for i, (dst, out) in enumerate(((gin, in_o), (out2, sk_o))):
            weight_wait(i)
            turned(dacc, g0, i, True)
            def copy(r): dst[r, :] = dacc[r, :]
            row_loop(full, 16, copy)
            if length > full: dst[full:length, :] = dacc[full:length, :]
            pltpu.make_async_copy(dst, out, osem.at[i]).start()
    vcopies = []
    nv = vpart.shape[2]
    def vec_send():
        full = jnp.concatenate([sums[i] for i in range(7)] + [natural_lanes([sums[7 + u] for u in range(4)], chips)], 1)
        for k in range(ndp): vpart[k] = full[:, k * nv:(k + 1) * nv]
        for k, d in enumerate(dps):
            cp = pltpu.make_async_remote_copy(vpart.at[d[0]], vgot.at[k], vsend.at[k], vrecv.at[k], device_id=d, device_id_type=MESH)
            cp.start(); vcopies.append(cp)
    def vec_first():
        s = vpart[dp]
        for k in range(len(dps)):
            pltpu.make_async_remote_copy(vgot.at[k], vgot.at[k], vsend.at[k], vrecv.at[k], device_id=pp, device_id_type=MESH).wait_recv()
            s = s + vgot[k]
        vall[f] = s
        for k, d in enumerate(fs):
            cp = pltpu.make_async_remote_copy(vall.at[f], vall.at[f], wsend.at[k], wrecv.at[k], device_id=d, device_id_type=MESH)
            cp.start(); vcopies.append(cp)
    def vec_last():
        for k in range(3):
            src = lax.rem(f - (k + 1) + 4, 4)
            pltpu.make_async_remote_copy(vall.at[src], vall.at[src], wsend.at[k], wrecv.at[k], device_id=pp, device_id_type=MESH).wait_recv()
        vec_o[...] = vall[0] + vall[1] + vall[2] + vall[3]

    dt[...] = jnp.zeros_like(dt)
    stage1(0)
    widen_back()
    stage1(1); stage2(0)
    norm_two()
    stage1(2); stage2(1); stage3(0)
    attend(0, 4)
    stage1(3)
    late_left()
    stage2(2); stage3(1); stage4(0)
    attend(4, 10)
    stage2(3); stage3(2); stage4(1)
    attend(10, 16)
    late_right()
    stage1(4)
    stage3(3); stage4(2)
    stage1(5); stage2(4); stage4(3)
    project_back()
    norm_one()
    vec_send()
    stage2(5); stage3(4)
    stage1(6)
    vec_first()
    join_back()
    stage5(3)
    stage2(6); stage3(5); stage4(4)
    vec_last()
    stage3(6); stage4(5); stage5(4)
    stage5(5)
    stage4(6)
    for j in range(3, 7):
        for cp in started[j]: cp.wait_send()
    for cp in pcopies.values(): cp.wait_send()
    for cp in vcopies: cp.wait_send()
    for n in (0, 1, 2, 3, 4, 5, 8, 9, 10, 11): locals_[n + 100].wait_send()
    for n in (6, 7):
        pltpu.make_async_remote_copy(gm_ref, left.at[0, other_rows], xsend.at[n], xrecv.at[n], device_id=pp, device_id_type=MESH).wait_send()
    pltpu.make_async_copy(gin, in_o, osem.at[0]).wait()
    pltpu.make_async_copy(out2, sk_o, osem.at[1]).wait()


def backward(cap, vec, skip, qp, fc1, out_grad, acts, dpn):
    length, wide = out_grad.shape
    Z = dpn // 2; rows = 2 * wide // (4 * dpn)
    padded = acts[1].shape[0]
    lanes_a = (wide // 128 * 2 + 1) // 3 * 128
    lc = wide - lanes_a
    hbm = pl.BlockSpec(memory_space=pl.ANY); vm = pl.BlockSpec(memory_space=pltpu.VMEM)
    D = pltpu.SemaphoreType.DMA
    half = rows // 2; hp = -(-half // 8) * 8
    nv = vec.shape[1] // dpn
    nz = Z - 1; ns = 5 + 2 * nz
    nb = 4
    V = pltpu.VMEM
    S = jax.ShapeDtypeStruct
    act = (padded, wide)
    outs = [rows * wide // 128, 3 * half * wide // 128, half * wide // 128, 4 * half * wide // 128, 2 * rows * wide // 128]
    res = pl.pallas_call(
        functools.partial(backward_kernel, Z, wide, rows, lanes_a, length, padded),
        out_shape=(S((length, wide), F32),) * 2 + tuple(S((n, 128), F32) for n in outs) + (S((1, nv), F32),),
        in_specs=[pl.BlockSpec(memory_space=pltpu.SMEM), vm] + [hbm] * 14, out_specs=(hbm,) * 2 + (vm,) * 6,
        scratch_shapes=[V((3, 2 * padded, wide), BF), V((3, 2 * padded, wide), BF), V((nb, Z, 2, 2, rows, wide), BF),
                        V((nb, 2, Z, rows, lanes_a), BF), V((nb, Z, rows, lanes_a), BF), V((nb, nz, rows, lanes_a), BF),
                        V((nb, Z, 2, rows, lc), BF), V((nb, nz, 2, rows, lc), BF), V((nb, rows, lc), BF),
                        V((4, hp, wide), F32), V((4, hp, wide), F32), V((4, hp, wide), F32),
                        V((dpn, 1, nv), F32), V((dpn - 1, 1, nv), F32), V((4, 1, nv), F32),
                        V((length, wide), F32), V(act, F32), V(act, F32), V(act, F32), V((length, wide), F32), V((2,) + act, BF), V((3,) + act, BF),
                        V(act, BF), V(act, BF), V((3,) + act, BF), V(act, BF), V((11, 1, wide), F32), V((3, 8, wide), F32), V((2, Z, 2, 2, rows, wide), BF),
                        D((12,)), D((12,)), D((12,)), D((7, ns)), D((7, ns)), D((4,)), D((4,)), D((dpn - 1,)), D((dpn - 1,)), D((3,)), D((3,)),
                        D((3,)), D((2,)), D((2,)), D((2,)), pltpu.SemaphoreType.REGULAR],
        compiler_params=pltpu.CompilerParams(collective_id=1, has_side_effects=True, vmem_limit_bytes=63 << 20),
        name="backward",
    )(cap, vec, skip, qp, fc1, out_grad, *acts)
    return res[:2] + tuple(r.reshape(-1) for r in res[2:])


def whole_rows(width, dp, fsdp, items, heads, hidden):
    return (
        fsdp == 4 and dp % 2 == 0 and width % (dp * 16) == 0 and items == 1 and hidden == 4 * width
        and width % SPLIT == 0 and width // heads <= 128
    )


def fast_body(block_in, skip_in, out_grad, caption_len, skip_w, qkv_w, proj_w, fc1_w, fc2_w, vectors):
    shape = block_in.shape
    dpn = lax.axis_size("dp")
    res = forward(
        caption_len, skip_w, qkv_w, proj_w, fc1_w, fc2_w, vectors,
        block_in.reshape(shape[1:]), skip_in.reshape(shape[1:]), out_grad.reshape(shape[1:]), dpn,
    )
    skip_m, qp_m, fc1_m, fc2_m, vec, block_out = res[:6]
    grads = backward(caption_len, vec, skip_m, qp_m, fc1_m, out_grad.reshape(shape[1:]), res[6:], dpn)
    return (block_out.reshape(shape), grads[0].reshape(shape), grads[1].reshape(shape)) + tuple(grads[2:])


def body(block_in, skip_in, out_grad, caption_len, skip_w, qkv_w, proj_w, fc1_w, fc2_w, vectors):
    items, length, width = block_in.shape
    if whole_rows(width, lax.axis_size("dp"), lax.axis_size("fsdp"), items, HEADS, FF):
        return fast_body(
            block_in, skip_in, out_grad, caption_len, skip_w, qkv_w, proj_w, fc1_w, fc2_w, vectors
        )
    heads = HEADS
    head_dim = width // heads
    hidden = FF
    rows = items * length
    scale = head_dim ** (-0.5)
    gathered = (
        lax.all_gather(skip_w.astype(jnp.bfloat16), ("dp", "fsdp"), axis=0, tiled=True),
        lax.all_gather(qkv_w.astype(jnp.bfloat16), ("dp", "fsdp"), axis=0, tiled=True),
        lax.all_gather(proj_w.astype(jnp.bfloat16), ("dp", "fsdp"), axis=0, tiled=True),
        lax.all_gather(fc1_w.astype(jnp.bfloat16), ("dp", "fsdp"), axis=0, tiled=True),
        lax.all_gather(fc2_w.astype(jnp.bfloat16), ("dp", "fsdp"), axis=0, tiled=True),
    )
    skip_m, qkv_m, proj_m, fc1_m, fc2_m = unpack(gathered, width, hidden)
    vec = lax.all_gather(vectors, "dp", axis=0, tiled=True)
    gain_one = vec[0:width]
    shift_one = vec[width : 2 * width]
    gain_two = vec[2 * width : 3 * width]
    shift_two = vec[3 * width : 4 * width]
    skip_bias = vec[4 * width : 5 * width]
    proj_bias = vec[5 * width : 6 * width]
    fc2_bias = vec[6 * width : 7 * width]
    fc1_bias = vec[7 * width :]
    valid = key_valid(caption_len, length, CAPTION)
    joined = jnp.concatenate([block_in, skip_in], -1).reshape(rows, 2 * width).astype(jnp.bfloat16)
    first = product(joined, skip_m) + skip_bias
    normed_one = norm_rows(first, gain_one, shift_one).astype(jnp.bfloat16)
    triple = (
        product(normed_one, qkv_m).astype(jnp.bfloat16).reshape(items, length, 3, heads, head_dim)
    )
    query = triple[:, :, 0]
    keys = triple[:, :, 1]
    values = triple[:, :, 2]
    scores = attention_scores(query, keys, valid, scale)
    top = jnp.max(scores, -1, keepdims=True)
    expd = jnp.exp(scores - top)
    total = jnp.sum(expd, -1, keepdims=True)
    probs = expd / total
    log_total = top + jnp.log(total)
    mixed = (
        jnp.einsum(
            "ihst,ithd->ishd",
            probs.astype(jnp.bfloat16),
            values,
            preferred_element_type=jnp.float32,
        )
        .astype(jnp.bfloat16)
        .reshape(rows, width)
    )
    second = first + (product(mixed, proj_m) + proj_bias)
    normed_two = norm_rows(second, gain_two, shift_two).astype(jnp.bfloat16)
    inner = product(normed_two, fc1_m) + fc1_bias
    active = gelu_exact(inner).astype(jnp.bfloat16)
    block_out = second + (product(active, fc2_m) + fc2_bias)
    again = (
        lax.all_gather(skip_w.astype(jnp.bfloat16), ("dp", "fsdp"), axis=0, tiled=True),
        lax.all_gather(qkv_w.astype(jnp.bfloat16), ("dp", "fsdp"), axis=0, tiled=True),
        lax.all_gather(proj_w.astype(jnp.bfloat16), ("dp", "fsdp"), axis=0, tiled=True),
        lax.all_gather(fc1_w.astype(jnp.bfloat16), ("dp", "fsdp"), axis=0, tiled=True),
        lax.all_gather(fc2_w.astype(jnp.bfloat16), ("dp", "fsdp"), axis=0, tiled=True),
    )
    skip_m, qkv_m, proj_m, fc1_m, fc2_m = unpack(again, width, hidden)
    grad_out = out_grad.reshape(rows, width)
    grad_mlp = grad_out.astype(jnp.bfloat16)
    d_fc2_bias = column_sum(grad_mlp)
    d_active = right_product(grad_mlp, fc2_m)
    gelu_value, gelu_pull = jax.vjp(gelu_exact, inner)
    grad_inner = gelu_pull(d_active)[0].astype(jnp.bfloat16)
    d_fc1_bias = column_sum(grad_inner)
    d_normed_two = right_product(grad_inner, fc1_m)
    norm_value_two, norm_pull_two = jax.vjp(norm_rows, second, gain_two, shift_two)
    d_second_norm, d_gain_two, d_shift_two = norm_pull_two(d_normed_two)
    grad_second = grad_out + d_second_norm
    grad_attn = grad_second.astype(jnp.bfloat16)
    d_proj_bias = column_sum(grad_attn)
    grad_mixed = (
        right_product(grad_attn, proj_m)
        .astype(jnp.bfloat16)
        .reshape(items, length, heads, head_dim)
    )
    again_scores = attention_scores(query, keys, valid, scale)
    again_probs = jnp.exp(again_scores - log_total)
    d_probs = jnp.einsum("ishd,ithd->ihst", grad_mixed, values, preferred_element_type=jnp.float32)
    inner_sum = jnp.sum(again_probs * d_probs, -1, keepdims=True)
    grad_scores = (again_probs * (d_probs - inner_sum)).astype(jnp.bfloat16)
    d_query = (
        jnp.einsum("ihst,ithd->ishd", grad_scores, keys, preferred_element_type=jnp.float32) * scale
    )
    d_keys = (
        jnp.einsum("ihst,ishd->ithd", grad_scores, query, preferred_element_type=jnp.float32)
        * scale
    )
    d_values = jnp.einsum(
        "ihst,ishd->ithd",
        again_probs.astype(jnp.bfloat16),
        grad_mixed,
        preferred_element_type=jnp.float32,
    )
    grad_triple = (
        jnp.stack([d_query, d_keys, d_values], 2).astype(jnp.bfloat16).reshape(rows, 3 * width)
    )
    d_normed_one = right_product(grad_triple, qkv_m)
    norm_value_one, norm_pull_one = jax.vjp(norm_rows, first, gain_one, shift_one)
    d_first_norm, d_gain_one, d_shift_one = norm_pull_one(d_normed_one)
    grad_first = (grad_second + d_first_norm).astype(jnp.bfloat16)
    d_skip_bias = column_sum(grad_first)
    grad_joined = right_product(grad_first, skip_m).reshape(items, length, 2 * width)
    in_grad = grad_joined[:, :, 0:width]
    skip_grad = grad_joined[:, :, width:]
    owners = lax.axis_size(("dp", "fsdp"))
    pairs = (
        (joined, grad_first),
        (normed_one, grad_triple),
        (mixed, grad_attn),
        (normed_two, grad_inner),
        (active, grad_mlp),
    )
    shard_sizes = [pair[0].shape[1] * pair[1].shape[1] // owners for pair in pairs]
    blocks = []
    for pair, owner_share in zip(pairs, shard_sizes):
        blocks.append(
            flat_piece(pair[0], pair[1]).reshape(1 * lax.axis_size(("dp", "fsdp")), owner_share)
        )
    owned = lax.psum_scatter(
        jnp.concatenate(blocks, 1), ("dp", "fsdp"), scatter_dimension=0, tiled=True
    ).reshape(-1)
    pieces = []
    offset = 0
    for share in shard_sizes:
        pieces.append(owned[offset : offset + share])
        offset = offset + share
    vec_grad = jnp.concatenate(
        [
            d_gain_one,
            d_shift_one,
            d_gain_two,
            d_shift_two,
            d_skip_bias,
            d_proj_bias,
            d_fc2_bias,
            d_fc1_bias,
        ]
    )
    vec_rows = lax.psum_scatter(vec_grad, "dp", scatter_dimension=0, tiled=True)
    vec_total = lax.psum(vec_rows, "fsdp")
    return (
        block_out.reshape(items, length, width),
        in_grad,
        skip_grad,
        pieces[0],
        pieces[1],
        pieces[2],
        pieces[3],
        pieces[4],
        vec_total,
    )


def solution(mesh):
    placed = (
        P(("dp", "fsdp"), None, None),
        P(("dp", "fsdp"), None, None),
        P(("dp", "fsdp"), None, None),
        P(("dp", "fsdp")),
        P(("dp", "fsdp")),
        P(("dp", "fsdp")),
        P(("dp", "fsdp")),
        P(("dp", "fsdp")),
        P(("dp", "fsdp")),
        P("dp"),
    )
    return jax.shard_map(
        body,
        mesh=mesh,
        in_specs=placed,
        out_specs=(
            P(("dp", "fsdp"), None, None),
            P(("dp", "fsdp"), None, None),
            P(("dp", "fsdp"), None, None),
            P(("dp", "fsdp")),
            P(("dp", "fsdp")),
            P(("dp", "fsdp")),
            P(("dp", "fsdp")),
            P(("dp", "fsdp")),
            P("dp"),
        ),
        check_vma=False,
    )
```

```python
import functools

import jax
import jax.numpy as jnp
from jax import lax
from jax.experimental import pallas as pl
from jax.experimental.pallas import tpu as pltpu
from jax.sharding import PartitionSpec as P

HEADS = 16
FF = 4608
CAPTION = 77


epsilon = 1e-05
masked_value = -1e30


def norm_rows(value, gain, shift):
    center = value - jnp.mean(value, -1, keepdims=True)
    spread = jnp.mean(center * center, -1, keepdims=True)
    return center * lax.rsqrt(spread + epsilon) * gain + shift


def gelu_exact(value):
    return jax.nn.gelu(value, approximate=False)


def key_valid(caption_len, length, caption):
    place = lax.broadcasted_iota(jnp.int32, (caption_len.shape[0], length), 1)
    return (place < 1 + caption_len[:, None]) | (place >= 1 + caption)


def product(left, right):
    return jnp.dot(left, right, preferred_element_type=jnp.float32)


def left_product(left, right):
    return lax.dot_general(
        left, right, (((0,), (0,)), ((), ())), preferred_element_type=jnp.float32
    )


def right_product(left, right):
    return lax.dot_general(
        left, right, (((1,), (1,)), ((), ())), preferred_element_type=jnp.float32
    )


def unpack(flat, width, hidden):
    return (
        flat[0].reshape(2 * width, width),
        flat[1].reshape(width, 3 * width),
        flat[2].reshape(width, width),
        flat[3].reshape(width, hidden),
        flat[4].reshape(hidden, width),
    )


def attention_scores(query, keys, valid, scale):
    raw = jnp.einsum("ishd,ithd->ihst", query, keys, preferred_element_type=jnp.float32) * scale
    return jnp.where(valid[:, None, None, :], raw, masked_value)


def column_sum(value):
    return jnp.sum(value.astype(jnp.float32), 0)


def flat_piece(left, right):
    grad_rows = left_product(left, right).reshape(-1)
    return grad_rows


MESH = pl.DeviceIdType.MESH
BF=jnp.bfloat16; F32=jnp.float32
SPLIT = 384


def unit_lanes(value, units, chips):
    seg = value.shape[1] // (units * chips)
    return [
        jnp.concatenate([value[:, (s * units + u) * seg : (s * units + u + 1) * seg] for s in range(chips)], 1)
        for u in range(units)
    ]


def row_loop(total, step, fn):
    def one(n, carry):
        fn(pl.ds(pl.multiple_of(n * step, step), step))
        return carry
    lax.fori_loop(0, total // step, one, 0)


def natural_lanes(units, chips):
    seg = units[0].shape[1] // chips
    return jnp.concatenate([u[:, s * seg : (s + 1) * seg] for s in range(chips) for u in units], 1)


def block_kernel(Z, wide, rows, lanes_a, length, padded,
                 cap_ref, skip_ref, qkv_ref, proj_ref, fc1_ref, fc2_ref, vec_ref, in_ref, sk_ref, og_ref,
                 out_o, in_o, sk_o, skip_g, qkv_g, proj_g, fc1_g, fc2_g, vec_o, skip_o, qp_o, fc1_o, fc2_o, j_o, h0_o,
                 skip_f, qkv_f, proj_f, fc1_f, fc2_f, own, keep, give, take, vbuf, vecs, b1s, vpart, vgot, vall, tok,
                 dtg, side, hid, am, t, m, zz, gu, gm, acc, tmp, sums, gacc, wbuf,
                 xl, xr, part, ra1, ra2, ra3, rc1, rc2, rc3,
                 send, recv, lsem, psend, precv, vsend, vrecv, isem, osem, wsem,
                 rsend, rrecv, xsend, xrecv, qsend, qrecv, ysend, yrecv, ssend, srecv, free):
    dp = lax.axis_index("dp"); f = lax.axis_index("fsdp")
    z = dp // 2; x = dp % 2; y = f // 2; c = f % 2
    o = 1 - c
    nt = wide // 128
    half = rows // 2
    chips = 4 * Z
    nz = Z - 1
    ndp = 2 * Z
    hd = wide // HEADS
    full = length // 16 * 16
    A = pl.ds(0, lanes_a); C = pl.ds(lanes_a, wide - lanes_a)
    zi = [lax.rem(z + k, Z) for k in range(1, Z)]
    zs = [(i * 2 + x, f) for i in zi]
    xp = (z * 2 + 1 - x, f)
    yp = (dp, (1 - y) * 2 + c)
    pp = (dp, y * 2 + o)
    dps = [(lax.rem(dp + k, ndp), f) for k in range(1, ndp)]
    fs = [(dp, lax.rem(f + k, 4)) for k in range(1, 4)]
    bar = pltpu.get_barrier_semaphore()
    for d in dps + fs:
        pl.semaphore_signal(bar, inc=1, device_id=d, device_id_type=MESH)
    flats = [(skip_ref, skip_f), (qkv_ref, qkv_f), (proj_ref, proj_f), (fc1_ref, fc1_f), (fc2_ref, fc2_f)]
    floads = [pltpu.make_async_copy(a, b, isem.at[n]) for n, (a, b) in enumerate(flats)]
    for cp in floads: cp.start()
    loads = [pltpu.make_async_copy(in_ref, tok.at[0], isem.at[5]), pltpu.make_async_copy(sk_ref, tok.at[1], isem.at[6])]
    for cp in loads: cp.start()
    def remote(src, dst, ssem, rsem, dev):
        return pltpu.make_async_remote_copy(src, dst, ssem, rsem, device_id=dev, device_id_type=MESH)
    floads[0].wait()
    for j in range(nt):
        own[0, :, 128 * j:128 * j + 128] = skip_f[pl.ds(j, rows, stride=nt), :].astype(BF)
    pl.semaphore_wait(bar, len(dps) + len(fs))

    waits = []
    def rc(i, slot, src, dst, dev):
        cp = remote(src, dst, send.at[i, slot], recv.at[i, slot], dev)
        cp.start(); waits.append(cp)
    def got(i, slot, dst):
        remote(dst, dst, send.at[i, slot], recv.at[i, slot], pp).wait_recv()
    def unit(i, cc):
        if i == 0: return skip_o.at[:, :, :, cc]
        if i in (1, 2): return qp_o.at[2 * (i - 1) + cc]
        if i in (3, 4): return fc1_o.at[2 * cc + (i - 3)]
        return fc2_o.at[2 * cc + (i - 5)]
    pc = {}
    lc = {}
    def exchange(i, first, second):
        keep[i - 1, 0:half, :] = jnp.where(c == 0, first, second)
        give[i - 1, 0:half, :] = jnp.where(c == 0, second, first)
        pc[i] = remote(give.at[i - 1], take.at[i - 1], psend.at[i - 1], precv.at[i - 1], pp)
        pc[i].start()
    def stage1(i):
        U = unit(i, c)
        if i in (1, 2, 3, 4):
            pc[i].wait_recv()
            p = keep[i - 1, 0:half, :]
            q = take[i - 1, 0:half, :]
            lo = jnp.where(c == 0, p, q); hi = jnp.where(c == 0, q, p)
            own[i, :, :] = jnp.concatenate([lo, hi], 0).astype(BF)
        lc[i] = pltpu.make_async_copy(own.at[i], U.at[z, x, y], lsem.at[i]); lc[i].start()
        rc(i, 2 * nz, own.at[i, :, C], U.at[z, x, y, :, C], yp)
        for k in range(1, Z):
            rc(i, k - 1, own.at[i, :, A], U.at[z, x, y, :, A], zs[k - 1])
    def stage2(i):
        U = unit(i, c)
        lc[i].wait()
        got(i, 2 * nz, U.at[z, x, 1 - y, :, C])
        for k in range(1, Z):
            rc(i, nz + k - 1, U.at[z, x, :, :, C], U.at[z, x, :, :, C], zs[k - 1])
        for k in range(1, Z):
            got(i, k - 1, U.at[lax.rem(z - k + Z, Z), x, y, :, A])
        L = U.at[:, x, y, :, A]
        rc(i, 2 * nz + 1, L, L, xp)
        rc(i, 2 * nz + 2, L, L, yp)
        rc(i, 2 * nz + 5, L, L, pp)
    def stage3(i):
        U = unit(i, c)
        for k in range(1, Z):
            got(i, nz + k - 1, U.at[lax.rem(z - k + Z, Z), x, :, :, C])
        L = U.at[:, x, :, :, C]
        rc(i, 2 * nz + 4, L, L, xp)
        rc(i, 2 * nz + 6, L, L, pp)
        L = U.at[:, 1 - x, y, :, A]
        got(i, 2 * nz + 1, L)
        rc(i, 2 * nz + 3, L, L, yp)
        rc(i, 2 * nz + 7, L, L, pp)
    def stage4(i):
        U = unit(i, c)
        L = U.at[:, x, 1 - y, :, A]
        got(i, 2 * nz + 2, L); rc(i, 2 * nz + 8, L, L, pp)
        L = U.at[:, 1 - x, 1 - y, :, A]
        got(i, 2 * nz + 3, L); rc(i, 2 * nz + 9, L, L, pp)
        L = U.at[:, 1 - x, :, :, C]
        got(i, 2 * nz + 4, L); rc(i, 2 * nz + 10, L, L, pp)
    def arrived(i):
        U = unit(i, 1 - c)
        got(i, 2 * nz + 5, U.at[:, x, y, :, A])
        got(i, 2 * nz + 7, U.at[:, 1 - x, y, :, A])
        got(i, 2 * nz + 8, U.at[:, x, 1 - y, :, A])
        got(i, 2 * nz + 9, U.at[:, 1 - x, 1 - y, :, A])
        got(i, 2 * nz + 6, U.at[:, x, :, :, C])
        got(i, 2 * nz + 10, U.at[:, 1 - x, :, :, C])
    def read(ref, first, stride):
        return jnp.concatenate([ref[pl.ds(first + j, half, stride=stride), :] for j in range(nt)], 1)

    stage1(0)
    vcopies = []
    vbuf[dp] = vec_ref[...]
    for k, d in enumerate(dps):
        cp = remote(vec_ref, vbuf.at[dp], vsend.at[k], vrecv.at[k], d)
        cp.start(); vcopies.append(cp)
    floads[1].wait(); floads[2].wait()
    exchange(1, read(qkv_f, 0, 3 * nt), read(qkv_f, nt, 3 * nt))
    exchange(2, read(qkv_f, 2 * nt, 3 * nt), read(proj_f, 0, nt))
    def prepare_late():
        floads[3].wait(); floads[4].wait()
        for j in range(nt):
            own[5, :, 128 * j:128 * j + 128] = fc2_f[pl.ds(j, rows, stride=nt), :].astype(BF)
            own[6, :, 128 * j:128 * j + 128] = fc2_f[pl.ds(j + nt * rows, rows, stride=nt), :].astype(BF)
        nat = jnp.concatenate([read(fc1_f, nt * v, 4 * nt) for v in range(4)], 1)
        u = unit_lanes(nat, 4, chips)
        exchange(3, u[0], u[2])
        exchange(4, u[1], u[3])

    def keep_out(n, src, dst):
        cp = pltpu.make_async_copy(src, dst, osem.at[n]); cp.start()
        return cp
    def weight(n, ref):
        pltpu.make_async_copy(ref, wbuf.at[n], wsem.at[n]).start()
    def weight_wait(k):
        pltpu.make_async_copy(wbuf.at[k], wbuf.at[k], wsem.at[k]).wait()
    def both_skip():
        for k in range(2):
            for i in range(Z // 2):
                pltpu.make_async_copy(skip_o.at[k * (Z // 2) + i], wbuf.at[k, pl.ds(2 * i, 2)], wsem.at[k]).start()
    def cols(k, l):
        return wbuf[k, :, :, :, :, l].reshape(wide, SPLIT)
    def lanes_loop(fn):
        def one(n, carry):
            fn(pl.ds(pl.multiple_of(n * SPLIT, 128), SPLIT))
            return carry
        lax.fori_loop(0, wide // SPLIT, one, 0)
    def vector(n):
        return vecs[0:1, n * wide:(n + 1) * wide]
    def rows_of(k, first, n):
        return jnp.concatenate([tok[k, pl.ds(first * nt + j, n, stride=nt), :] for j in range(nt)], 1)
    def put_rows(k, src):
        def part_of(first, n, v):
            for j in range(nt):
                tok[k, pl.ds(first * nt + j, n, stride=nt), :] = v[:, 128 * j:128 * j + 128]
        def one(r): part_of(r.start, 16, src[r, :])
        row_loop(full, 16, one)
        if length > full: part_of(full, length - full, src[full:length, :])
    def norm(src, gain, shift, dst):
        def one(r):
            v = src[r, :]
            cen = v - jnp.mean(v, -1, keepdims=True)
            s = jnp.mean(cen * cen, -1, keepdims=True)
            dst[r, :] = (cen * lax.rsqrt(s + epsilon) * gain + shift).astype(BF)
        row_loop(padded, 16, one)
    def take_rows(k, dst, at):
        if padded > full: dst[at + (slice(padded - 16, padded), slice(None))] = jnp.zeros((16, wide), dst.dtype)
        def one(r): dst[at + (r, slice(None))] = rows_of(k, r.start, 16).astype(dst.dtype)
        row_loop(full, 16, one)
        if length > full: dst[at + (slice(full, length), slice(None))] = rows_of(k, full, length - full).astype(dst.dtype)
    def inputs():
        for cp in loads: cp.wait()
        take_rows(0, dtg, (0,))
        take_rows(1, dtg, (1,))
        pltpu.make_async_copy(og_ref, tok.at[0], isem.at[5]).start()
        def two(r):
            u = unit_lanes(jnp.concatenate([dtg[0, r, :], dtg[1, r, :]], 1), 2, chips)
            side[0, r, :] = u[0]
            side[1, r, :] = u[1]
        row_loop(padded, 16, two)
        keep_out(0, side, j_o)
    def vectors():
        for k in range(len(dps)):
            remote(vec_ref, vbuf.at[lax.rem(dp - (k + 1) + ndp, ndp)], vsend.at[k], vrecv.at[k], pp).wait_recv()
        vecs[...] = jnp.concatenate([vbuf[k] for k in range(ndp)], 1)
        b = unit_lanes(vecs[0:1, 7 * wide:11 * wide], 4, chips)
        for u in range(4): b1s[u] = b[u]
        pltpu.make_async_copy(og_ref, tok.at[0], isem.at[5]).wait()
        take_rows(0, gm, ())
        pltpu.make_async_copy(og_ref, tok.at[1], isem.at[6]).start()
    def first_part():
        arrived(0)
        both_skip()
        weight_wait(0); weight_wait(1)
        def one(l):
            v = jnp.dot(dtg[0], cols(0, l), preferred_element_type=F32)
            v = v + jnp.dot(dtg[1], cols(1, l), preferred_element_type=F32)
            hid[:, l] = v + vecs[0:1, pl.ds(4 * wide + l.start, SPLIT)]
        lanes_loop(one)
        norm(hid, vector(0), vector(1), am.at[0])
        keep_out(1, hid, h0_o)
    def project(n, u):
        def one(l):
            t[u, :, l] = jnp.dot(am[0], cols(n, l), preferred_element_type=F32).astype(BF)
        lanes_loop(one)
    def query_keys():
        arrived(1)
        for u in range(2): weight(u, qp_o.at[u])
        for u in range(2):
            weight_wait(u)
            project(u, u)
    def values():
        arrived(2)
        weight(0, qp_o.at[2]); weight(1, qp_o.at[3])
        weight_wait(0)
        project(0, 2)
    def window(h):
        base = pl.multiple_of(jnp.minimum((h * hd) // 128, nt - 2) * 128, 128)
        lane = lax.broadcasted_iota(jnp.int32, (1, 256), 1) + (base - h * hd)
        return pl.ds(base, 256), (lane >= 0) & (lane < hd)
    def attend(first, last):
        cap = cap_ref[0]
        key = lax.broadcasted_iota(jnp.int32, (1, padded), 1)
        live = ((key < 1 + cap) | (key >= 1 + CAPTION)) & (key < length)
        def head(h, carry):
            win, inside = window(h)
            q = jnp.where(inside, t[0, :, win].astype(F32), 0.0).astype(BF)
            s = lax.dot_general(q, t[1, :, win], (((1,), (1,)), ((), ())), preferred_element_type=F32) * hd ** (-0.5)
            s = jnp.where(live, s, masked_value)
            e = jnp.exp(s - jnp.max(s, -1, keepdims=True))
            p = (e / jnp.sum(e, -1, keepdims=True)).astype(BF)
            v = jnp.dot(p, t[2, :, win], preferred_element_type=F32)
            am[1, :, win] = jnp.where(inside, v, am[1, :, win].astype(F32)).astype(BF)
            return carry
        lax.fori_loop(first, last, head, 0)
    def second_part():
        weight_wait(1)
        pltpu.make_async_copy(hid, h0_o, osem.at[1]).wait()
        def one(l):
            v = jnp.dot(am[1], cols(1, l), preferred_element_type=F32)
            h = hid[:, l] + (v + vecs[0:1, pl.ds(5 * wide + l.start, SPLIT)])
            hid[:, l] = h
            acc[:, l] = h + vecs[0:1, pl.ds(6 * wide + l.start, SPLIT)]
        lanes_loop(one)
        norm(hid, vector(2), vector(3), m)
    def widen_load(i):
        arrived(i)
        for k in range(2): weight(k, fc1_o.at[2 * k + i - 3])
    def widen(k, u):
        weight_wait(k)
        def one(l):
            tmp[:, l] = jnp.dot(m[...], cols(k, l), preferred_element_type=F32)
        lanes_loop(one)
        def two(r):
            v = tmp[r, :] + b1s[u]
            cdf = 0.5 * (1.0 + lax.erf(v * 0.7071067811865476))
            pdf = jnp.exp(-0.5 * v * v) * 0.3989422804014327
            zz[u, r, :] = (v * cdf).astype(BF)
            gu[u, r, :] = (cdf + v * pdf).astype(BF)
        row_loop(padded, 16, two)
    def narrow_load(i):
        arrived(i)
        for k in range(2): weight(k, fc2_o.at[2 * k + i - 5])
    def narrow(k, u):
        weight_wait(k)
        tmp[...] = jnp.zeros_like(tmp)
        def one(l):
            w = cols(k, l)
            acc[:, l] += jnp.dot(zz[u], w, preferred_element_type=F32)
            tmp[...] += lax.dot_general(gm[:, l], w, (((1,), (1,)), ((), ())), preferred_element_type=F32)
        lanes_loop(one)
        def two(r):
            gu[u, r, :] = (tmp[r, :] * gu[u, r, :].astype(F32)).astype(BF)
        row_loop(padded, 16, two)

    xcopies = {}
    def swap(n, src, dst):
        xcopies[n] = remote(src, dst, xsend.at[n], xrecv.at[n], pp)
        xcopies[n].start()
    nb = 4
    started = {j: [] for j in range(7)}
    def sc(j, slot, src, dst, dev):
        cp = remote(src, dst, rsend.at[j, slot], rrecv.at[j, slot], dev)
        cp.start(); started[j].append(cp)
    def came(j, slot, dst):
        remote(dst, dst, rsend.at[j, slot], rrecv.at[j, slot], pp).wait_recv()
    need = [(0, 1), (2,), (3, 4), (5,), (6, 7), (8, 9), (10, 11)]
    def operands(j):
        if j < 2: return zz.at[2 * c + j], gm, xl.at[j], xr.at[0]
        if j < 4: return m, gu.at[2 * c + j - 2], xl.at[2], xr.at[j - 1]
        if j == 4: return am.at[c], dtg.at[2 + c], xl.at[0], xr.at[0]
        if j == 5: return am.at[0], dtg.at[c], xl.at[1], xr.at[1]
        return side.at[0], side.at[1], xl.at[2], xr.at[2]
    def reduce1(j):
        for n in need[j]: xcopies[n].wait_recv()
        if j >= nb:
            for cp in started[j - nb]: cp.wait_send()
        b = j % nb
        D = part.at[b]
        l1, r1, l2, r2 = operands(j)
        step = wide - lanes_a
        dims = (((0,), (0,)), ((), ()))
        def chunk(n, carry):
            lanes = pl.ds(pl.multiple_of(n * step, 128), step)
            r = lax.dot_general(l1[...], r1[:, lanes], dims, preferred_element_type=F32)
            r = r + lax.dot_general(l2[...], r2[:, lanes], dims, preferred_element_type=F32)
            D[:, :, :, :, lanes] = r.reshape(Z, 2, 2, rows, step).astype(BF)
            return carry
        lax.fori_loop(0, wide // step, chunk, 0)
        sc(j, 0, D.at[:, 1 - x, 1 - y, :, A], ra1.at[b, 0], yp)
        sc(j, 2, D.at[:, 1 - x, :, :, C], rc1.at[b], xp)
        sc(j, 1, D.at[:, x, 1 - y, :, A], ra1.at[b, 1], yp)
    def reduce2(j):
        b = j % nb
        D = part.at[b]
        came(j, 0, ra1.at[b, 0])
        for zz in range(Z):
            va = D.at[zz, 1 - x, y, :, A]
            va[...] = (va[...].astype(F32) + ra1[b, 0, zz].astype(F32)).astype(BF)
        sc(j, 3, D.at[:, 1 - x, y, :, A], ra2.at[b], xp)
        came(j, 2, rc1.at[b])
        for zz in range(Z):
            for yy in range(2):
                va = D.at[zz, x, yy, :, C]
                va[...] = (va[...].astype(F32) + rc1[b, zz, yy].astype(F32)).astype(BF)
        for k in range(nz):
            sc(j, 4 + k, D.at[zi[k], x, :, :, C], rc2.at[b, k], zs[k])
    def reduce3(j):
        b = j % nb
        D = part.at[b]
        came(j, 1, ra1.at[b, 1])
        came(j, 3, ra2.at[b])
        for zz in range(Z):
            va = D.at[zz, x, y, :, A]
            va[...] = (va[...].astype(F32) + ra1[b, 1, zz].astype(F32) + ra2[b, zz].astype(F32)).astype(BF)
        for k in range(nz):
            sc(j, 4 + nz + k, D.at[zi[k], x, y, :, A], ra3.at[b, k], zs[k])
        for k in range(nz):
            came(j, 4 + k, rc2.at[b, k])
        for yy in range(2):
            va = D.at[z, x, yy, :, C]
            s = va[...].astype(F32)
            for k in range(nz):
                s = s + rc2[b, k, yy].astype(F32)
            va[...] = s.astype(BF)
        sc(j, 4 + 2 * nz, D.at[z, x, 1 - y, :, C], rc3.at[b], yp)
    pcopies = {}
    def lay(ref, val, first, stride, n):
        for i in range(val.shape[1] // 128):
            ref[pl.ds(first + i, n, stride=stride), :] = val[:, 128 * i:128 * i + 128]
    def reduce4(j):
        b = j % nb
        D = part.at[b]
        for k in range(nz):
            came(j, 4 + nz + k, ra3.at[b, k])
        came(j, 4 + 2 * nz, rc3.at[b])
        p = D[z, x, y, :, 0:lanes_a].astype(F32)
        for k in range(nz):
            p = p + ra3[b, k].astype(F32)
        q = D[z, x, y, :, lanes_a:wide].astype(F32) + rc3[b].astype(F32)
        v = jnp.concatenate([p, q], 1)
        if j in (0, 1):
            lay(fc2_f, v, j * rows * nt, nt, rows)
            if j == 1: keep_out(9, fc2_f, fc2_g)
        elif j == 6:
            lay(skip_f, v, 0, nt, rows)
            keep_out(5, skip_f, skip_g)
        else:
            lo = v[0:half]; hi = v[half:rows]
            keep[j - 2, 0:half, :] = jnp.where(c == 0, lo, hi)
            give[j - 2, 0:half, :] = jnp.where(c == 0, hi, lo)
            cp = remote(give.at[j - 2], take.at[j - 2], qsend.at[j - 2], qrecv.at[j - 2], pp)
            cp.start(); pcopies[j] = cp
    def both(j):
        pcopies[j].wait_recv()
        p = keep[j - 2, 0:half, :]; q = take[j - 2, 0:half, :]
        return jnp.where(c == 0, p, q), jnp.where(c == 0, q, p)
    def reduce5(j):
        if j == 3:
            p, q = both(2), both(3)
            lay(fc1_f, natural_lanes([p[0], q[0], p[1], q[1]], chips), 0, 4 * nt, half)
            keep_out(8, fc1_f, fc1_g)
        elif j == 5:
            first, second = both(5)
            lay(qkv_f, first, 0, 3 * nt, half)
            lay(qkv_f, second, nt, 3 * nt, half)
            keep_out(6, qkv_f, qkv_g)
        elif j == 4:
            first, second = both(4)
            lay(qkv_f, first, 2 * nt, 3 * nt, half)
            lay(proj_f, second, 0, nt, half)
            keep_out(7, proj_f, proj_g)


    def zero(n): gacc[n] = jnp.zeros((8, wide), F32)
    def add_rows(n, v):
        gacc[n] += v[0:8] + v[8:16]
    def close(n):
        return jnp.sum(gacc[n], 0, keepdims=True)
    def column_sums(src):
        zero(0)
        def one(r): add_rows(0, src[r, :].astype(F32))
        row_loop(padded, 16, one)
        return close(0)
    def norm_back(dy, src, gain, fn):
        zero(0); zero(1); zero(2)
        def one(r):
            d = dy[r, :]
            v = src[r, :]
            cen = v - jnp.mean(v, -1, keepdims=True)
            rs = lax.rsqrt(jnp.mean(cen * cen, -1, keepdims=True) + epsilon)
            xh = cen * rs
            dx = d * gain
            g = rs * (dx - jnp.mean(dx, -1, keepdims=True) - xh * jnp.mean(dx * xh, -1, keepdims=True))
            add_rows(0, d * xh)
            add_rows(1, d)
            fn(r, g)
        row_loop(padded, 16, one)
    def turned(lhs, n, fresh):
        if fresh: tmp[...] = jnp.zeros_like(tmp)
        def one(l):
            tmp[...] += lax.dot_general(lhs[:, l], cols(n, l), (((1,), (1,)), ((), ())), preferred_element_type=F32)
        lanes_loop(one)
    def widen_back(us):
        for i, u in enumerate(us):
            weight_wait(i)
            turned(gu.at[u], i, u == 0)
            sums[7 + u] = column_sums(gu.at[u])
    def widen_back_load(us):
        for i, u in enumerate(us): weight(i, fc1_o.at[u])
    def norm_two():
        weight(0, qp_o.at[3])
        pltpu.make_async_copy(og_ref, tok.at[1], isem.at[6]).wait()
        take_rows(1, acc, ())
        def fn(r, g):
            s = acc[r, :] + g
            acc[r, :] = s
            b = s.astype(BF)
            dtg[3, r, :] = b
            add_rows(2, b.astype(F32))
        norm_back(tmp, hid, vector(2), fn)
        sums[2] = close(0); sums[3] = close(1); sums[5] = close(2)
        pltpu.make_async_copy(h0_o, hid, isem.at[5]).start()
        sums[6] = column_sums(gm)
        weight_wait(0)
        turned(dtg.at[3], 0, True)
        def two(r): side[0, r, :] = tmp[r, :].astype(BF)
        row_loop(padded, 16, two)
    def attend_back(first, last):
        cap = cap_ref[0]
        key = lax.broadcasted_iota(jnp.int32, (padded, 1), 0)
        live = ((key < 1 + cap) | (key >= 1 + CAPTION)) & (key < length)
        def head(h, carry):
            win, inside = window(h)
            q = jnp.where(inside, t[0, :, win].astype(F32), 0.0).astype(BF)
            k = t[1, :, win]
            g = jnp.where(inside, side[0, :, win].astype(F32), 0.0).astype(BF)
            s = lax.dot_general(k, q, (((1,), (1,)), ((), ())), preferred_element_type=F32) * hd ** (-0.5)
            s = jnp.where(live, s, masked_value)
            e = jnp.exp(s - jnp.max(s, 0, keepdims=True))
            p = e * (1.0 / jnp.sum(e, 0, keepdims=True))
            d = lax.dot_general(t[2, :, win], g, (((1,), (1,)), ((), ())), preferred_element_type=F32)
            ds = (p * (d - jnp.sum(p * d, 0, keepdims=True))).astype(BF)
            dq = lax.dot_general(ds, k, (((0,), (0,)), ((), ())), preferred_element_type=F32) * hd ** (-0.5)
            dk = jnp.dot(ds, q, preferred_element_type=F32) * hd ** (-0.5)
            dv = jnp.dot(p.astype(BF), g, preferred_element_type=F32)
            for i, v in enumerate((dq, dk, dv)):
                dtg[i, :, win] = jnp.where(inside, v, dtg[i, :, win].astype(F32)).astype(BF)
            return carry
        lax.fori_loop(first, last, head, 0)
    def late_left():
        pl.semaphore_signal(free, inc=1, device_id=pp, device_id_type=MESH)
        pl.semaphore_wait(free, 1)
        pltpu.make_async_copy(side, j_o, osem.at[0]).wait()
        swap(6, am.at[o], xl.at[0])
        swap(8, am.at[0], xl.at[1])
        swap(10, j_o.at[o], xl.at[2])
    def late_right():
        swap(7, dtg.at[2 + o], xr.at[0])
        swap(9, dtg.at[o], xr.at[1])
        pltpu.make_async_copy(j_o.at[c], side.at[0], isem.at[7]).start()
        weight(0, qp_o.at[0]); weight(1, qp_o.at[1])
    def project_back():
        for i in range(3):
            weight_wait(i % 2)
            turned(dtg.at[i], i % 2, i == 0)
            if i == 0: weight(0, qp_o.at[2])
    def norm_one():
        pltpu.make_async_copy(h0_o, hid, isem.at[5]).wait()
        both_skip()
        def fn(r, g):
            b = (acc[r, :] + g).astype(BF)
            side[1, r, :] = b
            add_rows(2, b.astype(F32))
        norm_back(tmp, hid, vector(0), fn)
        sums[0] = close(0); sums[1] = close(1); sums[4] = close(2)
        swap(11, side.at[1], xr.at[2])
    def join_back(i, dst):
        weight_wait(i)
        turned(side.at[1], i, True)
        put_rows(i, tmp)
        keep_out(3 + i, tok.at[i], dst)
    nv = vpart.shape[2]
    def vec_send():
        total = jnp.concatenate([sums[i] for i in range(7)] + [natural_lanes([sums[7 + u] for u in range(4)], chips)], 1)
        for k in range(ndp): vpart[k] = total[:, k * nv:(k + 1) * nv]
        for k, d in enumerate(dps):
            cp = remote(vpart.at[d[0]], vgot.at[k], ysend.at[k], yrecv.at[k], d)
            cp.start(); vcopies.append(cp)
    def vec_first():
        s = vpart[dp]
        for k in range(len(dps)):
            remote(vgot.at[k], vgot.at[k], ysend.at[k], yrecv.at[k], pp).wait_recv()
            s = s + vgot[k]
        vall[f] = s
        for k, d in enumerate(fs):
            cp = remote(vall.at[f], vall.at[f], ssend.at[k], srecv.at[k], d)
            cp.start(); vcopies.append(cp)
    def vec_last():
        for k in range(3):
            src = lax.rem(f - (k + 1) + 4, 4)
            remote(vall.at[src], vall.at[src], ssend.at[k], srecv.at[k], pp).wait_recv()
        vec_o[...] = vall[0] + vall[1] + vall[2] + vall[3]

    stage2(0)
    prepare_late()
    stage1(1)
    stage3(0)
    inputs()
    vectors()
    stage2(1); stage1(2)
    stage3(1); stage4(0)
    first_part()
    stage2(2); stage1(3)
    stage3(2); stage4(1)
    query_keys()
    stage2(3); stage1(4)
    stage3(3); stage4(2)
    values()
    attend(0, 4)
    stage2(4); stage1(5)
    attend(4, 11)
    stage3(4); stage4(3)
    attend(11, 16)
    second_part()
    stage2(5); stage1(6)
    widen_load(3)
    widen(0, 0)
    stage3(5); stage4(4)
    widen(1, 2)
    stage2(6)
    widen_load(4)
    widen(0, 1)
    stage3(6); stage4(5)
    widen(1, 3)
    for cp in pc.values(): cp.wait_send()
    swap(0, zz.at[2 * o], xl.at[0])
    swap(1, gm, xr.at[0])
    swap(2, zz.at[2 * o + 1], xl.at[1])
    swap(3, m, xl.at[2])
    narrow_load(5)
    reduce1(0)
    narrow(0, 0)
    stage4(6)
    narrow(1, 2)
    swap(4, gu.at[2 * o], xr.at[1])
    reduce1(1); reduce2(0)
    narrow_load(6)
    narrow(0, 1)
    narrow(1, 3)
    swap(5, gu.at[2 * o + 1], xr.at[2])
    widen_back_load((0, 1))
    reduce1(2); reduce2(1); reduce3(0)
    put_rows(0, acc)
    keep_out(2, tok.at[0], out_o)
    widen_back((0, 1))
    widen_back_load((2, 3))
    reduce1(3)
    widen_back((2, 3))
    reduce2(2); reduce3(1); reduce4(0)
    late_left()
    norm_two()
    attend_back(0, 4)
    reduce2(3); reduce3(2); reduce4(1)
    attend_back(4, 10)
    reduce3(3); reduce4(2)
    attend_back(10, 16)
    late_right()
    reduce1(4); reduce4(3)
    reduce1(5); reduce2(4)
    project_back()
    norm_one()
    vec_send()
    reduce2(5); reduce3(4)
    pltpu.make_async_copy(j_o.at[c], side.at[0], isem.at[7]).wait()
    reduce1(6)
    vec_first()
    pltpu.make_async_copy(tok.at[0], out_o, osem.at[2]).wait()
    join_back(0, in_o)
    reduce3(5); reduce4(4)
    join_back(1, sk_o)
    reduce5(3)
    reduce2(6)
    vec_last()
    reduce4(5); reduce5(4)
    reduce3(6)
    reduce5(5)
    reduce4(6)
    for k in (0, 1): pltpu.make_async_copy(tok.at[k], (in_o, sk_o)[k], osem.at[3 + k]).wait()
    for n, (a, b) in zip((5, 6, 7, 8, 9), ((skip_f, skip_g), (qkv_f, qkv_g), (proj_f, proj_g), (fc1_f, fc1_g), (fc2_f, fc2_g))):
        pltpu.make_async_copy(a, b, osem.at[n]).wait()
    for j in range(3, 7):
        for cp in started[j]: cp.wait_send()
    for cp in waits: cp.wait_send()
    for cp in pcopies.values(): cp.wait_send()
    for cp in vcopies: cp.wait_send()
    for cp in xcopies.values(): cp.wait_send()


def block(cap, skip, qkv, proj, fc1, fc2, vectors, block_in, skip_in, out_grad, dpn):
    _, length, wide = block_in.shape
    Z = dpn // 2; rows = skip.shape[0] // wide
    padded = -(-length // 16) * 16
    lanes_a = (wide // 128 * 2 + 1) // 3 * 128
    lc = wide - lanes_a
    U = (Z, 2, 2, rows, wide)
    hbm = pl.BlockSpec(memory_space=pl.ANY); vm = pl.BlockSpec(memory_space=pltpu.VMEM)
    ns = 2 * (Z - 1) + 11
    nr = 2 * (Z - 1) + 5
    nv = vectors.shape[0]
    D = pltpu.SemaphoreType.DMA
    V = pltpu.VMEM
    hp = -(-rows // 2 // 8) * 8
    S = jax.ShapeDtypeStruct
    act = (padded, wide)
    flat = [(w.shape[0] // 128, 128) for w in (skip, qkv, proj, fc1, fc2)]
    tokens = (length * wide // 128, 128)
    nb = 4
    nz = Z - 1
    res = pl.pallas_call(
        functools.partial(block_kernel, Z, wide, rows, lanes_a, length, padded),
        out_shape=(S(tokens, F32),) * 3 + tuple(S(s, F32) for s in flat) + (S((1, nv), F32),
                   S((Z, 2, 2, 2, rows, wide), BF), S((4,) + U, BF), S((4,) + U, BF), S((4,) + U, BF), S((2,) + act, BF), S(act, F32)),
        in_specs=[pl.BlockSpec(memory_space=pltpu.SMEM)] + [hbm] * 5 + [vm] + [hbm] * 3,
        out_specs=(hbm,) * 8 + (vm,) + (hbm,) * 6,
        scratch_shapes=[V(s, F32) for s in flat] + [
                        V((7, rows, wide), BF), V((4, hp, wide), F32), V((4, hp, wide), F32), V((4, hp, wide), F32),
                        V((dpn, 1, nv), F32), V((1, nv * dpn), F32), V((4, 1, wide), F32), V((dpn, 1, nv), F32), V((dpn - 1, 1, nv), F32), V((4, 1, nv), F32),
                        V((2,) + tokens, F32),
                        V((4,) + act, BF), V((2,) + act, BF), V(act, F32), V((2,) + act, BF), V((3,) + act, BF), V(act, BF), V((4,) + act, BF), V((4,) + act, BF), V(act, BF),
                        V(act, F32), V(act, F32), V((11, 1, wide), F32), V((3, 8, wide), F32), V((2,) + U, BF),
                        V((3,) + act, BF), V((3,) + act, BF), V((nb,) + U, BF),
                        V((nb, 2, Z, rows, lanes_a), BF), V((nb, Z, rows, lanes_a), BF), V((nb, nz, rows, lanes_a), BF),
                        V((nb, Z, 2, rows, lc), BF), V((nb, nz, 2, rows, lc), BF), V((nb, rows, lc), BF),
                        D((7, ns)), D((7, ns)), D((7,)), D((4,)), D((4,)), D((dpn - 1,)), D((dpn - 1,)), D((8,)), D((10,)), D((2,)),
                        D((7, nr)), D((7, nr)), D((12,)), D((12,)), D((4,)), D((4,)), D((dpn - 1,)), D((dpn - 1,)), D((3,)), D((3,)), pltpu.SemaphoreType.REGULAR],
        compiler_params=pltpu.CompilerParams(collective_id=0, has_side_effects=True, vmem_limit_bytes=67043328),
        name="block",
    )(cap, *(w.reshape(-1, 128) for w in (skip, qkv, proj, fc1, fc2)), vectors.reshape(1, nv),
      *(v.reshape(tokens) for v in (block_in, skip_in, out_grad)))
    shape = block_in.shape
    return tuple(r.reshape(shape) for r in res[:3]) + tuple(r.reshape(-1) for r in res[3:9])


def whole_rows(width, dp, fsdp, items, heads, hidden):
    return (
        fsdp == 4 and dp % 2 == 0 and width % (dp * 16) == 0 and items == 1 and hidden == 4 * width
        and width % SPLIT == 0 and width // heads <= 128
    )


def body(block_in, skip_in, out_grad, caption_len, skip_w, qkv_w, proj_w, fc1_w, fc2_w, vectors):
    items, length, width = block_in.shape
    if whole_rows(width, lax.axis_size("dp"), lax.axis_size("fsdp"), items, HEADS, FF):
        return block(
            caption_len, skip_w, qkv_w, proj_w, fc1_w, fc2_w, vectors, block_in, skip_in, out_grad,
            lax.axis_size("dp"),
        )
    heads = HEADS
    head_dim = width // heads
    hidden = FF
    rows = items * length
    scale = head_dim ** (-0.5)
    gathered = (
        lax.all_gather(skip_w.astype(jnp.bfloat16), ("dp", "fsdp"), axis=0, tiled=True),
        lax.all_gather(qkv_w.astype(jnp.bfloat16), ("dp", "fsdp"), axis=0, tiled=True),
        lax.all_gather(proj_w.astype(jnp.bfloat16), ("dp", "fsdp"), axis=0, tiled=True),
        lax.all_gather(fc1_w.astype(jnp.bfloat16), ("dp", "fsdp"), axis=0, tiled=True),
        lax.all_gather(fc2_w.astype(jnp.bfloat16), ("dp", "fsdp"), axis=0, tiled=True),
    )
    skip_m, qkv_m, proj_m, fc1_m, fc2_m = unpack(gathered, width, hidden)
    vec = lax.all_gather(vectors, "dp", axis=0, tiled=True)
    gain_one = vec[0:width]
    shift_one = vec[width : 2 * width]
    gain_two = vec[2 * width : 3 * width]
    shift_two = vec[3 * width : 4 * width]
    skip_bias = vec[4 * width : 5 * width]
    proj_bias = vec[5 * width : 6 * width]
    fc2_bias = vec[6 * width : 7 * width]
    fc1_bias = vec[7 * width :]
    valid = key_valid(caption_len, length, CAPTION)
    joined = jnp.concatenate([block_in, skip_in], -1).reshape(rows, 2 * width).astype(jnp.bfloat16)
    first = product(joined, skip_m) + skip_bias
    normed_one = norm_rows(first, gain_one, shift_one).astype(jnp.bfloat16)
    triple = (
        product(normed_one, qkv_m).astype(jnp.bfloat16).reshape(items, length, 3, heads, head_dim)
    )
    query = triple[:, :, 0]
    keys = triple[:, :, 1]
    values = triple[:, :, 2]
    scores = attention_scores(query, keys, valid, scale)
    top = jnp.max(scores, -1, keepdims=True)
    expd = jnp.exp(scores - top)
    total = jnp.sum(expd, -1, keepdims=True)
    probs = expd / total
    log_total = top + jnp.log(total)
    mixed = (
        jnp.einsum(
            "ihst,ithd->ishd",
            probs.astype(jnp.bfloat16),
            values,
            preferred_element_type=jnp.float32,
        )
        .astype(jnp.bfloat16)
        .reshape(rows, width)
    )
    second = first + (product(mixed, proj_m) + proj_bias)
    normed_two = norm_rows(second, gain_two, shift_two).astype(jnp.bfloat16)
    inner = product(normed_two, fc1_m) + fc1_bias
    active = gelu_exact(inner).astype(jnp.bfloat16)
    block_out = second + (product(active, fc2_m) + fc2_bias)
    again = (
        lax.all_gather(skip_w.astype(jnp.bfloat16), ("dp", "fsdp"), axis=0, tiled=True),
        lax.all_gather(qkv_w.astype(jnp.bfloat16), ("dp", "fsdp"), axis=0, tiled=True),
        lax.all_gather(proj_w.astype(jnp.bfloat16), ("dp", "fsdp"), axis=0, tiled=True),
        lax.all_gather(fc1_w.astype(jnp.bfloat16), ("dp", "fsdp"), axis=0, tiled=True),
        lax.all_gather(fc2_w.astype(jnp.bfloat16), ("dp", "fsdp"), axis=0, tiled=True),
    )
    skip_m, qkv_m, proj_m, fc1_m, fc2_m = unpack(again, width, hidden)
    grad_out = out_grad.reshape(rows, width)
    grad_mlp = grad_out.astype(jnp.bfloat16)
    d_fc2_bias = column_sum(grad_mlp)
    d_active = right_product(grad_mlp, fc2_m)
    gelu_value, gelu_pull = jax.vjp(gelu_exact, inner)
    grad_inner = gelu_pull(d_active)[0].astype(jnp.bfloat16)
    d_fc1_bias = column_sum(grad_inner)
    d_normed_two = right_product(grad_inner, fc1_m)
    norm_value_two, norm_pull_two = jax.vjp(norm_rows, second, gain_two, shift_two)
    d_second_norm, d_gain_two, d_shift_two = norm_pull_two(d_normed_two)
    grad_second = grad_out + d_second_norm
    grad_attn = grad_second.astype(jnp.bfloat16)
    d_proj_bias = column_sum(grad_attn)
    grad_mixed = (
        right_product(grad_attn, proj_m)
        .astype(jnp.bfloat16)
        .reshape(items, length, heads, head_dim)
    )
    again_scores = attention_scores(query, keys, valid, scale)
    again_probs = jnp.exp(again_scores - log_total)
    d_probs = jnp.einsum("ishd,ithd->ihst", grad_mixed, values, preferred_element_type=jnp.float32)
    inner_sum = jnp.sum(again_probs * d_probs, -1, keepdims=True)
    grad_scores = (again_probs * (d_probs - inner_sum)).astype(jnp.bfloat16)
    d_query = (
        jnp.einsum("ihst,ithd->ishd", grad_scores, keys, preferred_element_type=jnp.float32) * scale
    )
    d_keys = (
        jnp.einsum("ihst,ishd->ithd", grad_scores, query, preferred_element_type=jnp.float32)
        * scale
    )
    d_values = jnp.einsum(
        "ihst,ishd->ithd",
        again_probs.astype(jnp.bfloat16),
        grad_mixed,
        preferred_element_type=jnp.float32,
    )
    grad_triple = (
        jnp.stack([d_query, d_keys, d_values], 2).astype(jnp.bfloat16).reshape(rows, 3 * width)
    )
    d_normed_one = right_product(grad_triple, qkv_m)
    norm_value_one, norm_pull_one = jax.vjp(norm_rows, first, gain_one, shift_one)
    d_first_norm, d_gain_one, d_shift_one = norm_pull_one(d_normed_one)
    grad_first = (grad_second + d_first_norm).astype(jnp.bfloat16)
    d_skip_bias = column_sum(grad_first)
    grad_joined = right_product(grad_first, skip_m).reshape(items, length, 2 * width)
    in_grad = grad_joined[:, :, 0:width]
    skip_grad = grad_joined[:, :, width:]
    owners = lax.axis_size(("dp", "fsdp"))
    pairs = (
        (joined, grad_first),
        (normed_one, grad_triple),
        (mixed, grad_attn),
        (normed_two, grad_inner),
        (active, grad_mlp),
    )
    shard_sizes = [pair[0].shape[1] * pair[1].shape[1] // owners for pair in pairs]
    blocks = []
    for pair, owner_share in zip(pairs, shard_sizes):
        blocks.append(
            flat_piece(pair[0], pair[1]).reshape(1 * lax.axis_size(("dp", "fsdp")), owner_share)
        )
    owned = lax.psum_scatter(
        jnp.concatenate(blocks, 1), ("dp", "fsdp"), scatter_dimension=0, tiled=True
    ).reshape(-1)
    pieces = []
    offset = 0
    for share in shard_sizes:
        pieces.append(owned[offset : offset + share])
        offset = offset + share
    vec_grad = jnp.concatenate(
        [
            d_gain_one,
            d_shift_one,
            d_gain_two,
            d_shift_two,
            d_skip_bias,
            d_proj_bias,
            d_fc2_bias,
            d_fc1_bias,
        ]
    )
    vec_rows = lax.psum_scatter(vec_grad, "dp", scatter_dimension=0, tiled=True)
    vec_total = lax.psum(vec_rows, "fsdp")
    return (
        block_out.reshape(items, length, width),
        in_grad,
        skip_grad,
        pieces[0],
        pieces[1],
        pieces[2],
        pieces[3],
        pieces[4],
        vec_total,
    )


def solution(mesh):
    placed = (
        P(("dp", "fsdp"), None, None),
        P(("dp", "fsdp"), None, None),
        P(("dp", "fsdp"), None, None),
        P(("dp", "fsdp")),
        P(("dp", "fsdp")),
        P(("dp", "fsdp")),
        P(("dp", "fsdp")),
        P(("dp", "fsdp")),
        P(("dp", "fsdp")),
        P("dp"),
    )
    return jax.shard_map(
        body,
        mesh=mesh,
        in_specs=placed,
        out_specs=(
            P(("dp", "fsdp"), None, None),
            P(("dp", "fsdp"), None, None),
            P(("dp", "fsdp"), None, None),
            P(("dp", "fsdp")),
            P(("dp", "fsdp")),
            P(("dp", "fsdp")),
            P(("dp", "fsdp")),
            P(("dp", "fsdp")),
            P("dp"),
        ),
        check_vma=False,
    )
```

```python
import functools

import jax
import jax.numpy as jnp
from jax import lax
from jax.experimental import pallas as pl
from jax.experimental.pallas import tpu as pltpu
from jax.sharding import PartitionSpec as P

HEADS = 16
FF = 4608
CAPTION = 77


epsilon = 1e-05
masked_value = -1e30


def norm_rows(value, gain, shift):
    center = value - jnp.mean(value, -1, keepdims=True)
    spread = jnp.mean(center * center, -1, keepdims=True)
    return center * lax.rsqrt(spread + epsilon) * gain + shift


def gelu_exact(value):
    return jax.nn.gelu(value, approximate=False)


def key_valid(caption_len, length, caption):
    place = lax.broadcasted_iota(jnp.int32, (caption_len.shape[0], length), 1)
    return (place < 1 + caption_len[:, None]) | (place >= 1 + caption)


def product(left, right):
    return jnp.dot(left, right, preferred_element_type=jnp.float32)


def left_product(left, right):
    return lax.dot_general(
        left, right, (((0,), (0,)), ((), ())), preferred_element_type=jnp.float32
    )


def right_product(left, right):
    return lax.dot_general(
        left, right, (((1,), (1,)), ((), ())), preferred_element_type=jnp.float32
    )


def unpack(flat, width, hidden):
    return (
        flat[0].reshape(2 * width, width),
        flat[1].reshape(width, 3 * width),
        flat[2].reshape(width, width),
        flat[3].reshape(width, hidden),
        flat[4].reshape(hidden, width),
    )


def attention_scores(query, keys, valid, scale):
    raw = jnp.einsum("ishd,ithd->ihst", query, keys, preferred_element_type=jnp.float32) * scale
    return jnp.where(valid[:, None, None, :], raw, masked_value)


def column_sum(value):
    return jnp.sum(value.astype(jnp.float32), 0)


def flat_piece(left, right):
    grad_rows = left_product(left, right).reshape(-1)
    return grad_rows


MESH = pl.DeviceIdType.MESH
BF=jnp.bfloat16; F32=jnp.float32
SPLIT = 384


def unit_lanes(value, units, chips):
    seg = value.shape[1] // (units * chips)
    return [
        jnp.concatenate([value[:, (s * units + u) * seg : (s * units + u + 1) * seg] for s in range(chips)], 1)
        for u in range(units)
    ]


def row_loop(total, step, fn):
    def one(n, carry):
        fn(pl.ds(pl.multiple_of(n * step, step), step))
        return carry
    lax.fori_loop(0, total // step, one, 0)


def natural_lanes(units, chips):
    seg = units[0].shape[1] // chips
    return jnp.concatenate([u[:, s * seg : (s + 1) * seg] for s in range(chips) for u in units], 1)


def block_kernel(Z, wide, rows, lanes_a, length, padded,
                 cap_ref, skip_ref, qkv_ref, proj_ref, fc1_ref, fc2_ref, vec_ref, in_ref, sk_ref, og_ref,
                 out_o, in_o, sk_o, skip_g, qkv_g, proj_g, fc1_g, fc2_g, vec_o, skip_o, qp_o, fc1_o, fc2_o, j_o, h0_o,
                 skip_f, qkv_f, proj_f, fc1_f, fc2_f, own, keep, give, take, vbuf, vecs, b1s, vpart, vgot, vall, tok,
                 dtg, side, hid, am, t, m, zz, gu, gm, acc, tmp, sums, gacc, wbuf,
                 xl, xr, part, ra1, ra2, ra3, rc1, rc2, rc3,
                 send, recv, lsem, psend, precv, vsend, vrecv, isem, osem, wsem,
                 rsend, rrecv, xsend, xrecv, qsend, qrecv, ysend, yrecv, ssend, srecv, free):
    dp = lax.axis_index("dp"); f = lax.axis_index("fsdp")
    z = dp // 2; x = dp % 2; y = f // 2; c = f % 2
    o = 1 - c
    nt = wide // 128
    half = rows // 2
    chips = 4 * Z
    nz = Z - 1
    ndp = 2 * Z
    hd = wide // HEADS
    full = length // 16 * 16
    A = pl.ds(0, lanes_a); C = pl.ds(lanes_a, wide - lanes_a)
    zi = [lax.rem(z + k, Z) for k in range(1, Z)]
    zs = [(i * 2 + x, f) for i in zi]
    xp = (z * 2 + 1 - x, f)
    yp = (dp, (1 - y) * 2 + c)
    pp = (dp, y * 2 + o)
    dps = [(lax.rem(dp + k, ndp), f) for k in range(1, ndp)]
    fs = [(dp, lax.rem(f + k, 4)) for k in range(1, 4)]
    bar = pltpu.get_barrier_semaphore()
    for d in dps + fs:
        pl.semaphore_signal(bar, inc=1, device_id=d, device_id_type=MESH)
    flats = [(skip_ref, skip_f), (qkv_ref, qkv_f), (proj_ref, proj_f), (fc1_ref, fc1_f), (fc2_ref, fc2_f)]
    floads = [pltpu.make_async_copy(a, b, isem.at[n]) for n, (a, b) in enumerate(flats)]
    for cp in floads: cp.start()
    loads = [pltpu.make_async_copy(in_ref.at[:, 0, :], tok.at[0], isem.at[5]), pltpu.make_async_copy(sk_ref.at[:, 0, :], tok.at[1], isem.at[6])]
    for cp in loads: cp.start()
    def remote(src, dst, ssem, rsem, dev):
        return pltpu.make_async_remote_copy(src, dst, ssem, rsem, device_id=dev, device_id_type=MESH)
    floads[0].wait()
    for j in range(nt):
        own[0, :, 128 * j:128 * j + 128] = skip_f[pl.ds(j, rows, stride=nt), :].astype(BF)
    pl.semaphore_wait(bar, len(dps) + len(fs))

    waits = []
    def rc(i, slot, src, dst, dev):
        cp = remote(src, dst, send.at[i, slot], recv.at[i, slot], dev)
        cp.start(); waits.append(cp)
    def got(i, slot, dst):
        remote(dst, dst, send.at[i, slot], recv.at[i, slot], pp).wait_recv()
    def unit(i, cc):
        if i == 0: return skip_o.at[:, :, :, cc]
        if i in (1, 2): return qp_o.at[2 * (i - 1) + cc]
        if i in (3, 4): return fc1_o.at[2 * cc + (i - 3)]
        return fc2_o.at[2 * cc + (i - 5)]
    pc = {}
    lc = {}
    def exchange(i, first, second):
        keep[i - 1, 0:half, :] = jnp.where(c == 0, first, second)
        give[i - 1, 0:half, :] = jnp.where(c == 0, second, first)
        pc[i] = remote(give.at[i - 1], take.at[i - 1], psend.at[i - 1], precv.at[i - 1], pp)
        pc[i].start()
    def stage1(i):
        U = unit(i, c)
        if i in (1, 2, 3, 4):
            pc[i].wait_recv()
            p = keep[i - 1, 0:half, :]
            q = take[i - 1, 0:half, :]
            lo = jnp.where(c == 0, p, q); hi = jnp.where(c == 0, q, p)
            own[i, :, :] = jnp.concatenate([lo, hi], 0).astype(BF)
        lc[i] = pltpu.make_async_copy(own.at[i], U.at[z, x, y], lsem.at[i]); lc[i].start()
        rc(i, 2 * nz, own.at[i, :, C], U.at[z, x, y, :, C], yp)
        for k in range(1, Z):
            rc(i, k - 1, own.at[i, :, A], U.at[z, x, y, :, A], zs[k - 1])
    def stage2(i):
        U = unit(i, c)
        lc[i].wait()
        got(i, 2 * nz, U.at[z, x, 1 - y, :, C])
        for k in range(1, Z):
            rc(i, nz + k - 1, U.at[z, x, :, :, C], U.at[z, x, :, :, C], zs[k - 1])
        for k in range(1, Z):
            got(i, k - 1, U.at[lax.rem(z - k + Z, Z), x, y, :, A])
        L = U.at[:, x, y, :, A]
        rc(i, 2 * nz + 1, L, L, xp)
        rc(i, 2 * nz + 2, L, L, yp)
        rc(i, 2 * nz + 5, L, L, pp)
    def stage3(i):
        U = unit(i, c)
        for k in range(1, Z):
            got(i, nz + k - 1, U.at[lax.rem(z - k + Z, Z), x, :, :, C])
        L = U.at[:, x, :, :, C]
        rc(i, 2 * nz + 4, L, L, xp)
        rc(i, 2 * nz + 6, L, L, pp)
        L = U.at[:, 1 - x, y, :, A]
        got(i, 2 * nz + 1, L)
        rc(i, 2 * nz + 3, L, L, yp)
        rc(i, 2 * nz + 7, L, L, pp)
    def stage4(i):
        U = unit(i, c)
        L = U.at[:, x, 1 - y, :, A]
        got(i, 2 * nz + 2, L); rc(i, 2 * nz + 8, L, L, pp)
        L = U.at[:, 1 - x, 1 - y, :, A]
        got(i, 2 * nz + 3, L); rc(i, 2 * nz + 9, L, L, pp)
        L = U.at[:, 1 - x, :, :, C]
        got(i, 2 * nz + 4, L); rc(i, 2 * nz + 10, L, L, pp)
    def arrived(i):
        U = unit(i, 1 - c)
        got(i, 2 * nz + 5, U.at[:, x, y, :, A])
        got(i, 2 * nz + 7, U.at[:, 1 - x, y, :, A])
        got(i, 2 * nz + 8, U.at[:, x, 1 - y, :, A])
        got(i, 2 * nz + 9, U.at[:, 1 - x, 1 - y, :, A])
        got(i, 2 * nz + 6, U.at[:, x, :, :, C])
        got(i, 2 * nz + 10, U.at[:, 1 - x, :, :, C])
    def read(ref, first, stride):
        return jnp.concatenate([ref[pl.ds(first + j, half, stride=stride), :] for j in range(nt)], 1)

    stage1(0)
    vcopies = []
    vbuf[dp] = vec_ref[...]
    for k, d in enumerate(dps):
        cp = remote(vec_ref, vbuf.at[dp], vsend.at[k], vrecv.at[k], d)
        cp.start(); vcopies.append(cp)
    floads[1].wait(); floads[2].wait()
    exchange(1, read(qkv_f, 0, 3 * nt), read(qkv_f, nt, 3 * nt))
    exchange(2, read(qkv_f, 2 * nt, 3 * nt), read(proj_f, 0, nt))
    def prepare_late():
        floads[3].wait(); floads[4].wait()
        for j in range(nt):
            own[5, :, 128 * j:128 * j + 128] = fc2_f[pl.ds(j, rows, stride=nt), :].astype(BF)
            own[6, :, 128 * j:128 * j + 128] = fc2_f[pl.ds(j + nt * rows, rows, stride=nt), :].astype(BF)
        nat = jnp.concatenate([read(fc1_f, nt * v, 4 * nt) for v in range(4)], 1)
        u = unit_lanes(nat, 4, chips)
        exchange(3, u[0], u[2])
        exchange(4, u[1], u[3])

    def keep_out(n, src, dst):
        cp = pltpu.make_async_copy(src, dst, osem.at[n]); cp.start()
        return cp
    def weight(n, ref):
        pltpu.make_async_copy(ref, wbuf.at[n], wsem.at[n]).start()
    def weight_wait(k):
        pltpu.make_async_copy(wbuf.at[k], wbuf.at[k], wsem.at[k]).wait()
    def both_skip():
        for k in range(2):
            for i in range(Z // 2):
                pltpu.make_async_copy(skip_o.at[k * (Z // 2) + i], wbuf.at[k, pl.ds(2 * i, 2)], wsem.at[k]).start()
    def cols(k, l):
        return wbuf[k, :, :, :, :, l].reshape(wide, SPLIT)
    def lanes_loop(fn):
        def one(n, carry):
            fn(pl.ds(pl.multiple_of(n * SPLIT, 128), SPLIT))
            return carry
        lax.fori_loop(0, wide // SPLIT, one, 0)
    def vector(n):
        return vecs[0:1, n * wide:(n + 1) * wide]
    def put_rows(k, src):
        def one(r): tok[k, r, :] = src[r, :]
        row_loop(full, 16, one)
        if length > full: tok[k, full:length, :] = src[full:length, :]
    def norm(src, gain, shift, dst):
        def one(r):
            v = src[r, :]
            cen = v - jnp.mean(v, -1, keepdims=True)
            s = jnp.mean(cen * cen, -1, keepdims=True)
            dst[r, :] = (cen * lax.rsqrt(s + epsilon) * gain + shift).astype(BF)
        row_loop(padded, 16, one)
    def take_rows(k, dst, at):
        if padded > full: dst[at + (slice(padded - 16, padded), slice(None))] = jnp.zeros((16, wide), dst.dtype)
        def one(r): dst[at + (r, slice(None))] = tok[k, r, :].astype(dst.dtype)
        row_loop(full, 16, one)
        if length > full: dst[at + (slice(full, length), slice(None))] = tok[k, full:length, :].astype(dst.dtype)
    def inputs():
        for cp in loads: cp.wait()
        take_rows(0, dtg, (0,))
        take_rows(1, dtg, (1,))
        pltpu.make_async_copy(og_ref.at[:, 0, :], tok.at[0], isem.at[5]).start()
        def two(r):
            u = unit_lanes(jnp.concatenate([dtg[0, r, :], dtg[1, r, :]], 1), 2, chips)
            side[0, r, :] = u[0]
            side[1, r, :] = u[1]
        row_loop(padded, 16, two)
        keep_out(0, side, j_o)
    def vectors():
        for k in range(len(dps)):
            remote(vec_ref, vbuf.at[lax.rem(dp - (k + 1) + ndp, ndp)], vsend.at[k], vrecv.at[k], pp).wait_recv()
        vecs[...] = jnp.concatenate([vbuf[k] for k in range(ndp)], 1)
        b = unit_lanes(vecs[0:1, 7 * wide:11 * wide], 4, chips)
        for u in range(4): b1s[u] = b[u]
        pltpu.make_async_copy(og_ref.at[:, 0, :], tok.at[0], isem.at[5]).wait()
        take_rows(0, gm, ())
        pltpu.make_async_copy(og_ref.at[:, 0, :], tok.at[1], isem.at[6]).start()
    def first_part():
        arrived(0)
        both_skip()
        weight_wait(0); weight_wait(1)
        def one(l):
            v = jnp.dot(dtg[0], cols(0, l), preferred_element_type=F32)
            v = v + jnp.dot(dtg[1], cols(1, l), preferred_element_type=F32)
            hid[:, l] = v + vecs[0:1, pl.ds(4 * wide + l.start, SPLIT)]
        lanes_loop(one)
        norm(hid, vector(0), vector(1), am.at[0])
        keep_out(1, hid, h0_o)
    def project(n, u):
        def one(l):
            t[u, :, l] = jnp.dot(am[0], cols(n, l), preferred_element_type=F32).astype(BF)
        lanes_loop(one)
    def query_keys():
        arrived(1)
        for u in range(2): weight(u, qp_o.at[u])
        for u in range(2):
            weight_wait(u)
            project(u, u)
    def values():
        arrived(2)
        weight(0, qp_o.at[2]); weight(1, qp_o.at[3])
        weight_wait(0)
        project(0, 2)
    def window(h):
        base = pl.multiple_of(jnp.minimum((h * hd) // 128, nt - 2) * 128, 128)
        lane = lax.broadcasted_iota(jnp.int32, (1, 256), 1) + (base - h * hd)
        return pl.ds(base, 256), (lane >= 0) & (lane < hd)
    def attend(first, last):
        cap = cap_ref[0]
        key = lax.broadcasted_iota(jnp.int32, (1, padded), 1)
        live = ((key < 1 + cap) | (key >= 1 + CAPTION)) & (key < length)
        def head(h, carry):
            win, inside = window(h)
            q = jnp.where(inside, t[0, :, win].astype(F32), 0.0).astype(BF)
            s = lax.dot_general(q, t[1, :, win], (((1,), (1,)), ((), ())), preferred_element_type=F32) * hd ** (-0.5)
            s = jnp.where(live, s, masked_value)
            e = jnp.exp(s - jnp.max(s, -1, keepdims=True))
            p = (e / jnp.sum(e, -1, keepdims=True)).astype(BF)
            v = jnp.dot(p, t[2, :, win], preferred_element_type=F32)
            am[1, :, win] = jnp.where(inside, v, am[1, :, win].astype(F32)).astype(BF)
            return carry
        lax.fori_loop(first, last, head, 0)
    def second_part():
        weight_wait(1)
        pltpu.make_async_copy(hid, h0_o, osem.at[1]).wait()
        def one(l):
            v = jnp.dot(am[1], cols(1, l), preferred_element_type=F32)
            h = hid[:, l] + (v + vecs[0:1, pl.ds(5 * wide + l.start, SPLIT)])
            hid[:, l] = h
            acc[:, l] = h + vecs[0:1, pl.ds(6 * wide + l.start, SPLIT)]
        lanes_loop(one)
        norm(hid, vector(2), vector(3), m)
    def widen_load(i):
        arrived(i)
        for k in range(2): weight(k, fc1_o.at[2 * k + i - 3])
    def widen(k, u):
        weight_wait(k)
        def one(l):
            tmp[:, l] = jnp.dot(m[...], cols(k, l), preferred_element_type=F32)
        lanes_loop(one)
        def two(r):
            v = tmp[r, :] + b1s[u]
            cdf = 0.5 * (1.0 + lax.erf(v * 0.7071067811865476))
            pdf = jnp.exp(-0.5 * v * v) * 0.3989422804014327
            zz[u, r, :] = (v * cdf).astype(BF)
            gu[u, r, :] = (cdf + v * pdf).astype(BF)
        row_loop(padded, 16, two)
    def narrow_load(i):
        arrived(i)
        for k in range(2): weight(k, fc2_o.at[2 * k + i - 5])
    def narrow(k, u):
        weight_wait(k)
        tmp[...] = jnp.zeros_like(tmp)
        def one(l):
            w = cols(k, l)
            acc[:, l] += jnp.dot(zz[u], w, preferred_element_type=F32)
            tmp[...] += lax.dot_general(gm[:, l], w, (((1,), (1,)), ((), ())), preferred_element_type=F32)
        lanes_loop(one)
        def two(r):
            gu[u, r, :] = (tmp[r, :] * gu[u, r, :].astype(F32)).astype(BF)
        row_loop(padded, 16, two)

    xcopies = {}
    def swap(n, src, dst):
        xcopies[n] = remote(src, dst, xsend.at[n], xrecv.at[n], pp)
        xcopies[n].start()
    nb = 4
    started = {j: [] for j in range(7)}
    def sc(j, slot, src, dst, dev):
        cp = remote(src, dst, rsend.at[j, slot], rrecv.at[j, slot], dev)
        cp.start(); started[j].append(cp)
    def came(j, slot, dst):
        remote(dst, dst, rsend.at[j, slot], rrecv.at[j, slot], pp).wait_recv()
    need = [(0, 1), (2,), (3, 4), (5,), (6, 7), (8, 9), (10, 11)]
    def operands(j):
        if j < 2: return zz.at[2 * c + j], gm, xl.at[j], xr.at[0]
        if j < 4: return m, gu.at[2 * c + j - 2], xl.at[2], xr.at[j - 1]
        if j == 4: return am.at[c], dtg.at[2 + c], xl.at[0], xr.at[0]
        if j == 5: return am.at[0], dtg.at[c], xl.at[1], xr.at[1]
        return side.at[0], side.at[1], xl.at[2], xr.at[2]
    def reduce1(j):
        for n in need[j]: xcopies[n].wait_recv()
        if j >= nb:
            for cp in started[j - nb]: cp.wait_send()
        b = j % nb
        D = part.at[b]
        l1, r1, l2, r2 = operands(j)
        step = wide - lanes_a
        dims = (((0,), (0,)), ((), ()))
        def chunk(n, carry):
            lanes = pl.ds(pl.multiple_of(n * step, 128), step)
            r = lax.dot_general(l1[...], r1[:, lanes], dims, preferred_element_type=F32)
            r = r + lax.dot_general(l2[...], r2[:, lanes], dims, preferred_element_type=F32)
            D[:, :, :, :, lanes] = r.reshape(Z, 2, 2, rows, step).astype(BF)
            return carry
        lax.fori_loop(0, wide // step, chunk, 0)
        sc(j, 0, D.at[:, 1 - x, 1 - y, :, A], ra1.at[b, 0], yp)
        sc(j, 2, D.at[:, 1 - x, :, :, C], rc1.at[b], xp)
        sc(j, 1, D.at[:, x, 1 - y, :, A], ra1.at[b, 1], yp)
    def reduce2(j):
        b = j % nb
        D = part.at[b]
        came(j, 0, ra1.at[b, 0])
        for zz in range(Z):
            va = D.at[zz, 1 - x, y, :, A]
            va[...] = (va[...].astype(F32) + ra1[b, 0, zz].astype(F32)).astype(BF)
        sc(j, 3, D.at[:, 1 - x, y, :, A], ra2.at[b], xp)
        came(j, 2, rc1.at[b])
        for zz in range(Z):
            for yy in range(2):
                va = D.at[zz, x, yy, :, C]
                va[...] = (va[...].astype(F32) + rc1[b, zz, yy].astype(F32)).astype(BF)
        for k in range(nz):
            sc(j, 4 + k, D.at[zi[k], x, :, :, C], rc2.at[b, k], zs[k])
    def reduce3(j):
        b = j % nb
        D = part.at[b]
        came(j, 1, ra1.at[b, 1])
        came(j, 3, ra2.at[b])
        for zz in range(Z):
            va = D.at[zz, x, y, :, A]
            va[...] = (va[...].astype(F32) + ra1[b, 1, zz].astype(F32) + ra2[b, zz].astype(F32)).astype(BF)
        for k in range(nz):
            sc(j, 4 + nz + k, D.at[zi[k], x, y, :, A], ra3.at[b, k], zs[k])
        for k in range(nz):
            came(j, 4 + k, rc2.at[b, k])
        for yy in range(2):
            va = D.at[z, x, yy, :, C]
            s = va[...].astype(F32)
            for k in range(nz):
                s = s + rc2[b, k, yy].astype(F32)
            va[...] = s.astype(BF)
        sc(j, 4 + 2 * nz, D.at[z, x, 1 - y, :, C], rc3.at[b], yp)
    pcopies = {}
    def lay(ref, val, first, stride, n):
        for i in range(val.shape[1] // 128):
            ref[pl.ds(first + i, n, stride=stride), :] = val[:, 128 * i:128 * i + 128]
    def reduce4(j):
        b = j % nb
        D = part.at[b]
        for k in range(nz):
            came(j, 4 + nz + k, ra3.at[b, k])
        came(j, 4 + 2 * nz, rc3.at[b])
        p = D[z, x, y, :, 0:lanes_a].astype(F32)
        for k in range(nz):
            p = p + ra3[b, k].astype(F32)
        q = D[z, x, y, :, lanes_a:wide].astype(F32) + rc3[b].astype(F32)
        v = jnp.concatenate([p, q], 1)
        if j in (0, 1):
            lay(fc2_f, v, j * rows * nt, nt, rows)
            if j == 1: keep_out(9, fc2_f, fc2_g)
        elif j == 6:
            lay(skip_f, v, 0, nt, rows)
            keep_out(5, skip_f, skip_g)
        else:
            lo = v[0:half]; hi = v[half:rows]
            keep[j - 2, 0:half, :] = jnp.where(c == 0, lo, hi)
            give[j - 2, 0:half, :] = jnp.where(c == 0, hi, lo)
            cp = remote(give.at[j - 2], take.at[j - 2], qsend.at[j - 2], qrecv.at[j - 2], pp)
            cp.start(); pcopies[j] = cp
    def both(j):
        pcopies[j].wait_recv()
        p = keep[j - 2, 0:half, :]; q = take[j - 2, 0:half, :]
        return jnp.where(c == 0, p, q), jnp.where(c == 0, q, p)
    def reduce5(j):
        if j == 3:
            p, q = both(2), both(3)
            lay(fc1_f, natural_lanes([p[0], q[0], p[1], q[1]], chips), 0, 4 * nt, half)
            keep_out(8, fc1_f, fc1_g)
        elif j == 5:
            first, second = both(5)
            lay(qkv_f, first, 0, 3 * nt, half)
            lay(qkv_f, second, nt, 3 * nt, half)
            keep_out(6, qkv_f, qkv_g)
        elif j == 4:
            first, second = both(4)
            lay(qkv_f, first, 2 * nt, 3 * nt, half)
            lay(proj_f, second, 0, nt, half)
            keep_out(7, proj_f, proj_g)


    def zero(n): gacc[n] = jnp.zeros((8, wide), F32)
    def add_rows(n, v):
        gacc[n] += v[0:8] + v[8:16]
    def close(n):
        return jnp.sum(gacc[n], 0, keepdims=True)
    def column_sums(src):
        zero(0)
        def one(r): add_rows(0, src[r, :].astype(F32))
        row_loop(padded, 16, one)
        return close(0)
    def norm_back(dy, src, gain, fn):
        zero(0); zero(1); zero(2)
        def one(r):
            d = dy[r, :]
            v = src[r, :]
            cen = v - jnp.mean(v, -1, keepdims=True)
            rs = lax.rsqrt(jnp.mean(cen * cen, -1, keepdims=True) + epsilon)
            xh = cen * rs
            dx = d * gain
            g = rs * (dx - jnp.mean(dx, -1, keepdims=True) - xh * jnp.mean(dx * xh, -1, keepdims=True))
            add_rows(0, d * xh)
            add_rows(1, d)
            fn(r, g)
        row_loop(padded, 16, one)
    def turned(lhs, n, fresh):
        if fresh: tmp[...] = jnp.zeros_like(tmp)
        def one(l):
            tmp[...] += lax.dot_general(lhs[:, l], cols(n, l), (((1,), (1,)), ((), ())), preferred_element_type=F32)
        lanes_loop(one)
    def widen_back(us):
        for i, u in enumerate(us):
            weight_wait(i)
            turned(gu.at[u], i, u == 0)
            sums[7 + u] = column_sums(gu.at[u])
    def widen_back_load(us):
        for i, u in enumerate(us): weight(i, fc1_o.at[u])
    def norm_two():
        weight(0, qp_o.at[3])
        pltpu.make_async_copy(og_ref.at[:, 0, :], tok.at[1], isem.at[6]).wait()
        take_rows(1, acc, ())
        def fn(r, g):
            s = acc[r, :] + g
            acc[r, :] = s
            b = s.astype(BF)
            dtg[3, r, :] = b
            add_rows(2, b.astype(F32))
        norm_back(tmp, hid, vector(2), fn)
        sums[2] = close(0); sums[3] = close(1); sums[5] = close(2)
        pltpu.make_async_copy(h0_o, hid, isem.at[5]).start()
        sums[6] = column_sums(gm)
        weight_wait(0)
        turned(dtg.at[3], 0, True)
        def two(r): side[0, r, :] = tmp[r, :].astype(BF)
        row_loop(padded, 16, two)
    def attend_back(first, last):
        cap = cap_ref[0]
        key = lax.broadcasted_iota(jnp.int32, (padded, 1), 0)
        live = ((key < 1 + cap) | (key >= 1 + CAPTION)) & (key < length)
        def head(h, carry):
            win, inside = window(h)
            q = jnp.where(inside, t[0, :, win].astype(F32), 0.0).astype(BF)
            k = t[1, :, win]
            g = jnp.where(inside, side[0, :, win].astype(F32), 0.0).astype(BF)
            s = lax.dot_general(k, q, (((1,), (1,)), ((), ())), preferred_element_type=F32) * hd ** (-0.5)
            s = jnp.where(live, s, masked_value)
            e = jnp.exp(s - jnp.max(s, 0, keepdims=True))
            p = e * (1.0 / jnp.sum(e, 0, keepdims=True))
            d = lax.dot_general(t[2, :, win], g, (((1,), (1,)), ((), ())), preferred_element_type=F32)
            ds = (p * (d - jnp.sum(p * d, 0, keepdims=True))).astype(BF)
            dq = lax.dot_general(ds, k, (((0,), (0,)), ((), ())), preferred_element_type=F32) * hd ** (-0.5)
            dk = jnp.dot(ds, q, preferred_element_type=F32) * hd ** (-0.5)
            dv = jnp.dot(p.astype(BF), g, preferred_element_type=F32)
            for i, v in enumerate((dq, dk, dv)):
                dtg[i, :, win] = jnp.where(inside, v, dtg[i, :, win].astype(F32)).astype(BF)
            return carry
        lax.fori_loop(first, last, head, 0)
    def late_left():
        pl.semaphore_signal(free, inc=1, device_id=pp, device_id_type=MESH)
        pl.semaphore_wait(free, 1)
        pltpu.make_async_copy(side, j_o, osem.at[0]).wait()
        swap(6, am.at[o], xl.at[0])
        swap(8, am.at[0], xl.at[1])
        swap(10, j_o.at[o], xl.at[2])
    def late_right():
        swap(7, dtg.at[2 + o], xr.at[0])
        swap(9, dtg.at[o], xr.at[1])
        pltpu.make_async_copy(j_o.at[c], side.at[0], isem.at[7]).start()
        weight(0, qp_o.at[0]); weight(1, qp_o.at[1])
    def project_back():
        for i in range(3):
            weight_wait(i % 2)
            turned(dtg.at[i], i % 2, i == 0)
            if i == 0: weight(0, qp_o.at[2])
    def norm_one():
        pltpu.make_async_copy(h0_o, hid, isem.at[5]).wait()
        both_skip()
        def fn(r, g):
            b = (acc[r, :] + g).astype(BF)
            side[1, r, :] = b
            add_rows(2, b.astype(F32))
        norm_back(tmp, hid, vector(0), fn)
        sums[0] = close(0); sums[1] = close(1); sums[4] = close(2)
        swap(11, side.at[1], xr.at[2])
    def join_back(i, dst):
        weight_wait(i)
        turned(side.at[1], i, True)
        put_rows(i, tmp)
        keep_out(3 + i, tok.at[i], dst.at[:, 0, :])
    nv = vpart.shape[2]
    def vec_send():
        total = jnp.concatenate([sums[i] for i in range(7)] + [natural_lanes([sums[7 + u] for u in range(4)], chips)], 1)
        for k in range(ndp): vpart[k] = total[:, k * nv:(k + 1) * nv]
        for k, d in enumerate(dps):
            cp = remote(vpart.at[d[0]], vgot.at[k], ysend.at[k], yrecv.at[k], d)
            cp.start(); vcopies.append(cp)
    def vec_first():
        s = vpart[dp]
        for k in range(len(dps)):
            remote(vgot.at[k], vgot.at[k], ysend.at[k], yrecv.at[k], pp).wait_recv()
            s = s + vgot[k]
        vall[f] = s
        for k, d in enumerate(fs):
            cp = remote(vall.at[f], vall.at[f], ssend.at[k], srecv.at[k], d)
            cp.start(); vcopies.append(cp)
    def vec_last():
        for k in range(3):
            src = lax.rem(f - (k + 1) + 4, 4)
            remote(vall.at[src], vall.at[src], ssend.at[k], srecv.at[k], pp).wait_recv()
        vec_o[...] = vall[0] + vall[1] + vall[2] + vall[3]

    stage2(0)
    prepare_late()
    stage1(1)
    stage3(0)
    inputs()
    vectors()
    stage2(1); stage1(2)
    stage3(1); stage4(0)
    first_part()
    stage2(2); stage1(3)
    stage3(2); stage4(1)
    query_keys()
    stage2(3); stage1(4)
    stage3(3); stage4(2)
    values()
    attend(0, 4)
    stage2(4); stage1(5)
    attend(4, 11)
    stage3(4); stage4(3)
    attend(11, 16)
    second_part()
    stage2(5); stage1(6)
    widen_load(3)
    widen(0, 0)
    stage3(5); stage4(4)
    widen(1, 2)
    stage2(6)
    widen_load(4)
    widen(0, 1)
    stage3(6); stage4(5)
    widen(1, 3)
    for cp in pc.values(): cp.wait_send()
    swap(0, zz.at[2 * o], xl.at[0])
    swap(1, gm, xr.at[0])
    swap(2, zz.at[2 * o + 1], xl.at[1])
    swap(3, m, xl.at[2])
    narrow_load(5)
    reduce1(0)
    narrow(0, 0)
    stage4(6)
    narrow(1, 2)
    swap(4, gu.at[2 * o], xr.at[1])
    reduce1(1); reduce2(0)
    narrow_load(6)
    narrow(0, 1)
    narrow(1, 3)
    swap(5, gu.at[2 * o + 1], xr.at[2])
    widen_back_load((0, 1))
    reduce1(2); reduce2(1); reduce3(0)
    put_rows(0, acc)
    keep_out(2, tok.at[0], out_o.at[:, 0, :])
    widen_back((0, 1))
    widen_back_load((2, 3))
    reduce1(3)
    widen_back((2, 3))
    reduce2(2); reduce3(1); reduce4(0)
    late_left()
    norm_two()
    attend_back(0, 4)
    reduce2(3); reduce3(2); reduce4(1)
    attend_back(4, 10)
    reduce3(3); reduce4(2)
    attend_back(10, 16)
    late_right()
    reduce1(4); reduce4(3)
    reduce1(5); reduce2(4)
    project_back()
    norm_one()
    vec_send()
    reduce2(5); reduce3(4)
    pltpu.make_async_copy(j_o.at[c], side.at[0], isem.at[7]).wait()
    reduce1(6)
    vec_first()
    pltpu.make_async_copy(tok.at[0], out_o.at[:, 0, :], osem.at[2]).wait()
    join_back(0, in_o)
    reduce3(5); reduce4(4)
    join_back(1, sk_o)
    reduce5(3)
    reduce2(6)
    vec_last()
    reduce4(5); reduce5(4)
    reduce3(6)
    reduce5(5)
    reduce4(6)
    for k in (0, 1): pltpu.make_async_copy(tok.at[k], (in_o, sk_o)[k].at[:, 0, :], osem.at[3 + k]).wait()
    for n, (a, b) in zip((5, 6, 7, 8, 9), ((skip_f, skip_g), (qkv_f, qkv_g), (proj_f, proj_g), (fc1_f, fc1_g), (fc2_f, fc2_g))):
        pltpu.make_async_copy(a, b, osem.at[n]).wait()
    for j in range(3, 7):
        for cp in started[j]: cp.wait_send()
    for cp in waits: cp.wait_send()
    for cp in pcopies.values(): cp.wait_send()
    for cp in vcopies: cp.wait_send()
    for cp in xcopies.values(): cp.wait_send()


def block(cap, skip, qkv, proj, fc1, fc2, vectors, block_in, skip_in, out_grad, dpn):
    _, length, wide = block_in.shape
    Z = dpn // 2; rows = skip.shape[0] // wide
    padded = -(-length // 16) * 16
    lanes_a = (wide // 128 * 2 + 1) // 3 * 128
    lc = wide - lanes_a
    U = (Z, 2, 2, rows, wide)
    hbm = pl.BlockSpec(memory_space=pl.ANY); vm = pl.BlockSpec(memory_space=pltpu.VMEM)
    ns = 2 * (Z - 1) + 11
    nr = 2 * (Z - 1) + 5
    nv = vectors.shape[0]
    D = pltpu.SemaphoreType.DMA
    V = pltpu.VMEM
    hp = -(-rows // 2 // 8) * 8
    S = jax.ShapeDtypeStruct
    act = (padded, wide)
    flat = [(w.shape[0] // 128, 128) for w in (skip, qkv, proj, fc1, fc2)]
    tokens = (length, 1, wide)
    nb = 4
    nz = Z - 1
    res = pl.pallas_call(
        functools.partial(block_kernel, Z, wide, rows, lanes_a, length, padded),
        out_shape=(S(tokens, F32),) * 3 + tuple(S(s, F32) for s in flat) + (S((1, nv), F32),
                   S((Z, 2, 2, 2, rows, wide), BF), S((4,) + U, BF), S((4,) + U, BF), S((4,) + U, BF), S((2,) + act, BF), S(act, F32)),
        in_specs=[pl.BlockSpec(memory_space=pltpu.SMEM)] + [hbm] * 5 + [vm] + [hbm] * 3,
        out_specs=(hbm,) * 8 + (vm,) + (hbm,) * 6,
        scratch_shapes=[V(s, F32) for s in flat] + [
                        V((7, rows, wide), BF), V((4, hp, wide), F32), V((4, hp, wide), F32), V((4, hp, wide), F32),
                        V((dpn, 1, nv), F32), V((1, nv * dpn), F32), V((4, 1, wide), F32), V((dpn, 1, nv), F32), V((dpn - 1, 1, nv), F32), V((4, 1, nv), F32),
                        V((2, length, wide), F32),
                        V((4,) + act, BF), V((2,) + act, BF), V(act, F32), V((2,) + act, BF), V((3,) + act, BF), V(act, BF), V((4,) + act, BF), V((4,) + act, BF), V(act, BF),
                        V(act, F32), V(act, F32), V((11, 1, wide), F32), V((3, 8, wide), F32), V((2,) + U, BF),
                        V((3,) + act, BF), V((3,) + act, BF), V((nb,) + U, BF),
                        V((nb, 2, Z, rows, lanes_a), BF), V((nb, Z, rows, lanes_a), BF), V((nb, nz, rows, lanes_a), BF),
                        V((nb, Z, 2, rows, lc), BF), V((nb, nz, 2, rows, lc), BF), V((nb, rows, lc), BF),
                        D((7, ns)), D((7, ns)), D((7,)), D((4,)), D((4,)), D((dpn - 1,)), D((dpn - 1,)), D((8,)), D((10,)), D((2,)),
                        D((7, nr)), D((7, nr)), D((12,)), D((12,)), D((4,)), D((4,)), D((dpn - 1,)), D((dpn - 1,)), D((3,)), D((3,)), pltpu.SemaphoreType.REGULAR],
        compiler_params=pltpu.CompilerParams(collective_id=0, has_side_effects=True, vmem_limit_bytes=67043328),
        name="block",
    )(cap, *(w.reshape(-1, 128) for w in (skip, qkv, proj, fc1, fc2)), vectors.reshape(1, nv),
      *(v.reshape(tokens) for v in (block_in, skip_in, out_grad)))
    shape = block_in.shape
    return tuple(r.reshape(shape) for r in res[:3]) + tuple(r.reshape(-1) for r in res[3:9])


def whole_rows(width, dp, fsdp, items, heads, hidden):
    return (
        fsdp == 4 and dp % 2 == 0 and width % (dp * 16) == 0 and items == 1 and hidden == 4 * width
        and width % SPLIT == 0 and width // heads <= 128
    )


def body(block_in, skip_in, out_grad, caption_len, skip_w, qkv_w, proj_w, fc1_w, fc2_w, vectors):
    items, length, width = block_in.shape
    if whole_rows(width, lax.axis_size("dp"), lax.axis_size("fsdp"), items, HEADS, FF):
        return block(
            caption_len, skip_w, qkv_w, proj_w, fc1_w, fc2_w, vectors, block_in, skip_in, out_grad,
            lax.axis_size("dp"),
        )
    heads = HEADS
    head_dim = width // heads
    hidden = FF
    rows = items * length
    scale = head_dim ** (-0.5)
    gathered = (
        lax.all_gather(skip_w.astype(jnp.bfloat16), ("dp", "fsdp"), axis=0, tiled=True),
        lax.all_gather(qkv_w.astype(jnp.bfloat16), ("dp", "fsdp"), axis=0, tiled=True),
        lax.all_gather(proj_w.astype(jnp.bfloat16), ("dp", "fsdp"), axis=0, tiled=True),
        lax.all_gather(fc1_w.astype(jnp.bfloat16), ("dp", "fsdp"), axis=0, tiled=True),
        lax.all_gather(fc2_w.astype(jnp.bfloat16), ("dp", "fsdp"), axis=0, tiled=True),
    )
    skip_m, qkv_m, proj_m, fc1_m, fc2_m = unpack(gathered, width, hidden)
    vec = lax.all_gather(vectors, "dp", axis=0, tiled=True)
    gain_one = vec[0:width]
    shift_one = vec[width : 2 * width]
    gain_two = vec[2 * width : 3 * width]
    shift_two = vec[3 * width : 4 * width]
    skip_bias = vec[4 * width : 5 * width]
    proj_bias = vec[5 * width : 6 * width]
    fc2_bias = vec[6 * width : 7 * width]
    fc1_bias = vec[7 * width :]
    valid = key_valid(caption_len, length, CAPTION)
    joined = jnp.concatenate([block_in, skip_in], -1).reshape(rows, 2 * width).astype(jnp.bfloat16)
    first = product(joined, skip_m) + skip_bias
    normed_one = norm_rows(first, gain_one, shift_one).astype(jnp.bfloat16)
    triple = (
        product(normed_one, qkv_m).astype(jnp.bfloat16).reshape(items, length, 3, heads, head_dim)
    )
    query = triple[:, :, 0]
    keys = triple[:, :, 1]
    values = triple[:, :, 2]
    scores = attention_scores(query, keys, valid, scale)
    top = jnp.max(scores, -1, keepdims=True)
    expd = jnp.exp(scores - top)
    total = jnp.sum(expd, -1, keepdims=True)
    probs = expd / total
    log_total = top + jnp.log(total)
    mixed = (
        jnp.einsum(
            "ihst,ithd->ishd",
            probs.astype(jnp.bfloat16),
            values,
            preferred_element_type=jnp.float32,
        )
        .astype(jnp.bfloat16)
        .reshape(rows, width)
    )
    second = first + (product(mixed, proj_m) + proj_bias)
    normed_two = norm_rows(second, gain_two, shift_two).astype(jnp.bfloat16)
    inner = product(normed_two, fc1_m) + fc1_bias
    active = gelu_exact(inner).astype(jnp.bfloat16)
    block_out = second + (product(active, fc2_m) + fc2_bias)
    again = (
        lax.all_gather(skip_w.astype(jnp.bfloat16), ("dp", "fsdp"), axis=0, tiled=True),
        lax.all_gather(qkv_w.astype(jnp.bfloat16), ("dp", "fsdp"), axis=0, tiled=True),
        lax.all_gather(proj_w.astype(jnp.bfloat16), ("dp", "fsdp"), axis=0, tiled=True),
        lax.all_gather(fc1_w.astype(jnp.bfloat16), ("dp", "fsdp"), axis=0, tiled=True),
        lax.all_gather(fc2_w.astype(jnp.bfloat16), ("dp", "fsdp"), axis=0, tiled=True),
    )
    skip_m, qkv_m, proj_m, fc1_m, fc2_m = unpack(again, width, hidden)
    grad_out = out_grad.reshape(rows, width)
    grad_mlp = grad_out.astype(jnp.bfloat16)
    d_fc2_bias = column_sum(grad_mlp)
    d_active = right_product(grad_mlp, fc2_m)
    gelu_value, gelu_pull = jax.vjp(gelu_exact, inner)
    grad_inner = gelu_pull(d_active)[0].astype(jnp.bfloat16)
    d_fc1_bias = column_sum(grad_inner)
    d_normed_two = right_product(grad_inner, fc1_m)
    norm_value_two, norm_pull_two = jax.vjp(norm_rows, second, gain_two, shift_two)
    d_second_norm, d_gain_two, d_shift_two = norm_pull_two(d_normed_two)
    grad_second = grad_out + d_second_norm
    grad_attn = grad_second.astype(jnp.bfloat16)
    d_proj_bias = column_sum(grad_attn)
    grad_mixed = (
        right_product(grad_attn, proj_m)
        .astype(jnp.bfloat16)
        .reshape(items, length, heads, head_dim)
    )
    again_scores = attention_scores(query, keys, valid, scale)
    again_probs = jnp.exp(again_scores - log_total)
    d_probs = jnp.einsum("ishd,ithd->ihst", grad_mixed, values, preferred_element_type=jnp.float32)
    inner_sum = jnp.sum(again_probs * d_probs, -1, keepdims=True)
    grad_scores = (again_probs * (d_probs - inner_sum)).astype(jnp.bfloat16)
    d_query = (
        jnp.einsum("ihst,ithd->ishd", grad_scores, keys, preferred_element_type=jnp.float32) * scale
    )
    d_keys = (
        jnp.einsum("ihst,ishd->ithd", grad_scores, query, preferred_element_type=jnp.float32)
        * scale
    )
    d_values = jnp.einsum(
        "ihst,ishd->ithd",
        again_probs.astype(jnp.bfloat16),
        grad_mixed,
        preferred_element_type=jnp.float32,
    )
    grad_triple = (
        jnp.stack([d_query, d_keys, d_values], 2).astype(jnp.bfloat16).reshape(rows, 3 * width)
    )
    d_normed_one = right_product(grad_triple, qkv_m)
    norm_value_one, norm_pull_one = jax.vjp(norm_rows, first, gain_one, shift_one)
    d_first_norm, d_gain_one, d_shift_one = norm_pull_one(d_normed_one)
    grad_first = (grad_second + d_first_norm).astype(jnp.bfloat16)
    d_skip_bias = column_sum(grad_first)
    grad_joined = right_product(grad_first, skip_m).reshape(items, length, 2 * width)
    in_grad = grad_joined[:, :, 0:width]
    skip_grad = grad_joined[:, :, width:]
    owners = lax.axis_size(("dp", "fsdp"))
    pairs = (
        (joined, grad_first),
        (normed_one, grad_triple),
        (mixed, grad_attn),
        (normed_two, grad_inner),
        (active, grad_mlp),
    )
    shard_sizes = [pair[0].shape[1] * pair[1].shape[1] // owners for pair in pairs]
    blocks = []
    for pair, owner_share in zip(pairs, shard_sizes):
        blocks.append(
            flat_piece(pair[0], pair[1]).reshape(1 * lax.axis_size(("dp", "fsdp")), owner_share)
        )
    owned = lax.psum_scatter(
        jnp.concatenate(blocks, 1), ("dp", "fsdp"), scatter_dimension=0, tiled=True
    ).reshape(-1)
    pieces = []
    offset = 0
    for share in shard_sizes:
        pieces.append(owned[offset : offset + share])
        offset = offset + share
    vec_grad = jnp.concatenate(
        [
            d_gain_one,
            d_shift_one,
            d_gain_two,
            d_shift_two,
            d_skip_bias,
            d_proj_bias,
            d_fc2_bias,
            d_fc1_bias,
        ]
    )
    vec_rows = lax.psum_scatter(vec_grad, "dp", scatter_dimension=0, tiled=True)
    vec_total = lax.psum(vec_rows, "fsdp")
    return (
        block_out.reshape(items, length, width),
        in_grad,
        skip_grad,
        pieces[0],
        pieces[1],
        pieces[2],
        pieces[3],
        pieces[4],
        vec_total,
    )


def solution(mesh):
    placed = (
        P(("dp", "fsdp"), None, None),
        P(("dp", "fsdp"), None, None),
        P(("dp", "fsdp"), None, None),
        P(("dp", "fsdp")),
        P(("dp", "fsdp")),
        P(("dp", "fsdp")),
        P(("dp", "fsdp")),
        P(("dp", "fsdp")),
        P(("dp", "fsdp")),
        P("dp"),
    )
    return jax.shard_map(
        body,
        mesh=mesh,
        in_specs=placed,
        out_specs=(
            P(("dp", "fsdp"), None, None),
            P(("dp", "fsdp"), None, None),
            P(("dp", "fsdp"), None, None),
            P(("dp", "fsdp")),
            P(("dp", "fsdp")),
            P(("dp", "fsdp")),
            P(("dp", "fsdp")),
            P(("dp", "fsdp")),
            P("dp"),
        ),
        check_vma=False,
    )
```

```python
import functools
import math

import jax
import jax.numpy as jnp
from jax import lax
from jax.experimental import pallas as pl
from jax.experimental.pallas import tpu as pltpu
from jax.sharding import PartitionSpec as P

HEADS = 16
FF = 4608
CAPTION = 77


epsilon = 1e-05
masked_value = -1e30


def norm_rows(value, gain, shift):
    center = value - jnp.mean(value, -1, keepdims=True)
    spread = jnp.mean(center * center, -1, keepdims=True)
    return center * lax.rsqrt(spread + epsilon) * gain + shift


def gelu_exact(value):
    return jax.nn.gelu(value, approximate=False)


def key_valid(caption_len, length, caption):
    place = lax.broadcasted_iota(jnp.int32, (caption_len.shape[0], length), 1)
    return (place < 1 + caption_len[:, None]) | (place >= 1 + caption)


def product(left, right):
    return jnp.dot(left, right, preferred_element_type=jnp.float32)


def left_product(left, right):
    return lax.dot_general(
        left, right, (((0,), (0,)), ((), ())), preferred_element_type=jnp.float32
    )


def right_product(left, right):
    return lax.dot_general(
        left, right, (((1,), (1,)), ((), ())), preferred_element_type=jnp.float32
    )


def unpack(flat, width, hidden):
    return (
        flat[0].reshape(2 * width, width),
        flat[1].reshape(width, 3 * width),
        flat[2].reshape(width, width),
        flat[3].reshape(width, hidden),
        flat[4].reshape(hidden, width),
    )


def attention_scores(query, keys, valid, scale):
    raw = jnp.einsum("ishd,ithd->ihst", query, keys, preferred_element_type=jnp.float32) * scale
    return jnp.where(valid[:, None, None, :], raw, masked_value)


def column_sum(value):
    return jnp.sum(value.astype(jnp.float32), 0)


def flat_piece(left, right):
    grad_rows = left_product(left, right).reshape(-1)
    return grad_rows


MESH = pl.DeviceIdType.MESH
BF=jnp.bfloat16; F32=jnp.float32
SPLIT = 384


def unit_lanes(value, units, chips):
    seg = value.shape[1] // (units * chips)
    return [
        jnp.concatenate([value[:, (s * units + u) * seg : (s * units + u + 1) * seg] for s in range(chips)], 1)
        for u in range(units)
    ]


def row_loop(total, step, fn):
    def one(n, carry):
        fn(pl.ds(pl.multiple_of(n * step, step), step))
        return carry
    lax.fori_loop(0, total // step, one, 0)


def natural_lanes(units, chips):
    seg = units[0].shape[1] // chips
    return jnp.concatenate([u[:, s * seg : (s + 1) * seg] for s in range(chips) for u in units], 1)


def block_kernel(Z, wide, rows, tiles, length, padded,
                 cap_ref, skip_ref, qkv_ref, proj_ref, fc1_ref, fc2_ref, vec_ref, in_ref, sk_ref, og_ref,
                 out_o, in_o, sk_o, skip_g, qkv_g, proj_g, fc1_g, fc2_g, vec_o, skip_o, qp_o, fc1_o, fc2_o, j_o, h0_o,
                 skip_f, qkv_f, proj_f, fc1_f, fc2_f, own, keep, give, take, vbuf, vecs, b1s, vpart, vgot, vall, tok,
                 dtg, side, hid, am, t, m, zz, gu, gm, acc, tmp, sums, gacc, wbuf,
                 xl, xr, part, ra1, ra2, ra3, raf, rc1, rc2, rcf, rc3, rb1, rbf, rb2, rb3,
                 send, recv, lsem, psend, precv, vsend, vrecv, isem, osem, wsem,
                 rsend, rrecv, xsend, xrecv, qsend, qrecv, ysend, yrecv, ssend, srecv, free):
    dp = lax.axis_index("dp"); f = lax.axis_index("fsdp")
    z = dp // 2; x = dp % 2; y = f // 2; c = f % 2
    o = 1 - c
    nt = wide // 128
    half = rows // 2
    chips = 4 * Z
    ndp = 2 * Z
    hd = wide // HEADS
    full = length // 16 * 16
    ta, tb, tc = tiles
    A = pl.ds(0, ta); B = pl.ds(ta, tb); C = pl.ds(ta + tb, tc)
    zt = [z + 1 - 2 * (z % 2), lax.rem(z + 2, 4), 3 - z]
    zd = [(i * 2 + x, f) for i in zt]
    middle = (z == 1) | (z == 2)
    ends = (z == 0) | (z == 3)
    xp = (z * 2 + 1 - x, f)
    yp = (dp, (1 - y) * 2 + c)
    pp = (dp, y * 2 + o)
    dps = [(lax.rem(dp + k, ndp), f) for k in range(1, ndp)]
    fs = [(dp, lax.rem(f + k, 4)) for k in range(1, 4)]
    bar = pltpu.get_barrier_semaphore()
    for d in dps + fs:
        pl.semaphore_signal(bar, inc=1, device_id=d, device_id_type=MESH)
    flats = [(skip_ref, skip_f), (qkv_ref, qkv_f), (proj_ref, proj_f), (fc1_ref, fc1_f), (fc2_ref, fc2_f)]
    floads = [pltpu.make_async_copy(a, b, isem.at[n]) for n, (a, b) in enumerate(flats)]
    for cp in floads: cp.start()
    loads = [pltpu.make_async_copy(in_ref.at[:, 0, :], tok.at[0], isem.at[5]), pltpu.make_async_copy(sk_ref.at[:, 0, :], tok.at[1], isem.at[6])]
    for cp in loads: cp.start()
    def remote(src, dst, ssem, rsem, dev):
        return pltpu.make_async_remote_copy(src, dst, ssem, rsem, device_id=dev, device_id_type=MESH)
    @pl.when(ends)
    def _():
        for buf in (ra3, rc2, rb1):
            for b in range(buf.shape[0]): buf[b, 2] = jnp.zeros(buf.shape[2:], BF)
    floads[0].wait()
    for j in range(nt):
        own[0, :, 128 * j:128 * j + 128] = skip_f[pl.ds(j, rows, stride=nt), :].astype(BF)
    pl.semaphore_wait(bar, len(dps) + len(fs))

    waits = []
    def rc(i, slot, src, dst, dev):
        cp = remote(src, dst, send.at[i, slot], recv.at[i, slot], dev)
        cp.start(); waits.append(cp)
    def got(i, slot, dst):
        remote(dst, dst, send.at[i, slot], recv.at[i, slot], pp).wait_recv()
    def unit(i, cc):
        if i == 0: return skip_o.at[:, :, :, cc]
        if i in (1, 2): return qp_o.at[2 * (i - 1) + cc]
        if i in (3, 4): return fc1_o.at[2 * cc + (i - 3)]
        return fc2_o.at[2 * cc + (i - 5)]
    pc = {}
    lc = {}
    def exchange(i, first, second):
        keep[i - 1, 0:half, :] = jnp.where(c == 0, first, second)
        give[i - 1, 0:half, :] = jnp.where(c == 0, second, first)
        pc[i] = remote(give.at[i - 1], take.at[i - 1], psend.at[i - 1], precv.at[i - 1], pp)
        pc[i].start()
    whens = []
    def cond(cp):
        whens.append(cp)
        pl.when(middle)(lambda: cp.start())
    def zsend(i, base, view):
        for k in (1, 2, 3):
            v = view(z)
            cp = remote(v, v, send.at[i, base + k - 1], recv.at[i, base + k - 1], zd[k - 1])
            if k == 3: cond(cp)
            else: cp.start(); waits.append(cp)
    def zforward(i, base, view):
        got(i, base + 1, view(zt[1]))
        v = view(zt[1])
        cond(remote(v, v, send.at[i, base + 3], recv.at[i, base + 2], zd[0]))
    def zgot(i, base, view):
        got(i, base, view(zt[0])); got(i, base + 2, view(zt[2]))
    lc = {}
    def ready(i):
        if i in (1, 2, 3, 4):
            pc[i].wait_recv()
            p = keep[i - 1, 0:half, :]
            q = take[i - 1, 0:half, :]
            lo = jnp.where(c == 0, p, q); hi = jnp.where(c == 0, q, p)
            own[i, :, :] = jnp.concatenate([lo, hi], 0).astype(BF)
        lc[i] = pltpu.make_async_copy(own.at[i], unit(i, c).at[z, x, y], lsem.at[i]); lc[i].start()
    SA, SC, SB = 0, 4, 8
    def gA1(i):
        U = unit(i, c); lc[i].wait()
        zsend(i, SA, lambda t: U.at[t, x, y, :, A])
    def gC1(i):
        rc(i, 12, own.at[i, :, C], unit(i, c).at[z, x, y, :, C], yp)
    def gB1(i):
        rc(i, 13, own.at[i, :, B], unit(i, c).at[z, x, y, :, B], xp)
    def gAF(i):
        U = unit(i, c); zforward(i, SA, lambda t: U.at[t, x, y, :, A])
    def gA2(i):
        U = unit(i, c)
        zgot(i, SA, lambda t: U.at[t, x, y, :, A])
        L = U.at[:, x, y, :, A]
        rc(i, 14, L, L, yp); rc(i, 15, L, L, xp); rc(i, 16, L, L, pp)
    def gA3(i):
        L = unit(i, c).at[:, 1 - x, y, :, A]
        got(i, 15, L); rc(i, 17, L, L, yp); rc(i, 18, L, L, pp)
    def gC2(i):
        U = unit(i, c)
        got(i, 12, U.at[z, x, 1 - y, :, C])
        zsend(i, SC, lambda t: U.at[t, x, :, :, C])
    def gCF(i):
        U = unit(i, c); zforward(i, SC, lambda t: U.at[t, x, :, :, C])
    def gC3(i):
        U = unit(i, c)
        zgot(i, SC, lambda t: U.at[t, x, :, :, C])
        L = U.at[:, x, :, :, C]
        rc(i, 19, L, L, xp); rc(i, 20, L, L, pp)
    def gB2(i):
        U = unit(i, c)
        got(i, 13, U.at[z, 1 - x, y, :, B])
        L = U.at[z, :, y, :, B]
        rc(i, 21, L, L, yp)
    def gB3(i):
        U = unit(i, c)
        got(i, 21, U.at[z, :, 1 - y, :, B])
        zsend(i, SB, lambda t: U.at[t, :, :, :, B])
    def gBF(i):
        U = unit(i, c); zforward(i, SB, lambda t: U.at[t, :, :, :, B])
    def gPA(i):
        U = unit(i, c)
        L = U.at[:, x, 1 - y, :, A]
        got(i, 14, L); rc(i, 22, L, L, pp)
        L = U.at[:, 1 - x, 1 - y, :, A]
        got(i, 17, L); rc(i, 23, L, L, pp)
    def gPC(i):
        L = unit(i, c).at[:, 1 - x, :, :, C]
        got(i, 19, L); rc(i, 24, L, L, pp)
    def gPB(i):
        U = unit(i, c)
        zgot(i, SB, lambda t: U.at[t, :, :, :, B])
        L = U.at[:, :, :, :, B]
        rc(i, 25, L, L, pp)
    def arrived(i):
        U = unit(i, 1 - c)
        got(i, 16, U.at[:, x, y, :, A])
        got(i, 18, U.at[:, 1 - x, y, :, A])
        got(i, 22, U.at[:, x, 1 - y, :, A])
        got(i, 23, U.at[:, 1 - x, 1 - y, :, A])
        got(i, 20, U.at[:, x, :, :, C])
        got(i, 24, U.at[:, 1 - x, :, :, C])
        got(i, 25, U.at[:, :, :, :, B])
    def read(ref, first, stride):
        return jnp.concatenate([ref[pl.ds(first + j, half, stride=stride), :] for j in range(nt)], 1)

    ready(0)
    gB1(0); gC1(0)
    gA1(0)
    vcopies = []
    vbuf[dp] = vec_ref[...]
    for k, d in enumerate(dps):
        cp = remote(vec_ref, vbuf.at[dp], vsend.at[k], vrecv.at[k], d)
        cp.start(); vcopies.append(cp)
    floads[1].wait(); floads[2].wait()
    exchange(1, read(qkv_f, 0, 3 * nt), read(qkv_f, nt, 3 * nt))
    exchange(2, read(qkv_f, 2 * nt, 3 * nt), read(proj_f, 0, nt))
    def prepare_late():
        floads[3].wait(); floads[4].wait()
        for j in range(nt):
            own[5, :, 128 * j:128 * j + 128] = fc2_f[pl.ds(j, rows, stride=nt), :].astype(BF)
            own[6, :, 128 * j:128 * j + 128] = fc2_f[pl.ds(j + nt * rows, rows, stride=nt), :].astype(BF)
        nat = jnp.concatenate([read(fc1_f, nt * v, 4 * nt) for v in range(4)], 1)
        u = unit_lanes(nat, 4, chips)
        exchange(3, u[0], u[2])
        exchange(4, u[1], u[3])

    def keep_out(n, src, dst):
        cp = pltpu.make_async_copy(src, dst, osem.at[n]); cp.start()
        return cp
    def weight(n, ref):
        pltpu.make_async_copy(ref, wbuf.at[n], wsem.at[n]).start()
    def weight_wait(k):
        pltpu.make_async_copy(wbuf.at[k], wbuf.at[k], wsem.at[k]).wait()
    def both_skip():
        for k in range(2):
            for i in range(Z // 2):
                pltpu.make_async_copy(skip_o.at[k * (Z // 2) + i], wbuf.at[k, pl.ds(2 * i, 2)], wsem.at[k]).start()
    def cols(k, l):
        return wbuf[k, :, :, :, :, l].reshape(wide, SPLIT)
    def lanes_loop(fn):
        def one(n, carry):
            fn(pl.ds(pl.multiple_of(n * SPLIT, 128), SPLIT))
            return carry
        lax.fori_loop(0, wide // SPLIT, one, 0)
    def vector(n):
        return vecs[0:1, n * wide:(n + 1) * wide]
    def put_rows(k, src):
        def one(r): tok[k, r, :] = src[r, :]
        row_loop(full, 16, one)
        if length > full: tok[k, full:length, :] = src[full:length, :]
    def norm(src, gain, shift, dst):
        def one(r):
            v = src[r, :]
            cen = v - jnp.mean(v, -1, keepdims=True)
            s = jnp.mean(cen * cen, -1, keepdims=True)
            dst[r, :] = (cen * lax.rsqrt(s + epsilon) * gain + shift).astype(BF)
        row_loop(padded, 16, one)
    def take_rows(k, dst, at):
        if padded > full: dst[at + (slice(padded - 16, padded), slice(None))] = jnp.zeros((16, wide), dst.dtype)
        def one(r): dst[at + (r, slice(None))] = tok[k, r, :].astype(dst.dtype)
        row_loop(full, 16, one)
        if length > full: dst[at + (slice(full, length), slice(None))] = tok[k, full:length, :].astype(dst.dtype)
    def inputs():
        for cp in loads: cp.wait()
        take_rows(0, dtg, (0,))
        take_rows(1, dtg, (1,))
        pltpu.make_async_copy(og_ref.at[:, 0, :], tok.at[0], isem.at[5]).start()
        def two(r):
            u = unit_lanes(jnp.concatenate([dtg[0, r, :], dtg[1, r, :]], 1), 2, chips)
            side[0, r, :] = u[0]
            side[1, r, :] = u[1]
        row_loop(padded, 16, two)
        keep_out(0, side, j_o)
    def vectors():
        for k in range(len(dps)):
            remote(vec_ref, vbuf.at[lax.rem(dp - (k + 1) + ndp, ndp)], vsend.at[k], vrecv.at[k], pp).wait_recv()
        vecs[...] = jnp.concatenate([vbuf[k] for k in range(ndp)], 1)
        b = unit_lanes(vecs[0:1, 7 * wide:11 * wide], 4, chips)
        for u in range(4): b1s[u] = b[u]
        pltpu.make_async_copy(og_ref.at[:, 0, :], tok.at[0], isem.at[5]).wait()
        take_rows(0, gm, ())
        pltpu.make_async_copy(og_ref.at[:, 0, :], tok.at[1], isem.at[6]).start()
    def first_part():
        arrived(0)
        both_skip()
        weight_wait(0); weight_wait(1)
        def one(l):
            v = jnp.dot(dtg[0], cols(0, l), preferred_element_type=F32)
            v = v + jnp.dot(dtg[1], cols(1, l), preferred_element_type=F32)
            hid[:, l] = v + vecs[0:1, pl.ds(4 * wide + l.start, SPLIT)]
        lanes_loop(one)
        norm(hid, vector(0), vector(1), am.at[0])
        keep_out(1, hid, h0_o)
    def project(n, u):
        def one(l):
            t[u, :, l] = jnp.dot(am[0], cols(n, l), preferred_element_type=F32).astype(BF)
        lanes_loop(one)
    def query_keys():
        arrived(1)
        for u in range(2): weight(u, qp_o.at[u])
        for u in range(2):
            weight_wait(u)
            project(u, u)
    def values():
        arrived(2)
        weight(0, qp_o.at[2]); weight(1, qp_o.at[3])
        weight_wait(0)
        project(0, 2)
    def window(h):
        base = pl.multiple_of(jnp.minimum((h * hd) // 128, nt - 2) * 128, 128)
        lane = lax.broadcasted_iota(jnp.int32, (1, 256), 1) + (base - h * hd)
        return pl.ds(base, 256), (lane >= 0) & (lane < hd)
    def attend(first, last):
        cap = cap_ref[0]
        key = lax.broadcasted_iota(jnp.int32, (1, padded), 1)
        live = ((key < 1 + cap) | (key >= 1 + CAPTION)) & (key < length)
        def head(h, carry):
            win, inside = window(h)
            q = jnp.where(inside, t[0, :, win].astype(F32), 0.0).astype(BF)
            s = lax.dot_general(q, t[1, :, win], (((1,), (1,)), ((), ())), preferred_element_type=F32) * hd ** (-0.5)
            s = jnp.where(live, s, masked_value)
            e = jnp.exp(s - jnp.max(s, -1, keepdims=True))
            p = (e / jnp.sum(e, -1, keepdims=True)).astype(BF)
            v = jnp.dot(p, t[2, :, win], preferred_element_type=F32)
            am[1, :, win] = jnp.where(inside, v, am[1, :, win].astype(F32)).astype(BF)
            return carry
        lax.fori_loop(first, last, head, 0)
    def second_part():
        weight_wait(1)
        pltpu.make_async_copy(hid, h0_o, osem.at[1]).wait()
        def one(l):
            v = jnp.dot(am[1], cols(1, l), preferred_element_type=F32)
            h = hid[:, l] + (v + vecs[0:1, pl.ds(5 * wide + l.start, SPLIT)])
            hid[:, l] = h
            acc[:, l] = h + vecs[0:1, pl.ds(6 * wide + l.start, SPLIT)]
        lanes_loop(one)
        norm(hid, vector(2), vector(3), m)
    def widen_load(i):
        arrived(i)
        for k in range(2): weight(k, fc1_o.at[2 * k + i - 3])
    def widen(k, u):
        weight_wait(k)
        def one(l):
            tmp[:, l] = jnp.dot(m[...], cols(k, l), preferred_element_type=F32)
        lanes_loop(one)
        def two(r):
            v = tmp[r, :] + b1s[u]
            cdf = 0.5 * (1.0 + lax.erf(v * 0.7071067811865476))
            pdf = jnp.exp(-0.5 * v * v) * 0.3989422804014327
            zz[u, r, :] = (v * cdf).astype(BF)
            gu[u, r, :] = (cdf + v * pdf).astype(BF)
        row_loop(padded, 16, two)
    def narrow_load(i):
        arrived(i)
        for k in range(2): weight(k, fc2_o.at[2 * k + i - 5])
    def narrow(k, u):
        weight_wait(k)
        tmp[...] = jnp.zeros_like(tmp)
        def one(l):
            w = cols(k, l)
            acc[:, l] += jnp.dot(zz[u], w, preferred_element_type=F32)
            tmp[...] += lax.dot_general(gm[:, l], w, (((1,), (1,)), ((), ())), preferred_element_type=F32)
        lanes_loop(one)
        def two(r):
            gu[u, r, :] = (tmp[r, :] * gu[u, r, :].astype(F32)).astype(BF)
        row_loop(padded, 16, two)

    xcopies = {}
    def swap(n, src, dst):
        xcopies[n] = remote(src, dst, xsend.at[n], xrecv.at[n], pp)
        xcopies[n].start()
    nb = 4
    started = {j: [] for j in range(7)}
    def sc(j, slot, src, dst, dev):
        cp = remote(src, dst, rsend.at[j, slot], rrecv.at[j, slot], dev)
        cp.start(); started[j].append((None, cp))
    def settle(j):
        for which, cp in started[j]:
            if which is None: cp.wait_send()
            else: pl.when(which)(lambda: cp.wait_send())
    def came(j, slot, dst):
        remote(dst, dst, rsend.at[j, slot], rrecv.at[j, slot], pp).wait_recv()
    need = [(0, 1), (2,), (3, 4), (5,), (6, 7), (8, 9), (10, 11)]
    def operands(j):
        if j < 2: return zz.at[2 * c + j], gm, xl.at[j], xr.at[0]
        if j < 4: return m, gu.at[2 * c + j - 2], xl.at[2], xr.at[j - 1]
        if j == 4: return am.at[c], dtg.at[2 + c], xl.at[0], xr.at[0]
        if j == 5: return am.at[0], dtg.at[c], xl.at[1], xr.at[1]
        return side.at[0], side.at[1], xl.at[2], xr.at[2]
    def reduce1(j):
        for n in need[j]: xcopies[n].wait_recv()
        if j >= nb:
            settle(j - nb)
        b = j % nb
        D = part.at[b]
        l1, r1, l2, r2 = operands(j)
        step = SPLIT
        dims = (((0,), (0,)), ((), ()))
        def chunk(n, carry):
            at = pl.ds(pl.multiple_of(n * step, 128), step)
            r = lax.dot_general(l1[...], r1[:, at], dims, preferred_element_type=F32)
            r = r + lax.dot_general(l2[...], r2[:, at], dims, preferred_element_type=F32)
            D[:, :, :, :, at] = r.reshape(Z, 2, 2, rows, step).astype(BF)
            return carry
        lax.fori_loop(0, wide // step, chunk, 0)
        sc(j, 0, D.at[:, 1 - x, 1 - y, :, A], ra1.at[b, 0], yp)
        sc(j, 2, D.at[:, 1 - x, :, :, C], rc1.at[b], xp)
        sc(j, 1, D.at[:, x, 1 - y, :, A], ra1.at[b, 1], yp)
        line_send(j, 12, lambda i: D.at[i, :, :, :, B], rb1.at[b], rbf.at[b])
    def only(j, which, slot, src, dst, dev):
        cp = remote(src, dst, rsend.at[j, slot], rrecv.at[j, slot], dev)
        pl.when(which)(lambda: cp.start())
        return cp
    def line_send(j, base, view, buf, fbuf):
        sc(j, base, view(zt[0]), buf.at[0], zd[0])
        started[j].append((ends, only(j, ends, base + 3, view(zt[2]), fbuf, zd[0])))
        started[j].append((None, only(j, ends, base + 1, view(zt[1]), buf.at[1], zd[1])))
        started[j].append((middle, only(j, middle, base + 2, view(zt[2]), buf.at[2], zd[2])))
    def line_relay(j, base, view, buf, fbuf):
        cp = remote(view(zt[1]), buf.at[1], rsend.at[j, base + 1], rrecv.at[j, base + 1], zd[1])
        @pl.when(middle)
        def _():
            came(j, base + 3, fbuf)
            plus(view(zt[1]), fbuf)
            cp.start()
    def line_came(j, base, buf):
        came(j, base, buf.at[0]); came(j, base + 1, buf.at[1])
        pl.when(middle)(lambda: came(j, base + 2, buf.at[2]))
    def plus(dst, *srcs):
        lead = dst.shape[:-2]
        for n in range(math.prod(lead)):
            at = ()
            for d in reversed(lead):
                at = (n % d,) + at
                n = n // d
            v = dst[at + (slice(None), slice(None))].astype(F32)
            for r in srcs: v = v + r[at + (slice(None), slice(None))].astype(F32)
            dst[at + (slice(None), slice(None))] = v.astype(BF)
    def reduce2(j):
        b = j % nb
        D = part.at[b]
        came(j, 0, ra1.at[b, 0])
        plus(D.at[:, 1 - x, y, :, A], ra1.at[b, 0])
        sc(j, 3, D.at[:, 1 - x, y, :, A], ra2.at[b], xp)
        came(j, 2, rc1.at[b])
        plus(D.at[:, x, :, :, C], rc1.at[b])
        line_send(j, 8, lambda i: D.at[i, x, :, :, C], rc2.at[b], rcf.at[b])
        line_relay(j, 12, lambda i: D.at[i, :, :, :, B], rb1.at[b], rbf.at[b])
    def reduce3(j):
        b = j % nb
        D = part.at[b]
        line_came(j, 12, rb1.at[b])
        plus(D.at[z, :, :, :, B], rb1.at[b, 0], rb1.at[b, 1], rb1.at[b, 2])
        sc(j, 17, D.at[z, :, 1 - y, :, B], rb2.at[b], yp)
        came(j, 1, ra1.at[b, 1])
        came(j, 3, ra2.at[b])
        plus(D.at[:, x, y, :, A], ra1.at[b, 1], ra2.at[b])
        line_send(j, 4, lambda i: D.at[i, x, y, :, A], ra3.at[b], raf.at[b])
        line_relay(j, 8, lambda i: D.at[i, x, :, :, C], rc2.at[b], rcf.at[b])
    def reduce4(j):
        b = j % nb
        D = part.at[b]
        line_relay(j, 4, lambda i: D.at[i, x, y, :, A], ra3.at[b], raf.at[b])
        line_came(j, 8, rc2.at[b])
        plus(D.at[z, x, :, :, C], rc2.at[b, 0], rc2.at[b, 1], rc2.at[b, 2])
        sc(j, 16, D.at[z, x, 1 - y, :, C], rc3.at[b], yp)
        came(j, 17, rb2.at[b])
        plus(D.at[z, :, y, :, B], rb2.at[b])
        sc(j, 18, D.at[z, 1 - x, y, :, B], rb3.at[b], xp)
    pcopies = {}
    def lay(ref, val, first, stride, n):
        for i in range(val.shape[1] // 128):
            ref[pl.ds(first + i, n, stride=stride), :] = val[:, 128 * i:128 * i + 128]
    def reduce5(j):
        b = j % nb
        D = part.at[b]
        line_came(j, 4, ra3.at[b])
        came(j, 16, rc3.at[b])
        came(j, 18, rb3.at[b])
        p = D[z, x, y, :, A].astype(F32)
        for k in range(3):
            p = p + ra3[b, k].astype(F32)
        q = D[z, x, y, :, B].astype(F32) + rb3[b].astype(F32)
        r = D[z, x, y, :, C].astype(F32) + rc3[b].astype(F32)
        v = jnp.concatenate([p, q, r], 1)
        if j in (0, 1):
            lay(fc2_f, v, j * rows * nt, nt, rows)
            if j == 1: keep_out(9, fc2_f, fc2_g)
        elif j == 6:
            lay(skip_f, v, 0, nt, rows)
            keep_out(5, skip_f, skip_g)
        else:
            lo = v[0:half]; hi = v[half:rows]
            keep[j - 2, 0:half, :] = jnp.where(c == 0, lo, hi)
            give[j - 2, 0:half, :] = jnp.where(c == 0, hi, lo)
            cp = remote(give.at[j - 2], take.at[j - 2], qsend.at[j - 2], qrecv.at[j - 2], pp)
            cp.start(); pcopies[j] = cp
    def both(j):
        pcopies[j].wait_recv()
        p = keep[j - 2, 0:half, :]; q = take[j - 2, 0:half, :]
        return jnp.where(c == 0, p, q), jnp.where(c == 0, q, p)
    def settle_pair(j):
        if j == 3:
            p, q = both(2), both(3)
            lay(fc1_f, natural_lanes([p[0], q[0], p[1], q[1]], chips), 0, 4 * nt, half)
            keep_out(8, fc1_f, fc1_g)
        elif j == 5:
            first, second = both(5)
            lay(qkv_f, first, 0, 3 * nt, half)
            lay(qkv_f, second, nt, 3 * nt, half)
            keep_out(6, qkv_f, qkv_g)
        elif j == 4:
            first, second = both(4)
            lay(qkv_f, first, 2 * nt, 3 * nt, half)
            lay(proj_f, second, 0, nt, half)
            keep_out(7, proj_f, proj_g)


    def zero(n): gacc[n] = jnp.zeros((8, wide), F32)
    def add_rows(n, v):
        gacc[n] += v[0:8] + v[8:16]
    def close(n):
        return jnp.sum(gacc[n], 0, keepdims=True)
    def column_sums(src):
        zero(0)
        def one(r): add_rows(0, src[r, :].astype(F32))
        row_loop(padded, 16, one)
        return close(0)
    def norm_back(dy, src, gain, fn):
        zero(0); zero(1); zero(2)
        def one(r):
            d = dy[r, :]
            v = src[r, :]
            cen = v - jnp.mean(v, -1, keepdims=True)
            rs = lax.rsqrt(jnp.mean(cen * cen, -1, keepdims=True) + epsilon)
            xh = cen * rs
            dx = d * gain
            g = rs * (dx - jnp.mean(dx, -1, keepdims=True) - xh * jnp.mean(dx * xh, -1, keepdims=True))
            add_rows(0, d * xh)
            add_rows(1, d)
            fn(r, g)
        row_loop(padded, 16, one)
    def turned(lhs, n, fresh):
        if fresh: tmp[...] = jnp.zeros_like(tmp)
        def one(l):
            tmp[...] += lax.dot_general(lhs[:, l], cols(n, l), (((1,), (1,)), ((), ())), preferred_element_type=F32)
        lanes_loop(one)
    def widen_back(us):
        for i, u in enumerate(us):
            weight_wait(i)
            turned(gu.at[u], i, u == 0)
            sums[7 + u] = column_sums(gu.at[u])
    def widen_back_load(us):
        for i, u in enumerate(us): weight(i, fc1_o.at[u])
    def norm_two():
        weight(0, qp_o.at[3])
        pltpu.make_async_copy(og_ref.at[:, 0, :], tok.at[1], isem.at[6]).wait()
        take_rows(1, acc, ())
        def fn(r, g):
            s = acc[r, :] + g
            acc[r, :] = s
            b = s.astype(BF)
            dtg[3, r, :] = b
            add_rows(2, b.astype(F32))
        norm_back(tmp, hid, vector(2), fn)
        sums[2] = close(0); sums[3] = close(1); sums[5] = close(2)
        pltpu.make_async_copy(h0_o, hid, isem.at[5]).start()
        sums[6] = column_sums(gm)
        weight_wait(0)
        turned(dtg.at[3], 0, True)
        def two(r): side[0, r, :] = tmp[r, :].astype(BF)
        row_loop(padded, 16, two)
    def attend_back(first, last):
        cap = cap_ref[0]
        key = lax.broadcasted_iota(jnp.int32, (padded, 1), 0)
        live = ((key < 1 + cap) | (key >= 1 + CAPTION)) & (key < length)
        def head(h, carry):
            win, inside = window(h)
            q = jnp.where(inside, t[0, :, win].astype(F32), 0.0).astype(BF)
            k = t[1, :, win]
            g = jnp.where(inside, side[0, :, win].astype(F32), 0.0).astype(BF)
            s = lax.dot_general(k, q, (((1,), (1,)), ((), ())), preferred_element_type=F32) * hd ** (-0.5)
            s = jnp.where(live, s, masked_value)
            e = jnp.exp(s - jnp.max(s, 0, keepdims=True))
            p = e * (1.0 / jnp.sum(e, 0, keepdims=True))
            d = lax.dot_general(t[2, :, win], g, (((1,), (1,)), ((), ())), preferred_element_type=F32)
            ds = (p * (d - jnp.sum(p * d, 0, keepdims=True))).astype(BF)
            dq = lax.dot_general(ds, k, (((0,), (0,)), ((), ())), preferred_element_type=F32) * hd ** (-0.5)
            dk = jnp.dot(ds, q, preferred_element_type=F32) * hd ** (-0.5)
            dv = jnp.dot(p.astype(BF), g, preferred_element_type=F32)
            for i, v in enumerate((dq, dk, dv)):
                dtg[i, :, win] = jnp.where(inside, v, dtg[i, :, win].astype(F32)).astype(BF)
            return carry
        lax.fori_loop(first, last, head, 0)
    def late_left():
        pl.semaphore_signal(free, inc=1, device_id=pp, device_id_type=MESH)
        pl.semaphore_wait(free, 1)
        pltpu.make_async_copy(side, j_o, osem.at[0]).wait()
        swap(6, am.at[o], xl.at[0])
        swap(8, am.at[0], xl.at[1])
        swap(10, j_o.at[o], xl.at[2])
    def late_right():
        swap(7, dtg.at[2 + o], xr.at[0])
        swap(9, dtg.at[o], xr.at[1])
        pltpu.make_async_copy(j_o.at[c], side.at[0], isem.at[7]).start()
        weight(0, qp_o.at[0]); weight(1, qp_o.at[1])
    def project_back():
        for i in range(3):
            weight_wait(i % 2)
            turned(dtg.at[i], i % 2, i == 0)
            if i == 0: weight(0, qp_o.at[2])
    def norm_one():
        pltpu.make_async_copy(h0_o, hid, isem.at[5]).wait()
        both_skip()
        def fn(r, g):
            b = (acc[r, :] + g).astype(BF)
            side[1, r, :] = b
            add_rows(2, b.astype(F32))
        norm_back(tmp, hid, vector(0), fn)
        sums[0] = close(0); sums[1] = close(1); sums[4] = close(2)
        swap(11, side.at[1], xr.at[2])
    def join_back(i, dst):
        weight_wait(i)
        turned(side.at[1], i, True)
        put_rows(i, tmp)
        keep_out(3 + i, tok.at[i], dst.at[:, 0, :])
    nv = vpart.shape[2]
    def vec_send():
        total = jnp.concatenate([sums[i] for i in range(7)] + [natural_lanes([sums[7 + u] for u in range(4)], chips)], 1)
        for k in range(ndp): vpart[k] = total[:, k * nv:(k + 1) * nv]
        for k, d in enumerate(dps):
            cp = remote(vpart.at[d[0]], vgot.at[k], ysend.at[k], yrecv.at[k], d)
            cp.start(); vcopies.append(cp)
    def vec_first():
        s = vpart[dp]
        for k in range(len(dps)):
            remote(vgot.at[k], vgot.at[k], ysend.at[k], yrecv.at[k], pp).wait_recv()
            s = s + vgot[k]
        vall[f] = s
        for k, d in enumerate(fs):
            cp = remote(vall.at[f], vall.at[f], ssend.at[k], srecv.at[k], d)
            cp.start(); vcopies.append(cp)
    def vec_last():
        for k in range(3):
            src = lax.rem(f - (k + 1) + 4, 4)
            remote(vall.at[src], vall.at[src], ssend.at[k], srecv.at[k], pp).wait_recv()
        vec_o[...] = vall[0] + vall[1] + vall[2] + vall[3]

    ready(1); gB1(1); gB2(0)
    gC2(0); gAF(0); gA2(0)
    ready(2); gB1(2)
    gC1(1); gA1(1); gB2(1)
    gB3(0)
    prepare_late()
    gCF(0); gC3(0); gA3(0)
    inputs()
    gC2(1); gAF(1); gA2(1)
    ready(3); gB1(3)
    gC1(2); gA1(2); gB2(2)
    gB3(1)
    vectors()
    gCF(1); gC3(1); gA3(1)
    gBF(0); gPA(0); gPC(0)
    gC2(2); gAF(2); gA2(2)
    ready(4); gB1(4)
    gC1(3); gA1(3); gB2(3)
    gB3(2)
    gCF(2); gC3(2); gA3(2)
    gBF(1); gPA(1); gPC(1)
    gPB(0)
    first_part()
    gC2(3); gAF(3); gA2(3)
    ready(5); gB1(5)
    gC1(4); gA1(4); gB2(4)
    gB3(3)
    gCF(3); gC3(3); gA3(3)
    gBF(2); gPA(2); gPC(2)
    gPB(1)
    query_keys()
    gC2(4); gAF(4); gA2(4)
    ready(6); gB1(6)
    gC1(5); gA1(5); gB2(5)
    gB3(4)
    gCF(4); gC3(4); gA3(4)
    gBF(3); gPA(3); gPC(3)
    gPB(2)
    values()
    attend(0, 5)
    gC2(5); gAF(5); gA2(5)
    gC1(6); gA1(6); gB2(6)
    gB3(5)
    attend(5, 11)
    gCF(5); gC3(5); gA3(5)
    gBF(4); gPA(4); gPC(4)
    gPB(3)
    attend(11, 16)
    second_part()
    gC2(6); gAF(6); gA2(6)
    gB3(6)
    widen_load(3)
    widen(0, 0)
    gCF(6); gC3(6); gA3(6)
    gBF(5); gPA(5); gPC(5)
    gPB(4)
    widen(1, 2)
    for cp in pc.values(): cp.wait_send()
    swap(0, zz.at[2 * o], xl.at[0])
    swap(1, gm, xr.at[0])
    swap(3, m, xl.at[2])
    widen_load(4)
    reduce1(0)
    gBF(6); gPA(6); gPC(6); gPB(5)
    widen(0, 1)
    widen(1, 3)
    swap(2, zz.at[2 * o + 1], xl.at[1])
    narrow_load(5)
    reduce1(1)
    gPB(6)
    reduce2(0)
    narrow(0, 0)
    narrow(1, 2)
    swap(4, gu.at[2 * o], xr.at[1])
    narrow_load(6)
    reduce1(2); reduce2(1)
    narrow(0, 1)
    narrow(1, 3)
    swap(5, gu.at[2 * o + 1], xr.at[2])
    widen_back_load((0, 1))
    reduce3(0)
    put_rows(0, acc)
    keep_out(2, tok.at[0], out_o.at[:, 0, :])
    reduce4(0)
    reduce1(3)
    widen_back((0, 1))
    widen_back_load((2, 3))
    reduce2(2); reduce3(1)
    widen_back((2, 3))
    late_left()
    norm_two()
    reduce5(0); reduce4(1)
    attend_back(0, 5)
    reduce2(3); reduce3(2)
    attend_back(5, 16)
    late_right()
    reduce1(4)
    reduce5(1); reduce4(2); reduce3(3)
    reduce1(5); reduce2(4)
    project_back()
    reduce5(2); reduce4(3)
    norm_one()
    vec_send()
    pltpu.make_async_copy(j_o.at[c], side.at[0], isem.at[7]).wait()
    reduce2(5); reduce3(4)
    reduce1(6)
    vec_first()
    pltpu.make_async_copy(tok.at[0], out_o.at[:, 0, :], osem.at[2]).wait()
    join_back(0, in_o)
    reduce5(3); reduce4(4)
    join_back(1, sk_o)
    settle_pair(3)
    reduce2(6); reduce3(5)
    vec_last()
    reduce5(4); reduce4(5); settle_pair(4)
    reduce3(6)
    reduce5(5); settle_pair(5)
    reduce4(6)
    reduce5(6)
    for k in (0, 1): pltpu.make_async_copy(tok.at[k], (in_o, sk_o)[k].at[:, 0, :], osem.at[3 + k]).wait()
    for n, (a, b) in zip((5, 6, 7, 8, 9), ((skip_f, skip_g), (qkv_f, qkv_g), (proj_f, proj_g), (fc1_f, fc1_g), (fc2_f, fc2_g))):
        pltpu.make_async_copy(a, b, osem.at[n]).wait()
    for j in range(3, 7): settle(j)
    for cp in whens: pl.when(middle)(lambda: cp.wait_send())
    for cp in waits: cp.wait_send()
    for cp in pcopies.values(): cp.wait_send()
    for cp in vcopies: cp.wait_send()
    for cp in xcopies.values(): cp.wait_send()


def block(cap, skip, qkv, proj, fc1, fc2, vectors, block_in, skip_in, out_grad, dpn):
    _, length, wide = block_in.shape
    Z = dpn // 2; rows = skip.shape[0] // wide
    padded = -(-length // 16) * 16
    nt = wide // 128
    tb = 128 * max(1, nt // 9); tc = 128 * (nt // 3); ta = wide - tb - tc
    tiles = (ta, tb, tc)
    U = (Z, 2, 2, rows, wide)
    hbm = pl.BlockSpec(memory_space=pl.ANY); vm = pl.BlockSpec(memory_space=pltpu.VMEM)
    ns = 26
    nr = 19
    nv = vectors.shape[0]
    D = pltpu.SemaphoreType.DMA
    V = pltpu.VMEM
    hp = -(-rows // 2 // 8) * 8
    S = jax.ShapeDtypeStruct
    act = (padded, wide)
    flat = [(w.shape[0] // 128, 128) for w in (skip, qkv, proj, fc1, fc2)]
    tokens = (length, 1, wide)
    nb = 4
    res = pl.pallas_call(
        functools.partial(block_kernel, Z, wide, rows, tiles, length, padded),
        out_shape=(S(tokens, F32),) * 3 + tuple(S(s, F32) for s in flat) + (S((1, nv), F32),
                   S((Z, 2, 2, 2, rows, wide), BF), S((4,) + U, BF), S((4,) + U, BF), S((4,) + U, BF), S((2,) + act, BF), S(act, F32)),
        in_specs=[pl.BlockSpec(memory_space=pltpu.SMEM)] + [hbm] * 5 + [vm] + [hbm] * 3,
        out_specs=(hbm,) * 8 + (vm,) + (hbm,) * 6,
        scratch_shapes=[V(s, F32) for s in flat] + [
                        V((7, rows, wide), BF), V((4, hp, wide), F32), V((4, hp, wide), F32), V((4, hp, wide), F32),
                        V((dpn, 1, nv), F32), V((1, nv * dpn), F32), V((4, 1, wide), F32), V((dpn, 1, nv), F32), V((dpn - 1, 1, nv), F32), V((4, 1, nv), F32),
                        V((2, length, wide), F32),
                        V((4,) + act, BF), V((2,) + act, BF), V(act, F32), V((2,) + act, BF), V((3,) + act, BF), V(act, BF), V((4,) + act, BF), V((4,) + act, BF), V(act, BF),
                        V(act, F32), V(act, F32), V((11, 1, wide), F32), V((3, 8, wide), F32), V((2,) + U, BF),
                        V((3,) + act, BF), V((3,) + act, BF), V((nb,) + U, BF),
                        V((nb, 2, Z, rows, ta), BF), V((nb, Z, rows, ta), BF), V((nb, 3, rows, ta), BF), V((nb, rows, ta), BF),
                        V((nb, Z, 2, rows, tc), BF), V((nb, 3, 2, rows, tc), BF), V((nb, 2, rows, tc), BF), V((nb, rows, tc), BF),
                        V((nb, 3, 2, 2, rows, tb), BF), V((nb, 2, 2, rows, tb), BF), V((nb, 2, rows, tb), BF), V((nb, rows, tb), BF),
                        D((7, ns)), D((7, ns)), D((7,)), D((4,)), D((4,)), D((dpn - 1,)), D((dpn - 1,)), D((8,)), D((10,)), D((2,)),
                        D((7, nr)), D((7, nr)), D((12,)), D((12,)), D((4,)), D((4,)), D((dpn - 1,)), D((dpn - 1,)), D((3,)), D((3,)), pltpu.SemaphoreType.REGULAR],
        compiler_params=pltpu.CompilerParams(collective_id=0, has_side_effects=True, vmem_limit_bytes=67043328),
        name="block",
    )(cap, *(w.reshape(-1, 128) for w in (skip, qkv, proj, fc1, fc2)), vectors.reshape(1, nv),
      *(v.reshape(tokens) for v in (block_in, skip_in, out_grad)))
    shape = block_in.shape
    res = hand_out(res[:8]) + (res[8],)
    return tuple(r.reshape(shape) for r in res[:3]) + tuple(r.reshape(-1) for r in res[3:])


def hand_out_kernel(*refs):
    n = (len(refs) - 2) // 3
    src, dst, buf, (first, second) = refs[:n], refs[n:2 * n], refs[2 * n:3 * n], refs[3 * n:]
    ins = [pltpu.make_async_copy(src[i], buf[i], first.at[i]) for i in range(n)]
    outs = [pltpu.make_async_copy(buf[i], dst[i], second.at[i]) for i in range(n)]
    for cp in ins: cp.start()
    for a, b in zip(ins, outs):
        a.wait()
        b.start()
    for cp in outs: cp.wait()


def hand_out(arrays):
    hbm = pl.BlockSpec(memory_space=pl.ANY)
    n = len(arrays)
    return tuple(pl.pallas_call(
        hand_out_kernel,
        out_shape=tuple(jax.ShapeDtypeStruct(v.shape, v.dtype) for v in arrays),
        in_specs=[hbm] * n, out_specs=(hbm,) * n,
        scratch_shapes=[pltpu.VMEM(v.shape, v.dtype) for v in arrays] + [pltpu.SemaphoreType.DMA((n,))] * 2,
        compiler_params=pltpu.CompilerParams(vmem_limit_bytes=67043328),
        name="hand_out",
    )(*arrays))


def whole_rows(width, dp, fsdp, items, heads, hidden):
    return (
        fsdp == 4 and dp == 8 and width % (dp * 16) == 0 and items == 1 and hidden == 4 * width
        and width % SPLIT == 0 and width // heads <= 128
    )


def body(block_in, skip_in, out_grad, caption_len, skip_w, qkv_w, proj_w, fc1_w, fc2_w, vectors):
    items, length, width = block_in.shape
    if whole_rows(width, lax.axis_size("dp"), lax.axis_size("fsdp"), items, HEADS, FF):
        return block(
            caption_len, skip_w, qkv_w, proj_w, fc1_w, fc2_w, vectors, block_in, skip_in, out_grad,
            lax.axis_size("dp"),
        )
    heads = HEADS
    head_dim = width // heads
    hidden = FF
    rows = items * length
    scale = head_dim ** (-0.5)
    gathered = (
        lax.all_gather(skip_w.astype(jnp.bfloat16), ("dp", "fsdp"), axis=0, tiled=True),
        lax.all_gather(qkv_w.astype(jnp.bfloat16), ("dp", "fsdp"), axis=0, tiled=True),
        lax.all_gather(proj_w.astype(jnp.bfloat16), ("dp", "fsdp"), axis=0, tiled=True),
        lax.all_gather(fc1_w.astype(jnp.bfloat16), ("dp", "fsdp"), axis=0, tiled=True),
        lax.all_gather(fc2_w.astype(jnp.bfloat16), ("dp", "fsdp"), axis=0, tiled=True),
    )
    skip_m, qkv_m, proj_m, fc1_m, fc2_m = unpack(gathered, width, hidden)
    vec = lax.all_gather(vectors, "dp", axis=0, tiled=True)
    gain_one = vec[0:width]
    shift_one = vec[width : 2 * width]
    gain_two = vec[2 * width : 3 * width]
    shift_two = vec[3 * width : 4 * width]
    skip_bias = vec[4 * width : 5 * width]
    proj_bias = vec[5 * width : 6 * width]
    fc2_bias = vec[6 * width : 7 * width]
    fc1_bias = vec[7 * width :]
    valid = key_valid(caption_len, length, CAPTION)
    joined = jnp.concatenate([block_in, skip_in], -1).reshape(rows, 2 * width).astype(jnp.bfloat16)
    first = product(joined, skip_m) + skip_bias
    normed_one = norm_rows(first, gain_one, shift_one).astype(jnp.bfloat16)
    triple = (
        product(normed_one, qkv_m).astype(jnp.bfloat16).reshape(items, length, 3, heads, head_dim)
    )
    query = triple[:, :, 0]
    keys = triple[:, :, 1]
    values = triple[:, :, 2]
    scores = attention_scores(query, keys, valid, scale)
    top = jnp.max(scores, -1, keepdims=True)
    expd = jnp.exp(scores - top)
    total = jnp.sum(expd, -1, keepdims=True)
    probs = expd / total
    log_total = top + jnp.log(total)
    mixed = (
        jnp.einsum(
            "ihst,ithd->ishd",
            probs.astype(jnp.bfloat16),
            values,
            preferred_element_type=jnp.float32,
        )
        .astype(jnp.bfloat16)
        .reshape(rows, width)
    )
    second = first + (product(mixed, proj_m) + proj_bias)
    normed_two = norm_rows(second, gain_two, shift_two).astype(jnp.bfloat16)
    inner = product(normed_two, fc1_m) + fc1_bias
    active = gelu_exact(inner).astype(jnp.bfloat16)
    block_out = second + (product(active, fc2_m) + fc2_bias)
    again = (
        lax.all_gather(skip_w.astype(jnp.bfloat16), ("dp", "fsdp"), axis=0, tiled=True),
        lax.all_gather(qkv_w.astype(jnp.bfloat16), ("dp", "fsdp"), axis=0, tiled=True),
        lax.all_gather(proj_w.astype(jnp.bfloat16), ("dp", "fsdp"), axis=0, tiled=True),
        lax.all_gather(fc1_w.astype(jnp.bfloat16), ("dp", "fsdp"), axis=0, tiled=True),
        lax.all_gather(fc2_w.astype(jnp.bfloat16), ("dp", "fsdp"), axis=0, tiled=True),
    )
    skip_m, qkv_m, proj_m, fc1_m, fc2_m = unpack(again, width, hidden)
    grad_out = out_grad.reshape(rows, width)
    grad_mlp = grad_out.astype(jnp.bfloat16)
    d_fc2_bias = column_sum(grad_mlp)
    d_active = right_product(grad_mlp, fc2_m)
    gelu_value, gelu_pull = jax.vjp(gelu_exact, inner)
    grad_inner = gelu_pull(d_active)[0].astype(jnp.bfloat16)
    d_fc1_bias = column_sum(grad_inner)
    d_normed_two = right_product(grad_inner, fc1_m)
    norm_value_two, norm_pull_two = jax.vjp(norm_rows, second, gain_two, shift_two)
    d_second_norm, d_gain_two, d_shift_two = norm_pull_two(d_normed_two)
    grad_second = grad_out + d_second_norm
    grad_attn = grad_second.astype(jnp.bfloat16)
    d_proj_bias = column_sum(grad_attn)
    grad_mixed = (
        right_product(grad_attn, proj_m)
        .astype(jnp.bfloat16)
        .reshape(items, length, heads, head_dim)
    )
    again_scores = attention_scores(query, keys, valid, scale)
    again_probs = jnp.exp(again_scores - log_total)
    d_probs = jnp.einsum("ishd,ithd->ihst", grad_mixed, values, preferred_element_type=jnp.float32)
    inner_sum = jnp.sum(again_probs * d_probs, -1, keepdims=True)
    grad_scores = (again_probs * (d_probs - inner_sum)).astype(jnp.bfloat16)
    d_query = (
        jnp.einsum("ihst,ithd->ishd", grad_scores, keys, preferred_element_type=jnp.float32) * scale
    )
    d_keys = (
        jnp.einsum("ihst,ishd->ithd", grad_scores, query, preferred_element_type=jnp.float32)
        * scale
    )
    d_values = jnp.einsum(
        "ihst,ishd->ithd",
        again_probs.astype(jnp.bfloat16),
        grad_mixed,
        preferred_element_type=jnp.float32,
    )
    grad_triple = (
        jnp.stack([d_query, d_keys, d_values], 2).astype(jnp.bfloat16).reshape(rows, 3 * width)
    )
    d_normed_one = right_product(grad_triple, qkv_m)
    norm_value_one, norm_pull_one = jax.vjp(norm_rows, first, gain_one, shift_one)
    d_first_norm, d_gain_one, d_shift_one = norm_pull_one(d_normed_one)
    grad_first = (grad_second + d_first_norm).astype(jnp.bfloat16)
    d_skip_bias = column_sum(grad_first)
    grad_joined = right_product(grad_first, skip_m).reshape(items, length, 2 * width)
    in_grad = grad_joined[:, :, 0:width]
    skip_grad = grad_joined[:, :, width:]
    owners = lax.axis_size(("dp", "fsdp"))
    pairs = (
        (joined, grad_first),
        (normed_one, grad_triple),
        (mixed, grad_attn),
        (normed_two, grad_inner),
        (active, grad_mlp),
    )
    shard_sizes = [pair[0].shape[1] * pair[1].shape[1] // owners for pair in pairs]
    blocks = []
    for pair, owner_share in zip(pairs, shard_sizes):
        blocks.append(
            flat_piece(pair[0], pair[1]).reshape(1 * lax.axis_size(("dp", "fsdp")), owner_share)
        )
    owned = lax.psum_scatter(
        jnp.concatenate(blocks, 1), ("dp", "fsdp"), scatter_dimension=0, tiled=True
    ).reshape(-1)
    pieces = []
    offset = 0
    for share in shard_sizes:
        pieces.append(owned[offset : offset + share])
        offset = offset + share
    vec_grad = jnp.concatenate(
        [
            d_gain_one,
            d_shift_one,
            d_gain_two,
            d_shift_two,
            d_skip_bias,
            d_proj_bias,
            d_fc2_bias,
            d_fc1_bias,
        ]
    )
    vec_rows = lax.psum_scatter(vec_grad, "dp", scatter_dimension=0, tiled=True)
    vec_total = lax.psum(vec_rows, "fsdp")
    return (
        block_out.reshape(items, length, width),
        in_grad,
        skip_grad,
        pieces[0],
        pieces[1],
        pieces[2],
        pieces[3],
        pieces[4],
        vec_total,
    )


def solution(mesh):
    placed = (
        P(("dp", "fsdp"), None, None),
        P(("dp", "fsdp"), None, None),
        P(("dp", "fsdp"), None, None),
        P(("dp", "fsdp")),
        P(("dp", "fsdp")),
        P(("dp", "fsdp")),
        P(("dp", "fsdp")),
        P(("dp", "fsdp")),
        P(("dp", "fsdp")),
        P("dp"),
    )
    return jax.shard_map(
        body,
        mesh=mesh,
        in_specs=placed,
        out_specs=(
            P(("dp", "fsdp"), None, None),
            P(("dp", "fsdp"), None, None),
            P(("dp", "fsdp"), None, None),
            P(("dp", "fsdp")),
            P(("dp", "fsdp")),
            P(("dp", "fsdp")),
            P(("dp", "fsdp")),
            P(("dp", "fsdp")),
            P("dp"),
        ),
        check_vma=False,
    )
```

```python
import functools
import math

import jax
import jax.numpy as jnp
from jax import lax
from jax.experimental import pallas as pl
from jax.experimental.pallas import tpu as pltpu
from jax.sharding import PartitionSpec as P

HEADS = 16
FF = 4608
CAPTION = 77


epsilon = 1e-05
masked_value = -1e30


def norm_rows(value, gain, shift):
    center = value - jnp.mean(value, -1, keepdims=True)
    spread = jnp.mean(center * center, -1, keepdims=True)
    return center * lax.rsqrt(spread + epsilon) * gain + shift


def gelu_exact(value):
    return jax.nn.gelu(value, approximate=False)


def key_valid(caption_len, length, caption):
    place = lax.broadcasted_iota(jnp.int32, (caption_len.shape[0], length), 1)
    return (place < 1 + caption_len[:, None]) | (place >= 1 + caption)


def product(left, right):
    return jnp.dot(left, right, preferred_element_type=jnp.float32)


def left_product(left, right):
    return lax.dot_general(
        left, right, (((0,), (0,)), ((), ())), preferred_element_type=jnp.float32
    )


def right_product(left, right):
    return lax.dot_general(
        left, right, (((1,), (1,)), ((), ())), preferred_element_type=jnp.float32
    )


def unpack(flat, width, hidden):
    return (
        flat[0].reshape(2 * width, width),
        flat[1].reshape(width, 3 * width),
        flat[2].reshape(width, width),
        flat[3].reshape(width, hidden),
        flat[4].reshape(hidden, width),
    )


def attention_scores(query, keys, valid, scale):
    raw = jnp.einsum("ishd,ithd->ihst", query, keys, preferred_element_type=jnp.float32) * scale
    return jnp.where(valid[:, None, None, :], raw, masked_value)


def column_sum(value):
    return jnp.sum(value.astype(jnp.float32), 0)


def flat_piece(left, right):
    grad_rows = left_product(left, right).reshape(-1)
    return grad_rows


MESH = pl.DeviceIdType.MESH
BF=jnp.bfloat16; F32=jnp.float32
SPLIT = 384
STEP = 112


def unit_lanes(value, units, chips):
    seg = value.shape[1] // (units * chips)
    return [
        jnp.concatenate([value[:, (s * units + u) * seg : (s * units + u + 1) * seg] for s in range(chips)], 1)
        for u in range(units)
    ]


def row_loop(total, step, fn):
    def one(n, carry):
        fn(pl.ds(pl.multiple_of(n * step, step), step))
        return carry
    lax.fori_loop(0, total // step, one, 0)


def natural_lanes(units, chips):
    seg = units[0].shape[1] // chips
    return jnp.concatenate([u[:, s * seg : (s + 1) * seg] for s in range(chips) for u in units], 1)


def block_kernel(Z, wide, rows, tiles, length, padded,
                 cap_ref, skip_ref, qkv_ref, proj_ref, fc1_ref, fc2_ref, vec_ref, in_ref, sk_ref, og_ref,
                 out_o, in_o, sk_o, skip_g, qkv_g, proj_g, fc1_g, fc2_g, vec_o, skip_o, qp_o, fc1_o, fc2_o, j_o, h0_o, acc_o,
                 skip_f, qkv_f, proj_f, fc1_f, fc2_f, own, keep, give, take, vbuf, vecs, b1s, vpart, vgot, vall, tok,
                 dtg, side, hid, am, t, m, zz, gu, gm, acc, tmp, sums, gacc, wbuf,
                 xl, xr, part, ra1, ra2, ra3, raf, rc1, rc2, rcf, rc3, rb1, rbf, rb2, rb3,
                 send, recv, lsem, psend, precv, vsend, vrecv, isem, osem, wsem,
                 rsend, rrecv, xsend, xrecv, qsend, qrecv, ysend, yrecv, ssend, srecv, free):
    dp = lax.axis_index("dp"); f = lax.axis_index("fsdp")
    z = dp // 2; x = dp % 2; y = f // 2; c = f % 2
    o = 1 - c
    nt = wide // 128
    half = rows // 2
    chips = 4 * Z
    ndp = 2 * Z
    hd = wide // HEADS
    full = length // 16 * 16
    ta, tb, tc = tiles
    A = pl.ds(0, ta); B = pl.ds(ta, tb); C = pl.ds(ta + tb, tc)
    zt = [z + 1 - 2 * (z % 2), lax.rem(z + 2, 4), 3 - z]
    zd = [(i * 2 + x, f) for i in zt]
    middle = (z == 1) | (z == 2)
    ends = (z == 0) | (z == 3)
    xp = (z * 2 + 1 - x, f)
    yp = (dp, (1 - y) * 2 + c)
    pp = (dp, y * 2 + o)
    dps = [(lax.rem(dp + k, ndp), f) for k in range(1, ndp)]
    fs = [(dp, lax.rem(f + k, 4)) for k in range(1, 4)]
    bar = pltpu.get_barrier_semaphore()
    for d in dps + fs:
        pl.semaphore_signal(bar, inc=1, device_id=d, device_id_type=MESH)
    flats = [(skip_ref, skip_f), (qkv_ref, qkv_f), (proj_ref, proj_f), (fc1_ref, fc1_f), (fc2_ref, fc2_f)]
    floads = [pltpu.make_async_copy(a, b, isem.at[n]) for n, (a, b) in enumerate(flats)]
    for cp in floads: cp.start()
    loads = [pltpu.make_async_copy(in_ref.at[:, 0, :], tok.at[0], isem.at[5]), pltpu.make_async_copy(sk_ref.at[:, 0, :], tok.at[1], isem.at[6])]
    for cp in loads: cp.start()
    def remote(src, dst, ssem, rsem, dev):
        return pltpu.make_async_remote_copy(src, dst, ssem, rsem, device_id=dev, device_id_type=MESH)
    @pl.when(ends)
    def _():
        for buf in (ra3, rc2, rb1):
            for b in range(buf.shape[0]): buf[b, 2] = jnp.zeros(buf.shape[2:], BF)
    floads[0].wait()
    for j in range(nt):
        own[0, :, 128 * j:128 * j + 128] = skip_f[pl.ds(j, rows, stride=nt), :].astype(BF)
    pl.semaphore_wait(bar, len(dps) + len(fs))

    waits = []
    def rc(i, slot, src, dst, dev):
        cp = remote(src, dst, send.at[i, slot], recv.at[i, slot], dev)
        cp.start(); waits.append(cp)
    def got(i, slot, dst):
        remote(dst, dst, send.at[i, slot], recv.at[i, slot], pp).wait_recv()
    def unit(i, cc):
        if i == 0: return skip_o.at[:, :, :, cc]
        if i in (1, 2): return qp_o.at[2 * (i - 1) + cc]
        if i in (3, 4): return fc1_o.at[2 * cc + (i - 3)]
        return fc2_o.at[2 * cc + (i - 5)]
    pc = {}
    lc = {}
    def exchange(i, first, second):
        keep[i - 1, 0:half, :] = jnp.where(c == 0, first, second)
        give[i - 1, 0:half, :] = jnp.where(c == 0, second, first)
        pc[i] = remote(give.at[i - 1], take.at[i - 1], psend.at[i - 1], precv.at[i - 1], pp)
        pc[i].start()
    whens = []
    def cond(cp):
        whens.append(cp)
        pl.when(middle)(lambda: cp.start())
    def zsend(i, base, view):
        for k in (1, 2, 3):
            v = view(z)
            cp = remote(v, v, send.at[i, base + k - 1], recv.at[i, base + k - 1], zd[k - 1])
            if k == 3: cond(cp)
            else: cp.start(); waits.append(cp)
    def zforward(i, base, view):
        got(i, base + 1, view(zt[1]))
        v = view(zt[1])
        cond(remote(v, v, send.at[i, base + 3], recv.at[i, base + 2], zd[0]))
    def zgot(i, base, view):
        got(i, base, view(zt[0])); got(i, base + 2, view(zt[2]))
    lc = {}
    def ready(i):
        if i in (1, 2, 3, 4):
            pc[i].wait_recv()
            p = keep[i - 1, 0:half, :]
            q = take[i - 1, 0:half, :]
            lo = jnp.where(c == 0, p, q); hi = jnp.where(c == 0, q, p)
            own[i, :, :] = jnp.concatenate([lo, hi], 0).astype(BF)
        lc[i] = pltpu.make_async_copy(own.at[i], unit(i, c).at[z, x, y], lsem.at[i]); lc[i].start()
    SA, SC, SB = 0, 4, 8
    def gA1(i):
        U = unit(i, c); lc[i].wait()
        zsend(i, SA, lambda t: U.at[t, x, y, :, A])
    def gC1(i):
        rc(i, 12, own.at[i, :, C], unit(i, c).at[z, x, y, :, C], yp)
    def gB1(i):
        rc(i, 13, own.at[i, :, B], unit(i, c).at[z, x, y, :, B], xp)
    def gAF(i):
        U = unit(i, c); zforward(i, SA, lambda t: U.at[t, x, y, :, A])
    def gA2(i):
        U = unit(i, c)
        zgot(i, SA, lambda t: U.at[t, x, y, :, A])
        L = U.at[:, x, y, :, A]
        rc(i, 14, L, L, yp); rc(i, 15, L, L, xp); rc(i, 16, L, L, pp)
    def gA3(i):
        L = unit(i, c).at[:, 1 - x, y, :, A]
        got(i, 15, L); rc(i, 17, L, L, yp); rc(i, 18, L, L, pp)
    def gC2(i):
        U = unit(i, c)
        got(i, 12, U.at[z, x, 1 - y, :, C])
        zsend(i, SC, lambda t: U.at[t, x, :, :, C])
    def gCF(i):
        U = unit(i, c); zforward(i, SC, lambda t: U.at[t, x, :, :, C])
    def gC3(i):
        U = unit(i, c)
        zgot(i, SC, lambda t: U.at[t, x, :, :, C])
        L = U.at[:, x, :, :, C]
        rc(i, 19, L, L, xp); rc(i, 20, L, L, pp)
    def gB2(i):
        U = unit(i, c)
        got(i, 13, U.at[z, 1 - x, y, :, B])
        L = U.at[z, :, y, :, B]
        rc(i, 21, L, L, yp)
    def gB3(i):
        U = unit(i, c)
        got(i, 21, U.at[z, :, 1 - y, :, B])
        zsend(i, SB, lambda t: U.at[t, :, :, :, B])
    def gBF(i):
        U = unit(i, c); zforward(i, SB, lambda t: U.at[t, :, :, :, B])
    def gPA(i):
        U = unit(i, c)
        L = U.at[:, x, 1 - y, :, A]
        got(i, 14, L); rc(i, 22, L, L, pp)
        L = U.at[:, 1 - x, 1 - y, :, A]
        got(i, 17, L); rc(i, 23, L, L, pp)
    def gPC(i):
        L = unit(i, c).at[:, 1 - x, :, :, C]
        got(i, 19, L); rc(i, 24, L, L, pp)
    def gPB(i):
        U = unit(i, c)
        zgot(i, SB, lambda t: U.at[t, :, :, :, B])
        L = U.at[:, :, :, :, B]
        rc(i, 25, L, L, pp)
    def arrived(i):
        U = unit(i, 1 - c)
        got(i, 16, U.at[:, x, y, :, A])
        got(i, 18, U.at[:, 1 - x, y, :, A])
        got(i, 22, U.at[:, x, 1 - y, :, A])
        got(i, 23, U.at[:, 1 - x, 1 - y, :, A])
        got(i, 20, U.at[:, x, :, :, C])
        got(i, 24, U.at[:, 1 - x, :, :, C])
        got(i, 25, U.at[:, :, :, :, B])
    def read(ref, first, stride):
        return jnp.concatenate([ref[pl.ds(first + j, half, stride=stride), :] for j in range(nt)], 1)

    ready(0)
    gB1(0); gC1(0)
    gA1(0)
    vcopies = []
    vbuf[dp] = vec_ref[...]
    for k, d in enumerate(dps):
        cp = remote(vec_ref, vbuf.at[dp], vsend.at[k], vrecv.at[k], d)
        cp.start(); vcopies.append(cp)
    floads[1].wait(); floads[2].wait()
    exchange(1, read(qkv_f, 0, 3 * nt), read(qkv_f, nt, 3 * nt))
    exchange(2, read(qkv_f, 2 * nt, 3 * nt), read(proj_f, 0, nt))
    def prepare_late():
        floads[3].wait(); floads[4].wait()
        for j in range(nt):
            own[5, :, 128 * j:128 * j + 128] = fc2_f[pl.ds(j, rows, stride=nt), :].astype(BF)
            own[6, :, 128 * j:128 * j + 128] = fc2_f[pl.ds(j + nt * rows, rows, stride=nt), :].astype(BF)
        nat = jnp.concatenate([read(fc1_f, nt * v, 4 * nt) for v in range(4)], 1)
        u = unit_lanes(nat, 4, chips)
        exchange(3, u[0], u[2])
        exchange(4, u[1], u[3])

    def keep_out(n, src, dst):
        cp = pltpu.make_async_copy(src, dst, osem.at[n]); cp.start()
        return cp
    def weight(n, ref):
        pltpu.make_async_copy(ref, wbuf.at[n], wsem.at[n]).start()
    def weight_wait(k):
        pltpu.make_async_copy(wbuf.at[k], wbuf.at[k], wsem.at[k]).wait()
    def both_skip():
        for k in range(2):
            for i in range(Z // 2):
                pltpu.make_async_copy(skip_o.at[k * (Z // 2) + i], wbuf.at[k, pl.ds(2 * i, 2)], wsem.at[k]).start()
    def cols(k, l):
        return wbuf[k, :, :, :, :, l].reshape(wide, SPLIT)
    def lanes_loop(fn):
        def one(n, carry):
            fn(pl.ds(pl.multiple_of(n * SPLIT, 128), SPLIT))
            return carry
        lax.fori_loop(0, wide // SPLIT, one, 0)
    def vector(n):
        return vecs[0:1, n * wide:(n + 1) * wide]
    def put_rows(k, src):
        def one(r): tok[k, r, :] = src[r, :]
        row_loop(full, 16, one)
        if length > full: tok[k, full:length, :] = src[full:length, :]
    def norm(src, gain, shift, dst):
        def one(r):
            v = src[r, :]
            cen = v - jnp.mean(v, -1, keepdims=True)
            s = jnp.mean(cen * cen, -1, keepdims=True)
            dst[r, :] = (cen * lax.rsqrt(s + epsilon) * gain + shift).astype(BF)
        row_loop(padded, STEP, one)
    def take_rows(k, dst, at):
        if padded > full: dst[at + (slice(padded - 16, padded), slice(None))] = jnp.zeros((16, wide), dst.dtype)
        def one(r): dst[at + (r, slice(None))] = tok[k, r, :].astype(dst.dtype)
        row_loop(full, 16, one)
        if length > full: dst[at + (slice(full, length), slice(None))] = tok[k, full:length, :].astype(dst.dtype)
    def inputs():
        for cp in loads: cp.wait()
        take_rows(0, dtg, (0,))
        take_rows(1, dtg, (1,))
        pltpu.make_async_copy(og_ref.at[:, 0, :], tok.at[0], isem.at[5]).start()
        def two(r):
            u = unit_lanes(jnp.concatenate([dtg[0, r, :], dtg[1, r, :]], 1), 2, chips)
            side[0, r, :] = u[0]
            side[1, r, :] = u[1]
        row_loop(padded, STEP, two)
        keep_out(0, side, j_o)
    def vectors():
        for k in range(len(dps)):
            remote(vec_ref, vbuf.at[lax.rem(dp - (k + 1) + ndp, ndp)], vsend.at[k], vrecv.at[k], pp).wait_recv()
        vecs[...] = jnp.concatenate([vbuf[k] for k in range(ndp)], 1)
        b = unit_lanes(vecs[0:1, 7 * wide:11 * wide], 4, chips)
        for u in range(4): b1s[u] = b[u]
        pltpu.make_async_copy(og_ref.at[:, 0, :], tok.at[0], isem.at[5]).wait()
        take_rows(0, gm, ())
        pltpu.make_async_copy(og_ref.at[:, 0, :], tok.at[1], isem.at[6]).start()
    def first_part():
        arrived(0)
        both_skip()
        weight_wait(0); weight_wait(1)
        def one(l):
            v = jnp.dot(dtg[0], cols(0, l), preferred_element_type=F32)
            v = v + jnp.dot(dtg[1], cols(1, l), preferred_element_type=F32)
            hid[:, l] = v + vecs[0:1, pl.ds(4 * wide + l.start, SPLIT)]
        lanes_loop(one)
        norm(hid, vector(0), vector(1), am.at[0])
        keep_out(1, hid, h0_o)
    def project(n, u):
        def one(l):
            t[u, :, l] = jnp.dot(am[0], cols(n, l), preferred_element_type=F32).astype(BF)
        lanes_loop(one)
    def query_keys():
        arrived(1)
        for u in range(2): weight(u, qp_o.at[u])
        def each(u, carry):
            weight_wait(u)
            project(u, u)
            return carry
        lax.fori_loop(0, 2, each, 0)
    def values():
        arrived(2)
        weight(0, qp_o.at[2]); weight(1, qp_o.at[3])
        weight_wait(0)
        project(0, 2)
    def window(h):
        base = pl.multiple_of(jnp.minimum((h * hd) // 128, nt - 2) * 128, 128)
        lane = lax.broadcasted_iota(jnp.int32, (1, 256), 1) + (base - h * hd)
        return pl.ds(base, 256), (lane >= 0) & (lane < hd)
    def attend(first, last):
        cap = cap_ref[0]
        key = lax.broadcasted_iota(jnp.int32, (1, padded), 1)
        live = ((key < 1 + cap) | (key >= 1 + CAPTION)) & (key < length)
        def head(h, carry):
            win, inside = window(h)
            q = jnp.where(inside, t[0, :, win].astype(F32), 0.0).astype(BF)
            s = lax.dot_general(q, t[1, :, win], (((1,), (1,)), ((), ())), preferred_element_type=F32) * hd ** (-0.5)
            s = jnp.where(live, s, masked_value)
            e = jnp.exp(s - jnp.max(s, -1, keepdims=True))
            p = (e / jnp.sum(e, -1, keepdims=True)).astype(BF)
            v = jnp.dot(p, t[2, :, win], preferred_element_type=F32)
            am[1, :, win] = jnp.where(inside, v, am[1, :, win].astype(F32)).astype(BF)
            return carry
        lax.fori_loop(first, last, head, 0)
    def second_part():
        weight_wait(1)
        pltpu.make_async_copy(hid, h0_o, osem.at[1]).wait()
        def one(l):
            v = jnp.dot(am[1], cols(1, l), preferred_element_type=F32)
            h = hid[:, l] + (v + vecs[0:1, pl.ds(5 * wide + l.start, SPLIT)])
            hid[:, l] = h
            acc[:, l] = h + vecs[0:1, pl.ds(6 * wide + l.start, SPLIT)]
        lanes_loop(one)
        keep_out(10, acc, acc_o)
        norm(hid, vector(2), vector(3), m)
    def widen_load(i):
        arrived(i)
        for k in range(2): weight(k, fc1_o.at[2 * k + i - 3])
    def pair_loop(fn, first):
        def one(k, carry):
            fn(k, 2 * k + first)
            return carry
        lax.fori_loop(0, 2, one, 0)
    def widen(k, u):
        weight_wait(k)
        def one(l):
            tmp[:, l] = jnp.dot(m[...], cols(k, l), preferred_element_type=F32)
        lanes_loop(one)
        def two(r):
            v = tmp[r, :] + b1s[u]
            cdf = 0.5 * (1.0 + lax.erf(v * 0.7071067811865476))
            pdf = jnp.exp(-0.5 * v * v) * 0.3989422804014327
            zz[u, r, :] = (v * cdf).astype(BF)
            gu[u, r, :] = (cdf + v * pdf).astype(BF)
        row_loop(padded, STEP, two)
    def narrow_load(i):
        arrived(i)
        for k in range(2): weight(k, fc2_o.at[2 * k + i - 5])
    def narrow(k, u):
        weight_wait(k)
        tmp[...] = jnp.zeros_like(tmp)
        def one(l):
            tmp[...] += lax.dot_general(gm[:, l], cols(k, l), (((1,), (1,)), ((), ())), preferred_element_type=F32)
        lanes_loop(one)
        def two(r):
            gu[u, r, :] = (tmp[r, :] * gu[u, r, :].astype(F32)).astype(BF)
        row_loop(padded, STEP, two)
    def finish():
        pltpu.make_async_copy(acc_o, acc, isem.at[8]).wait()
        for u in range(2): weight(u, fc2_o.at[u])
        def each(u, carry):
            k = u % 2
            weight_wait(k)
            def one(l):
                acc[:, l] += jnp.dot(zz[u], cols(k, l), preferred_element_type=F32)
            lanes_loop(one)
            pl.when(u < 2)(lambda: weight(k, fc2_o.at[u + 2]))
            return carry
        lax.fori_loop(0, 4, each, 0)
    def finish_out():
        pltpu.make_async_copy(tok.at[0], in_o.at[:, 0, :], osem.at[3]).wait()
        put_rows(0, acc)
        keep_out(2, tok.at[0], out_o.at[:, 0, :])

    xcopies = {}
    def swap(n, src, dst):
        xcopies[n] = remote(src, dst, xsend.at[n], xrecv.at[n], pp)
        xcopies[n].start()
    nb = 4
    started = {j: [] for j in range(7)}
    def sc(j, slot, src, dst, dev):
        cp = remote(src, dst, rsend.at[j, slot], rrecv.at[j, slot], dev)
        cp.start(); started[j].append((None, cp))
    def settle(j):
        for which, cp in started[j]:
            if which is None: cp.wait_send()
            else: pl.when(which)(lambda: cp.wait_send())
    def came(j, slot, dst):
        remote(dst, dst, rsend.at[j, slot], rrecv.at[j, slot], pp).wait_recv()
    need = [(0, 1), (2,), (3, 4), (5,), (6, 7), (8, 9), (10, 11)]
    def operands(j):
        if j < 2: return zz.at[2 * c + j], gm, xl.at[j], xr.at[0]
        if j < 4: return m, gu.at[2 * c + j - 2], xl.at[2], xr.at[j - 1]
        if j == 4: return am.at[c], dtg.at[2 + c], xl.at[0], xr.at[0]
        if j == 5: return am.at[0], dtg.at[c], xl.at[1], xr.at[1]
        return side.at[0], side.at[1], xl.at[2], xr.at[2]
    def reduce1(j):
        for n in need[j]: xcopies[n].wait_recv()
        if j >= nb:
            settle(j - nb)
        b = j % nb
        D = part.at[b]
        l1, r1, l2, r2 = operands(j)
        step = SPLIT
        dims = (((0,), (0,)), ((), ()))
        def chunk(n, carry):
            at = pl.ds(pl.multiple_of(n * step, 128), step)
            r = lax.dot_general(l1[...], r1[:, at], dims, preferred_element_type=F32)
            r = r + lax.dot_general(l2[...], r2[:, at], dims, preferred_element_type=F32)
            D[:, :, :, :, at] = r.reshape(Z, 2, 2, rows, step).astype(BF)
            return carry
        lax.fori_loop(0, wide // step, chunk, 0)
        sc(j, 0, D.at[:, 1 - x, 1 - y, :, A], ra1.at[b, 0], yp)
        sc(j, 2, D.at[:, 1 - x, :, :, C], rc1.at[b], xp)
        sc(j, 1, D.at[:, x, 1 - y, :, A], ra1.at[b, 1], yp)
        line_send(j, 12, lambda i: D.at[i, :, :, :, B], rb1.at[b], rbf.at[b])
    def only(j, which, slot, src, dst, dev):
        cp = remote(src, dst, rsend.at[j, slot], rrecv.at[j, slot], dev)
        pl.when(which)(lambda: cp.start())
        return cp
    def line_send(j, base, view, buf, fbuf):
        sc(j, base, view(zt[0]), buf.at[0], zd[0])
        started[j].append((ends, only(j, ends, base + 3, view(zt[2]), fbuf, zd[0])))
        started[j].append((None, only(j, ends, base + 1, view(zt[1]), buf.at[1], zd[1])))
        started[j].append((middle, only(j, middle, base + 2, view(zt[2]), buf.at[2], zd[2])))
    def line_relay(j, base, view, buf, fbuf):
        cp = remote(view(zt[1]), buf.at[1], rsend.at[j, base + 1], rrecv.at[j, base + 1], zd[1])
        @pl.when(middle)
        def _():
            came(j, base + 3, fbuf)
            plus(view(zt[1]), fbuf)
            cp.start()
    def line_came(j, base, buf):
        came(j, base, buf.at[0]); came(j, base + 1, buf.at[1])
        pl.when(middle)(lambda: came(j, base + 2, buf.at[2]))
    def plus(dst, *srcs):
        lead = dst.shape[:-2]
        for n in range(math.prod(lead)):
            at = ()
            for d in reversed(lead):
                at = (n % d,) + at
                n = n // d
            v = dst[at + (slice(None), slice(None))].astype(F32)
            for r in srcs: v = v + r[at + (slice(None), slice(None))].astype(F32)
            dst[at + (slice(None), slice(None))] = v.astype(BF)
    def reduce2(j):
        b = j % nb
        D = part.at[b]
        came(j, 0, ra1.at[b, 0])
        plus(D.at[:, 1 - x, y, :, A], ra1.at[b, 0])
        sc(j, 3, D.at[:, 1 - x, y, :, A], ra2.at[b], xp)
        came(j, 2, rc1.at[b])
        plus(D.at[:, x, :, :, C], rc1.at[b])
        line_send(j, 8, lambda i: D.at[i, x, :, :, C], rc2.at[b], rcf.at[b])
        line_relay(j, 12, lambda i: D.at[i, :, :, :, B], rb1.at[b], rbf.at[b])
    def reduce3(j):
        b = j % nb
        D = part.at[b]
        line_came(j, 12, rb1.at[b])
        plus(D.at[z, :, :, :, B], rb1.at[b, 0], rb1.at[b, 1], rb1.at[b, 2])
        sc(j, 17, D.at[z, :, 1 - y, :, B], rb2.at[b], yp)
        came(j, 1, ra1.at[b, 1])
        came(j, 3, ra2.at[b])
        plus(D.at[:, x, y, :, A], ra1.at[b, 1], ra2.at[b])
        line_send(j, 4, lambda i: D.at[i, x, y, :, A], ra3.at[b], raf.at[b])
        line_relay(j, 8, lambda i: D.at[i, x, :, :, C], rc2.at[b], rcf.at[b])
    def reduce4(j):
        b = j % nb
        D = part.at[b]
        line_relay(j, 4, lambda i: D.at[i, x, y, :, A], ra3.at[b], raf.at[b])
        line_came(j, 8, rc2.at[b])
        plus(D.at[z, x, :, :, C], rc2.at[b, 0], rc2.at[b, 1], rc2.at[b, 2])
        sc(j, 16, D.at[z, x, 1 - y, :, C], rc3.at[b], yp)
        came(j, 17, rb2.at[b])
        plus(D.at[z, :, y, :, B], rb2.at[b])
        sc(j, 18, D.at[z, 1 - x, y, :, B], rb3.at[b], xp)
    pcopies = {}
    def lay(ref, val, first, stride, n):
        for i in range(val.shape[1] // 128):
            ref[pl.ds(first + i, n, stride=stride), :] = val[:, 128 * i:128 * i + 128]
    def reduce5(j):
        b = j % nb
        D = part.at[b]
        line_came(j, 4, ra3.at[b])
        came(j, 16, rc3.at[b])
        came(j, 18, rb3.at[b])
        p = D[z, x, y, :, A].astype(F32)
        for k in range(3):
            p = p + ra3[b, k].astype(F32)
        q = D[z, x, y, :, B].astype(F32) + rb3[b].astype(F32)
        r = D[z, x, y, :, C].astype(F32) + rc3[b].astype(F32)
        v = jnp.concatenate([p, q, r], 1)
        if j in (0, 1):
            lay(fc2_f, v, j * rows * nt, nt, rows)
            if j == 1: keep_out(9, fc2_f, fc2_g)
        elif j == 6:
            lay(skip_f, v, 0, nt, rows)
            keep_out(5, skip_f, skip_g)
        else:
            lo = v[0:half]; hi = v[half:rows]
            keep[j - 2, 0:half, :] = jnp.where(c == 0, lo, hi)
            give[j - 2, 0:half, :] = jnp.where(c == 0, hi, lo)
            cp = remote(give.at[j - 2], take.at[j - 2], qsend.at[j - 2], qrecv.at[j - 2], pp)
            cp.start(); pcopies[j] = cp
    def both(j):
        pcopies[j].wait_recv()
        p = keep[j - 2, 0:half, :]; q = take[j - 2, 0:half, :]
        return jnp.where(c == 0, p, q), jnp.where(c == 0, q, p)
    def settle_pair(j):
        if j == 3:
            p, q = both(2), both(3)
            lay(fc1_f, natural_lanes([p[0], q[0], p[1], q[1]], chips), 0, 4 * nt, half)
            keep_out(8, fc1_f, fc1_g)
        elif j == 5:
            first, second = both(5)
            lay(qkv_f, first, 0, 3 * nt, half)
            lay(qkv_f, second, nt, 3 * nt, half)
            keep_out(6, qkv_f, qkv_g)
        elif j == 4:
            first, second = both(4)
            lay(qkv_f, first, 2 * nt, 3 * nt, half)
            lay(proj_f, second, 0, nt, half)
            keep_out(7, proj_f, proj_g)


    def zero(n): gacc[n] = jnp.zeros((8, wide), F32)
    def add_rows(n, v):
        gacc[n] += jnp.sum(v.reshape(v.shape[0] // 8, 8, wide), 0)
    def close(n):
        return jnp.sum(gacc[n], 0, keepdims=True)
    def column_sums(src):
        zero(0)
        def one(r): add_rows(0, src[r, :].astype(F32))
        row_loop(padded, STEP, one)
        return close(0)
    def norm_back(dy, src, gain, fn):
        zero(0); zero(1); zero(2)
        def one(r):
            d = dy[r, :]
            v = src[r, :]
            cen = v - jnp.mean(v, -1, keepdims=True)
            rs = lax.rsqrt(jnp.mean(cen * cen, -1, keepdims=True) + epsilon)
            xh = cen * rs
            dx = d * gain
            g = rs * (dx - jnp.mean(dx, -1, keepdims=True) - xh * jnp.mean(dx * xh, -1, keepdims=True))
            add_rows(0, d * xh)
            add_rows(1, d)
            fn(r, g)
        row_loop(padded, STEP, one)
    def turned(lhs, n, fresh):
        if fresh: tmp[...] = jnp.zeros_like(tmp)
        def one(l):
            tmp[...] += lax.dot_general(lhs[:, l], cols(n, l), (((1,), (1,)), ((), ())), preferred_element_type=F32)
        lanes_loop(one)
    def widen_back():
        tmp[...] = jnp.zeros_like(tmp)
        def each(u, carry):
            k = u % 2
            weight_wait(k)
            turned(gu.at[u], k, False)
            pl.when(u < 2)(lambda: weight(k, fc1_o.at[u + 2]))
            sums[7 + u] = column_sums(gu.at[u])
            return carry
        lax.fori_loop(0, 4, each, 0)
    def norm_two():
        weight(0, qp_o.at[3])
        pltpu.make_async_copy(og_ref.at[:, 0, :], tok.at[1], isem.at[6]).wait()
        pltpu.make_async_copy(acc, acc_o, osem.at[10]).wait()
        take_rows(1, acc, ())
        def fn(r, g):
            s = acc[r, :] + g
            acc[r, :] = s
            b = s.astype(BF)
            dtg[3, r, :] = b
            add_rows(2, b.astype(F32))
        norm_back(tmp, hid, vector(2), fn)
        sums[2] = close(0); sums[3] = close(1); sums[5] = close(2)
        pltpu.make_async_copy(h0_o, hid, isem.at[5]).start()
        sums[6] = column_sums(gm)
        weight_wait(0)
        turned(dtg.at[3], 0, True)
        def two(r): side[0, r, :] = tmp[r, :].astype(BF)
        row_loop(padded, STEP, two)
    def attend_back(first, last):
        cap = cap_ref[0]
        key = lax.broadcasted_iota(jnp.int32, (padded, 1), 0)
        live = ((key < 1 + cap) | (key >= 1 + CAPTION)) & (key < length)
        def head(h, carry):
            win, inside = window(h)
            q = jnp.where(inside, t[0, :, win].astype(F32), 0.0).astype(BF)
            k = t[1, :, win]
            g = jnp.where(inside, side[0, :, win].astype(F32), 0.0).astype(BF)
            s = lax.dot_general(k, q, (((1,), (1,)), ((), ())), preferred_element_type=F32) * hd ** (-0.5)
            s = jnp.where(live, s, masked_value)
            e = jnp.exp(s - jnp.max(s, 0, keepdims=True))
            p = e * (1.0 / jnp.sum(e, 0, keepdims=True))
            d = lax.dot_general(t[2, :, win], g, (((1,), (1,)), ((), ())), preferred_element_type=F32)
            ds = (p * (d - jnp.sum(p * d, 0, keepdims=True))).astype(BF)
            dq = lax.dot_general(ds, k, (((0,), (0,)), ((), ())), preferred_element_type=F32) * hd ** (-0.5)
            dk = jnp.dot(ds, q, preferred_element_type=F32) * hd ** (-0.5)
            dv = jnp.dot(p.astype(BF), g, preferred_element_type=F32)
            for i, v in enumerate((dq, dk, dv)):
                dtg[i, :, win] = jnp.where(inside, v, dtg[i, :, win].astype(F32)).astype(BF)
            return carry
        lax.fori_loop(first, last, head, 0)
    def late_left():
        pl.semaphore_signal(free, inc=1, device_id=pp, device_id_type=MESH)
        pl.semaphore_wait(free, 1)
        pltpu.make_async_copy(side, j_o, osem.at[0]).wait()
        swap(6, am.at[o], xl.at[0])
        swap(8, am.at[0], xl.at[1])
        swap(10, j_o.at[o], xl.at[2])
    def late_right():
        swap(7, dtg.at[2 + o], xr.at[0])
        swap(9, dtg.at[o], xr.at[1])
        pltpu.make_async_copy(j_o.at[c], side.at[0], isem.at[7]).start()
        weight(0, qp_o.at[0]); weight(1, qp_o.at[1])
    def project_back():
        tmp[...] = jnp.zeros_like(tmp)
        def each(i, carry):
            k = i % 2
            weight_wait(k)
            turned(dtg.at[i], k, False)
            pl.when(i == 0)(lambda: weight(0, qp_o.at[2]))
            return carry
        lax.fori_loop(0, 3, each, 0)
    def norm_one():
        pltpu.make_async_copy(h0_o, hid, isem.at[5]).wait()
        both_skip()
        def fn(r, g):
            b = (acc[r, :] + g).astype(BF)
            side[1, r, :] = b
            add_rows(2, b.astype(F32))
        norm_back(tmp, hid, vector(0), fn)
        sums[0] = close(0); sums[1] = close(1); sums[4] = close(2)
        swap(11, side.at[1], xr.at[2])
        pltpu.make_async_copy(acc_o, acc, isem.at[8]).start()
    def join_back(i, dst):
        weight_wait(i)
        turned(side.at[1], i, True)
        put_rows(i, tmp)
        keep_out(3 + i, tok.at[i], dst.at[:, 0, :])
    nv = vpart.shape[2]
    def vec_send():
        total = jnp.concatenate([sums[i] for i in range(7)] + [natural_lanes([sums[7 + u] for u in range(4)], chips)], 1)
        for k in range(ndp): vpart[k] = total[:, k * nv:(k + 1) * nv]
        for k, d in enumerate(dps):
            cp = remote(vpart.at[d[0]], vgot.at[k], ysend.at[k], yrecv.at[k], d)
            cp.start(); vcopies.append(cp)
    def vec_first():
        s = vpart[dp]
        for k in range(len(dps)):
            remote(vgot.at[k], vgot.at[k], ysend.at[k], yrecv.at[k], pp).wait_recv()
            s = s + vgot[k]
        vall[f] = s
        for k, d in enumerate(fs):
            cp = remote(vall.at[f], vall.at[f], ssend.at[k], srecv.at[k], d)
            cp.start(); vcopies.append(cp)
    def vec_last():
        for k in range(3):
            src = lax.rem(f - (k + 1) + 4, 4)
            remote(vall.at[src], vall.at[src], ssend.at[k], srecv.at[k], pp).wait_recv()
        vec_o[...] = vall[0] + vall[1] + vall[2] + vall[3]

    ready(1); gB1(1); gB2(0)
    gC2(0); gAF(0); gA2(0)
    ready(2); gB1(2)
    gC1(1); gA1(1); gB2(1)
    gB3(0)
    prepare_late()
    gCF(0); gC3(0); gA3(0)
    inputs()
    gC2(1); gAF(1); gA2(1)
    ready(3); gB1(3)
    gC1(2); gA1(2); gB2(2)
    gB3(1)
    vectors()
    gCF(1); gC3(1); gA3(1)
    gBF(0); gPA(0); gPC(0)
    gC2(2); gAF(2); gA2(2)
    ready(4); gB1(4)
    gC1(3); gA1(3); gB2(3)
    gB3(2)
    gCF(2); gC3(2); gA3(2)
    gBF(1); gPA(1); gPC(1)
    gPB(0)
    first_part()
    gC2(3); gAF(3); gA2(3)
    ready(5); gB1(5)
    gC1(4); gA1(4); gB2(4)
    gB3(3)
    gCF(3); gC3(3); gA3(3)
    gBF(2); gPA(2); gPC(2)
    gPB(1)
    query_keys()
    gC2(4); gAF(4); gA2(4)
    ready(6); gB1(6)
    gC1(5); gA1(5); gB2(5)
    gB3(4)
    gCF(4); gC3(4); gA3(4)
    gBF(3); gPA(3); gPC(3)
    gPB(2)
    values()
    attend(0, 5)
    gC2(5); gAF(5); gA2(5)
    gC1(6); gA1(6); gB2(6)
    gB3(5)
    attend(5, 11)
    gCF(5); gC3(5); gA3(5)
    gBF(4); gPA(4); gPC(4)
    gPB(3)
    attend(11, 16)
    second_part()
    gC2(6); gAF(6); gA2(6)
    gB3(6)
    widen_load(3)
    widen(0, 0)
    gCF(6); gC3(6); gA3(6)
    gBF(5); gPA(5); gPC(5)
    gPB(4)
    widen(1, 2)
    for cp in pc.values(): cp.wait_send()
    swap(0, zz.at[2 * o], xl.at[0])
    swap(1, gm, xr.at[0])
    swap(3, m, xl.at[2])
    widen_load(4)
    reduce1(0)
    gBF(6); gPA(6); gPC(6); gPB(5)
    pair_loop(widen, 1)
    swap(2, zz.at[2 * o + 1], xl.at[1])
    narrow_load(5)
    reduce1(1)
    gPB(6)
    reduce2(0)
    pair_loop(narrow, 0)
    swap(4, gu.at[2 * o], xr.at[1])
    narrow_load(6)
    reduce1(2); reduce2(1)
    pair_loop(narrow, 1)
    swap(5, gu.at[2 * o + 1], xr.at[2])
    weight(0, fc1_o.at[0]); weight(1, fc1_o.at[1])
    reduce3(0)
    reduce4(0)
    reduce1(3)
    reduce2(2); reduce3(1)
    widen_back()
    late_left()
    norm_two()
    reduce5(0); reduce4(1)
    attend_back(0, 5)
    reduce2(3); reduce3(2)
    attend_back(5, 16)
    late_right()
    reduce1(4)
    reduce5(1); reduce4(2); reduce3(3)
    reduce1(5); reduce2(4)
    project_back()
    reduce5(2); reduce4(3)
    norm_one()
    vec_send()
    pltpu.make_async_copy(j_o.at[c], side.at[0], isem.at[7]).wait()
    reduce2(5); reduce3(4)
    reduce1(6)
    vec_first()
    join_back(0, in_o)
    reduce5(3); reduce4(4)
    join_back(1, sk_o)
    settle_pair(3)
    reduce3(5); reduce2(6)
    vec_last()
    reduce5(4); reduce4(5); settle_pair(4)
    finish()
    finish_out()
    reduce3(6)
    reduce5(5); settle_pair(5)
    reduce4(6)
    reduce5(6)
    pltpu.make_async_copy(tok.at[1], sk_o.at[:, 0, :], osem.at[4]).wait()
    pltpu.make_async_copy(tok.at[0], out_o.at[:, 0, :], osem.at[2]).wait()
    for n, (a, b) in zip((5, 6, 7, 8, 9), ((skip_f, skip_g), (qkv_f, qkv_g), (proj_f, proj_g), (fc1_f, fc1_g), (fc2_f, fc2_g))):
        pltpu.make_async_copy(a, b, osem.at[n]).wait()
    for j in range(3, 7): settle(j)
    for cp in whens: pl.when(middle)(lambda: cp.wait_send())
    for cp in waits: cp.wait_send()
    for cp in pcopies.values(): cp.wait_send()
    for cp in vcopies: cp.wait_send()
    for cp in xcopies.values(): cp.wait_send()


def block(cap, skip, qkv, proj, fc1, fc2, vectors, block_in, skip_in, out_grad, dpn):
    _, length, wide = block_in.shape
    Z = dpn // 2; rows = skip.shape[0] // wide
    padded = -(-length // 16) * 16
    nt = wide // 128
    tb = 128 * max(1, nt // 9); tc = 128 * (nt // 3); ta = wide - tb - tc
    tiles = (ta, tb, tc)
    U = (Z, 2, 2, rows, wide)
    hbm = pl.BlockSpec(memory_space=pl.ANY); vm = pl.BlockSpec(memory_space=pltpu.VMEM)
    ns = 26
    nr = 19
    nv = vectors.shape[0]
    D = pltpu.SemaphoreType.DMA
    V = pltpu.VMEM
    hp = -(-rows // 2 // 8) * 8
    S = jax.ShapeDtypeStruct
    act = (padded, wide)
    flat = [(w.shape[0] // 128, 128) for w in (skip, qkv, proj, fc1, fc2)]
    tokens = (length, 1, wide)
    nb = 4
    res = pl.pallas_call(
        functools.partial(block_kernel, Z, wide, rows, tiles, length, padded),
        out_shape=(S(tokens, F32),) * 3 + tuple(S(s, F32) for s in flat) + (S((1, nv), F32),
                   S((Z, 2, 2, 2, rows, wide), BF), S((4,) + U, BF), S((4,) + U, BF), S((4,) + U, BF), S((2,) + act, BF), S(act, F32), S(act, F32)),
        in_specs=[pl.BlockSpec(memory_space=pltpu.SMEM)] + [hbm] * 5 + [vm] + [hbm] * 3,
        out_specs=(hbm,) * 8 + (vm,) + (hbm,) * 7,
        scratch_shapes=[V(s, F32) for s in flat] + [
                        V((7, rows, wide), BF), V((4, hp, wide), F32), V((4, hp, wide), F32), V((4, hp, wide), F32),
                        V((dpn, 1, nv), F32), V((1, nv * dpn), F32), V((4, 1, wide), F32), V((dpn, 1, nv), F32), V((dpn - 1, 1, nv), F32), V((4, 1, nv), F32),
                        V((2, length, wide), F32),
                        V((4,) + act, BF), V((2,) + act, BF), V(act, F32), V((2,) + act, BF), V((3,) + act, BF), V(act, BF), V((4,) + act, BF), V((4,) + act, BF), V(act, BF),
                        V(act, F32), V(act, F32), V((11, 1, wide), F32), V((3, 8, wide), F32), V((2,) + U, BF),
                        V((3,) + act, BF), V((3,) + act, BF), V((nb,) + U, BF),
                        V((nb, 2, Z, rows, ta), BF), V((nb, Z, rows, ta), BF), V((nb, 3, rows, ta), BF), V((nb, rows, ta), BF),
                        V((nb, Z, 2, rows, tc), BF), V((nb, 3, 2, rows, tc), BF), V((nb, 2, rows, tc), BF), V((nb, rows, tc), BF),
                        V((nb, 3, 2, 2, rows, tb), BF), V((nb, 2, 2, rows, tb), BF), V((nb, 2, rows, tb), BF), V((nb, rows, tb), BF),
                        D((7, ns)), D((7, ns)), D((7,)), D((4,)), D((4,)), D((dpn - 1,)), D((dpn - 1,)), D((9,)), D((11,)), D((2,)),
                        D((7, nr)), D((7, nr)), D((12,)), D((12,)), D((4,)), D((4,)), D((dpn - 1,)), D((dpn - 1,)), D((3,)), D((3,)), pltpu.SemaphoreType.REGULAR],
        compiler_params=pltpu.CompilerParams(collective_id=0, has_side_effects=True, vmem_limit_bytes=67043328),
        name="block",
    )(cap, *(w.reshape(-1, 128) for w in (skip, qkv, proj, fc1, fc2)), vectors.reshape(1, nv),
      *(v.reshape(tokens) for v in (block_in, skip_in, out_grad)))
    shape = block_in.shape
    res = hand_out(res[:8]) + (res[8],)
    return tuple(r.reshape(shape) for r in res[:3]) + tuple(r.reshape(-1) for r in res[3:])


def hand_out_kernel(*refs):
    n = (len(refs) - 2) // 3
    src, dst, buf, (first, second) = refs[:n], refs[n:2 * n], refs[2 * n:3 * n], refs[3 * n:]
    ins = [pltpu.make_async_copy(src[i], buf[i], first.at[i]) for i in range(n)]
    outs = [pltpu.make_async_copy(buf[i], dst[i], second.at[i]) for i in range(n)]
    for cp in ins: cp.start()
    for a, b in zip(ins, outs):
        a.wait()
        b.start()
    for cp in outs: cp.wait()


def hand_out(arrays):
    hbm = pl.BlockSpec(memory_space=pl.ANY)
    n = len(arrays)
    return tuple(pl.pallas_call(
        hand_out_kernel,
        out_shape=tuple(jax.ShapeDtypeStruct(v.shape, v.dtype) for v in arrays),
        in_specs=[hbm] * n, out_specs=(hbm,) * n,
        scratch_shapes=[pltpu.VMEM(v.shape, v.dtype) for v in arrays] + [pltpu.SemaphoreType.DMA((n,))] * 2,
        compiler_params=pltpu.CompilerParams(vmem_limit_bytes=67043328),
        name="hand_out",
    )(*arrays))


def whole_rows(width, dp, fsdp, items, heads, hidden, length):
    return (
        fsdp == 4 and dp == 8 and width % (dp * 16) == 0 and items == 1 and hidden == 4 * width
        and width % SPLIT == 0 and -(-length // 16) * 16 % STEP == 0 and width // heads <= 128
    )


def body(block_in, skip_in, out_grad, caption_len, skip_w, qkv_w, proj_w, fc1_w, fc2_w, vectors):
    items, length, width = block_in.shape
    if whole_rows(width, lax.axis_size("dp"), lax.axis_size("fsdp"), items, HEADS, FF, length):
        return block(
            caption_len, skip_w, qkv_w, proj_w, fc1_w, fc2_w, vectors, block_in, skip_in, out_grad,
            lax.axis_size("dp"),
        )
    heads = HEADS
    head_dim = width // heads
    hidden = FF
    rows = items * length
    scale = head_dim ** (-0.5)
    gathered = (
        lax.all_gather(skip_w.astype(jnp.bfloat16), ("dp", "fsdp"), axis=0, tiled=True),
        lax.all_gather(qkv_w.astype(jnp.bfloat16), ("dp", "fsdp"), axis=0, tiled=True),
        lax.all_gather(proj_w.astype(jnp.bfloat16), ("dp", "fsdp"), axis=0, tiled=True),
        lax.all_gather(fc1_w.astype(jnp.bfloat16), ("dp", "fsdp"), axis=0, tiled=True),
        lax.all_gather(fc2_w.astype(jnp.bfloat16), ("dp", "fsdp"), axis=0, tiled=True),
    )
    skip_m, qkv_m, proj_m, fc1_m, fc2_m = unpack(gathered, width, hidden)
    vec = lax.all_gather(vectors, "dp", axis=0, tiled=True)
    gain_one = vec[0:width]
    shift_one = vec[width : 2 * width]
    gain_two = vec[2 * width : 3 * width]
    shift_two = vec[3 * width : 4 * width]
    skip_bias = vec[4 * width : 5 * width]
    proj_bias = vec[5 * width : 6 * width]
    fc2_bias = vec[6 * width : 7 * width]
    fc1_bias = vec[7 * width :]
    valid = key_valid(caption_len, length, CAPTION)
    joined = jnp.concatenate([block_in, skip_in], -1).reshape(rows, 2 * width).astype(jnp.bfloat16)
    first = product(joined, skip_m) + skip_bias
    normed_one = norm_rows(first, gain_one, shift_one).astype(jnp.bfloat16)
    triple = (
        product(normed_one, qkv_m).astype(jnp.bfloat16).reshape(items, length, 3, heads, head_dim)
    )
    query = triple[:, :, 0]
    keys = triple[:, :, 1]
    values = triple[:, :, 2]
    scores = attention_scores(query, keys, valid, scale)
    top = jnp.max(scores, -1, keepdims=True)
    expd = jnp.exp(scores - top)
    total = jnp.sum(expd, -1, keepdims=True)
    probs = expd / total
    log_total = top + jnp.log(total)
    mixed = (
        jnp.einsum(
            "ihst,ithd->ishd",
            probs.astype(jnp.bfloat16),
            values,
            preferred_element_type=jnp.float32,
        )
        .astype(jnp.bfloat16)
        .reshape(rows, width)
    )
    second = first + (product(mixed, proj_m) + proj_bias)
    normed_two = norm_rows(second, gain_two, shift_two).astype(jnp.bfloat16)
    inner = product(normed_two, fc1_m) + fc1_bias
    active = gelu_exact(inner).astype(jnp.bfloat16)
    block_out = second + (product(active, fc2_m) + fc2_bias)
    again = (
        lax.all_gather(skip_w.astype(jnp.bfloat16), ("dp", "fsdp"), axis=0, tiled=True),
        lax.all_gather(qkv_w.astype(jnp.bfloat16), ("dp", "fsdp"), axis=0, tiled=True),
        lax.all_gather(proj_w.astype(jnp.bfloat16), ("dp", "fsdp"), axis=0, tiled=True),
        lax.all_gather(fc1_w.astype(jnp.bfloat16), ("dp", "fsdp"), axis=0, tiled=True),
        lax.all_gather(fc2_w.astype(jnp.bfloat16), ("dp", "fsdp"), axis=0, tiled=True),
    )
    skip_m, qkv_m, proj_m, fc1_m, fc2_m = unpack(again, width, hidden)
    grad_out = out_grad.reshape(rows, width)
    grad_mlp = grad_out.astype(jnp.bfloat16)
    d_fc2_bias = column_sum(grad_mlp)
    d_active = right_product(grad_mlp, fc2_m)
    gelu_value, gelu_pull = jax.vjp(gelu_exact, inner)
    grad_inner = gelu_pull(d_active)[0].astype(jnp.bfloat16)
    d_fc1_bias = column_sum(grad_inner)
    d_normed_two = right_product(grad_inner, fc1_m)
    norm_value_two, norm_pull_two = jax.vjp(norm_rows, second, gain_two, shift_two)
    d_second_norm, d_gain_two, d_shift_two = norm_pull_two(d_normed_two)
    grad_second = grad_out + d_second_norm
    grad_attn = grad_second.astype(jnp.bfloat16)
    d_proj_bias = column_sum(grad_attn)
    grad_mixed = (
        right_product(grad_attn, proj_m)
        .astype(jnp.bfloat16)
        .reshape(items, length, heads, head_dim)
    )
    again_scores = attention_scores(query, keys, valid, scale)
    again_probs = jnp.exp(again_scores - log_total)
    d_probs = jnp.einsum("ishd,ithd->ihst", grad_mixed, values, preferred_element_type=jnp.float32)
    inner_sum = jnp.sum(again_probs * d_probs, -1, keepdims=True)
    grad_scores = (again_probs * (d_probs - inner_sum)).astype(jnp.bfloat16)
    d_query = (
        jnp.einsum("ihst,ithd->ishd", grad_scores, keys, preferred_element_type=jnp.float32) * scale
    )
    d_keys = (
        jnp.einsum("ihst,ishd->ithd", grad_scores, query, preferred_element_type=jnp.float32)
        * scale
    )
    d_values = jnp.einsum(
        "ihst,ishd->ithd",
        again_probs.astype(jnp.bfloat16),
        grad_mixed,
        preferred_element_type=jnp.float32,
    )
    grad_triple = (
        jnp.stack([d_query, d_keys, d_values], 2).astype(jnp.bfloat16).reshape(rows, 3 * width)
    )
    d_normed_one = right_product(grad_triple, qkv_m)
    norm_value_one, norm_pull_one = jax.vjp(norm_rows, first, gain_one, shift_one)
    d_first_norm, d_gain_one, d_shift_one = norm_pull_one(d_normed_one)
    grad_first = (grad_second + d_first_norm).astype(jnp.bfloat16)
    d_skip_bias = column_sum(grad_first)
    grad_joined = right_product(grad_first, skip_m).reshape(items, length, 2 * width)
    in_grad = grad_joined[:, :, 0:width]
    skip_grad = grad_joined[:, :, width:]
    owners = lax.axis_size(("dp", "fsdp"))
    pairs = (
        (joined, grad_first),
        (normed_one, grad_triple),
        (mixed, grad_attn),
        (normed_two, grad_inner),
        (active, grad_mlp),
    )
    shard_sizes = [pair[0].shape[1] * pair[1].shape[1] // owners for pair in pairs]
    blocks = []
    for pair, owner_share in zip(pairs, shard_sizes):
        blocks.append(
            flat_piece(pair[0], pair[1]).reshape(1 * lax.axis_size(("dp", "fsdp")), owner_share)
        )
    owned = lax.psum_scatter(
        jnp.concatenate(blocks, 1), ("dp", "fsdp"), scatter_dimension=0, tiled=True
    ).reshape(-1)
    pieces = []
    offset = 0
    for share in shard_sizes:
        pieces.append(owned[offset : offset + share])
        offset = offset + share
    vec_grad = jnp.concatenate(
        [
            d_gain_one,
            d_shift_one,
            d_gain_two,
            d_shift_two,
            d_skip_bias,
            d_proj_bias,
            d_fc2_bias,
            d_fc1_bias,
        ]
    )
    vec_rows = lax.psum_scatter(vec_grad, "dp", scatter_dimension=0, tiled=True)
    vec_total = lax.psum(vec_rows, "fsdp")
    return (
        block_out.reshape(items, length, width),
        in_grad,
        skip_grad,
        pieces[0],
        pieces[1],
        pieces[2],
        pieces[3],
        pieces[4],
        vec_total,
    )


def solution(mesh):
    placed = (
        P(("dp", "fsdp"), None, None),
        P(("dp", "fsdp"), None, None),
        P(("dp", "fsdp"), None, None),
        P(("dp", "fsdp")),
        P(("dp", "fsdp")),
        P(("dp", "fsdp")),
        P(("dp", "fsdp")),
        P(("dp", "fsdp")),
        P(("dp", "fsdp")),
        P("dp"),
    )
    return jax.shard_map(
        body,
        mesh=mesh,
        in_specs=placed,
        out_specs=(
            P(("dp", "fsdp"), None, None),
            P(("dp", "fsdp"), None, None),
            P(("dp", "fsdp"), None, None),
            P(("dp", "fsdp")),
            P(("dp", "fsdp")),
            P(("dp", "fsdp")),
            P(("dp", "fsdp")),
            P(("dp", "fsdp")),
            P("dp"),
        ),
        check_vma=False,
    )
```

```python
import functools
import math

import jax
import jax.numpy as jnp
from jax import lax
from jax.experimental import pallas as pl
from jax.experimental.pallas import tpu as pltpu
from jax.sharding import PartitionSpec as P

HEADS = 16
FF = 4608
CAPTION = 77


epsilon = 1e-05
masked_value = -1e30


def norm_rows(value, gain, shift):
    center = value - jnp.mean(value, -1, keepdims=True)
    spread = jnp.mean(center * center, -1, keepdims=True)
    return center * lax.rsqrt(spread + epsilon) * gain + shift


def gelu_exact(value):
    return jax.nn.gelu(value, approximate=False)


def key_valid(caption_len, length, caption):
    place = lax.broadcasted_iota(jnp.int32, (caption_len.shape[0], length), 1)
    return (place < 1 + caption_len[:, None]) | (place >= 1 + caption)


def product(left, right):
    return jnp.dot(left, right, preferred_element_type=jnp.float32)


def left_product(left, right):
    return lax.dot_general(
        left, right, (((0,), (0,)), ((), ())), preferred_element_type=jnp.float32
    )


def right_product(left, right):
    return lax.dot_general(
        left, right, (((1,), (1,)), ((), ())), preferred_element_type=jnp.float32
    )


def unpack(flat, width, hidden):
    return (
        flat[0].reshape(2 * width, width),
        flat[1].reshape(width, 3 * width),
        flat[2].reshape(width, width),
        flat[3].reshape(width, hidden),
        flat[4].reshape(hidden, width),
    )


def attention_scores(query, keys, valid, scale):
    raw = jnp.einsum("ishd,ithd->ihst", query, keys, preferred_element_type=jnp.float32) * scale
    return jnp.where(valid[:, None, None, :], raw, masked_value)


def column_sum(value):
    return jnp.sum(value.astype(jnp.float32), 0)


def flat_piece(left, right):
    grad_rows = left_product(left, right).reshape(-1)
    return grad_rows


MESH = pl.DeviceIdType.MESH
BF=jnp.bfloat16; F32=jnp.float32
SPLIT = 384
STEP = 112


def unit_lanes(value, units, chips):
    seg = value.shape[1] // (units * chips)
    return [
        jnp.concatenate([value[:, (s * units + u) * seg : (s * units + u + 1) * seg] for s in range(chips)], 1)
        for u in range(units)
    ]


def row_loop(total, step, fn):
    def one(n, carry):
        fn(pl.ds(pl.multiple_of(n * step, step), step))
        return carry
    lax.fori_loop(0, total // step, one, 0)


def natural_lanes(units, chips):
    seg = units[0].shape[1] // chips
    return jnp.concatenate([u[:, s * seg : (s + 1) * seg] for s in range(chips) for u in units], 1)


def block_kernel(Z, wide, rows, tiles, length, padded,
                 cap_ref, skip_ref, qkv_ref, proj_ref, fc1_ref, fc2_ref, vec_ref, in_ref, sk_ref, og_ref,
                 out_o, in_o, sk_o, skip_g, qkv_g, proj_g, fc1_g, fc2_g, vec_o, skip_o, qp_o, fc1_o, fc2_o, j_o, h0_o, acc_o,
                 skip_f, qkv_f, proj_f, fc1_f, fc2_f, own, keep, give, take, vbuf, vecs, b1s, vpart, vgot, vall, tok,
                 dtg, side, hid, am, t, m, zz, gu, gm, acc, tmp, sums, gacc, wbuf,
                 xl, xr, part, ra1, ra2, ra3, raf, rc1, rc2, rcf, rc3, rb1, rbf, rb2, rb3,
                 send, recv, lsem, psend, precv, vsend, vrecv, isem, osem, wsem,
                 rsend, rrecv, xsend, xrecv, qsend, qrecv, ysend, yrecv, ssend, srecv, free):
    dp = lax.axis_index("dp"); f = lax.axis_index("fsdp")
    z = dp // 2; x = dp % 2; y = f // 2; c = f % 2
    o = 1 - c
    nt = wide // 128
    half = rows // 2
    chips = 4 * Z
    ndp = 2 * Z
    hd = wide // HEADS
    full = length // 16 * 16
    ta, tb, tc = tiles
    A = pl.ds(0, ta); B = pl.ds(ta, tb); C = pl.ds(ta + tb, tc)
    zt = [z + 1 - 2 * (z % 2), lax.rem(z + 2, 4), 3 - z]
    zd = [(i * 2 + x, f) for i in zt]
    middle = (z == 1) | (z == 2)
    ends = (z == 0) | (z == 3)
    xp = (z * 2 + 1 - x, f)
    yp = (dp, (1 - y) * 2 + c)
    pp = (dp, y * 2 + o)
    dps = [(lax.rem(dp + k, ndp), f) for k in range(1, ndp)]
    fs = [(dp, lax.rem(f + k, 4)) for k in range(1, 4)]
    bar = pltpu.get_barrier_semaphore()
    for d in dps + fs:
        pl.semaphore_signal(bar, inc=1, device_id=d, device_id_type=MESH)
    flats = [(skip_ref, skip_f), (qkv_ref, qkv_f), (proj_ref, proj_f), (fc1_ref, fc1_f), (fc2_ref, fc2_f)]
    floads = [pltpu.make_async_copy(a, b, isem.at[n]) for n, (a, b) in enumerate(flats)]
    for cp in floads: cp.start()
    loads = [pltpu.make_async_copy(in_ref.at[:, 0, :], tok.at[0], isem.at[5]), pltpu.make_async_copy(sk_ref.at[:, 0, :], tok.at[1], isem.at[6])]
    for cp in loads: cp.start()
    def remote(src, dst, ssem, rsem, dev):
        return pltpu.make_async_remote_copy(src, dst, ssem, rsem, device_id=dev, device_id_type=MESH)
    @pl.when(ends)
    def _():
        for buf in (ra3, rc2, rb1):
            for b in range(buf.shape[0]): buf[b, 2] = jnp.zeros(buf.shape[2:], BF)
    floads[0].wait()
    for j in range(nt):
        own[0, :, 128 * j:128 * j + 128] = skip_f[pl.ds(j, rows, stride=nt), :].astype(BF)
    pl.semaphore_wait(bar, len(dps) + len(fs))

    waits = []
    def rc(i, slot, src, dst, dev):
        cp = remote(src, dst, send.at[i, slot], recv.at[i, slot], dev)
        cp.start(); waits.append(cp)
    def got(i, slot, dst):
        remote(dst, dst, send.at[i, slot], recv.at[i, slot], pp).wait_recv()
    def unit(i, cc):
        if i == 0: return skip_o.at[:, :, :, cc]
        if i in (1, 2): return qp_o.at[2 * (i - 1) + cc]
        if i in (3, 4): return fc1_o.at[2 * cc + (i - 3)]
        return fc2_o.at[2 * cc + (i - 5)]
    pc = {}
    lc = {}
    def exchange(i, first, second):
        keep[i - 1, 0:half, :] = jnp.where(c == 0, first, second)
        give[i - 1, 0:half, :] = jnp.where(c == 0, second, first)
        pc[i] = remote(give.at[i - 1], take.at[i - 1], psend.at[i - 1], precv.at[i - 1], pp)
        pc[i].start()
    whens = []
    def cond(cp):
        whens.append(cp)
        pl.when(middle)(lambda: cp.start())
    def zsend(i, base, view):
        for k in (1, 2, 3):
            v = view(z)
            cp = remote(v, v, send.at[i, base + k - 1], recv.at[i, base + k - 1], zd[k - 1])
            if k == 3: cond(cp)
            else: cp.start(); waits.append(cp)
    def zforward(i, base, view):
        got(i, base + 1, view(zt[1]))
        v = view(zt[1])
        cond(remote(v, v, send.at[i, base + 3], recv.at[i, base + 2], zd[0]))
    def zgot(i, base, view):
        got(i, base, view(zt[0])); got(i, base + 2, view(zt[2]))
    lc = {}
    def ready(i):
        if i in (1, 2, 3, 4):
            pc[i].wait_recv()
            p = keep[i - 1, 0:half, :]
            q = take[i - 1, 0:half, :]
            lo = jnp.where(c == 0, p, q); hi = jnp.where(c == 0, q, p)
            own[i, :, :] = jnp.concatenate([lo, hi], 0).astype(BF)
        lc[i] = pltpu.make_async_copy(own.at[i], unit(i, c).at[z, x, y], lsem.at[i]); lc[i].start()
    SA, SC, SB = 0, 4, 8
    def gA1(i):
        U = unit(i, c); lc[i].wait()
        zsend(i, SA, lambda t: U.at[t, x, y, :, A])
    def gC1(i):
        rc(i, 12, own.at[i, :, C], unit(i, c).at[z, x, y, :, C], yp)
    def gB1(i):
        rc(i, 13, own.at[i, :, B], unit(i, c).at[z, x, y, :, B], xp)
    def gAF(i):
        U = unit(i, c); zforward(i, SA, lambda t: U.at[t, x, y, :, A])
    def gA2(i):
        U = unit(i, c)
        zgot(i, SA, lambda t: U.at[t, x, y, :, A])
        L = U.at[:, x, y, :, A]
        rc(i, 14, L, L, yp); rc(i, 15, L, L, xp); rc(i, 16, L, L, pp)
    def gA3(i):
        L = unit(i, c).at[:, 1 - x, y, :, A]
        got(i, 15, L); rc(i, 17, L, L, yp); rc(i, 18, L, L, pp)
    def gC2(i):
        U = unit(i, c)
        got(i, 12, U.at[z, x, 1 - y, :, C])
        zsend(i, SC, lambda t: U.at[t, x, :, :, C])
    def gCF(i):
        U = unit(i, c); zforward(i, SC, lambda t: U.at[t, x, :, :, C])
    def gC3(i):
        U = unit(i, c)
        zgot(i, SC, lambda t: U.at[t, x, :, :, C])
        L = U.at[:, x, :, :, C]
        rc(i, 19, L, L, xp); rc(i, 20, L, L, pp)
    def gB2(i):
        U = unit(i, c)
        got(i, 13, U.at[z, 1 - x, y, :, B])
        L = U.at[z, :, y, :, B]
        rc(i, 21, L, L, yp)
    def gB3(i):
        U = unit(i, c)
        got(i, 21, U.at[z, :, 1 - y, :, B])
        zsend(i, SB, lambda t: U.at[t, :, :, :, B])
    def gBF(i):
        U = unit(i, c); zforward(i, SB, lambda t: U.at[t, :, :, :, B])
    def gPA(i):
        U = unit(i, c)
        L = U.at[:, x, 1 - y, :, A]
        got(i, 14, L); rc(i, 22, L, L, pp)
        L = U.at[:, 1 - x, 1 - y, :, A]
        got(i, 17, L); rc(i, 23, L, L, pp)
    def gPC(i):
        L = unit(i, c).at[:, 1 - x, :, :, C]
        got(i, 19, L); rc(i, 24, L, L, pp)
    def gPB(i):
        U = unit(i, c)
        zgot(i, SB, lambda t: U.at[t, :, :, :, B])
        L = U.at[:, :, :, :, B]
        rc(i, 25, L, L, pp)
    def arrived(i):
        U = unit(i, 1 - c)
        got(i, 16, U.at[:, x, y, :, A])
        got(i, 18, U.at[:, 1 - x, y, :, A])
        got(i, 22, U.at[:, x, 1 - y, :, A])
        got(i, 23, U.at[:, 1 - x, 1 - y, :, A])
        got(i, 20, U.at[:, x, :, :, C])
        got(i, 24, U.at[:, 1 - x, :, :, C])
        got(i, 25, U.at[:, :, :, :, B])
    def read(ref, first, stride):
        return jnp.concatenate([ref[pl.ds(first + j, half, stride=stride), :] for j in range(nt)], 1)

    ready(0)
    gB1(0); gC1(0)
    gA1(0)
    vcopies = []
    vbuf[dp] = vec_ref[...].reshape(1, vec_ref.shape[0])
    for k, d in enumerate(dps):
        cp = remote(vbuf.at[dp], vbuf.at[dp], vsend.at[k], vrecv.at[k], d)
        cp.start(); vcopies.append(cp)
    floads[1].wait(); floads[2].wait()
    exchange(1, read(qkv_f, 0, 3 * nt), read(qkv_f, nt, 3 * nt))
    exchange(2, read(qkv_f, 2 * nt, 3 * nt), read(proj_f, 0, nt))
    def prepare_late():
        floads[3].wait(); floads[4].wait()
        for j in range(nt):
            own[5, :, 128 * j:128 * j + 128] = fc2_f[pl.ds(j, rows, stride=nt), :].astype(BF)
            own[6, :, 128 * j:128 * j + 128] = fc2_f[pl.ds(j + nt * rows, rows, stride=nt), :].astype(BF)
        nat = jnp.concatenate([read(fc1_f, nt * v, 4 * nt) for v in range(4)], 1)
        u = unit_lanes(nat, 4, chips)
        exchange(3, u[0], u[2])
        exchange(4, u[1], u[3])

    def keep_out(n, src, dst):
        cp = pltpu.make_async_copy(src, dst, osem.at[n]); cp.start()
        return cp
    def weight(n, ref):
        pltpu.make_async_copy(ref, wbuf.at[n], wsem.at[n]).start()
    def weight_wait(k):
        pltpu.make_async_copy(wbuf.at[k], wbuf.at[k], wsem.at[k]).wait()
    def both_skip():
        for k in range(2):
            for i in range(Z // 2):
                pltpu.make_async_copy(skip_o.at[k * (Z // 2) + i], wbuf.at[k, pl.ds(2 * i, 2)], wsem.at[k]).start()
    def cols(k, l):
        return wbuf[k, :, :, :, :, l].reshape(wide, SPLIT)
    def lanes_loop(fn):
        def one(n, carry):
            fn(pl.ds(pl.multiple_of(n * SPLIT, 128), SPLIT))
            return carry
        lax.fori_loop(0, wide // SPLIT, one, 0)
    def vector(n):
        return vecs[0:1, n * wide:(n + 1) * wide]
    def put_rows(k, src):
        def one(r): tok[k, r, :] = src[r, :]
        row_loop(full, 16, one)
        if length > full: tok[k, full:length, :] = src[full:length, :]
    def norm(src, gain, shift, dst):
        def one(r):
            v = src[r, :]
            cen = v - jnp.mean(v, -1, keepdims=True)
            s = jnp.mean(cen * cen, -1, keepdims=True)
            dst[r, :] = (cen * lax.rsqrt(s + epsilon) * gain + shift).astype(BF)
        row_loop(padded, STEP, one)
    def take_rows(k, dst, at):
        if padded > full: dst[at + (slice(padded - 16, padded), slice(None))] = jnp.zeros((16, wide), dst.dtype)
        def one(r): dst[at + (r, slice(None))] = tok[k, r, :].astype(dst.dtype)
        row_loop(full, 16, one)
        if length > full: dst[at + (slice(full, length), slice(None))] = tok[k, full:length, :].astype(dst.dtype)
    def inputs():
        for cp in loads: cp.wait()
        take_rows(0, dtg, (0,))
        take_rows(1, dtg, (1,))
        pltpu.make_async_copy(og_ref.at[:, 0, :], tok.at[0], isem.at[5]).start()
        def two(r):
            u = unit_lanes(jnp.concatenate([dtg[0, r, :], dtg[1, r, :]], 1), 2, chips)
            side[0, r, :] = u[0]
            side[1, r, :] = u[1]
        row_loop(padded, STEP, two)
        keep_out(0, side, j_o)
    def vectors():
        for k in range(len(dps)):
            remote(vbuf.at[dp], vbuf.at[lax.rem(dp - (k + 1) + ndp, ndp)], vsend.at[k], vrecv.at[k], pp).wait_recv()
        vecs[...] = jnp.concatenate([vbuf[k] for k in range(ndp)], 1)
        b = unit_lanes(vecs[0:1, 7 * wide:11 * wide], 4, chips)
        for u in range(4): b1s[u] = b[u]
        pltpu.make_async_copy(og_ref.at[:, 0, :], tok.at[0], isem.at[5]).wait()
        take_rows(0, gm, ())
        pltpu.make_async_copy(og_ref.at[:, 0, :], tok.at[1], isem.at[6]).start()
    def first_part():
        arrived(0)
        both_skip()
        weight_wait(0); weight_wait(1)
        def one(l):
            v = jnp.dot(dtg[0], cols(0, l), preferred_element_type=F32)
            v = v + jnp.dot(dtg[1], cols(1, l), preferred_element_type=F32)
            hid[:, l] = v + vecs[0:1, pl.ds(4 * wide + l.start, SPLIT)]
        lanes_loop(one)
        norm(hid, vector(0), vector(1), am.at[0])
        keep_out(1, hid, h0_o)
    def project(n, u):
        def one(l):
            t[u, :, l] = jnp.dot(am[0], cols(n, l), preferred_element_type=F32).astype(BF)
        lanes_loop(one)
    def query_keys():
        arrived(1)
        for u in range(2): weight(u, qp_o.at[u])
        def each(u, carry):
            weight_wait(u)
            project(u, u)
            return carry
        lax.fori_loop(0, 2, each, 0)
    def values():
        arrived(2)
        weight(0, qp_o.at[2]); weight(1, qp_o.at[3])
        weight_wait(0)
        project(0, 2)
    def window(h):
        base = pl.multiple_of(jnp.minimum((h * hd) // 128, nt - 2) * 128, 128)
        lane = lax.broadcasted_iota(jnp.int32, (1, 256), 1) + (base - h * hd)
        return pl.ds(base, 256), (lane >= 0) & (lane < hd)
    def attend(first, last):
        cap = cap_ref[0]
        key = lax.broadcasted_iota(jnp.int32, (1, padded), 1)
        live = ((key < 1 + cap) | (key >= 1 + CAPTION)) & (key < length)
        def head(h, carry):
            win, inside = window(h)
            q = jnp.where(inside, t[0, :, win].astype(F32), 0.0).astype(BF)
            s = lax.dot_general(q, t[1, :, win], (((1,), (1,)), ((), ())), preferred_element_type=F32) * hd ** (-0.5)
            s = jnp.where(live, s, masked_value)
            e = jnp.exp(s - jnp.max(s, -1, keepdims=True))
            p = (e / jnp.sum(e, -1, keepdims=True)).astype(BF)
            v = jnp.dot(p, t[2, :, win], preferred_element_type=F32)
            am[1, :, win] = jnp.where(inside, v, am[1, :, win].astype(F32)).astype(BF)
            return carry
        lax.fori_loop(first, last, head, 0)
    def second_part():
        weight_wait(1)
        pltpu.make_async_copy(hid, h0_o, osem.at[1]).wait()
        def one(l):
            v = jnp.dot(am[1], cols(1, l), preferred_element_type=F32)
            h = hid[:, l] + (v + vecs[0:1, pl.ds(5 * wide + l.start, SPLIT)])
            hid[:, l] = h
            acc[:, l] = h + vecs[0:1, pl.ds(6 * wide + l.start, SPLIT)]
        lanes_loop(one)
        keep_out(10, acc, acc_o)
        norm(hid, vector(2), vector(3), m)
    def widen_load(i):
        arrived(i)
        for k in range(2): weight(k, fc1_o.at[2 * k + i - 3])
    def pair_loop(fn, first):
        def one(k, carry):
            fn(k, 2 * k + first)
            return carry
        lax.fori_loop(0, 2, one, 0)
    def widen(k, u):
        weight_wait(k)
        def one(l):
            tmp[:, l] = jnp.dot(m[...], cols(k, l), preferred_element_type=F32)
        lanes_loop(one)
        def two(r):
            v = tmp[r, :] + b1s[u]
            cdf = 0.5 * (1.0 + lax.erf(v * 0.7071067811865476))
            pdf = jnp.exp(-0.5 * v * v) * 0.3989422804014327
            zz[u, r, :] = (v * cdf).astype(BF)
            gu[u, r, :] = (cdf + v * pdf).astype(BF)
        row_loop(padded, STEP, two)
    def narrow_load(i):
        arrived(i)
        for k in range(2): weight(k, fc2_o.at[2 * k + i - 5])
    def narrow(k, u):
        weight_wait(k)
        tmp[...] = jnp.zeros_like(tmp)
        def one(l):
            tmp[...] += lax.dot_general(gm[:, l], cols(k, l), (((1,), (1,)), ((), ())), preferred_element_type=F32)
        lanes_loop(one)
        def two(r):
            gu[u, r, :] = (tmp[r, :] * gu[u, r, :].astype(F32)).astype(BF)
        row_loop(padded, STEP, two)
    def finish():
        pltpu.make_async_copy(acc_o, acc, isem.at[8]).wait()
        for u in range(2): weight(u, fc2_o.at[u])
        def each(u, carry):
            k = u % 2
            weight_wait(k)
            def one(l):
                acc[:, l] += jnp.dot(zz[u], cols(k, l), preferred_element_type=F32)
            lanes_loop(one)
            pl.when(u < 2)(lambda: weight(k, fc2_o.at[u + 2]))
            return carry
        lax.fori_loop(0, 4, each, 0)
    def finish_out():
        pltpu.make_async_copy(tok.at[0], in_o.at[:, 0, :], osem.at[3]).wait()
        put_rows(0, acc)
        keep_out(2, tok.at[0], out_o.at[:, 0, :])

    xcopies = {}
    def swap(n, src, dst):
        xcopies[n] = remote(src, dst, xsend.at[n], xrecv.at[n], pp)
        xcopies[n].start()
    nb = 4
    started = {j: [] for j in range(7)}
    def sc(j, slot, src, dst, dev):
        cp = remote(src, dst, rsend.at[j, slot], rrecv.at[j, slot], dev)
        cp.start(); started[j].append((None, cp))
    def settle(j):
        for which, cp in started[j]:
            if which is None: cp.wait_send()
            else: pl.when(which)(lambda: cp.wait_send())
    def came(j, slot, dst):
        remote(dst, dst, rsend.at[j, slot], rrecv.at[j, slot], pp).wait_recv()
    need = [(0, 1), (2,), (3, 4), (5,), (6, 7), (8, 9), (10, 11)]
    def operands(j):
        if j < 2: return zz.at[2 * c + j], gm, xl.at[j], xr.at[0]
        if j < 4: return m, gu.at[2 * c + j - 2], xl.at[2], xr.at[j - 1]
        if j == 4: return am.at[c], dtg.at[2 + c], xl.at[0], xr.at[0]
        if j == 5: return am.at[0], dtg.at[c], xl.at[1], xr.at[1]
        return side.at[0], side.at[1], xl.at[2], xr.at[2]
    def partial(j):
        for n in need[j]: xcopies[n].wait_recv()
        if j >= nb:
            settle(j - nb)
        b = j % nb
        D = part.at[b]
        l1, r1, l2, r2 = operands(j)
        step = SPLIT
        dims = (((0,), (0,)), ((), ()))
        def chunk(n, carry):
            at = pl.ds(pl.multiple_of(n * step, 128), step)
            r = lax.dot_general(l1[...], r1[:, at], dims, preferred_element_type=F32)
            r = r + lax.dot_general(l2[...], r2[:, at], dims, preferred_element_type=F32)
            D[:, :, :, :, at] = r.reshape(Z, 2, 2, rows, step).astype(BF)
            return carry
        lax.fori_loop(0, wide // step, chunk, 0)
    def reduce1(j):
        partial(j)
        ship(j)
    def ship(j):
        b = j % nb
        D = part.at[b]
        sc(j, 0, D.at[:, 1 - x, 1 - y, :, A], ra1.at[b, 0], yp)
        sc(j, 2, D.at[:, 1 - x, :, :, C], rc1.at[b], xp)
        sc(j, 1, D.at[:, x, 1 - y, :, A], ra1.at[b, 1], yp)
        line_send(j, 12, lambda i: D.at[i, :, :, :, B], rb1.at[b], rbf.at[b])
    def only(j, which, slot, src, dst, dev):
        cp = remote(src, dst, rsend.at[j, slot], rrecv.at[j, slot], dev)
        pl.when(which)(lambda: cp.start())
        return cp
    def line_send(j, base, view, buf, fbuf):
        sc(j, base, view(zt[0]), buf.at[0], zd[0])
        started[j].append((ends, only(j, ends, base + 3, view(zt[2]), fbuf, zd[0])))
        started[j].append((None, only(j, ends, base + 1, view(zt[1]), buf.at[1], zd[1])))
        started[j].append((middle, only(j, middle, base + 2, view(zt[2]), buf.at[2], zd[2])))
    def line_relay(j, base, view, buf, fbuf):
        cp = remote(view(zt[1]), buf.at[1], rsend.at[j, base + 1], rrecv.at[j, base + 1], zd[1])
        @pl.when(middle)
        def _():
            came(j, base + 3, fbuf)
            plus(view(zt[1]), fbuf)
            cp.start()
    def line_came(j, base, buf):
        came(j, base, buf.at[0]); came(j, base + 1, buf.at[1])
        pl.when(middle)(lambda: came(j, base + 2, buf.at[2]))
    def plus(dst, *srcs):
        lead = dst.shape[:-2]
        for n in range(math.prod(lead)):
            at = ()
            for d in reversed(lead):
                at = (n % d,) + at
                n = n // d
            v = dst[at + (slice(None), slice(None))].astype(F32)
            for r in srcs: v = v + r[at + (slice(None), slice(None))].astype(F32)
            dst[at + (slice(None), slice(None))] = v.astype(BF)
    def reduce2(j):
        b = j % nb
        D = part.at[b]
        came(j, 0, ra1.at[b, 0])
        plus(D.at[:, 1 - x, y, :, A], ra1.at[b, 0])
        sc(j, 3, D.at[:, 1 - x, y, :, A], ra2.at[b], xp)
        came(j, 2, rc1.at[b])
        plus(D.at[:, x, :, :, C], rc1.at[b])
        line_send(j, 8, lambda i: D.at[i, x, :, :, C], rc2.at[b], rcf.at[b])
        line_relay(j, 12, lambda i: D.at[i, :, :, :, B], rb1.at[b], rbf.at[b])
    def reduce3(j):
        b = j % nb
        D = part.at[b]
        line_came(j, 12, rb1.at[b])
        plus(D.at[z, :, :, :, B], rb1.at[b, 0], rb1.at[b, 1], rb1.at[b, 2])
        sc(j, 17, D.at[z, :, 1 - y, :, B], rb2.at[b], yp)
        came(j, 1, ra1.at[b, 1])
        came(j, 3, ra2.at[b])
        plus(D.at[:, x, y, :, A], ra1.at[b, 1], ra2.at[b])
        line_send(j, 4, lambda i: D.at[i, x, y, :, A], ra3.at[b], raf.at[b])
        line_relay(j, 8, lambda i: D.at[i, x, :, :, C], rc2.at[b], rcf.at[b])
    def reduce4(j):
        b = j % nb
        D = part.at[b]
        line_relay(j, 4, lambda i: D.at[i, x, y, :, A], ra3.at[b], raf.at[b])
        line_came(j, 8, rc2.at[b])
        plus(D.at[z, x, :, :, C], rc2.at[b, 0], rc2.at[b, 1], rc2.at[b, 2])
        sc(j, 16, D.at[z, x, 1 - y, :, C], rc3.at[b], yp)
        came(j, 17, rb2.at[b])
        plus(D.at[z, :, y, :, B], rb2.at[b])
        sc(j, 18, D.at[z, 1 - x, y, :, B], rb3.at[b], xp)
    pcopies = {}
    def lay(ref, val, first, stride, n):
        for i in range(val.shape[1] // 128):
            ref[pl.ds(first + i, n, stride=stride), :] = val[:, 128 * i:128 * i + 128]
    def reduce5(j):
        b = j % nb
        D = part.at[b]
        line_came(j, 4, ra3.at[b])
        came(j, 16, rc3.at[b])
        came(j, 18, rb3.at[b])
        p = D[z, x, y, :, A].astype(F32)
        for k in range(3):
            p = p + ra3[b, k].astype(F32)
        q = D[z, x, y, :, B].astype(F32) + rb3[b].astype(F32)
        r = D[z, x, y, :, C].astype(F32) + rc3[b].astype(F32)
        v = jnp.concatenate([p, q, r], 1)
        if j in (0, 1):
            lay(fc2_f, v, j * rows * nt, nt, rows)
            if j == 1: keep_out(9, fc2_f, fc2_g)
        elif j == 6:
            lay(skip_f, v, 0, nt, rows)
            keep_out(5, skip_f, skip_g)
        else:
            lo = v[0:half]; hi = v[half:rows]
            keep[j - 2, 0:half, :] = jnp.where(c == 0, lo, hi)
            give[j - 2, 0:half, :] = jnp.where(c == 0, hi, lo)
            cp = remote(give.at[j - 2], take.at[j - 2], qsend.at[j - 2], qrecv.at[j - 2], pp)
            cp.start(); pcopies[j] = cp
    def both(j):
        pcopies[j].wait_recv()
        p = keep[j - 2, 0:half, :]; q = take[j - 2, 0:half, :]
        return jnp.where(c == 0, p, q), jnp.where(c == 0, q, p)
    def settle_pair(j):
        if j == 3:
            p, q = both(2), both(3)
            lay(fc1_f, natural_lanes([p[0], q[0], p[1], q[1]], chips), 0, 4 * nt, half)
            keep_out(8, fc1_f, fc1_g)
        elif j == 5:
            first, second = both(5)
            lay(qkv_f, first, 0, 3 * nt, half)
            lay(qkv_f, second, nt, 3 * nt, half)
            keep_out(6, qkv_f, qkv_g)
        elif j == 4:
            first, second = both(4)
            lay(qkv_f, first, 2 * nt, 3 * nt, half)
            lay(proj_f, second, 0, nt, half)
            keep_out(7, proj_f, proj_g)


    def zero(n): gacc[n] = jnp.zeros((8, wide), F32)
    def add_rows(n, v):
        gacc[n] += jnp.sum(v.reshape(v.shape[0] // 8, 8, wide), 0)
    def close(n):
        return jnp.sum(gacc[n], 0, keepdims=True)
    def column_sums(src):
        zero(0)
        def one(r): add_rows(0, src[r, :].astype(F32))
        row_loop(padded, STEP, one)
        return close(0)
    def norm_back(dy, src, gain, fn):
        zero(0); zero(1); zero(2)
        def one(r):
            d = dy[r, :]
            v = src[r, :]
            cen = v - jnp.mean(v, -1, keepdims=True)
            rs = lax.rsqrt(jnp.mean(cen * cen, -1, keepdims=True) + epsilon)
            xh = cen * rs
            dx = d * gain
            g = rs * (dx - jnp.mean(dx, -1, keepdims=True) - xh * jnp.mean(dx * xh, -1, keepdims=True))
            add_rows(0, d * xh)
            add_rows(1, d)
            fn(r, g)
        row_loop(padded, STEP, one)
    def turned(lhs, n, fresh):
        if fresh: tmp[...] = jnp.zeros_like(tmp)
        def one(l):
            tmp[...] += lax.dot_general(lhs[:, l], cols(n, l), (((1,), (1,)), ((), ())), preferred_element_type=F32)
        lanes_loop(one)
    def widen_back():
        tmp[...] = jnp.zeros_like(tmp)
        def each(u, carry):
            k = u % 2
            weight_wait(k)
            turned(gu.at[u], k, False)
            pl.when(u < 2)(lambda: weight(k, fc1_o.at[u + 2]))
            sums[7 + u] = column_sums(gu.at[u])
            return carry
        lax.fori_loop(0, 4, each, 0)
    def norm_two():
        weight(0, qp_o.at[3])
        pltpu.make_async_copy(og_ref.at[:, 0, :], tok.at[1], isem.at[6]).wait()
        pltpu.make_async_copy(acc, acc_o, osem.at[10]).wait()
        take_rows(1, acc, ())
        def fn(r, g):
            s = acc[r, :] + g
            acc[r, :] = s
            b = s.astype(BF)
            dtg[3, r, :] = b
            add_rows(2, b.astype(F32))
        norm_back(tmp, hid, vector(2), fn)
        sums[2] = close(0); sums[3] = close(1); sums[5] = close(2)
        pltpu.make_async_copy(h0_o, hid, isem.at[5]).start()
        sums[6] = column_sums(gm)
        weight_wait(0)
        turned(dtg.at[3], 0, True)
        def two(r): side[0, r, :] = tmp[r, :].astype(BF)
        row_loop(padded, STEP, two)
    def attend_back(first, last):
        cap = cap_ref[0]
        key = lax.broadcasted_iota(jnp.int32, (padded, 1), 0)
        live = ((key < 1 + cap) | (key >= 1 + CAPTION)) & (key < length)
        def head(h, carry):
            win, inside = window(h)
            q = jnp.where(inside, t[0, :, win].astype(F32), 0.0).astype(BF)
            k = t[1, :, win]
            g = jnp.where(inside, side[0, :, win].astype(F32), 0.0).astype(BF)
            s = lax.dot_general(k, q, (((1,), (1,)), ((), ())), preferred_element_type=F32) * hd ** (-0.5)
            s = jnp.where(live, s, masked_value)
            e = jnp.exp(s - jnp.max(s, 0, keepdims=True))
            p = e * (1.0 / jnp.sum(e, 0, keepdims=True))
            d = lax.dot_general(t[2, :, win], g, (((1,), (1,)), ((), ())), preferred_element_type=F32)
            ds = (p * (d - jnp.sum(p * d, 0, keepdims=True))).astype(BF)
            dq = lax.dot_general(ds, k, (((0,), (0,)), ((), ())), preferred_element_type=F32) * hd ** (-0.5)
            dk = jnp.dot(ds, q, preferred_element_type=F32) * hd ** (-0.5)
            dv = jnp.dot(p.astype(BF), g, preferred_element_type=F32)
            for i, v in enumerate((dq, dk, dv)):
                dtg[i, :, win] = jnp.where(inside, v, dtg[i, :, win].astype(F32)).astype(BF)
            return carry
        lax.fori_loop(first, last, head, 0)
    def late_left():
        pl.semaphore_signal(free, inc=1, device_id=pp, device_id_type=MESH)
        pl.semaphore_wait(free, 1)
        pltpu.make_async_copy(side, j_o, osem.at[0]).wait()
        swap(6, am.at[o], xl.at[0])
        swap(8, am.at[0], xl.at[1])
        swap(10, j_o.at[o], xl.at[2])
    def late_right():
        swap(7, dtg.at[2 + o], xr.at[0])
        swap(9, dtg.at[o], xr.at[1])
        pltpu.make_async_copy(j_o.at[c], side.at[0], isem.at[7]).start()
        weight(0, qp_o.at[0]); weight(1, qp_o.at[1])
    def project_back():
        tmp[...] = jnp.zeros_like(tmp)
        def each(i, carry):
            k = i % 2
            weight_wait(k)
            turned(dtg.at[i], k, False)
            pl.when(i == 0)(lambda: weight(0, qp_o.at[2]))
            return carry
        lax.fori_loop(0, 3, each, 0)
    def norm_one():
        pltpu.make_async_copy(h0_o, hid, isem.at[5]).wait()
        both_skip()
        def fn(r, g):
            b = (acc[r, :] + g).astype(BF)
            side[1, r, :] = b
            add_rows(2, b.astype(F32))
        norm_back(tmp, hid, vector(0), fn)
        sums[0] = close(0); sums[1] = close(1); sums[4] = close(2)
        swap(11, side.at[1], xr.at[2])
        pltpu.make_async_copy(acc_o, acc, isem.at[8]).start()
    def join_back(i, dst):
        weight_wait(i)
        turned(side.at[1], i, True)
        put_rows(i, tmp)
        keep_out(3 + i, tok.at[i], dst.at[:, 0, :])
    nv = vpart.shape[2]
    def vec_send():
        total = jnp.concatenate([sums[i] for i in range(7)] + [natural_lanes([sums[7 + u] for u in range(4)], chips)], 1)
        for k in range(ndp): vpart[k] = total[:, k * nv:(k + 1) * nv]
        for k, d in enumerate(dps):
            cp = remote(vpart.at[d[0]], vgot.at[k], ysend.at[k], yrecv.at[k], d)
            cp.start(); vcopies.append(cp)
    def vec_first():
        s = vpart[dp]
        for k in range(len(dps)):
            remote(vgot.at[k], vgot.at[k], ysend.at[k], yrecv.at[k], pp).wait_recv()
            s = s + vgot[k]
        vall[f] = s
        for k, d in enumerate(fs):
            cp = remote(vall.at[f], vall.at[f], ssend.at[k], srecv.at[k], d)
            cp.start(); vcopies.append(cp)
    def vec_last():
        for k in range(3):
            src = lax.rem(f - (k + 1) + 4, 4)
            remote(vall.at[src], vall.at[src], ssend.at[k], srecv.at[k], pp).wait_recv()
        vec_o[...] = (vall[0] + vall[1] + vall[2] + vall[3]).reshape(vec_o.shape[0])

    ready(1); gB1(1); gB2(0)
    gC2(0); gAF(0); gA2(0)
    ready(2); gB1(2)
    gC1(1); gA1(1); gB2(1)
    gB3(0)
    prepare_late()
    gCF(0); gC3(0); gA3(0)
    inputs()
    gC2(1); gAF(1); gA2(1)
    ready(3); gB1(3)
    gC1(2); gA1(2); gB2(2)
    gB3(1)
    vectors()
    gCF(1); gC3(1); gA3(1)
    gBF(0); gPA(0); gPC(0)
    gC2(2); gAF(2); gA2(2)
    ready(4); gB1(4)
    gC1(3); gA1(3); gB2(3)
    gB3(2)
    gCF(2); gC3(2); gA3(2)
    gBF(1); gPA(1); gPC(1)
    gPB(0)
    first_part()
    gC2(3); gAF(3); gA2(3)
    ready(5); gB1(5)
    gC1(4); gA1(4); gB2(4)
    gB3(3)
    gCF(3); gC3(3); gA3(3)
    gBF(2); gPA(2); gPC(2)
    gPB(1)
    query_keys()
    gC2(4); gAF(4); gA2(4)
    ready(6); gB1(6)
    gC1(5); gA1(5); gB2(5)
    gB3(4)
    gCF(4); gC3(4); gA3(4)
    gBF(3); gPA(3); gPC(3)
    gPB(2)
    values()
    attend(0, 5)
    gC2(5); gAF(5); gA2(5)
    gC1(6); gA1(6); gB2(6)
    gB3(5)
    attend(5, 11)
    gCF(5); gC3(5); gA3(5)
    gBF(4); gPA(4); gPC(4)
    gPB(3)
    attend(11, 16)
    second_part()
    gC2(6); gAF(6); gA2(6)
    gB3(6)
    widen_load(3)
    widen(0, 0)
    gCF(6); gC3(6); gA3(6)
    gBF(5); gPA(5); gPC(5)
    gPB(4)
    widen(1, 2)
    for cp in pc.values(): cp.wait_send()
    swap(0, zz.at[2 * o], xl.at[0])
    swap(1, gm, xr.at[0])
    swap(3, m, xl.at[2])
    widen_load(4)
    reduce1(0)
    gBF(6); gPA(6); gPC(6); gPB(5)
    pair_loop(widen, 1)
    swap(2, zz.at[2 * o + 1], xl.at[1])
    narrow_load(5)
    reduce1(1)
    gPB(6)
    reduce2(0)
    pair_loop(narrow, 0)
    swap(4, gu.at[2 * o], xr.at[1])
    narrow_load(6)
    reduce3(0)
    reduce1(2); reduce2(1)
    pair_loop(narrow, 1)
    swap(5, gu.at[2 * o + 1], xr.at[2])
    weight(0, fc1_o.at[0]); weight(1, fc1_o.at[1])
    reduce4(0)
    reduce1(3)
    reduce2(2); reduce3(1)
    widen_back()
    late_left()
    norm_two()
    reduce5(0); reduce4(1)
    attend_back(0, 5)
    reduce2(3); reduce3(2)
    attend_back(5, 16)
    late_right()
    reduce1(4)
    reduce5(1); reduce4(2); reduce3(3)
    reduce1(5); reduce2(4)
    project_back()
    reduce5(2); reduce4(3)
    norm_one()
    vec_send()
    pltpu.make_async_copy(j_o.at[c], side.at[0], isem.at[7]).wait()
    reduce2(5); reduce3(4)
    reduce1(6)
    vec_first()
    join_back(0, in_o)
    reduce5(3); reduce4(4)
    join_back(1, sk_o)
    settle_pair(3)
    reduce3(5); reduce2(6)
    vec_last()
    reduce5(4); reduce4(5); settle_pair(4)
    finish()
    finish_out()
    reduce3(6)
    reduce5(5); settle_pair(5)
    reduce4(6)
    reduce5(6)
    pltpu.make_async_copy(tok.at[1], sk_o.at[:, 0, :], osem.at[4]).wait()
    pltpu.make_async_copy(tok.at[0], out_o.at[:, 0, :], osem.at[2]).wait()
    for n, (a, b) in zip((5, 6, 7, 8, 9), ((skip_f, skip_g), (qkv_f, qkv_g), (proj_f, proj_g), (fc1_f, fc1_g), (fc2_f, fc2_g))):
        pltpu.make_async_copy(a, b, osem.at[n]).wait()
    for j in range(3, 7): settle(j)
    for cp in whens: pl.when(middle)(lambda: cp.wait_send())
    for cp in waits: cp.wait_send()
    for cp in pcopies.values(): cp.wait_send()
    for cp in vcopies: cp.wait_send()
    for cp in xcopies.values(): cp.wait_send()


def block(cap, skip, qkv, proj, fc1, fc2, vectors, block_in, skip_in, out_grad, dpn):
    _, length, wide = block_in.shape
    Z = dpn // 2; rows = skip.shape[0] // wide
    padded = -(-length // 16) * 16
    nt = wide // 128
    tb = 128 * max(1, nt // 9); tc = 128 * (nt // 3); ta = wide - tb - tc
    tiles = (ta, tb, tc)
    U = (Z, 2, 2, rows, wide)
    hbm = pl.BlockSpec(memory_space=pl.ANY); vm = pl.BlockSpec(memory_space=pltpu.VMEM)
    ns = 26
    nr = 19
    nv = vectors.shape[0]
    D = pltpu.SemaphoreType.DMA
    V = pltpu.VMEM
    hp = -(-rows // 2 // 8) * 8
    S = jax.ShapeDtypeStruct
    act = (padded, wide)
    flat = [(w.shape[0] // 128, 128) for w in (skip, qkv, proj, fc1, fc2)]
    tokens = (length, 1, wide)
    nb = 4
    res = pl.pallas_call(
        functools.partial(block_kernel, Z, wide, rows, tiles, length, padded),
        out_shape=(S(tokens, F32),) * 3 + tuple(S(s, F32) for s in flat) + (S((nv,), F32),
                   S((Z, 2, 2, 2, rows, wide), BF), S((4,) + U, BF), S((4,) + U, BF), S((4,) + U, BF), S((2,) + act, BF), S(act, F32), S(act, F32)),
        in_specs=[pl.BlockSpec(memory_space=pltpu.SMEM)] + [hbm] * 5 + [vm] + [hbm] * 3,
        out_specs=(hbm,) * 8 + (vm,) + (hbm,) * 7,
        scratch_shapes=[V(s, F32) for s in flat] + [
                        V((7, rows, wide), BF), V((4, hp, wide), F32), V((4, hp, wide), F32), V((4, hp, wide), F32),
                        V((dpn, 1, nv), F32), V((1, nv * dpn), F32), V((4, 1, wide), F32), V((dpn, 1, nv), F32), V((dpn - 1, 1, nv), F32), V((4, 1, nv), F32),
                        V((2, length, wide), F32),
                        V((4,) + act, BF), V((2,) + act, BF), V(act, F32), V((2,) + act, BF), V((3,) + act, BF), V(act, BF), V((4,) + act, BF), V((4,) + act, BF), V(act, BF),
                        V(act, F32), V(act, F32), V((11, 1, wide), F32), V((3, 8, wide), F32), V((2,) + U, BF),
                        V((3,) + act, BF), V((3,) + act, BF), V((nb,) + U, BF),
                        V((nb, 2, Z, rows, ta), BF), V((nb, Z, rows, ta), BF), V((nb, 3, rows, ta), BF), V((nb, rows, ta), BF),
                        V((nb, Z, 2, rows, tc), BF), V((nb, 3, 2, rows, tc), BF), V((nb, 2, rows, tc), BF), V((nb, rows, tc), BF),
                        V((nb, 3, 2, 2, rows, tb), BF), V((nb, 2, 2, rows, tb), BF), V((nb, 2, rows, tb), BF), V((nb, rows, tb), BF),
                        D((7, ns)), D((7, ns)), D((7,)), D((4,)), D((4,)), D((dpn - 1,)), D((dpn - 1,)), D((9,)), D((11,)), D((2,)),
                        D((7, nr)), D((7, nr)), D((12,)), D((12,)), D((4,)), D((4,)), D((dpn - 1,)), D((dpn - 1,)), D((3,)), D((3,)), pltpu.SemaphoreType.REGULAR],
        compiler_params=pltpu.CompilerParams(collective_id=0, has_side_effects=True, vmem_limit_bytes=67043328),
        name="block",
    )(cap, *(w.reshape(-1, 128) for w in (skip, qkv, proj, fc1, fc2)), vectors,
      *(v.reshape(tokens) for v in (block_in, skip_in, out_grad)))
    shape = block_in.shape
    res = hand_out(res[:9])
    return tuple(r.reshape(shape) for r in res[:3]) + tuple(r.reshape(-1) for r in res[3:])


def hand_out_kernel(*refs):
    n = (len(refs) - 2) // 3
    src, dst, buf, (first, second) = refs[:n], refs[n:2 * n], refs[2 * n:3 * n], refs[3 * n:]
    ins = [pltpu.make_async_copy(src[i], buf[i], first.at[i]) for i in range(n)]
    outs = [pltpu.make_async_copy(buf[i], dst[i], second.at[i]) for i in range(n)]
    for cp in ins: cp.start()
    for a, b in zip(ins, outs):
        a.wait()
        b.start()
    for cp in outs: cp.wait()


def hand_out(arrays):
    hbm = pl.BlockSpec(memory_space=pl.ANY)
    n = len(arrays)
    return tuple(pl.pallas_call(
        hand_out_kernel,
        out_shape=tuple(jax.ShapeDtypeStruct(v.shape, v.dtype) for v in arrays),
        in_specs=[hbm] * n, out_specs=(hbm,) * n,
        scratch_shapes=[pltpu.VMEM(v.shape, v.dtype) for v in arrays] + [pltpu.SemaphoreType.DMA((n,))] * 2,
        compiler_params=pltpu.CompilerParams(vmem_limit_bytes=67043328),
        name="hand_out",
    )(*arrays))


def whole_rows(width, dp, fsdp, items, heads, hidden, length):
    return (
        fsdp == 4 and dp == 8 and width % (dp * 16) == 0 and items == 1 and hidden == 4 * width
        and width % SPLIT == 0 and -(-length // 16) * 16 % STEP == 0 and width // heads <= 128
    )


def body(block_in, skip_in, out_grad, caption_len, skip_w, qkv_w, proj_w, fc1_w, fc2_w, vectors):
    items, length, width = block_in.shape
    if whole_rows(width, lax.axis_size("dp"), lax.axis_size("fsdp"), items, HEADS, FF, length):
        return block(
            caption_len, skip_w, qkv_w, proj_w, fc1_w, fc2_w, vectors, block_in, skip_in, out_grad,
            lax.axis_size("dp"),
        )
    heads = HEADS
    head_dim = width // heads
    hidden = FF
    rows = items * length
    scale = head_dim ** (-0.5)
    gathered = (
        lax.all_gather(skip_w.astype(jnp.bfloat16), ("dp", "fsdp"), axis=0, tiled=True),
        lax.all_gather(qkv_w.astype(jnp.bfloat16), ("dp", "fsdp"), axis=0, tiled=True),
        lax.all_gather(proj_w.astype(jnp.bfloat16), ("dp", "fsdp"), axis=0, tiled=True),
        lax.all_gather(fc1_w.astype(jnp.bfloat16), ("dp", "fsdp"), axis=0, tiled=True),
        lax.all_gather(fc2_w.astype(jnp.bfloat16), ("dp", "fsdp"), axis=0, tiled=True),
    )
    skip_m, qkv_m, proj_m, fc1_m, fc2_m = unpack(gathered, width, hidden)
    vec = lax.all_gather(vectors, "dp", axis=0, tiled=True)
    gain_one = vec[0:width]
    shift_one = vec[width : 2 * width]
    gain_two = vec[2 * width : 3 * width]
    shift_two = vec[3 * width : 4 * width]
    skip_bias = vec[4 * width : 5 * width]
    proj_bias = vec[5 * width : 6 * width]
    fc2_bias = vec[6 * width : 7 * width]
    fc1_bias = vec[7 * width :]
    valid = key_valid(caption_len, length, CAPTION)
    joined = jnp.concatenate([block_in, skip_in], -1).reshape(rows, 2 * width).astype(jnp.bfloat16)
    first = product(joined, skip_m) + skip_bias
    normed_one = norm_rows(first, gain_one, shift_one).astype(jnp.bfloat16)
    triple = (
        product(normed_one, qkv_m).astype(jnp.bfloat16).reshape(items, length, 3, heads, head_dim)
    )
    query = triple[:, :, 0]
    keys = triple[:, :, 1]
    values = triple[:, :, 2]
    scores = attention_scores(query, keys, valid, scale)
    top = jnp.max(scores, -1, keepdims=True)
    expd = jnp.exp(scores - top)
    total = jnp.sum(expd, -1, keepdims=True)
    probs = expd / total
    log_total = top + jnp.log(total)
    mixed = (
        jnp.einsum(
            "ihst,ithd->ishd",
            probs.astype(jnp.bfloat16),
            values,
            preferred_element_type=jnp.float32,
        )
        .astype(jnp.bfloat16)
        .reshape(rows, width)
    )
    second = first + (product(mixed, proj_m) + proj_bias)
    normed_two = norm_rows(second, gain_two, shift_two).astype(jnp.bfloat16)
    inner = product(normed_two, fc1_m) + fc1_bias
    active = gelu_exact(inner).astype(jnp.bfloat16)
    block_out = second + (product(active, fc2_m) + fc2_bias)
    again = (
        lax.all_gather(skip_w.astype(jnp.bfloat16), ("dp", "fsdp"), axis=0, tiled=True),
        lax.all_gather(qkv_w.astype(jnp.bfloat16), ("dp", "fsdp"), axis=0, tiled=True),
        lax.all_gather(proj_w.astype(jnp.bfloat16), ("dp", "fsdp"), axis=0, tiled=True),
        lax.all_gather(fc1_w.astype(jnp.bfloat16), ("dp", "fsdp"), axis=0, tiled=True),
        lax.all_gather(fc2_w.astype(jnp.bfloat16), ("dp", "fsdp"), axis=0, tiled=True),
    )
    skip_m, qkv_m, proj_m, fc1_m, fc2_m = unpack(again, width, hidden)
    grad_out = out_grad.reshape(rows, width)
    grad_mlp = grad_out.astype(jnp.bfloat16)
    d_fc2_bias = column_sum(grad_mlp)
    d_active = right_product(grad_mlp, fc2_m)
    gelu_value, gelu_pull = jax.vjp(gelu_exact, inner)
    grad_inner = gelu_pull(d_active)[0].astype(jnp.bfloat16)
    d_fc1_bias = column_sum(grad_inner)
    d_normed_two = right_product(grad_inner, fc1_m)
    norm_value_two, norm_pull_two = jax.vjp(norm_rows, second, gain_two, shift_two)
    d_second_norm, d_gain_two, d_shift_two = norm_pull_two(d_normed_two)
    grad_second = grad_out + d_second_norm
    grad_attn = grad_second.astype(jnp.bfloat16)
    d_proj_bias = column_sum(grad_attn)
    grad_mixed = (
        right_product(grad_attn, proj_m)
        .astype(jnp.bfloat16)
        .reshape(items, length, heads, head_dim)
    )
    again_scores = attention_scores(query, keys, valid, scale)
    again_probs = jnp.exp(again_scores - log_total)
    d_probs = jnp.einsum("ishd,ithd->ihst", grad_mixed, values, preferred_element_type=jnp.float32)
    inner_sum = jnp.sum(again_probs * d_probs, -1, keepdims=True)
    grad_scores = (again_probs * (d_probs - inner_sum)).astype(jnp.bfloat16)
    d_query = (
        jnp.einsum("ihst,ithd->ishd", grad_scores, keys, preferred_element_type=jnp.float32) * scale
    )
    d_keys = (
        jnp.einsum("ihst,ishd->ithd", grad_scores, query, preferred_element_type=jnp.float32)
        * scale
    )
    d_values = jnp.einsum(
        "ihst,ishd->ithd",
        again_probs.astype(jnp.bfloat16),
        grad_mixed,
        preferred_element_type=jnp.float32,
    )
    grad_triple = (
        jnp.stack([d_query, d_keys, d_values], 2).astype(jnp.bfloat16).reshape(rows, 3 * width)
    )
    d_normed_one = right_product(grad_triple, qkv_m)
    norm_value_one, norm_pull_one = jax.vjp(norm_rows, first, gain_one, shift_one)
    d_first_norm, d_gain_one, d_shift_one = norm_pull_one(d_normed_one)
    grad_first = (grad_second + d_first_norm).astype(jnp.bfloat16)
    d_skip_bias = column_sum(grad_first)
    grad_joined = right_product(grad_first, skip_m).reshape(items, length, 2 * width)
    in_grad = grad_joined[:, :, 0:width]
    skip_grad = grad_joined[:, :, width:]
    owners = lax.axis_size(("dp", "fsdp"))
    pairs = (
        (joined, grad_first),
        (normed_one, grad_triple),
        (mixed, grad_attn),
        (normed_two, grad_inner),
        (active, grad_mlp),
    )
    shard_sizes = [pair[0].shape[1] * pair[1].shape[1] // owners for pair in pairs]
    blocks = []
    for pair, owner_share in zip(pairs, shard_sizes):
        blocks.append(
            flat_piece(pair[0], pair[1]).reshape(1 * lax.axis_size(("dp", "fsdp")), owner_share)
        )
    owned = lax.psum_scatter(
        jnp.concatenate(blocks, 1), ("dp", "fsdp"), scatter_dimension=0, tiled=True
    ).reshape(-1)
    pieces = []
    offset = 0
    for share in shard_sizes:
        pieces.append(owned[offset : offset + share])
        offset = offset + share
    vec_grad = jnp.concatenate(
        [
            d_gain_one,
            d_shift_one,
            d_gain_two,
            d_shift_two,
            d_skip_bias,
            d_proj_bias,
            d_fc2_bias,
            d_fc1_bias,
        ]
    )
    vec_rows = lax.psum_scatter(vec_grad, "dp", scatter_dimension=0, tiled=True)
    vec_total = lax.psum(vec_rows, "fsdp")
    return (
        block_out.reshape(items, length, width),
        in_grad,
        skip_grad,
        pieces[0],
        pieces[1],
        pieces[2],
        pieces[3],
        pieces[4],
        vec_total,
    )


def solution(mesh):
    placed = (
        P(("dp", "fsdp"), None, None),
        P(("dp", "fsdp"), None, None),
        P(("dp", "fsdp"), None, None),
        P(("dp", "fsdp")),
        P(("dp", "fsdp")),
        P(("dp", "fsdp")),
        P(("dp", "fsdp")),
        P(("dp", "fsdp")),
        P(("dp", "fsdp")),
        P("dp"),
    )
    return jax.shard_map(
        body,
        mesh=mesh,
        in_specs=placed,
        out_specs=(
            P(("dp", "fsdp"), None, None),
            P(("dp", "fsdp"), None, None),
            P(("dp", "fsdp"), None, None),
            P(("dp", "fsdp")),
            P(("dp", "fsdp")),
            P(("dp", "fsdp")),
            P(("dp", "fsdp")),
            P(("dp", "fsdp")),
            P("dp"),
        ),
        check_vma=False,
    )
```

```python
import functools
import math

import jax
import jax.numpy as jnp
from jax import lax
from jax.experimental import pallas as pl
from jax.experimental.pallas import tpu as pltpu
from jax.sharding import PartitionSpec as P

HEADS = 16
FF = 4608
CAPTION = 77


epsilon = 1e-05
masked_value = -1e30


def norm_rows(value, gain, shift):
    center = value - jnp.mean(value, -1, keepdims=True)
    spread = jnp.mean(center * center, -1, keepdims=True)
    return center * lax.rsqrt(spread + epsilon) * gain + shift


def gelu_exact(value):
    return jax.nn.gelu(value, approximate=False)


def key_valid(caption_len, length, caption):
    place = lax.broadcasted_iota(jnp.int32, (caption_len.shape[0], length), 1)
    return (place < 1 + caption_len[:, None]) | (place >= 1 + caption)


def product(left, right):
    return jnp.dot(left, right, preferred_element_type=jnp.float32)


def left_product(left, right):
    return lax.dot_general(
        left, right, (((0,), (0,)), ((), ())), preferred_element_type=jnp.float32
    )


def right_product(left, right):
    return lax.dot_general(
        left, right, (((1,), (1,)), ((), ())), preferred_element_type=jnp.float32
    )


def unpack(flat, width, hidden):
    return (
        flat[0].reshape(2 * width, width),
        flat[1].reshape(width, 3 * width),
        flat[2].reshape(width, width),
        flat[3].reshape(width, hidden),
        flat[4].reshape(hidden, width),
    )


def attention_scores(query, keys, valid, scale):
    raw = jnp.einsum("ishd,ithd->ihst", query, keys, preferred_element_type=jnp.float32) * scale
    return jnp.where(valid[:, None, None, :], raw, masked_value)


def column_sum(value):
    return jnp.sum(value.astype(jnp.float32), 0)


def flat_piece(left, right):
    grad_rows = left_product(left, right).reshape(-1)
    return grad_rows


MESH = pl.DeviceIdType.MESH
BF=jnp.bfloat16; F32=jnp.float32
SPLIT = 384
STEP = 112


def unit_lanes(value, units, chips):
    seg = value.shape[1] // (units * chips)
    return [
        jnp.concatenate([value[:, (s * units + u) * seg : (s * units + u + 1) * seg] for s in range(chips)], 1)
        for u in range(units)
    ]


def row_loop(total, step, fn):
    def one(n, carry):
        fn(pl.ds(pl.multiple_of(n * step, step), step))
        return carry
    lax.fori_loop(0, total // step, one, 0)


def natural_lanes(units, chips):
    seg = units[0].shape[1] // chips
    return jnp.concatenate([u[:, s * seg : (s + 1) * seg] for s in range(chips) for u in units], 1)


def block_kernel(Z, wide, rows, tiles, length, padded,
                 cap_ref, skip_ref, qkv_ref, proj_ref, fc1_ref, fc2_ref, vec_ref, in_ref, sk_ref, og_ref,
                 out_o, in_o, sk_o, skip_g, qkv_g, proj_g, fc1_g, fc2_g, vec_o, skip_o, qp_o, fc1_o, fc2_o, j_o, h0_o, acc_o,
                 skip_f, qkv_f, proj_f, fc1_f, fc2_f, own, keep, give, take, vbuf, vecs, b1s, vpart, vgot, vall, tok,
                 dtg, side, hid, am, t, m, zz, gu, gm, acc, tmp, sums, gacc, wbuf,
                 xl, xr, part, ra1, ra2, ra3, raf, rc1, rc2, rcf, rc3, rb1, rbf, rb2, rb3,
                 send, recv, lsem, psend, precv, vsend, vrecv, isem, osem, wsem,
                 rsend, rrecv, xsend, xrecv, qsend, qrecv, ysend, yrecv, ssend, srecv, free):
    dp = lax.axis_index("dp"); f = lax.axis_index("fsdp")
    z = dp // 2; x = dp % 2; y = f // 2; c = f % 2
    o = 1 - c
    nt = wide // 128
    half = rows // 2
    chips = 4 * Z
    ndp = 2 * Z
    hd = wide // HEADS
    full = length // 16 * 16
    ta, tb, tc = tiles
    A = pl.ds(0, ta); B = pl.ds(ta, tb); C = pl.ds(ta + tb, tc)
    zt = [z + 1 - 2 * (z % 2), lax.rem(z + 2, 4), 3 - z]
    zd = [(i * 2 + x, f) for i in zt]
    middle = (z == 1) | (z == 2)
    ends = (z == 0) | (z == 3)
    xp = (z * 2 + 1 - x, f)
    yp = (dp, (1 - y) * 2 + c)
    pp = (dp, y * 2 + o)
    dps = [(lax.rem(dp + k, ndp), f) for k in range(1, ndp)]
    fs = [(dp, lax.rem(f + k, 4)) for k in range(1, 4)]
    bar = pltpu.get_barrier_semaphore()
    for d in dps + fs:
        pl.semaphore_signal(bar, inc=1, device_id=d, device_id_type=MESH)
    flats = [(skip_ref, skip_f), (qkv_ref, qkv_f), (proj_ref, proj_f), (fc1_ref, fc1_f), (fc2_ref, fc2_f)]
    floads = [pltpu.make_async_copy(a, b, isem.at[n]) for n, (a, b) in enumerate(flats)]
    for cp in floads: cp.start()
    loads = [pltpu.make_async_copy(in_ref.at[:, 0, :], tok.at[0], isem.at[5]), pltpu.make_async_copy(sk_ref.at[:, 0, :], tok.at[1], isem.at[6])]
    for cp in loads: cp.start()
    def remote(src, dst, ssem, rsem, dev):
        return pltpu.make_async_remote_copy(src, dst, ssem, rsem, device_id=dev, device_id_type=MESH)
    @pl.when(ends)
    def _():
        for buf in (ra3, rc2, rb1):
            for b in range(buf.shape[0]): buf[b, 2] = jnp.zeros(buf.shape[2:], BF)
    floads[0].wait()
    for j in range(nt):
        own[0, :, 128 * j:128 * j + 128] = skip_f[pl.ds(j, rows, stride=nt), :].astype(BF)
    pl.semaphore_wait(bar, len(dps) + len(fs))

    waits = []
    def rc(i, slot, src, dst, dev):
        cp = remote(src, dst, send.at[i, slot], recv.at[i, slot], dev)
        cp.start(); waits.append(cp)
    def got(i, slot, dst):
        remote(dst, dst, send.at[i, slot], recv.at[i, slot], pp).wait_recv()
    def unit(i, cc):
        if i == 0: return skip_o.at[:, :, :, cc]
        if i in (1, 2): return qp_o.at[2 * (i - 1) + cc]
        if i in (3, 4): return fc1_o.at[2 * cc + (i - 3)]
        return fc2_o.at[2 * cc + (i - 5)]
    pc = {}
    lc = {}
    def exchange(i, first, second):
        keep[i - 1, 0:half, :] = jnp.where(c == 0, first, second)
        give[i - 1, 0:half, :] = jnp.where(c == 0, second, first)
        pc[i] = remote(give.at[i - 1], take.at[i - 1], psend.at[i - 1], precv.at[i - 1], pp)
        pc[i].start()
    whens = []
    def cond(cp):
        whens.append(cp)
        pl.when(middle)(lambda: cp.start())
    def zsend(i, base, view):
        for k in (1, 2, 3):
            v = view(z)
            cp = remote(v, v, send.at[i, base + k - 1], recv.at[i, base + k - 1], zd[k - 1])
            if k == 3: cond(cp)
            else: cp.start(); waits.append(cp)
    def zforward(i, base, view):
        got(i, base + 1, view(zt[1]))
        v = view(zt[1])
        cond(remote(v, v, send.at[i, base + 3], recv.at[i, base + 2], zd[0]))
    def zgot(i, base, view):
        got(i, base, view(zt[0])); got(i, base + 2, view(zt[2]))
    lc = {}
    def ready(i):
        if i in (1, 2, 3, 4):
            pc[i].wait_recv()
            p = keep[i - 1, 0:half, :]
            q = take[i - 1, 0:half, :]
            lo = jnp.where(c == 0, p, q); hi = jnp.where(c == 0, q, p)
            own[i, :, :] = jnp.concatenate([lo, hi], 0).astype(BF)
        lc[i] = pltpu.make_async_copy(own.at[i], unit(i, c).at[z, x, y], lsem.at[i]); lc[i].start()
    SA, SC, SB = 0, 4, 8
    def gA1(i):
        U = unit(i, c); lc[i].wait()
        zsend(i, SA, lambda t: U.at[t, x, y, :, A])
    def gC1(i):
        rc(i, 12, own.at[i, :, C], unit(i, c).at[z, x, y, :, C], yp)
    def gB1(i):
        rc(i, 13, own.at[i, :, B], unit(i, c).at[z, x, y, :, B], xp)
    def gAF(i):
        U = unit(i, c); zforward(i, SA, lambda t: U.at[t, x, y, :, A])
    def gA2(i):
        U = unit(i, c)
        zgot(i, SA, lambda t: U.at[t, x, y, :, A])
        L = U.at[:, x, y, :, A]
        rc(i, 14, L, L, yp); rc(i, 15, L, L, xp); rc(i, 16, L, L, pp)
    def gA3(i):
        L = unit(i, c).at[:, 1 - x, y, :, A]
        got(i, 15, L); rc(i, 17, L, L, yp); rc(i, 18, L, L, pp)
    def gC2(i):
        U = unit(i, c)
        got(i, 12, U.at[z, x, 1 - y, :, C])
        zsend(i, SC, lambda t: U.at[t, x, :, :, C])
    def gCF(i):
        U = unit(i, c); zforward(i, SC, lambda t: U.at[t, x, :, :, C])
    def gC3(i):
        U = unit(i, c)
        zgot(i, SC, lambda t: U.at[t, x, :, :, C])
        L = U.at[:, x, :, :, C]
        rc(i, 19, L, L, xp); rc(i, 20, L, L, pp)
    def gB2(i):
        U = unit(i, c)
        got(i, 13, U.at[z, 1 - x, y, :, B])
        L = U.at[z, :, y, :, B]
        rc(i, 21, L, L, yp)
    def gB3(i):
        U = unit(i, c)
        got(i, 21, U.at[z, :, 1 - y, :, B])
        zsend(i, SB, lambda t: U.at[t, :, :, :, B])
    def gBF(i):
        U = unit(i, c); zforward(i, SB, lambda t: U.at[t, :, :, :, B])
    def gPA(i):
        U = unit(i, c)
        L = U.at[:, x, 1 - y, :, A]
        got(i, 14, L); rc(i, 22, L, L, pp)
        L = U.at[:, 1 - x, 1 - y, :, A]
        got(i, 17, L); rc(i, 23, L, L, pp)
    def gPC(i):
        L = unit(i, c).at[:, 1 - x, :, :, C]
        got(i, 19, L); rc(i, 24, L, L, pp)
    def gPB(i):
        U = unit(i, c)
        zgot(i, SB, lambda t: U.at[t, :, :, :, B])
        L = U.at[:, :, :, :, B]
        rc(i, 25, L, L, pp)
    def arrived(i):
        U = unit(i, 1 - c)
        got(i, 16, U.at[:, x, y, :, A])
        got(i, 18, U.at[:, 1 - x, y, :, A])
        got(i, 22, U.at[:, x, 1 - y, :, A])
        got(i, 23, U.at[:, 1 - x, 1 - y, :, A])
        got(i, 20, U.at[:, x, :, :, C])
        got(i, 24, U.at[:, 1 - x, :, :, C])
        got(i, 25, U.at[:, :, :, :, B])
    def read(ref, first, stride):
        return jnp.concatenate([ref[pl.ds(first + j, half, stride=stride), :] for j in range(nt)], 1)

    ready(0)
    gB1(0); gC1(0)
    gA1(0)
    vcopies = []
    vbuf[dp] = vec_ref[...].reshape(1, vec_ref.shape[0])
    for k, d in enumerate(dps):
        cp = remote(vbuf.at[dp], vbuf.at[dp], vsend.at[k], vrecv.at[k], d)
        cp.start(); vcopies.append(cp)
    floads[1].wait(); floads[2].wait()
    exchange(1, read(qkv_f, 0, 3 * nt), read(qkv_f, nt, 3 * nt))
    exchange(2, read(qkv_f, 2 * nt, 3 * nt), read(proj_f, 0, nt))
    def prepare_late():
        floads[3].wait(); floads[4].wait()
        for j in range(nt):
            own[5, :, 128 * j:128 * j + 128] = fc2_f[pl.ds(j, rows, stride=nt), :].astype(BF)
            own[6, :, 128 * j:128 * j + 128] = fc2_f[pl.ds(j + nt * rows, rows, stride=nt), :].astype(BF)
        nat = jnp.concatenate([read(fc1_f, nt * v, 4 * nt) for v in range(4)], 1)
        u = unit_lanes(nat, 4, chips)
        exchange(3, u[0], u[2])
        exchange(4, u[1], u[3])

    def keep_out(n, src, dst):
        cp = pltpu.make_async_copy(src, dst, osem.at[n]); cp.start()
        return cp
    def weight(n, ref):
        pltpu.make_async_copy(ref, wbuf.at[n], wsem.at[n]).start()
    def weight_wait(k):
        pltpu.make_async_copy(wbuf.at[k], wbuf.at[k], wsem.at[k]).wait()
    def both_skip():
        for k in range(2):
            for i in range(Z // 2):
                pltpu.make_async_copy(skip_o.at[k * (Z // 2) + i], wbuf.at[k, pl.ds(2 * i, 2)], wsem.at[k]).start()
    def cols(k, l):
        return wbuf[k, :, :, :, :, l].reshape(wide, SPLIT)
    def lanes_loop(fn):
        def one(n, carry):
            fn(pl.ds(pl.multiple_of(n * SPLIT, 128), SPLIT))
            return carry
        lax.fori_loop(0, wide // SPLIT, one, 0)
    def vector(n):
        return vecs[0:1, n * wide:(n + 1) * wide]
    def put_rows(k, src):
        def one(r): tok[k, r, :] = src[r, :]
        row_loop(full, 16, one)
        if length > full: tok[k, full:length, :] = src[full:length, :]
    def norm(src, gain, shift, dst):
        def one(r):
            v = src[r, :]
            cen = v - jnp.mean(v, -1, keepdims=True)
            s = jnp.mean(cen * cen, -1, keepdims=True)
            dst[r, :] = (cen * lax.rsqrt(s + epsilon) * gain + shift).astype(BF)
        row_loop(padded, STEP, one)
    def take_rows(k, dst, at):
        if padded > full: dst[at + (slice(padded - 16, padded), slice(None))] = jnp.zeros((16, wide), dst.dtype)
        def one(r): dst[at + (r, slice(None))] = tok[k, r, :].astype(dst.dtype)
        row_loop(full, 16, one)
        if length > full: dst[at + (slice(full, length), slice(None))] = tok[k, full:length, :].astype(dst.dtype)
    def inputs():
        for cp in loads: cp.wait()
        take_rows(0, dtg, (0,))
        take_rows(1, dtg, (1,))
        pltpu.make_async_copy(og_ref.at[:, 0, :], tok.at[0], isem.at[5]).start()
        def two(r):
            u = unit_lanes(jnp.concatenate([dtg[0, r, :], dtg[1, r, :]], 1), 2, chips)
            side[0, r, :] = u[0]
            side[1, r, :] = u[1]
        row_loop(padded, STEP, two)
        keep_out(0, side, j_o)
    def vectors():
        for k in range(len(dps)):
            remote(vbuf.at[dp], vbuf.at[lax.rem(dp - (k + 1) + ndp, ndp)], vsend.at[k], vrecv.at[k], pp).wait_recv()
        vecs[...] = jnp.concatenate([vbuf[k] for k in range(ndp)], 1)
        b = unit_lanes(vecs[0:1, 7 * wide:11 * wide], 4, chips)
        for u in range(4): b1s[u] = b[u]
        pltpu.make_async_copy(og_ref.at[:, 0, :], tok.at[0], isem.at[5]).wait()
        take_rows(0, gm, ())
        pltpu.make_async_copy(og_ref.at[:, 0, :], tok.at[1], isem.at[6]).start()
    def first_part():
        arrived(0)
        both_skip()
        weight_wait(0); weight_wait(1)
        def one(l):
            v = jnp.dot(dtg[0], cols(0, l), preferred_element_type=F32)
            v = v + jnp.dot(dtg[1], cols(1, l), preferred_element_type=F32)
            hid[:, l] = v + vecs[0:1, pl.ds(4 * wide + l.start, SPLIT)]
        lanes_loop(one)
        norm(hid, vector(0), vector(1), am.at[0])
        keep_out(1, hid, h0_o)
    def project(n, u):
        def one(l):
            t[u, :, l] = jnp.dot(am[0], cols(n, l), preferred_element_type=F32).astype(BF)
        lanes_loop(one)
    def query_keys():
        arrived(1)
        for u in range(2): weight(u, qp_o.at[u])
        def each(u, carry):
            weight_wait(u)
            project(u, u)
            return carry
        lax.fori_loop(0, 2, each, 0)
    def values():
        arrived(2)
        weight(0, qp_o.at[2]); weight(1, qp_o.at[3])
        weight_wait(0)
        project(0, 2)
    def window(h):
        base = pl.multiple_of(jnp.minimum((h * hd) // 128, nt - 2) * 128, 128)
        lane = lax.broadcasted_iota(jnp.int32, (1, 256), 1) + (base - h * hd)
        return pl.ds(base, 256), (lane >= 0) & (lane < hd)
    def attend(first, last):
        cap = cap_ref[0]
        key = lax.broadcasted_iota(jnp.int32, (1, padded), 1)
        live = ((key < 1 + cap) | (key >= 1 + CAPTION)) & (key < length)
        def head(h, carry):
            win, inside = window(h)
            q = jnp.where(inside, t[0, :, win].astype(F32), 0.0).astype(BF)
            s = lax.dot_general(q, t[1, :, win], (((1,), (1,)), ((), ())), preferred_element_type=F32) * hd ** (-0.5)
            s = jnp.where(live, s, masked_value)
            e = jnp.exp(s - jnp.max(s, -1, keepdims=True))
            p = (e / jnp.sum(e, -1, keepdims=True)).astype(BF)
            v = jnp.dot(p, t[2, :, win], preferred_element_type=F32)
            am[1, :, win] = jnp.where(inside, v, am[1, :, win].astype(F32)).astype(BF)
            return carry
        lax.fori_loop(first, last, head, 0)
    def second_part():
        weight_wait(1)
        pltpu.make_async_copy(hid, h0_o, osem.at[1]).wait()
        def one(l):
            v = jnp.dot(am[1], cols(1, l), preferred_element_type=F32)
            h = hid[:, l] + (v + vecs[0:1, pl.ds(5 * wide + l.start, SPLIT)])
            hid[:, l] = h
            acc[:, l] = h + vecs[0:1, pl.ds(6 * wide + l.start, SPLIT)]
        lanes_loop(one)
        keep_out(10, acc, acc_o)
        norm(hid, vector(2), vector(3), m)
    def widen_load(i):
        arrived(i)
        for k in range(2): weight(k, fc1_o.at[2 * k + i - 3])
    def pair_loop(fn, first):
        def one(k, carry):
            fn(k, 2 * k + first)
            return carry
        lax.fori_loop(0, 2, one, 0)
    def widen(k, u):
        weight_wait(k)
        def one(l):
            tmp[:, l] = jnp.dot(m[...], cols(k, l), preferred_element_type=F32)
        lanes_loop(one)
        def two(r):
            v = tmp[r, :] + b1s[u]
            cdf = 0.5 * (1.0 + lax.erf(v * 0.7071067811865476))
            pdf = jnp.exp(-0.5 * v * v) * 0.3989422804014327
            zz[u, r, :] = (v * cdf).astype(BF)
            gu[u, r, :] = (cdf + v * pdf).astype(BF)
        row_loop(padded, STEP, two)
    def narrow_load(i):
        arrived(i)
        for k in range(2): weight(k, fc2_o.at[2 * k + i - 5])
    def narrow(k, u):
        weight_wait(k)
        tmp[...] = jnp.zeros_like(tmp)
        def one(l):
            tmp[...] += lax.dot_general(gm[:, l], cols(k, l), (((1,), (1,)), ((), ())), preferred_element_type=F32)
        lanes_loop(one)
        def two(r):
            gu[u, r, :] = (tmp[r, :] * gu[u, r, :].astype(F32)).astype(BF)
        row_loop(padded, STEP, two)
    def finish():
        pltpu.make_async_copy(acc_o, acc, isem.at[8]).wait()
        for u in range(2): weight(u, fc2_o.at[u])
        def each(u, carry):
            k = u % 2
            weight_wait(k)
            def one(l):
                acc[:, l] += jnp.dot(zz[u], cols(k, l), preferred_element_type=F32)
            lanes_loop(one)
            pl.when(u < 2)(lambda: weight(k, fc2_o.at[u + 2]))
            return carry
        lax.fori_loop(0, 4, each, 0)
    def finish_out():
        pltpu.make_async_copy(tok.at[0], in_o.at[:, 0, :], osem.at[3]).wait()
        put_rows(0, acc)
        keep_out(2, tok.at[0], out_o.at[:, 0, :])

    xcopies = {}
    def swap(n, src, dst):
        xcopies[n] = remote(src, dst, xsend.at[n], xrecv.at[n], pp)
        xcopies[n].start()
    nb = 4
    started = {j: [] for j in range(7)}
    def sc(j, slot, src, dst, dev):
        cp = remote(src, dst, rsend.at[j, slot], rrecv.at[j, slot], dev)
        cp.start(); started[j].append((None, cp))
    def settle(j):
        for which, cp in started[j]:
            if which is None: cp.wait_send()
            else: pl.when(which)(lambda: cp.wait_send())
    def came(j, slot, dst):
        remote(dst, dst, rsend.at[j, slot], rrecv.at[j, slot], pp).wait_recv()
    need = [(0, 1), (2,), (3, 4), (5,), (6, 7), (8, 9), (10, 11)]
    def operands(j):
        if j < 2: return zz.at[2 * c + j], gm, xl.at[j], xr.at[0]
        if j < 4: return m, gu.at[2 * c + j - 2], xl.at[2], xr.at[j - 1]
        if j == 4: return am.at[c], dtg.at[2 + c], xl.at[0], xr.at[0]
        if j == 5: return am.at[0], dtg.at[c], xl.at[1], xr.at[1]
        return side.at[0], side.at[1], xl.at[2], xr.at[2]
    def partial(j):
        for n in need[j]: xcopies[n].wait_recv()
        if j >= nb:
            settle(j - nb)
        b = j % nb
        D = part.at[b]
        l1, r1, l2, r2 = operands(j)
        step = SPLIT
        dims = (((0,), (0,)), ((), ()))
        def chunk(n, carry):
            at = pl.ds(pl.multiple_of(n * step, 128), step)
            r = lax.dot_general(l1[...], r1[:, at], dims, preferred_element_type=F32)
            r = r + lax.dot_general(l2[...], r2[:, at], dims, preferred_element_type=F32)
            D[:, :, :, :, at] = r.reshape(Z, 2, 2, rows, step).astype(BF)
            return carry
        lax.fori_loop(0, wide // step, chunk, 0)
    def reduce1(j):
        partial(j)
        ship(j)
    def ship(j):
        b = j % nb
        D = part.at[b]
        sc(j, 0, D.at[:, 1 - x, 1 - y, :, A], ra1.at[b, 0], yp)
        sc(j, 2, D.at[:, 1 - x, :, :, C], rc1.at[b], xp)
        sc(j, 1, D.at[:, x, 1 - y, :, A], ra1.at[b, 1], yp)
        line_send(j, 12, lambda i: D.at[i, :, :, :, B], rb1.at[b], rbf.at[b])
    def only(j, which, slot, src, dst, dev):
        cp = remote(src, dst, rsend.at[j, slot], rrecv.at[j, slot], dev)
        pl.when(which)(lambda: cp.start())
        return cp
    def line_send(j, base, view, buf, fbuf):
        sc(j, base, view(zt[0]), buf.at[0], zd[0])
        started[j].append((ends, only(j, ends, base + 3, view(zt[2]), fbuf, zd[0])))
        started[j].append((None, only(j, ends, base + 1, view(zt[1]), buf.at[1], zd[1])))
        started[j].append((middle, only(j, middle, base + 2, view(zt[2]), buf.at[2], zd[2])))
    def line_relay(j, base, view, buf, fbuf):
        cp = remote(view(zt[1]), buf.at[1], rsend.at[j, base + 1], rrecv.at[j, base + 1], zd[1])
        @pl.when(middle)
        def _():
            came(j, base + 3, fbuf)
            plus(view(zt[1]), fbuf)
            cp.start()
    def line_came(j, base, buf):
        came(j, base, buf.at[0]); came(j, base + 1, buf.at[1])
        pl.when(middle)(lambda: came(j, base + 2, buf.at[2]))
    def plus(dst, *srcs):
        lead = dst.shape[:-2]
        for n in range(math.prod(lead)):
            at = ()
            for d in reversed(lead):
                at = (n % d,) + at
                n = n // d
            v = dst[at + (slice(None), slice(None))].astype(F32)
            for r in srcs: v = v + r[at + (slice(None), slice(None))].astype(F32)
            dst[at + (slice(None), slice(None))] = v.astype(BF)
    def reduce2(j):
        b = j % nb
        D = part.at[b]
        came(j, 0, ra1.at[b, 0])
        plus(D.at[:, 1 - x, y, :, A], ra1.at[b, 0])
        sc(j, 3, D.at[:, 1 - x, y, :, A], ra2.at[b], xp)
        came(j, 2, rc1.at[b])
        plus(D.at[:, x, :, :, C], rc1.at[b])
        line_send(j, 8, lambda i: D.at[i, x, :, :, C], rc2.at[b], rcf.at[b])
        line_relay(j, 12, lambda i: D.at[i, :, :, :, B], rb1.at[b], rbf.at[b])
    def reduce3(j):
        b = j % nb
        D = part.at[b]
        line_came(j, 12, rb1.at[b])
        plus(D.at[z, :, :, :, B], rb1.at[b, 0], rb1.at[b, 1], rb1.at[b, 2])
        sc(j, 17, D.at[z, :, 1 - y, :, B], rb2.at[b], yp)
        came(j, 1, ra1.at[b, 1])
        came(j, 3, ra2.at[b])
        plus(D.at[:, x, y, :, A], ra1.at[b, 1], ra2.at[b])
        line_send(j, 4, lambda i: D.at[i, x, y, :, A], ra3.at[b], raf.at[b])
        line_relay(j, 8, lambda i: D.at[i, x, :, :, C], rc2.at[b], rcf.at[b])
    def reduce4(j):
        b = j % nb
        D = part.at[b]
        line_relay(j, 4, lambda i: D.at[i, x, y, :, A], ra3.at[b], raf.at[b])
        line_came(j, 8, rc2.at[b])
        plus(D.at[z, x, :, :, C], rc2.at[b, 0], rc2.at[b, 1], rc2.at[b, 2])
        sc(j, 16, D.at[z, x, 1 - y, :, C], rc3.at[b], yp)
        came(j, 17, rb2.at[b])
        plus(D.at[z, :, y, :, B], rb2.at[b])
        sc(j, 18, D.at[z, 1 - x, y, :, B], rb3.at[b], xp)
    pcopies = {}
    def lay(ref, val, first, stride, n):
        for i in range(val.shape[1] // 128):
            ref[pl.ds(first + i, n, stride=stride), :] = val[:, 128 * i:128 * i + 128]
    def reduce5(j):
        b = j % nb
        D = part.at[b]
        line_came(j, 4, ra3.at[b])
        came(j, 16, rc3.at[b])
        came(j, 18, rb3.at[b])
        p = D[z, x, y, :, A].astype(F32)
        for k in range(3):
            p = p + ra3[b, k].astype(F32)
        q = D[z, x, y, :, B].astype(F32) + rb3[b].astype(F32)
        r = D[z, x, y, :, C].astype(F32) + rc3[b].astype(F32)
        v = jnp.concatenate([p, q, r], 1)
        if j in (0, 1):
            lay(fc2_f, v, j * rows * nt, nt, rows)
            if j == 1: keep_out(9, fc2_f, fc2_g)
        elif j == 6:
            lay(skip_f, v, 0, nt, rows)
            keep_out(5, skip_f, skip_g)
        else:
            lo = v[0:half]; hi = v[half:rows]
            keep[j - 2, 0:half, :] = jnp.where(c == 0, lo, hi)
            give[j - 2, 0:half, :] = jnp.where(c == 0, hi, lo)
            cp = remote(give.at[j - 2], take.at[j - 2], qsend.at[j - 2], qrecv.at[j - 2], pp)
            cp.start(); pcopies[j] = cp
    def both(j):
        pcopies[j].wait_recv()
        p = keep[j - 2, 0:half, :]; q = take[j - 2, 0:half, :]
        return jnp.where(c == 0, p, q), jnp.where(c == 0, q, p)
    def settle_pair(j):
        if j == 3:
            p, q = both(2), both(3)
            lay(fc1_f, natural_lanes([p[0], q[0], p[1], q[1]], chips), 0, 4 * nt, half)
            keep_out(8, fc1_f, fc1_g)
        elif j == 5:
            first, second = both(5)
            lay(qkv_f, first, 0, 3 * nt, half)
            lay(qkv_f, second, nt, 3 * nt, half)
            keep_out(6, qkv_f, qkv_g)
        elif j == 4:
            first, second = both(4)
            lay(qkv_f, first, 2 * nt, 3 * nt, half)
            lay(proj_f, second, 0, nt, half)
            keep_out(7, proj_f, proj_g)


    def zero(n): gacc[n] = jnp.zeros((8, wide), F32)
    def add_rows(n, v):
        gacc[n] += jnp.sum(v.reshape(v.shape[0] // 8, 8, wide), 0)
    def close(n):
        return jnp.sum(gacc[n], 0, keepdims=True)
    def column_sums(src):
        zero(0)
        def one(r): add_rows(0, src[r, :].astype(F32))
        row_loop(padded, STEP, one)
        return close(0)
    def norm_back(dy, src, gain, fn):
        zero(0); zero(1); zero(2)
        def one(r):
            d = dy[r, :]
            v = src[r, :]
            cen = v - jnp.mean(v, -1, keepdims=True)
            rs = lax.rsqrt(jnp.mean(cen * cen, -1, keepdims=True) + epsilon)
            xh = cen * rs
            dx = d * gain
            g = rs * (dx - jnp.mean(dx, -1, keepdims=True) - xh * jnp.mean(dx * xh, -1, keepdims=True))
            add_rows(0, d * xh)
            add_rows(1, d)
            fn(r, g)
        row_loop(padded, STEP, one)
    def turned(lhs, n, fresh):
        if fresh: tmp[...] = jnp.zeros_like(tmp)
        def one(l):
            tmp[...] += lax.dot_general(lhs[:, l], cols(n, l), (((1,), (1,)), ((), ())), preferred_element_type=F32)
        lanes_loop(one)
    def widen_back():
        tmp[...] = jnp.zeros_like(tmp)
        def each(u, carry):
            k = u % 2
            weight_wait(k)
            turned(gu.at[u], k, False)
            pl.when(u < 2)(lambda: weight(k, fc1_o.at[u + 2]))
            sums[7 + u] = column_sums(gu.at[u])
            return carry
        lax.fori_loop(0, 4, each, 0)
    def norm_two():
        weight(0, qp_o.at[3])
        pltpu.make_async_copy(og_ref.at[:, 0, :], tok.at[1], isem.at[6]).wait()
        pltpu.make_async_copy(acc, acc_o, osem.at[10]).wait()
        take_rows(1, acc, ())
        def fn(r, g):
            s = acc[r, :] + g
            acc[r, :] = s
            b = s.astype(BF)
            dtg[3, r, :] = b
            add_rows(2, b.astype(F32))
        norm_back(tmp, hid, vector(2), fn)
        sums[2] = close(0); sums[3] = close(1); sums[5] = close(2)
        pltpu.make_async_copy(h0_o, hid, isem.at[5]).start()
        sums[6] = column_sums(gm)
        weight_wait(0)
        turned(dtg.at[3], 0, True)
        def two(r): side[0, r, :] = tmp[r, :].astype(BF)
        row_loop(padded, STEP, two)
    def attend_back(first, last):
        cap = cap_ref[0]
        key = lax.broadcasted_iota(jnp.int32, (padded, 1), 0)
        live = ((key < 1 + cap) | (key >= 1 + CAPTION)) & (key < length)
        def head(h, carry):
            win, inside = window(h)
            q = jnp.where(inside, t[0, :, win].astype(F32), 0.0).astype(BF)
            k = t[1, :, win]
            g = jnp.where(inside, side[0, :, win].astype(F32), 0.0).astype(BF)
            s = lax.dot_general(k, q, (((1,), (1,)), ((), ())), preferred_element_type=F32) * hd ** (-0.5)
            s = jnp.where(live, s, masked_value)
            e = jnp.exp(s - jnp.max(s, 0, keepdims=True))
            p = e * (1.0 / jnp.sum(e, 0, keepdims=True))
            d = lax.dot_general(t[2, :, win], g, (((1,), (1,)), ((), ())), preferred_element_type=F32)
            ds = (p * (d - jnp.sum(p * d, 0, keepdims=True))).astype(BF)
            dq = lax.dot_general(ds, k, (((0,), (0,)), ((), ())), preferred_element_type=F32) * hd ** (-0.5)
            dk = jnp.dot(ds, q, preferred_element_type=F32) * hd ** (-0.5)
            dv = jnp.dot(p.astype(BF), g, preferred_element_type=F32)
            for i, v in enumerate((dq, dk, dv)):
                dtg[i, :, win] = jnp.where(inside, v, dtg[i, :, win].astype(F32)).astype(BF)
            return carry
        lax.fori_loop(first, last, head, 0)
    def late_left():
        pl.semaphore_signal(free, inc=1, device_id=pp, device_id_type=MESH)
        pl.semaphore_wait(free, 1)
        pltpu.make_async_copy(side, j_o, osem.at[0]).wait()
        swap(6, am.at[o], xl.at[0])
        swap(8, am.at[0], xl.at[1])
        swap(10, j_o.at[o], xl.at[2])
    def late_right():
        swap(7, dtg.at[2 + o], xr.at[0])
        swap(9, dtg.at[o], xr.at[1])
        pltpu.make_async_copy(j_o.at[c], side.at[0], isem.at[7]).start()
        weight(0, qp_o.at[0]); weight(1, qp_o.at[1])
    def project_back():
        tmp[...] = jnp.zeros_like(tmp)
        def each(i, carry):
            k = i % 2
            weight_wait(k)
            turned(dtg.at[i], k, False)
            pl.when(i == 0)(lambda: weight(0, qp_o.at[2]))
            return carry
        lax.fori_loop(0, 3, each, 0)
    def norm_one():
        pltpu.make_async_copy(h0_o, hid, isem.at[5]).wait()
        both_skip()
        def fn(r, g):
            b = (acc[r, :] + g).astype(BF)
            side[1, r, :] = b
            add_rows(2, b.astype(F32))
        norm_back(tmp, hid, vector(0), fn)
        sums[0] = close(0); sums[1] = close(1); sums[4] = close(2)
        swap(11, side.at[1], xr.at[2])
        pltpu.make_async_copy(acc_o, acc, isem.at[8]).start()
    def join_back(i, dst):
        weight_wait(i)
        turned(side.at[1], i, True)
        put_rows(i, tmp)
        keep_out(3 + i, tok.at[i], dst.at[:, 0, :])
    nv = vpart.shape[2]
    def vec_send():
        total = jnp.concatenate([sums[i] for i in range(7)] + [natural_lanes([sums[7 + u] for u in range(4)], chips)], 1)
        for k in range(ndp): vpart[k] = total[:, k * nv:(k + 1) * nv]
        for k, d in enumerate(dps):
            cp = remote(vpart.at[d[0]], vgot.at[k], ysend.at[k], yrecv.at[k], d)
            cp.start(); vcopies.append(cp)
    def vec_first():
        s = vpart[dp]
        for k in range(len(dps)):
            remote(vgot.at[k], vgot.at[k], ysend.at[k], yrecv.at[k], pp).wait_recv()
            s = s + vgot[k]
        vall[f] = s
        for k, d in enumerate(fs):
            cp = remote(vall.at[f], vall.at[f], ssend.at[k], srecv.at[k], d)
            cp.start(); vcopies.append(cp)
    def vec_last():
        for k in range(3):
            src = lax.rem(f - (k + 1) + 4, 4)
            remote(vall.at[src], vall.at[src], ssend.at[k], srecv.at[k], pp).wait_recv()
        vec_o[...] = (vall[0] + vall[1] + vall[2] + vall[3]).reshape(vec_o.shape[0])

    ready(1); gB1(1); gB2(0)
    gC2(0); gAF(0); gA2(0)
    ready(2); gB1(2)
    gC1(1); gA1(1); gB2(1)
    gB3(0)
    gCF(0); gC3(0); gA3(0)
    prepare_late()
    inputs()
    gC2(1); gAF(1); gA2(1)
    ready(3); gB1(3)
    gC1(2); gA1(2); gB2(2)
    gB3(1)
    vectors()
    gCF(1); gC3(1); gA3(1)
    gBF(0); gPA(0); gPC(0)
    gC2(2); gAF(2); gA2(2)
    ready(4); gB1(4)
    gC1(3); gA1(3); gB2(3)
    gB3(2)
    gCF(2); gC3(2); gA3(2)
    gBF(1); gPA(1); gPC(1)
    gPB(0)
    first_part()
    gC2(3); gAF(3); gA2(3)
    ready(5); gB1(5)
    gC1(4); gA1(4); gB2(4)
    gB3(3)
    gCF(3); gC3(3); gA3(3)
    gBF(2); gPA(2); gPC(2)
    gPB(1)
    query_keys()
    gC2(4); gAF(4); gA2(4)
    ready(6); gB1(6)
    gC1(5); gA1(5); gB2(5)
    gB3(4)
    gCF(4); gC3(4); gA3(4)
    gBF(3); gPA(3); gPC(3)
    gPB(2)
    values()
    attend(0, 5)
    gC2(5); gAF(5); gA2(5)
    gC1(6); gA1(6); gB2(6)
    gB3(5)
    attend(5, 11)
    gCF(5); gC3(5); gA3(5)
    gBF(4); gPA(4); gPC(4)
    gPB(3)
    attend(11, 16)
    second_part()
    gC2(6); gAF(6); gA2(6)
    gB3(6)
    widen_load(3)
    widen(0, 0)
    gCF(6); gC3(6); gA3(6)
    gBF(5); gPA(5); gPC(5)
    gPB(4)
    widen(1, 2)
    for cp in pc.values(): cp.wait_send()
    swap(0, zz.at[2 * o], xl.at[0])
    swap(1, gm, xr.at[0])
    swap(3, m, xl.at[2])
    widen_load(4)
    reduce1(0)
    gBF(6); gPA(6); gPC(6); gPB(5)
    pair_loop(widen, 1)
    swap(2, zz.at[2 * o + 1], xl.at[1])
    narrow_load(5)
    reduce1(1)
    gPB(6)
    reduce2(0)
    pair_loop(narrow, 0)
    swap(4, gu.at[2 * o], xr.at[1])
    narrow_load(6)
    reduce3(0)
    reduce1(2); reduce2(1)
    pair_loop(narrow, 1)
    swap(5, gu.at[2 * o + 1], xr.at[2])
    weight(0, fc1_o.at[0]); weight(1, fc1_o.at[1])
    reduce4(0)
    reduce1(3)
    reduce2(2); reduce3(1)
    widen_back()
    late_left()
    norm_two()
    reduce5(0); reduce4(1)
    attend_back(0, 5)
    reduce2(3); reduce3(2)
    attend_back(5, 16)
    late_right()
    reduce1(4)
    reduce5(1); reduce4(2); reduce3(3)
    reduce1(5); reduce2(4)
    project_back()
    reduce5(2); reduce4(3)
    norm_one()
    vec_send()
    pltpu.make_async_copy(j_o.at[c], side.at[0], isem.at[7]).wait()
    reduce2(5); reduce3(4)
    reduce1(6)
    vec_first()
    join_back(0, in_o)
    reduce5(3); reduce4(4)
    join_back(1, sk_o)
    settle_pair(3)
    reduce3(5); reduce2(6)
    vec_last()
    reduce5(4); reduce4(5); settle_pair(4)
    finish()
    finish_out()
    reduce3(6)
    reduce5(5); settle_pair(5)
    reduce4(6)
    reduce5(6)
    pltpu.make_async_copy(tok.at[1], sk_o.at[:, 0, :], osem.at[4]).wait()
    pltpu.make_async_copy(tok.at[0], out_o.at[:, 0, :], osem.at[2]).wait()
    for n, (a, b) in zip((5, 6, 7, 8, 9), ((skip_f, skip_g), (qkv_f, qkv_g), (proj_f, proj_g), (fc1_f, fc1_g), (fc2_f, fc2_g))):
        pltpu.make_async_copy(a, b, osem.at[n]).wait()
    for j in range(3, 7): settle(j)
    for cp in whens: pl.when(middle)(lambda: cp.wait_send())
    for cp in waits: cp.wait_send()
    for cp in pcopies.values(): cp.wait_send()
    for cp in vcopies: cp.wait_send()
    for cp in xcopies.values(): cp.wait_send()


def block(cap, skip, qkv, proj, fc1, fc2, vectors, block_in, skip_in, out_grad, dpn):
    _, length, wide = block_in.shape
    Z = dpn // 2; rows = skip.shape[0] // wide
    padded = -(-length // 16) * 16
    nt = wide // 128
    tb = 128 * max(1, nt // 9); tc = 128 * (nt // 3); ta = wide - tb - tc
    tiles = (ta, tb, tc)
    U = (Z, 2, 2, rows, wide)
    hbm = pl.BlockSpec(memory_space=pl.ANY); vm = pl.BlockSpec(memory_space=pltpu.VMEM)
    ns = 26
    nr = 19
    nv = vectors.shape[0]
    D = pltpu.SemaphoreType.DMA
    V = pltpu.VMEM
    hp = -(-rows // 2 // 8) * 8
    S = jax.ShapeDtypeStruct
    act = (padded, wide)
    flat = [(w.shape[0] // 128, 128) for w in (skip, qkv, proj, fc1, fc2)]
    tokens = (length, 1, wide)
    nb = 4
    res = pl.pallas_call(
        functools.partial(block_kernel, Z, wide, rows, tiles, length, padded),
        out_shape=(S(tokens, F32),) * 3 + tuple(S(s, F32) for s in flat) + (S((nv,), F32),
                   S((Z, 2, 2, 2, rows, wide), BF), S((4,) + U, BF), S((4,) + U, BF), S((4,) + U, BF), S((2,) + act, BF), S(act, F32), S(act, F32)),
        in_specs=[pl.BlockSpec(memory_space=pltpu.SMEM)] + [hbm] * 5 + [vm] + [hbm] * 3,
        out_specs=(hbm,) * 8 + (vm,) + (hbm,) * 7,
        scratch_shapes=[V(s, F32) for s in flat] + [
                        V((7, rows, wide), BF), V((4, hp, wide), F32), V((4, hp, wide), F32), V((4, hp, wide), F32),
                        V((dpn, 1, nv), F32), V((1, nv * dpn), F32), V((4, 1, wide), F32), V((dpn, 1, nv), F32), V((dpn - 1, 1, nv), F32), V((4, 1, nv), F32),
                        V((2, length, wide), F32),
                        V((4,) + act, BF), V((2,) + act, BF), V(act, F32), V((2,) + act, BF), V((3,) + act, BF), V(act, BF), V((4,) + act, BF), V((4,) + act, BF), V(act, BF),
                        V(act, F32), V(act, F32), V((11, 1, wide), F32), V((3, 8, wide), F32), V((2,) + U, BF),
                        V((3,) + act, BF), V((3,) + act, BF), V((nb,) + U, BF),
                        V((nb, 2, Z, rows, ta), BF), V((nb, Z, rows, ta), BF), V((nb, 3, rows, ta), BF), V((nb, rows, ta), BF),
                        V((nb, Z, 2, rows, tc), BF), V((nb, 3, 2, rows, tc), BF), V((nb, 2, rows, tc), BF), V((nb, rows, tc), BF),
                        V((nb, 3, 2, 2, rows, tb), BF), V((nb, 2, 2, rows, tb), BF), V((nb, 2, rows, tb), BF), V((nb, rows, tb), BF),
                        D((7, ns)), D((7, ns)), D((7,)), D((4,)), D((4,)), D((dpn - 1,)), D((dpn - 1,)), D((9,)), D((11,)), D((2,)),
                        D((7, nr)), D((7, nr)), D((12,)), D((12,)), D((4,)), D((4,)), D((dpn - 1,)), D((dpn - 1,)), D((3,)), D((3,)), pltpu.SemaphoreType.REGULAR],
        compiler_params=pltpu.CompilerParams(collective_id=0, has_side_effects=True, vmem_limit_bytes=67043328),
        name="block",
    )(cap, *(w.reshape(-1, 128) for w in (skip, qkv, proj, fc1, fc2)), vectors,
      *(v.reshape(tokens) for v in (block_in, skip_in, out_grad)))
    shape = block_in.shape
    res = hand_out(res[:9])
    return tuple(r.reshape(shape) for r in res[:3]) + tuple(r.reshape(-1) for r in res[3:])


def hand_out_kernel(*refs):
    n = (len(refs) - 2) // 3
    src, dst, buf, (first, second) = refs[:n], refs[n:2 * n], refs[2 * n:3 * n], refs[3 * n:]
    ins = [pltpu.make_async_copy(src[i], buf[i], first.at[i]) for i in range(n)]
    outs = [pltpu.make_async_copy(buf[i], dst[i], second.at[i]) for i in range(n)]
    for cp in ins: cp.start()
    for a, b in zip(ins, outs):
        a.wait()
        b.start()
    for cp in outs: cp.wait()


def hand_out(arrays):
    hbm = pl.BlockSpec(memory_space=pl.ANY)
    n = len(arrays)
    return tuple(pl.pallas_call(
        hand_out_kernel,
        out_shape=tuple(jax.ShapeDtypeStruct(v.shape, v.dtype) for v in arrays),
        in_specs=[hbm] * n, out_specs=(hbm,) * n,
        scratch_shapes=[pltpu.VMEM(v.shape, v.dtype) for v in arrays] + [pltpu.SemaphoreType.DMA((n,))] * 2,
        compiler_params=pltpu.CompilerParams(vmem_limit_bytes=67043328),
        name="hand_out",
    )(*arrays))


def whole_rows(width, dp, fsdp, items, heads, hidden, length):
    return (
        fsdp == 4 and dp == 8 and width % (dp * 16) == 0 and items == 1 and hidden == 4 * width
        and width % SPLIT == 0 and -(-length // 16) * 16 % STEP == 0 and width // heads <= 128
    )


def body(block_in, skip_in, out_grad, caption_len, skip_w, qkv_w, proj_w, fc1_w, fc2_w, vectors):
    items, length, width = block_in.shape
    if whole_rows(width, lax.axis_size("dp"), lax.axis_size("fsdp"), items, HEADS, FF, length):
        return block(
            caption_len, skip_w, qkv_w, proj_w, fc1_w, fc2_w, vectors, block_in, skip_in, out_grad,
            lax.axis_size("dp"),
        )
    heads = HEADS
    head_dim = width // heads
    hidden = FF
    rows = items * length
    scale = head_dim ** (-0.5)
    gathered = (
        lax.all_gather(skip_w.astype(jnp.bfloat16), ("dp", "fsdp"), axis=0, tiled=True),
        lax.all_gather(qkv_w.astype(jnp.bfloat16), ("dp", "fsdp"), axis=0, tiled=True),
        lax.all_gather(proj_w.astype(jnp.bfloat16), ("dp", "fsdp"), axis=0, tiled=True),
        lax.all_gather(fc1_w.astype(jnp.bfloat16), ("dp", "fsdp"), axis=0, tiled=True),
        lax.all_gather(fc2_w.astype(jnp.bfloat16), ("dp", "fsdp"), axis=0, tiled=True),
    )
    skip_m, qkv_m, proj_m, fc1_m, fc2_m = unpack(gathered, width, hidden)
    vec = lax.all_gather(vectors, "dp", axis=0, tiled=True)
    gain_one = vec[0:width]
    shift_one = vec[width : 2 * width]
    gain_two = vec[2 * width : 3 * width]
    shift_two = vec[3 * width : 4 * width]
    skip_bias = vec[4 * width : 5 * width]
    proj_bias = vec[5 * width : 6 * width]
    fc2_bias = vec[6 * width : 7 * width]
    fc1_bias = vec[7 * width :]
    valid = key_valid(caption_len, length, CAPTION)
    joined = jnp.concatenate([block_in, skip_in], -1).reshape(rows, 2 * width).astype(jnp.bfloat16)
    first = product(joined, skip_m) + skip_bias
    normed_one = norm_rows(first, gain_one, shift_one).astype(jnp.bfloat16)
    triple = (
        product(normed_one, qkv_m).astype(jnp.bfloat16).reshape(items, length, 3, heads, head_dim)
    )
    query = triple[:, :, 0]
    keys = triple[:, :, 1]
    values = triple[:, :, 2]
    scores = attention_scores(query, keys, valid, scale)
    top = jnp.max(scores, -1, keepdims=True)
    expd = jnp.exp(scores - top)
    total = jnp.sum(expd, -1, keepdims=True)
    probs = expd / total
    log_total = top + jnp.log(total)
    mixed = (
        jnp.einsum(
            "ihst,ithd->ishd",
            probs.astype(jnp.bfloat16),
            values,
            preferred_element_type=jnp.float32,
        )
        .astype(jnp.bfloat16)
        .reshape(rows, width)
    )
    second = first + (product(mixed, proj_m) + proj_bias)
    normed_two = norm_rows(second, gain_two, shift_two).astype(jnp.bfloat16)
    inner = product(normed_two, fc1_m) + fc1_bias
    active = gelu_exact(inner).astype(jnp.bfloat16)
    block_out = second + (product(active, fc2_m) + fc2_bias)
    again = (
        lax.all_gather(skip_w.astype(jnp.bfloat16), ("dp", "fsdp"), axis=0, tiled=True),
        lax.all_gather(qkv_w.astype(jnp.bfloat16), ("dp", "fsdp"), axis=0, tiled=True),
        lax.all_gather(proj_w.astype(jnp.bfloat16), ("dp", "fsdp"), axis=0, tiled=True),
        lax.all_gather(fc1_w.astype(jnp.bfloat16), ("dp", "fsdp"), axis=0, tiled=True),
        lax.all_gather(fc2_w.astype(jnp.bfloat16), ("dp", "fsdp"), axis=0, tiled=True),
    )
    skip_m, qkv_m, proj_m, fc1_m, fc2_m = unpack(again, width, hidden)
    grad_out = out_grad.reshape(rows, width)
    grad_mlp = grad_out.astype(jnp.bfloat16)
    d_fc2_bias = column_sum(grad_mlp)
    d_active = right_product(grad_mlp, fc2_m)
    gelu_value, gelu_pull = jax.vjp(gelu_exact, inner)
    grad_inner = gelu_pull(d_active)[0].astype(jnp.bfloat16)
    d_fc1_bias = column_sum(grad_inner)
    d_normed_two = right_product(grad_inner, fc1_m)
    norm_value_two, norm_pull_two = jax.vjp(norm_rows, second, gain_two, shift_two)
    d_second_norm, d_gain_two, d_shift_two = norm_pull_two(d_normed_two)
    grad_second = grad_out + d_second_norm
    grad_attn = grad_second.astype(jnp.bfloat16)
    d_proj_bias = column_sum(grad_attn)
    grad_mixed = (
        right_product(grad_attn, proj_m)
        .astype(jnp.bfloat16)
        .reshape(items, length, heads, head_dim)
    )
    again_scores = attention_scores(query, keys, valid, scale)
    again_probs = jnp.exp(again_scores - log_total)
    d_probs = jnp.einsum("ishd,ithd->ihst", grad_mixed, values, preferred_element_type=jnp.float32)
    inner_sum = jnp.sum(again_probs * d_probs, -1, keepdims=True)
    grad_scores = (again_probs * (d_probs - inner_sum)).astype(jnp.bfloat16)
    d_query = (
        jnp.einsum("ihst,ithd->ishd", grad_scores, keys, preferred_element_type=jnp.float32) * scale
    )
    d_keys = (
        jnp.einsum("ihst,ishd->ithd", grad_scores, query, preferred_element_type=jnp.float32)
        * scale
    )
    d_values = jnp.einsum(
        "ihst,ishd->ithd",
        again_probs.astype(jnp.bfloat16),
        grad_mixed,
        preferred_element_type=jnp.float32,
    )
    grad_triple = (
        jnp.stack([d_query, d_keys, d_values], 2).astype(jnp.bfloat16).reshape(rows, 3 * width)
    )
    d_normed_one = right_product(grad_triple, qkv_m)
    norm_value_one, norm_pull_one = jax.vjp(norm_rows, first, gain_one, shift_one)
    d_first_norm, d_gain_one, d_shift_one = norm_pull_one(d_normed_one)
    grad_first = (grad_second + d_first_norm).astype(jnp.bfloat16)
    d_skip_bias = column_sum(grad_first)
    grad_joined = right_product(grad_first, skip_m).reshape(items, length, 2 * width)
    in_grad = grad_joined[:, :, 0:width]
    skip_grad = grad_joined[:, :, width:]
    owners = lax.axis_size(("dp", "fsdp"))
    pairs = (
        (joined, grad_first),
        (normed_one, grad_triple),
        (mixed, grad_attn),
        (normed_two, grad_inner),
        (active, grad_mlp),
    )
    shard_sizes = [pair[0].shape[1] * pair[1].shape[1] // owners for pair in pairs]
    blocks = []
    for pair, owner_share in zip(pairs, shard_sizes):
        blocks.append(
            flat_piece(pair[0], pair[1]).reshape(1 * lax.axis_size(("dp", "fsdp")), owner_share)
        )
    owned = lax.psum_scatter(
        jnp.concatenate(blocks, 1), ("dp", "fsdp"), scatter_dimension=0, tiled=True
    ).reshape(-1)
    pieces = []
    offset = 0
    for share in shard_sizes:
        pieces.append(owned[offset : offset + share])
        offset = offset + share
    vec_grad = jnp.concatenate(
        [
            d_gain_one,
            d_shift_one,
            d_gain_two,
            d_shift_two,
            d_skip_bias,
            d_proj_bias,
            d_fc2_bias,
            d_fc1_bias,
        ]
    )
    vec_rows = lax.psum_scatter(vec_grad, "dp", scatter_dimension=0, tiled=True)
    vec_total = lax.psum(vec_rows, "fsdp")
    return (
        block_out.reshape(items, length, width),
        in_grad,
        skip_grad,
        pieces[0],
        pieces[1],
        pieces[2],
        pieces[3],
        pieces[4],
        vec_total,
    )


def solution(mesh):
    placed = (
        P(("dp", "fsdp"), None, None),
        P(("dp", "fsdp"), None, None),
        P(("dp", "fsdp"), None, None),
        P(("dp", "fsdp")),
        P(("dp", "fsdp")),
        P(("dp", "fsdp")),
        P(("dp", "fsdp")),
        P(("dp", "fsdp")),
        P(("dp", "fsdp")),
        P("dp"),
    )
    return jax.shard_map(
        body,
        mesh=mesh,
        in_specs=placed,
        out_specs=(
            P(("dp", "fsdp"), None, None),
            P(("dp", "fsdp"), None, None),
            P(("dp", "fsdp"), None, None),
            P(("dp", "fsdp")),
            P(("dp", "fsdp")),
            P(("dp", "fsdp")),
            P(("dp", "fsdp")),
            P(("dp", "fsdp")),
            P("dp"),
        ),
        check_vma=False,
    )
```
